32 devices in a mesh: dp: 8 (over z, y), patch: 4 (over x, core).
Axes of the slice: x: 2, y: 2, z: 4, core: 2. Of those that a mesh axis runs over, the one named last changes fastest.
Arguments:
- media_tokens: float32 [72, 256, 1024], P('dp', 'patch'), may hold values from -6 to 6
- patch_mask: int32 [72, 256], P('dp', 'patch'), may hold values from 0 to 1, as said below
- latents: float32 [72, 64, 1024], P('dp', 'patch'), may hold values from -6 to 6
- cotangent: float32 [72, 64, 1024], P('dp', 'patch'), may hold values from -6 to 6
- weights: float32 [12, 1048576], P(None, ('dp', 'patch')), may hold values from -8 to 8
- weights_first: float32 [12, 1048576], P(None, ('dp', 'patch')), may hold values from -1 to 1
- weights_second: float32 [12, 1048576], P(None, ('dp', 'patch')), may hold values from 0 to 1
- weights_average: float32 [12, 1048576], P(None, ('dp', 'patch')), may hold values from -8 to 8
- norm_params: float32 [6, 1024], replicated, may hold values from -0.2 to 0.2
- norm_first: float32 [6, 1024], replicated, may hold values from -1 to 1
- norm_second: float32 [6, 1024], replicated, may hold values from 0 to 1
- norm_average: float32 [6, 1024], replicated, may hold values from -0.2 to 0.2
Outputs:
- latents_out: float32 [72, 64, 1024], P('dp', 'patch')
- media_grad: float32 [72, 256, 1024], P('dp', 'patch')
- latents_grad: float32 [72, 64, 1024], P('dp', 'patch')
- grad_norm: float32 [], replicated
- new_weights: float32 [12, 1048576], P(None, ('dp', 'patch'))
- weights_bf16: bfloat16 [12, 1048576], P(None, ('dp', 'patch'))
- new_first: float32 [12, 1048576], P(None, ('dp', 'patch'))
- new_second: float32 [12, 1048576], P(None, ('dp', 'patch'))
- new_average: float32 [12, 1048576], P(None, ('dp', 'patch'))
- new_norm_params: float32 [6, 1024], replicated
- new_norm_first: float32 [6, 1024], replicated
- new_norm_second: float32 [6, 1024], replicated
- new_norm_average: float32 [6, 1024], replicated
- ffn_norm_grads: float32 [2, 1024], replicated
The draws below stay inside these ranges and needn't reach their ends.
Inputs may be any that keep to these rules, and one draw needn't show every extreme that they name: `patch_mask`: in each image the real patches come first; at least 64 are real, and image 0 has exactly 64.
All inputs are finite; a program needn't handle non-finite values.
Results may differ from the reference program's by a relative error of at most 0.018.
Values may be sent and summed in bfloat16 or wider, within the bound.
A program may use at most 256 MiB of HBM per device.

```python
import math
import jax
import jax.numpy as jnp
from jax import lax

D = 1024
HEADS = 16
HEAD_DIM = 64
FF = 4096
LAT = 64
PATCHES = 256
STEP = 7
IMAGES = 72
BLOCKS = 12


def weight_scale():
    block_ids = jnp.arange(BLOCKS)
    inner_scale = 1.0 / math.sqrt(D)
    return jnp.where(block_ids < 3, inner_scale, jnp.where(block_ids == 3, 8.0 * inner_scale, jnp.where(block_ids < 4 + FF // D, inner_scale, 1.0 / math.sqrt(FF))))


def grad_energy():
    return D * D * (3.0 + 0.0225 + FF // D * 0.41)


def grad_scale():
    block_ids = jnp.arange(BLOCKS)
    share_rows = jnp.where(block_ids < 3, 1.0, jnp.where(block_ids == 3, 0.15, jnp.where(block_ids < 4 + FF // D, 0.5, 0.4)))
    return share_rows / math.sqrt(grad_energy())


def weight_draw(key):
    normal_part = jnp.clip(jax.random.normal(key, (BLOCKS, D * D), jnp.float32), -6.0, 6.0)
    return normal_part * weight_scale()[:, None]


def norm_draw(key):
    return 0.03 * jnp.clip(jax.random.normal(key, (6, D), jnp.float32), -6.0, 6.0)


def draw_weights(key, part):
    return weight_draw(jax.random.fold_in(key, 11))


def draw_weights_average(key, part):
    return weight_draw(jax.random.fold_in(key, 12))


def draw_weights_first(key, part):
    normal_part = jnp.clip(jax.random.normal(jax.random.fold_in(key, 13), (BLOCKS, D * D), jnp.float32), -6.0, 6.0)
    return normal_part * (0.11 * grad_scale())[:, None]


def draw_weights_second(key, part):
    spread = jnp.exp(jax.random.uniform(jax.random.fold_in(key, 14), (BLOCKS, D * D), jnp.float32, 0.0, math.log(4.0)))
    scale_rows = grad_scale()
    return spread * (0.001 * scale_rows * scale_rows)[:, None]


def draw_norm_params(key, part):
    return norm_draw(jax.random.fold_in(key, 21))


def draw_norm_average(key, part):
    return norm_draw(jax.random.fold_in(key, 22))


def draw_norm_first(key, part):
    entry_scale = 3.0 / math.sqrt(grad_energy())
    normal_part = jnp.clip(jax.random.normal(jax.random.fold_in(key, 23), (6, D), jnp.float32), -6.0, 6.0)
    return normal_part * (0.11 * entry_scale)


def draw_norm_second(key, part):
    entry_scale = 3.0 / math.sqrt(grad_energy())
    spread = jnp.exp(jax.random.uniform(jax.random.fold_in(key, 24), (6, D), jnp.float32, 0.0, math.log(4.0)))
    return spread * (0.001 * entry_scale * entry_scale)


def draw_patch_mask(key, part):
    counts = jax.random.randint(jax.random.fold_in(key, 31), (IMAGES,), PATCHES // 4, PATCHES + 1)
    counts = jnp.where(jnp.arange(IMAGES) == 0, PATCHES // 4, counts)
    return (jnp.arange(PATCHES)[None, :] < counts[:, None]).astype(jnp.int32)


def levels(stream_key, dims, cuts, smallest, largest):
    def one(position, shards_of):
        heights = jax.random.uniform(jax.random.fold_in(jax.random.fold_in(stream_key, 6), position), (shards_of,), jnp.float32, smallest / len(cuts), largest / len(cuts))
        return jnp.repeat(jnp.exp(heights), dims[position] // shards_of).reshape((-1,) + (1,) * (len(dims) - position - 1))

    factor_of = one(*cuts[0])
    for cut in cuts[1:]:
        factor_of = factor_of * one(*cut)
    return factor_of


def gaussian(key, dims, width, most, split=(), kind=jnp.bfloat16):
    factor_of = levels(key, dims, split, -0.22, 0.18) if split else 1.0
    values = jax.random.normal(key, dims, jnp.float32) * width * factor_of
    return jnp.minimum(jnp.maximum(values, -most), most).astype(kind)


def setup_inputs(seed: int = 0) -> dict:
    key_of = jax.random.split(jax.random.key(seed), 13)
    media_tokens = gaussian(key_of[0], (IMAGES, PATCHES, D), 1.0, 6.0, ((0, 8), (1, 4)), jnp.float32)
    patch_mask = draw_patch_mask(jax.random.fold_in(key_of[12], 71), 0)
    latents = gaussian(key_of[2], (IMAGES, LAT, D), 1.0, 6.0, ((0, 8), (1, 4)), jnp.float32)
    cotangent = gaussian(key_of[3], (IMAGES, LAT, D), 1.0, 6.0, ((0, 8), (1, 4)), jnp.float32)
    weights = draw_weights(jax.random.fold_in(key_of[12], 71), 0)
    weights_first = draw_weights_first(jax.random.fold_in(key_of[12], 71), 0)
    weights_second = draw_weights_second(jax.random.fold_in(key_of[12], 71), 0)
    weights_average = draw_weights_average(jax.random.fold_in(key_of[12], 71), 0)
    norm_params = draw_norm_params(jax.random.fold_in(key_of[12], 71), 0)
    norm_first = draw_norm_first(jax.random.fold_in(key_of[12], 71), 0)
    norm_second = draw_norm_second(jax.random.fold_in(key_of[12], 71), 0)
    norm_average = draw_norm_average(jax.random.fold_in(key_of[12], 71), 0)
    return {"media_tokens": media_tokens, "patch_mask": patch_mask, "latents": latents, "cotangent": cotangent, "weights": weights, "weights_first": weights_first, "weights_second": weights_second, "weights_average": weights_average, "norm_params": norm_params, "norm_first": norm_first, "norm_second": norm_second, "norm_average": norm_average}


highest = lax.Precision.HIGHEST

@jax.custom_vjp
def low(v):
    return lax.optimization_barrier(v.astype(jnp.bfloat16)).astype(jnp.float32)

@jax.custom_vjp
def low_back(v):
    return v

def low_keep(v):
    return (low(v), None)

def low_pass(kept, grad):
    return (grad,)

def back_keep(v):
    return (v, None)

def back_low(kept, grad):
    return (low(grad),)
low.defvjp(low_keep, low_pass)
low_back.defvjp(back_keep, back_low)

def layer_norm(values, gain_row, shift_row):
    average = lax.optimization_barrier(jnp.mean(values, axis=-1, keepdims=True))
    centred = values - average
    spread = lax.optimization_barrier(jnp.mean(centred * centred, axis=-1, keepdims=True))
    return centred * lax.rsqrt(spread + 1e-05) * gain_row + shift_row

def forward(media_part, latent_part, valid_keys, matrices, norm_rows):
    group_size = media_part.shape[0]
    matrices = low(matrices)
    w_query = matrices[0:D]
    w_key = matrices[D:2 * D]
    w_value = matrices[2 * D:3 * D]
    w_out = matrices[3 * D:4 * D]
    up_rows = matrices[4 * D:4 * D + FF]
    w_down = matrices[4 * D + FF:]
    media_low = low(layer_norm(media_part, 1.0 + norm_rows[0], norm_rows[1]))
    latent_low = low(layer_norm(latent_part, 1.0 + norm_rows[2], norm_rows[3]))
    queries = low_back(low(jnp.einsum('gld,de->gle', latent_low, w_query, precision=highest)))
    key_input = jnp.concatenate([media_low, latent_low], axis=1)
    key_rows = low_back(low(jnp.einsum('gkd,de->gke', key_input, w_key, precision=highest)))
    value_rows = low_back(low(jnp.einsum('gkd,de->gke', key_input, w_value, precision=highest)))
    key_total = PATCHES + LAT
    query_heads = queries.reshape(group_size, LAT, HEADS, HEAD_DIM)
    key_heads = key_rows.reshape(group_size, key_total, HEADS, HEAD_DIM)
    value_heads = value_rows.reshape(group_size, key_total, HEADS, HEAD_DIM)
    raw_scores = jnp.einsum('gqhe,gkhe->ghqk', query_heads, key_heads, precision=highest) * (1.0 / math.sqrt(HEAD_DIM))
    scores = low_back(jnp.where(valid_keys[:, None, None, :], raw_scores, -1e+30))
    attn_probs = jax.nn.softmax(scores, axis=-1)
    attended = jnp.einsum('ghqk,gkhe->gqhe', low(attn_probs), value_heads, precision=highest).reshape(group_size, LAT, D)
    attended = low_back(low(attended))
    hidden = latent_part + low_back(jnp.einsum('gld,de->gle', attended, w_out, precision=highest))
    ffn_low = low(layer_norm(hidden, 1.0 + norm_rows[4], norm_rows[5]))
    up_proj = low_back(jnp.einsum('gld,fd->glf', ffn_low, up_rows, precision=highest))
    active = low(jax.nn.gelu(up_proj, approximate=False))
    return hidden + low_back(jnp.einsum('glf,fd->gld', active, w_down, precision=highest))

def adamw_update(parameter, first_m, second_m, average, gradient, factor, decay_rate):
    clipped = gradient * factor
    new_first = 0.9 * first_m + 0.1 * clipped
    new_second = 0.999 * second_m + 0.001 * clipped * clipped
    first_hat = new_first / (1.0 - 0.9 ** STEP)
    second_hat = new_second / (1.0 - 0.999 ** STEP)
    new_param = parameter - 0.02 * (first_hat / (jnp.sqrt(second_hat) + 1e-08) + decay_rate * parameter)
    new_avg = 0.8 * average + 0.2 * new_param
    return (new_param, new_first, new_second, new_avg)

def reference(media_tokens, patch_mask, latents, cotangent, weights, weights_first, weights_second, weights_average, norm_params, norm_first, norm_second, norm_average):
    matrices = weights.reshape(BLOCKS * D, D)
    group_size = math.gcd(IMAGES, 8)
    group_count = IMAGES // group_size
    valid_keys = jnp.concatenate([patch_mask, jnp.ones((IMAGES, LAT), jnp.int32)], axis=1) > 0
    stacked = (media_tokens.reshape(group_count, group_size, PATCHES, D), valid_keys.reshape(group_count, group_size, PATCHES + LAT), latents.reshape(group_count, group_size, LAT, D), cotangent.reshape(group_count, group_size, LAT, D))

    def one_group(running, pieces):
        media_part, valid_part, latent_part, cot_part = pieces

        def one_pass(media_in, latent_in, matrix_in, norm_in):
            return forward(media_in, latent_in, valid_part, matrix_in, norm_in)
        result, pullback = jax.vjp(one_pass, media_part, latent_part, matrices, norm_params)
        grad_media, grad_latent, grad_matrix, grad_norms = pullback(cot_part)
        return ((running[0] + grad_matrix, running[1] + grad_norms), (result, grad_media, grad_latent))
    initial = (jnp.zeros((BLOCKS * D, D), jnp.float32), jnp.zeros((6, D), jnp.float32))
    (sum_matrix, sum_norms), (outputs, grad_media, grad_latent) = lax.scan(one_group, initial, stacked)
    grad_blocks = sum_matrix.reshape(BLOCKS, D * D)
    grad_norm = jnp.sqrt(jnp.sum(grad_blocks * grad_blocks) + jnp.sum(sum_norms * sum_norms))
    factor = jnp.minimum(1.0, 1.0 / (grad_norm + 1e-06))
    new_w, new_first, new_second, new_avg = adamw_update(weights, weights_first, weights_second, weights_average, grad_blocks, factor, 0.1)
    new_n, new_nf, new_ns, new_na = adamw_update(norm_params, norm_first, norm_second, norm_average, sum_norms, factor, 0.0)
    return (outputs.reshape(IMAGES, LAT, D), grad_media.reshape(IMAGES, PATCHES, D), grad_latent.reshape(IMAGES, LAT, D), grad_norm, new_w, new_w.astype(jnp.bfloat16), new_first, new_second, new_avg, new_n, new_nf, new_ns, new_na, sum_norms[4:6])
```

```python
import functools
import math

import jax
import jax.numpy as jnp
from jax import lax
from jax.experimental import pallas as pl
from jax.experimental.pallas import tpu as pltpu
from jax.sharding import PartitionSpec as P

HEADS = 16
FF = 4096
STEP = 7
MESH = pl.DeviceIdType.MESH
F32 = jnp.float32
BF16 = jnp.bfloat16
ANY = pl.BlockSpec(memory_space=pl.ANY)
VMEM = pl.BlockSpec(memory_space=pltpu.VMEM)
DMA = pltpu.SemaphoreType.DMA
VMEM_LIMIT = 64 * 1024 * 1024 - 65536


def struct(shape, kind):
    return jax.ShapeDtypeStruct(shape, kind)


def place():
    d, p = lax.axis_index("dp"), lax.axis_index("patch")
    return d, p, lax.div(d, 2), lax.rem(d, 2), lax.div(p, 2), lax.rem(p, 2)


def remote(src, dst, send, recv, to):
    return pltpu.make_async_remote_copy(
        src_ref=src, dst_ref=dst, send_sem=send, recv_sem=recv, device_id=to, device_id_type=MESH
    )


def meet(always, maybe=()):
    barrier = pltpu.get_barrier_semaphore()
    count = len(always)
    for to in always:
        pl.semaphore_signal(barrier, inc=1, device_id=to, device_id_type=MESH)
    for there, to in maybe:

        @pl.when(there)
        def _(to=to):
            pl.semaphore_signal(barrier, inc=1, device_id=to, device_id_type=MESH)

        count = count + there.astype(jnp.int32)
    pl.semaphore_wait(barrier, count)


def patch_peers(d, p, size):
    return [(d, lax.rem(p + k, size)) for k in range(1, size)]


def params(number):
    return pltpu.CompilerParams(
        collective_id=number, has_side_effects=True, vmem_limit_bytes=VMEM_LIMIT
    )


def spread_kernel(chain, size, qs, wos, ups, dns, nms, nls, dys, cns,
                  wqkv, wo, up, dn, nm, nl, dy, cn,
                  loc, a_s, a_r, su, sd, sy, rz, ry, xs, xr, cs, cr):
    d, p, z, y, x, c = place()
    above, below = z + 1 < chain, z > 0
    up_dev, dn_dev = ((z + 1) * 2 + y, p), ((z - 1) * 2 + y, p)
    y_dev, x_dev, c_dev = (z * 2 + 1 - y, p), (d, (1 - x) * 2 + c), (d, x * 2 + 1 - c)
    px, pc = (1 - x) * 2 + c, x * 2 + 1 - c
    pd = (1 - x) * 2 + 1 - c
    meet(patch_peers(d, p, size) + [y_dev], [(above, up_dev), (below, dn_dev)])

    own = [
        (qs.at[p], wqkv.at[:, d, p]), (wos, wo.at[d, p]), (ups, up.at[:, d]), (dns, dn.at[:, d]),
        (nms, nm.at[:, p]), (nls, nl.at[:, p]), (dys, dy.at[p]), (cns, cn.at[p]),
    ]
    local = [pltpu.make_async_copy(a, b, loc.at[i]) for i, (a, b) in enumerate(own)]
    for copy in local:
        copy.start()
    swaps = []
    for k in range(1, size):
        q = lax.rem(p + k, size)
        swaps.append(remote(qs.at[q], wqkv.at[:, d, p], a_s.at[k], a_r.at[k], (d, q)))
    for copy in swaps:
        copy.start()

    rows = [(nms, nm), (nls, nl), (cns, cn), (dys, dy)]

    def slot(j, q):
        ref = rows[j][1] if j < 4 else wo
        return ref.at[q] if j in (2, 3) else ref.at[:, q]

    def row_copies(j):
        src = rows[j][0] if j < 4 else slot(j, p)
        return (
            remote(src, slot(j, p), xs.at[j], xr.at[j], x_dev),
            remote(src, slot(j, p), cs.at[j, 0], cr.at[j, 0], c_dev),
            remote(slot(j, px), slot(j, px), cs.at[j, 1], cr.at[j, 1], c_dev),
        )

    def start_rows(j):
        to_x, to_c, _ = row_copies(j)
        to_x.start()
        to_c.start()

    def pass_rows(j):
        to_x, _, on = row_copies(j)
        to_x.wait_recv()
        on.start()

    def end_rows(j):
        to_x, to_c, on = row_copies(j)
        to_c.wait_recv()
        on.wait_recv()
        to_x.wait_send()
        to_c.wait_send()
        on.wait_send()

    for j in range(4):
        start_rows(j)

    def piece(i, dd):
        return (wqkv.at[:, dd], wo.at[dd, p], up.at[:, dd], dn.at[:, dd])[i]

    first = (wqkv.at[:, d], wos, ups, dns)

    def hop(i, zz, sends, to, own_src=False):
        src = first[i] if own_src else piece(i, zz * 2 + y)
        return remote(src, piece(i, zz * 2 + y), sends.at[i, zz], rz.at[i, zz], to)

    def over(i, zz, own_src=False):
        src = first[i] if own_src else piece(i, zz * 2 + y)
        return remote(src, piece(i, zz * 2 + y), sy.at[i, zz], ry.at[i, zz], y_dev)

    def start_own(i):
        @pl.when(above)
        def _():
            hop(i, z, su, up_dev, True).start()

        @pl.when(below)
        def _():
            hop(i, z, sd, dn_dev, True).start()

        over(i, z, True).start()

    def forward(i):
        def step(s, carry):
            @pl.when(z - s >= 0)
            def _():
                hop(i, z - s, su, up_dev).wait_recv()

                @pl.when(above)
                def _():
                    hop(i, z - s, su, up_dev).start()

                over(i, z - s).start()

            @pl.when(z + s < chain)
            def _():
                hop(i, z + s, sd, dn_dev).wait_recv()

                @pl.when(below)
                def _():
                    hop(i, z + s, sd, dn_dev).start()

                over(i, z + s).start()

            return carry

        lax.fori_loop(1, chain, step, 0)

    def arrived(i):
        def step(zz, carry):
            src = piece(i, zz * 2 + 1 - y)
            remote(src, src, sy.at[i, zz], ry.at[i, zz], y_dev).wait_recv()
            return carry

        lax.fori_loop(0, chain, step, 0)

    def sent(i):
        def step(zz, carry):
            over(i, zz).wait_send()

            @pl.when(jnp.logical_and(above, zz <= z))
            def _():
                hop(i, zz, su, up_dev).wait_send()

            @pl.when(jnp.logical_and(below, zz >= z))
            def _():
                hop(i, zz, sd, dn_dev).wait_send()

            return carry

        lax.fori_loop(0, chain, step, 0)

    local[0].wait()
    for copy in swaps:
        copy.wait_recv()
    start_own(0)
    start_own(1)
    forward(0)
    start_own(2)
    forward(1)
    start_own(3)
    local[1].wait()
    arrived(1)
    start_rows(4)
    forward(2)
    for j in range(5):
        pass_rows(j)
    forward(3)
    arrived(0)
    arrived(2)
    arrived(3)
    for j in range(5):
        end_rows(j)
    for copy in swaps:
        copy.wait_send()
    for i in range(4):
        sent(i)
    for copy in local[2:]:
        copy.wait()


def spread(qs, wos, ups, dns, nms, nls, dys, cns, n, size):
    _, three, r, cols = qs.shape
    width = wos.shape[1]
    chain = n // 2
    g, patches, _ = nms.shape
    lat = nls.shape[1]
    return pl.pallas_call(
        functools.partial(spread_kernel, chain, size),
        name="spread",
        out_shape=(
            struct((three, n, size, r, cols), BF16),
            struct((n, size, r, width), BF16),
            struct((ups.shape[0], n, r, width), BF16),
            struct((dns.shape[0], n, r, width), BF16),
            struct((g, size, patches, width), BF16),
            struct((g, size, lat, width), BF16),
            struct((size,) + dys.shape, BF16),
            struct((size,) + cns.shape, F32),
        ),
        in_specs=[VMEM] * 8,
        out_specs=(ANY,) * 8,
        scratch_shapes=[
            DMA((8,)), DMA((size,)), DMA((size,)),
            DMA((4, chain)), DMA((4, chain)), DMA((4, chain)), DMA((4, chain)), DMA((4, chain)),
            DMA((5,)), DMA((5,)), DMA((5, 2)), DMA((5, 2)),
        ],
        compiler_params=params(0),
    )(qs, wos, ups, dns, nms, nls, dys, cns)


def to_rows_kernel(size, src, out, loc, ss, rs):
    d, p = lax.axis_index("dp"), lax.axis_index("patch")
    cols = src.shape[3]
    meet(patch_peers(d, p, size))
    here = out.at[:, :, pl.ds(pl.multiple_of(p * cols, cols), cols)]
    copies = []
    for k in range(1, size):
        q = lax.rem(p + k, size)
        copies.append(remote(src.at[:, q], here, ss.at[k], rs.at[k], (d, q)))
    for copy in copies:
        copy.start()
    mine = pltpu.make_async_copy(src.at[:, p], here, loc)
    mine.start()
    mine.wait()
    for copy in copies:
        copy.wait()


def to_rows(src, size, number):
    g, _, lat, cols = src.shape
    return pl.pallas_call(
        functools.partial(to_rows_kernel, size),
        name="to_rows",
        out_shape=struct((g, lat, size * cols), src.dtype),
        in_specs=[VMEM],
        out_specs=VMEM,
        scratch_shapes=[DMA, DMA((size,)), DMA((size,))],
        compiler_params=params(number),
    )(src)


def to_heads_kernel(size, src, out, loc, ss, rs):
    d, p = lax.axis_index("dp"), lax.axis_index("patch")
    cols = out.shape[3]
    meet(patch_peers(d, p, size))

    def part(q):
        return src.at[:, :, pl.ds(pl.multiple_of(q * cols, cols), cols)]

    copies = []
    for k in range(1, size):
        q = lax.rem(p + k, size)
        copies.append(remote(part(q), out.at[:, p], ss.at[k], rs.at[k], (d, q)))
    for copy in copies:
        copy.start()
    mine = pltpu.make_async_copy(part(p), out.at[:, p], loc)
    mine.start()
    mine.wait()
    for copy in copies:
        copy.wait()


def to_heads(src, size, number):
    g, lat, width = src.shape
    return pl.pallas_call(
        functools.partial(to_heads_kernel, size),
        name="to_heads",
        out_shape=struct((g, size, lat, width // size), src.dtype),
        in_specs=[VMEM],
        out_specs=VMEM,
        scratch_shapes=[DMA, DMA((size,)), DMA((size,))],
        compiler_params=params(number),
    )(src)


def join_rows_kernel(src, out, loc, ss, rs):
    d, p, z, y, x, c = place()
    x_dev, c_dev = (d, (1 - x) * 2 + c), (d, x * 2 + 1 - c)
    px = (1 - x) * 2 + c
    meet([x_dev, c_dev])
    to_x = remote(src, out.at[p], ss.at[0], rs.at[0], x_dev)
    to_c = remote(src, out.at[p], ss.at[1], rs.at[1], c_dev)
    on = remote(out.at[px], out.at[px], ss.at[2], rs.at[2], c_dev)
    to_x.start()
    to_c.start()
    mine = pltpu.make_async_copy(src, out.at[p], loc)
    mine.start()
    to_x.wait_recv()
    on.start()
    mine.wait()
    to_c.wait()
    on.wait()
    to_x.wait_send()


def join_rows(src, size, number):
    return pl.pallas_call(
        join_rows_kernel,
        name="join_rows",
        out_shape=struct((size,) + src.shape, src.dtype),
        in_specs=[VMEM],
        out_specs=VMEM,
        scratch_shapes=[DMA, DMA((3,)), DMA((3,))],
        compiler_params=params(number),
    )(src)


def split_rows_kernel(ins, src, out, half, mid, quarter, ss, rs):
    d, p, z, y, x, c = place()
    x_dev, c_dev = (d, (1 - x) * 2 + c), (d, x * 2 + 1 - c)
    meet([x_dev, c_dev])
    first = [remote(src.at[i, :, 1 - c], half.at[i], ss.at[i], rs.at[i], c_dev) for i in range(ins)]
    for copy in first:
        copy.start()
    second = []
    for i in range(ins):
        first[i].wait_recv()
        mid[i] = (half[i, 1 - x].astype(F32) + src[i, 1 - x, c].astype(F32)).astype(BF16)
        copy = remote(mid.at[i], quarter.at[i], ss.at[ins + i], rs.at[ins + i], x_dev)
        copy.start()
        second.append(copy)
    for i in range(ins):
        out[i] = half[i, x].astype(F32) + src[i, x, c].astype(F32)
    for i in range(ins):
        second[i].wait_recv()
        out[i] = out[i] + quarter[i].astype(F32)
    for copy in first + second:
        copy.wait_send()


def split_rows(src, number):
    ins, _, _, rows, width = src.shape
    return pl.pallas_call(
        functools.partial(split_rows_kernel, ins),
        name="split_rows",
        out_shape=struct((ins, rows, width), F32),
        in_specs=[VMEM],
        out_specs=VMEM,
        scratch_shapes=[
            pltpu.VMEM((ins, 2, rows, width), BF16),
            pltpu.VMEM((ins, rows, width), BF16),
            pltpu.VMEM((ins, rows, width), BF16),
            DMA((2 * ins,)), DMA((2 * ins,)),
        ],
        compiler_params=params(number),
    )(src)


def head_rows(q, hands):
    rows, cols = q.shape
    size = cols // hands
    lane = lax.broadcasted_iota(jnp.int32, (rows, cols), 1)
    zero = jnp.zeros_like(q)
    parts = [
        jnp.where(jnp.logical_and(lane >= h * size, lane < (h + 1) * size), q, zero)
        for h in range(hands)
    ]
    return jnp.concatenate(parts, axis=0)


def own_columns(full, hands):
    rows, cols = full.shape[0] // hands, full.shape[1]
    size = cols // hands
    lane = lax.broadcasted_iota(jnp.int32, (rows, cols), 1)
    out = jnp.zeros((rows, cols), F32)
    for h in range(hands):
        keep = jnp.logical_and(lane >= h * size, lane < (h + 1) * size)
        out = jnp.where(keep, full[h * rows : (h + 1) * rows], out)
    return out


def nt(a, b):
    return lax.dot_general(a, b, (((1,), (1,)), ((), ())), preferred_element_type=F32)


def nn(a, b):
    return lax.dot_general(a, b, (((1,), (0,)), ((), ())), preferred_element_type=F32)


def tn(a, b):
    return lax.dot_general(a, b, (((0,), (0,)), ((), ())), preferred_element_type=F32)


def soft(qb, kp, kl, real, scale):
    sp = nt(qb, kp) * scale
    sl = nt(qb, kl) * scale
    key = lax.broadcasted_iota(jnp.int32, sp.shape, 1)
    sp = jnp.where(key < real, sp, -1e30)
    peak = jnp.maximum(jnp.max(sp, axis=1, keepdims=True), jnp.max(sl, axis=1, keepdims=True))
    ep, el = jnp.exp(sp - peak), jnp.exp(sl - peak)
    total = jnp.sum(ep, axis=1, keepdims=True) + jnp.sum(el, axis=1, keepdims=True)
    return ep / total, el / total


def attend_kernel(hands, scale, real, q, kp, kl, vp, vl, out):
    g = pl.program_id(0)
    qb = head_rows(q[0], hands)
    pp, plat = soft(qb, kp[0], kl[0], real[g], scale)
    full = nn(pp.astype(BF16), vp[0]) + nn(plat.astype(BF16), vl[0])
    out[0] = own_columns(full, hands).astype(BF16)


def attend(real, q, kp, kl, vp, vl, hands, scale):
    g, lat, cols = q.shape
    patches = kp.shape[1]

    def spec(rows):
        return pl.BlockSpec((1, rows, cols), lambda i, real: (i, 0, 0))

    return pl.pallas_call(
        functools.partial(attend_kernel, hands, scale),
        name="attend",
        grid_spec=pltpu.PrefetchScalarGridSpec(
            num_scalar_prefetch=1,
            grid=(g,),
            in_specs=[spec(lat), spec(patches), spec(lat), spec(patches), spec(lat)],
            out_specs=spec(lat),
        ),
        out_shape=struct((g, lat, cols), BF16),
        compiler_params=pltpu.CompilerParams(dimension_semantics=("arbitrary",)),
    )(real, q, kp, kl, vp, vl)


def attend_back_kernel(hands, scale, real, q, kp, kl, vp, vl, da, dq, dkp, dkl, dvp, dvl):
    g = pl.program_id(0)
    qb = head_rows(q[0], hands)
    dab = head_rows(da[0], hands)
    pp, plat = soft(qb, kp[0], kl[0], real[g], scale)
    gp, gl = nt(dab, vp[0]), nt(dab, vl[0])
    delta = jnp.sum(pp * gp, axis=1, keepdims=True) + jnp.sum(plat * gl, axis=1, keepdims=True)
    sp, sl = (pp * (gp - delta)).astype(BF16), (plat * (gl - delta)).astype(BF16)
    dvp[0] = tn(pp.astype(BF16), dab).astype(BF16)
    dvl[0] = tn(plat.astype(BF16), dab).astype(BF16)
    dkp[0] = (tn(sp, qb) * scale).astype(BF16)
    dkl[0] = (tn(sl, qb) * scale).astype(BF16)
    full = nn(sp, kp[0]) + nn(sl, kl[0])
    dq[0] = (own_columns(full, hands) * scale).astype(BF16)


def attend_back(real, q, kp, kl, vp, vl, da, hands, scale):
    g, lat, cols = q.shape
    patches = kp.shape[1]

    def spec(rows):
        return pl.BlockSpec((1, rows, cols), lambda i, real: (i, 0, 0))

    return pl.pallas_call(
        functools.partial(attend_back_kernel, hands, scale),
        name="attend_back",
        grid_spec=pltpu.PrefetchScalarGridSpec(
            num_scalar_prefetch=1,
            grid=(g,),
            in_specs=[spec(lat), spec(patches), spec(lat), spec(patches), spec(lat), spec(lat)],
            out_specs=[spec(lat), spec(patches), spec(lat), spec(patches), spec(lat)],
        ),
        out_shape=(
            struct((g, lat, cols), BF16),
            struct((g, patches, cols), BF16),
            struct((g, lat, cols), BF16),
            struct((g, patches, cols), BF16),
            struct((g, lat, cols), BF16),
        ),
        compiler_params=pltpu.CompilerParams(dimension_semantics=("arbitrary",)),
    )(real, q, kp, kl, vp, vl, da)


def collect_kernel(chain, size, gq, gw, gu, gd, kp, kl,
                   oq, ow, ou, od, okp, okl,
                   yq, yw, yu, yd, uq, uw, uu, ud, dq, dw, du, dd,
                   wc, wsum, wx, total, kc, kx, lc, lx, fin,
                   ys, yr, us, ur, ds, dr, ks, kr, qs, qr):
    d, p, z, y, x, c = place()
    above, below = z + 1 < chain, z > 0
    up_dev, dn_dev = ((z + 1) * 2 + y, p), ((z - 1) * 2 + y, p)
    y_dev, x_dev, c_dev = (z * 2 + 1 - y, p), (d, (1 - x) * 2 + c), (d, x * 2 + 1 - c)
    meet(patch_peers(d, p, size) + [y_dev], [(above, up_dev), (below, dn_dev)])

    mine = (
        lambda k: gq.at[:, k], lambda k: total.at[k], lambda k: gu.at[:, k], lambda k: gd.at[:, k]
    )
    land_y, land_u, land_d = (yq, yw, yu, yd), (uq, uw, uu, ud), (dq, dw, du, dd)

    def over(i, zz):
        return remote(
            mine[i](zz * 2 + 1 - y), land_y[i].at[zz], ys.at[i, zz], yr.at[i, zz], y_dev
        )

    def send_over(i):
        def step(zz, carry):
            over(i, zz).start()
            return carry

        lax.fori_loop(0, chain, step, 0)

    def add_over(i):
        def step(zz, carry):
            over(i, zz).wait_recv()
            have = mine[i](zz * 2 + y)
            land_y[i][zz] = (land_y[i][zz].astype(F32) + have[...].astype(F32)).astype(BF16)
            return carry

        lax.fori_loop(0, chain, step, 0)

    def rise(i, zz):
        return remote(land_y[i].at[zz], land_u[i].at[zz], us.at[i, zz], ur.at[i, zz], up_dev)

    def fall(i, zz):
        return remote(land_y[i].at[zz], land_d[i].at[zz], ds.at[i, zz], dr.at[i, zz], dn_dev)

    def gather(i, zz, land):
        land_y[i][zz] = (land_y[i][zz].astype(F32) + land[i][zz].astype(F32)).astype(BF16)

    def along(i):
        def step(k, carry):
            s = chain - k

            @pl.when(z + s < chain)
            def _():
                @pl.when(below)
                def _():
                    rise(i, z + s).wait_recv()
                    gather(i, z + s, land_u)

                rise(i, z + s).start()

            @pl.when(z - s >= 0)
            def _():
                @pl.when(above)
                def _():
                    fall(i, z - s).wait_recv()
                    gather(i, z - s, land_d)

                fall(i, z - s).start()

            return carry

        lax.fori_loop(1, chain, step, 0)

    def finish(i, write):
        write(land_y[i][z].astype(F32))

        @pl.when(below)
        def _():
            rise(i, z).wait_recv()
            write(land_u[i][z].astype(F32), True)

        @pl.when(above)
        def _():
            fall(i, z).wait_recv()
            write(land_d[i][z].astype(F32), True)

    def into(ref):
        def write(value, more=False):
            ref[...] = ref[...] + value if more else value

        return write

    def sent(i):
        def step(zz, carry):
            over(i, zz).wait_send()

            @pl.when(zz > z)
            def _():
                rise(i, zz).wait_send()

            @pl.when(zz < z)
            def _():
                fall(i, zz).wait_send()

            return carry

        lax.fori_loop(0, chain, step, 0)

    send_over(2)
    w_core = remote(gw.at[:, :, 1 - c], wc, ks.at[0], kr.at[0], c_dev)
    p_core = remote(kp.at[:, :, 1 - c], kc, ks.at[1], kr.at[1], c_dev)
    l_core = remote(kl.at[:, :, 1 - c], lc, ks.at[2], kr.at[2], c_dev)
    w_core.start()
    p_core.start()
    l_core.start()
    send_over(3)
    send_over(0)

    w_core.wait_recv()

    def w_add(k, carry):
        wsum[k] = (wc[k, 1 - x].astype(F32) + gw[k, 1 - x, c].astype(F32)).astype(BF16)
        return carry

    lax.fori_loop(0, 2 * chain, w_add, 0)
    w_x = remote(wsum, wx, ks.at[3], kr.at[3], x_dev)
    w_x.start()

    p_core.wait_recv()
    images = kp.shape[0]

    def p_add(k, carry):
        kc[k] = (kc[k].astype(F32) + kp[k, :, c].astype(F32)).astype(BF16)
        return carry

    lax.fori_loop(0, images, p_add, 0)
    p_x = remote(kc.at[:, 1 - x], kx, ks.at[4], kr.at[4], x_dev)
    p_x.start()
    l_core.wait_recv()

    def l_add(k, carry):
        lc[k] = (lc[k].astype(F32) + kl[k, :, c].astype(F32)).astype(BF16)
        return carry

    lax.fori_loop(0, images, l_add, 0)
    l_x = remote(lc.at[:, 1 - x], lx, ks.at[5], kr.at[5], x_dev)
    l_x.start()

    w_x.wait_recv()

    def w_last(k, carry):
        total[k] = (
            wc[k, x].astype(F32) + gw[k, x, c].astype(F32) + wx[k].astype(F32)
        ).astype(BF16)
        return carry

    lax.fori_loop(0, 2 * chain, w_last, 0)
    send_over(1)

    add_over(2)
    along(2)
    add_over(3)
    along(3)
    add_over(0)
    along(0)
    add_over(1)
    along(1)
    finish(2, into(ou))
    finish(3, into(od))
    finish(0, into(fin))
    swaps = []
    for k in range(1, size):
        q = lax.rem(p + k, size)
        swaps.append(remote(fin.at[:, q], oq.at[p], qs.at[k], qr.at[k], (d, q)))
    for copy in swaps:
        copy.start()
    finish(1, into(ow))
    oq[p] = fin[:, p]

    p_x.wait_recv()

    def p_last(k, carry):
        okp[k] = kc[k, x].astype(F32) + kx[k].astype(F32)
        return carry

    lax.fori_loop(0, images, p_last, 0)
    l_x.wait_recv()

    def l_last(k, carry):
        okl[k] = lc[k, x].astype(F32) + lx[k].astype(F32)
        return carry

    lax.fori_loop(0, images, l_last, 0)
    for copy in swaps:
        copy.wait()
    for i in range(4):
        sent(i)
    for copy in (w_core, p_core, l_core, w_x, p_x, l_x):
        copy.wait_send()


def collect(gq, gw, gu, gd, kp, kl, n, size):
    chain = n // 2
    three, _, _, r, cols = gq.shape
    width = gw.shape[-1]
    fu, fd = gu.shape[0], gd.shape[0]
    g, two, _, patches, _ = kp.shape
    lat = kl.shape[3]
    lands = [
        ((three, size, r, cols)), ((r, width)), ((fu, r, width)), ((fd, r, width)),
    ]
    stage = [pltpu.VMEM((chain,) + s, BF16) for s in lands]
    return pl.pallas_call(
        functools.partial(collect_kernel, chain, size),
        name="collect",
        out_shape=(
            struct((size, three, r, cols), F32),
            struct((r, width), F32),
            struct((fu, r, width), F32),
            struct((fd, r, width), F32),
            struct((g, patches, width), F32),
            struct((g, lat, width), F32),
        ),
        in_specs=[VMEM] * 6,
        out_specs=(VMEM,) * 6,
        scratch_shapes=stage * 3
        + [
            pltpu.VMEM((n, two, r, width), BF16),
            pltpu.VMEM((n, r, width), BF16),
            pltpu.VMEM((n, r, width), BF16),
            pltpu.VMEM((n, r, width), BF16),
            pltpu.VMEM((g, two, patches, width), BF16),
            pltpu.VMEM((g, patches, width), BF16),
            pltpu.VMEM((g, two, lat, width), BF16),
            pltpu.VMEM((g, lat, width), BF16),
            pltpu.VMEM((three, size, r, cols), F32),
        ]
        + [DMA((4, chain))] * 6
        + [DMA((6,)), DMA((6,)), DMA((size,)), DMA((size,))],
        compiler_params=params(6),
    )(gq, gw, gu, gd, kp, kl)


def total_kernel(hops, src, out, hold, land, ss, rs):
    d, p = lax.axis_index("dp"), lax.axis_index("patch")

    def flip(v, bit):
        return v + bit - 2 * bit * lax.rem(lax.div(v, bit), 2)

    to = [(d, flip(p, b)) if kind else (flip(d, b), p) for kind, b in hops]
    meet(to)
    sends = []
    for i, who in enumerate(to):
        copy = remote(src if i == 0 else hold.at[i], land.at[i], ss.at[i], rs.at[i], who)
        copy.start()
        copy.wait_recv()
        sends.append(copy)
        value = (src[...] if i == 0 else hold[i]) + land[i]
        if i + 1 < len(to):
            hold[i + 1] = value
        else:
            out[...] = value
    for copy in sends:
        copy.wait_send()


def total(src, n, size):
    hops = [(True, 1 << b) for b in range(size.bit_length() - 1)]
    hops += [(False, 1 << b) for b in range(n.bit_length() - 1)]
    return pl.pallas_call(
        functools.partial(total_kernel, hops),
        name="total",
        out_shape=struct(src.shape, F32),
        in_specs=[VMEM],
        out_specs=VMEM,
        scratch_shapes=[
            pltpu.VMEM((len(hops),) + src.shape, F32),
            pltpu.VMEM((len(hops),) + src.shape, F32),
            DMA((len(hops),)), DMA((len(hops),)),
        ],
        compiler_params=params(7),
    )(src)


def norm_parts(values, gain_row, shift_row):
    average = jnp.mean(values, axis=-1, keepdims=True)
    centred = values - average
    spread_ = jnp.mean(centred * centred, axis=-1, keepdims=True)
    scaled = lax.rsqrt(spread_ + 1e-05)
    unit_rows = centred * scaled
    return (unit_rows * gain_row + shift_row, unit_rows, scaled)


def norm_back(grad_out, unit_rows, scaled, gain_row):
    inner_grad = grad_out * gain_row
    plain_mean = jnp.mean(inner_grad, axis=-1, keepdims=True)
    cross_mean = jnp.mean(inner_grad * unit_rows, axis=-1, keepdims=True)
    return scaled * (inner_grad - plain_mean - unit_rows * cross_mean)


def gain_terms(grad_out, unit_rows):
    width = grad_out.shape[-1]
    flat_grad = grad_out.reshape(-1, width)
    flat_unit = unit_rows.reshape(-1, width)
    return [jnp.sum(flat_grad * flat_unit, axis=0), jnp.sum(flat_grad, axis=0)]


def exact_gelu(values):
    return jax.nn.gelu(values, approximate=False)


def adamw_update(parameter, first_m, second_m, average, gradient, factor, decay_rate):
    clipped = gradient * factor
    new_first = 0.9 * first_m + 0.1 * clipped
    new_second = 0.999 * second_m + 0.001 * clipped * clipped
    first_hat = new_first / (1.0 - 0.9**STEP)
    second_hat = new_second / (1.0 - 0.999**STEP)
    new_param = parameter - 0.02 * (
        first_hat / (jnp.sqrt(second_hat) + 1e-08) + decay_rate * parameter
    )
    new_avg = 0.8 * average + 0.2 * new_param
    return (new_param, new_first, new_second, new_avg)


def dot32(spec, a, b):
    return jnp.einsum(spec, a, b, preferred_element_type=F32)


def on_device(n, size, media_tokens, patch_mask, latents, cotangent, weights, weights_first,
              weights_second, weights_average, norm_params, norm_first, norm_second, norm_average):
    g, patches, width = media_tokens.shape
    lat = latents.shape[1]
    blocks = weights.shape[0]
    r = width // (n * size)
    cols = width // size
    hands = HEADS // size
    scale = 1.0 / math.sqrt(width // HEADS)
    ups = FF // width
    own = g * lat
    media_gain, latent_gain, ffn_gain = 1.0 + norm_params[0], 1.0 + norm_params[2], 1.0 + norm_params[4]

    held = weights.astype(BF16).reshape(blocks, r, width)
    qs = held[:3].reshape(3, r, size, cols).transpose(2, 0, 1, 3)
    media_norm, media_unit, media_scale = norm_parts(media_tokens, media_gain, norm_params[1])
    latent_norm, latent_unit, latent_scale = norm_parts(latents, latent_gain, norm_params[3])
    cot = cotangent.reshape(own, width)
    count_rows = (g + 15) // 16 * 16
    counts = jnp.sum((patch_mask > 0).astype(F32), axis=1)
    counts = jnp.broadcast_to(jnp.pad(counts, (0, count_rows - g))[:, None], (count_rows, 128))

    wqkv, wo, up, dn, nm, nl, dy, cn = spread(
        qs, held[3], held[4 : 4 + ups], held[4 + ups :],
        media_norm.astype(BF16), latent_norm.astype(BF16), cot.astype(BF16), counts, n, size,
    )
    wqkv = wqkv.reshape(3, width, cols)
    wo = wo.reshape(width, width)
    up = up.reshape(-1, width)
    dn = dn.reshape(-1, width)
    nm = nm.reshape(g * size * patches, width)
    nl = nl.reshape(g * size * lat, width)
    dy = dy.reshape(size * own, width)
    real = jnp.sum(cn[:, :g, 0], axis=0).astype(jnp.int32)

    def by_image(a):
        return a.astype(BF16).reshape(g, -1, cols)

    q = by_image(dot32("rd,de->re", nl, wqkv[0]))
    kp, kl = by_image(dot32("rd,de->re", nm, wqkv[1])), by_image(dot32("rd,de->re", nl, wqkv[1]))
    vp, vl = by_image(dot32("rd,de->re", nm, wqkv[2])), by_image(dot32("rd,de->re", nl, wqkv[2]))
    mixed = attend(real, q, kp, kl, vp, vl, hands, scale)
    ab = to_rows(mixed.reshape(g, size, lat, cols), size, 1).reshape(own, width)

    hidden = latents.reshape(own, width) + dot32("rd,de->re", ab, wo)
    ffn_norm, ffn_unit, ffn_scale = norm_parts(hidden, ffn_gain, norm_params[5])
    nf = join_rows(ffn_norm.astype(BF16), size, 2).reshape(size * own, width)
    u = dot32("rd,fd->rf", nf, up)
    active, pull = jax.vjp(exact_gelu, u)
    gb = active.astype(BF16)
    y_part = dot32("rf,fd->rd", gb, dn).astype(BF16)
    du = pull(dot32("rd,fd->rf", dy, dn))[0].astype(BF16)
    f_part = dot32("rf,fd->rd", du, up).astype(BF16)
    g_dn = dot32("rf,rd->fd", gb, dy).astype(BF16)
    g_up = dot32("rf,rd->fd", du, nf).astype(BF16)
    both = split_rows(jnp.stack([y_part, f_part]).reshape(2, 2, 2, own, width), 3)
    latents_out = (hidden + both[0]).reshape(g, lat, width)
    d_ffn = both[1]
    ffn_terms = gain_terms(d_ffn, ffn_unit)
    d_hidden = cot + norm_back(d_ffn, ffn_unit, ffn_scale, ffn_gain)

    do = d_hidden.astype(BF16)
    g_wo = dot32("rd,re->de", ab, do).astype(BF16)
    da = dot32("re,de->rd", do, wo).astype(BF16).reshape(g, lat, width)
    da = to_heads(da, size, 4).reshape(g, size * lat, cols)
    dq, dkp, dkl, dvp, dvl = attend_back(real, q, kp, kl, vp, vl, da, hands, scale)

    def flat(a):
        return a.reshape(-1, cols)

    dq, dkp, dkl, dvp, dvl = flat(dq), flat(dkp), flat(dkl), flat(dvp), flat(dvl)
    g_qkv = jnp.stack([
        dot32("rd,re->de", nl, dq),
        dot32("rd,re->de", nm, dkp) + dot32("rd,re->de", nl, dkl),
        dot32("rd,re->de", nm, dvp) + dot32("rd,re->de", nl, dvl),
    ]).astype(BF16)
    d_nm = (dot32("re,de->rd", dkp, wqkv[1]) + dot32("re,de->rd", dvp, wqkv[2])).astype(BF16)
    d_nl = (
        dot32("re,de->rd", dkl, wqkv[1]) + dot32("re,de->rd", dvl, wqkv[2])
        + dot32("re,de->rd", dq, wqkv[0])
    ).astype(BF16)

    oq, ow, ou, od, d_media, d_latent = collect(
        g_qkv.reshape(3, n, size, r, cols), g_wo.reshape(n, 2, 2, r, width),
        g_up.reshape(ups, n, r, width), g_dn.reshape(ups, n, r, width),
        d_nm.reshape(g, 2, 2, patches, width), d_nl.reshape(g, 2, 2, lat, width), n, size,
    )
    media_grad = norm_back(d_media, media_unit, media_scale, media_gain)
    latents_grad = d_hidden.reshape(g, lat, width) + norm_back(
        d_latent, latent_unit, latent_scale, latent_gain
    )
    grads = jnp.concatenate([
        oq.transpose(1, 2, 0, 3).reshape(3, r, width), ow[None], ou, od,
    ])
    square = jnp.broadcast_to(jnp.sum(grads * grads), (width,))
    rows = jnp.stack(
        gain_terms(d_media, media_unit) + gain_terms(d_latent, latent_unit) + ffn_terms
        + [square, jnp.zeros_like(square)]
    )
    sums = total(rows, n, size)
    norm_grads = sums[:6]
    grad_norm = jnp.sqrt(sums[6, 0] + jnp.sum(norm_grads * norm_grads))
    clip = jnp.minimum(1.0, 1.0 / (grad_norm + 1e-06))
    new_w, new_first, new_second, new_avg = adamw_update(
        weights, weights_first, weights_second, weights_average,
        grads.reshape(weights.shape), clip, 0.1,
    )
    new_n, new_nf, new_ns, new_na = adamw_update(
        norm_params, norm_first, norm_second, norm_average, norm_grads, clip, 0.0
    )
    return (
        latents_out, media_grad, latents_grad, grad_norm, new_w, new_w.astype(BF16), new_first,
        new_second, new_avg, new_n, new_nf, new_ns, new_na, norm_grads[4:6],
    )


def solution(mesh):
    n, size = mesh.shape["dp"], mesh.shape["patch"]
    rows, weight = P("dp", "patch", None), P(None, ("dp", "patch"))
    return jax.shard_map(
        functools.partial(on_device, n, size),
        mesh=mesh,
        in_specs=(rows, P("dp", "patch"), rows, rows) + (weight,) * 4 + (P(),) * 4,
        out_specs=(rows, rows, rows, P()) + (weight,) * 5 + (P(),) * 5,
        check_vma=False,
    )
```

```python
import functools
import math

import jax
import jax.numpy as jnp
from jax import lax
from jax.experimental import pallas as pl
from jax.experimental.pallas import tpu as pltpu
from jax.sharding import PartitionSpec as P

HEADS = 16
FF = 4096
STEP = 7
MESH = pl.DeviceIdType.MESH
F32 = jnp.float32
BF16 = jnp.bfloat16
ANY = pl.BlockSpec(memory_space=pl.ANY)
VMEM = pl.BlockSpec(memory_space=pltpu.VMEM)
DMA = pltpu.SemaphoreType.DMA
VMEM_LIMIT = 64 * 1024 * 1024 - 65536


def struct(shape, kind):
    return jax.ShapeDtypeStruct(shape, kind)


def place():
    d, p = lax.axis_index("dp"), lax.axis_index("patch")
    return d, p, lax.div(d, 2), lax.rem(d, 2), lax.div(p, 2), lax.rem(p, 2)


def remote(src, dst, send, recv, to):
    return pltpu.make_async_remote_copy(
        src_ref=src, dst_ref=dst, send_sem=send, recv_sem=recv, device_id=to, device_id_type=MESH
    )


def meet(always, maybe=()):
    barrier = pltpu.get_barrier_semaphore()
    count = len(always)
    for to in always:
        pl.semaphore_signal(barrier, inc=1, device_id=to, device_id_type=MESH)
    for there, to in maybe:

        @pl.when(there)
        def _(to=to):
            pl.semaphore_signal(barrier, inc=1, device_id=to, device_id_type=MESH)

        count = count + there.astype(jnp.int32)
    pl.semaphore_wait(barrier, count)


def patch_peers(d, p, size):
    return [(d, lax.rem(p + k, size)) for k in range(1, size)]


def params(number):
    return pltpu.CompilerParams(
        collective_id=number, has_side_effects=True, vmem_limit_bytes=VMEM_LIMIT
    )


def spread_kernel(chain, size, qs, wos, ups, dns, nms, nls, dys, cns,
                  wqkv, wo, up, dn, nm, nl, dy, cn,
                  loc, a_s, a_r, su, sd, sy, rz, ry, xs, xr, cs, cr):
    d, p, z, y, x, c = place()
    above, below = z + 1 < chain, z > 0
    up_dev, dn_dev = ((z + 1) * 2 + y, p), ((z - 1) * 2 + y, p)
    y_dev, x_dev, c_dev = (z * 2 + 1 - y, p), (d, (1 - x) * 2 + c), (d, x * 2 + 1 - c)
    px, pc = (1 - x) * 2 + c, x * 2 + 1 - c
    pd = (1 - x) * 2 + 1 - c
    meet(patch_peers(d, p, size) + [y_dev], [(above, up_dev), (below, dn_dev)])

    own = [
        (qs.at[p], wqkv.at[:, d, p]), (wos, wo.at[d, p]), (ups, up.at[:, d]), (dns, dn.at[:, d]),
        (nms, nm.at[:, p]), (nls, nl.at[:, p]), (dys, dy.at[p]), (cns, cn.at[p]),
    ]
    local = [pltpu.make_async_copy(a, b, loc.at[i]) for i, (a, b) in enumerate(own)]
    for copy in local:
        copy.start()
    swaps = []
    for k in range(1, size):
        q = lax.rem(p + k, size)
        swaps.append(remote(qs.at[q], wqkv.at[:, d, p], a_s.at[k], a_r.at[k], (d, q)))
    for copy in swaps:
        copy.start()

    rows = [(nms, nm), (nls, nl), (cns, cn), (dys, dy)]

    def slot(j, q):
        ref = rows[j][1] if j < 4 else wo
        return ref.at[q] if j in (2, 3) else ref.at[:, q]

    def row_copies(j):
        src = rows[j][0] if j < 4 else slot(j, p)
        return (
            remote(src, slot(j, p), xs.at[j], xr.at[j], x_dev),
            remote(src, slot(j, p), cs.at[j, 0], cr.at[j, 0], c_dev),
            remote(slot(j, px), slot(j, px), cs.at[j, 1], cr.at[j, 1], c_dev),
        )

    def start_rows(j):
        to_x, to_c, _ = row_copies(j)
        to_x.start()
        to_c.start()

    def pass_rows(j):
        to_x, _, on = row_copies(j)
        to_x.wait_recv()
        on.start()

    def end_rows(j):
        to_x, to_c, on = row_copies(j)
        to_c.wait_recv()
        on.wait_recv()
        to_x.wait_send()
        to_c.wait_send()
        on.wait_send()

    for j in range(4):
        start_rows(j)

    def piece(i, dd):
        return (wqkv.at[:, dd], wo.at[dd, p], up.at[:, dd], dn.at[:, dd])[i]

    first = (wqkv.at[:, d], wos, ups, dns)

    def hop(i, zz, sends, to, own_src=False):
        src = first[i] if own_src else piece(i, zz * 2 + y)
        return remote(src, piece(i, zz * 2 + y), sends.at[i, zz], rz.at[i, zz], to)

    def over(i, zz, own_src=False):
        src = first[i] if own_src else piece(i, zz * 2 + y)
        return remote(src, piece(i, zz * 2 + y), sy.at[i, zz], ry.at[i, zz], y_dev)

    def start_own(i):
        @pl.when(above)
        def _():
            hop(i, z, su, up_dev, True).start()

        @pl.when(below)
        def _():
            hop(i, z, sd, dn_dev, True).start()

        over(i, z, True).start()

    def forward(i):
        def step(s, carry):
            @pl.when(z - s >= 0)
            def _():
                hop(i, z - s, su, up_dev).wait_recv()

                @pl.when(above)
                def _():
                    hop(i, z - s, su, up_dev).start()

                over(i, z - s).start()

            @pl.when(z + s < chain)
            def _():
                hop(i, z + s, sd, dn_dev).wait_recv()

                @pl.when(below)
                def _():
                    hop(i, z + s, sd, dn_dev).start()

                over(i, z + s).start()

            return carry

        lax.fori_loop(1, chain, step, 0)

    def arrived(i):
        def step(zz, carry):
            src = piece(i, zz * 2 + 1 - y)
            remote(src, src, sy.at[i, zz], ry.at[i, zz], y_dev).wait_recv()
            return carry

        lax.fori_loop(0, chain, step, 0)

    def sent(i):
        def step(zz, carry):
            over(i, zz).wait_send()

            @pl.when(jnp.logical_and(above, zz <= z))
            def _():
                hop(i, zz, su, up_dev).wait_send()

            @pl.when(jnp.logical_and(below, zz >= z))
            def _():
                hop(i, zz, sd, dn_dev).wait_send()

            return carry

        lax.fori_loop(0, chain, step, 0)

    local[0].wait()
    for copy in swaps:
        copy.wait_recv()
    start_own(0)
    start_own(1)
    forward(0)
    start_own(2)
    forward(1)
    start_own(3)
    local[1].wait()
    arrived(1)
    start_rows(4)
    forward(2)
    for j in range(5):
        pass_rows(j)
    forward(3)
    arrived(0)
    arrived(2)
    arrived(3)
    for j in range(5):
        end_rows(j)
    for copy in swaps:
        copy.wait_send()
    for i in range(4):
        sent(i)
    for copy in local[2:]:
        copy.wait()


def spread(qs, wos, ups, dns, nms, nls, dys, cns, n, size):
    _, three, r, cols = qs.shape
    width = wos.shape[1]
    chain = n // 2
    g, patches, _ = nms.shape
    lat = nls.shape[1]
    return pl.pallas_call(
        functools.partial(spread_kernel, chain, size),
        name="spread",
        out_shape=(
            struct((three, n, size, r, cols), BF16),
            struct((n, size, r, width), BF16),
            struct((ups.shape[0], n, r, width), BF16),
            struct((dns.shape[0], n, r, width), BF16),
            struct((g, size, patches, width), BF16),
            struct((g, size, lat, width), BF16),
            struct((size,) + dys.shape, BF16),
            struct((size,) + cns.shape, F32),
        ),
        in_specs=[VMEM] * 8,
        out_specs=(ANY,) * 8,
        scratch_shapes=[
            DMA((8,)), DMA((size,)), DMA((size,)),
            DMA((4, chain)), DMA((4, chain)), DMA((4, chain)), DMA((4, chain)), DMA((4, chain)),
            DMA((5,)), DMA((5,)), DMA((5, 2)), DMA((5, 2)),
        ],
        compiler_params=params(0),
    )(qs, wos, ups, dns, nms, nls, dys, cns)


def to_rows_kernel(size, src, out, loc, ss, rs):
    d, p = lax.axis_index("dp"), lax.axis_index("patch")
    cols = src.shape[3]
    meet(patch_peers(d, p, size))
    here = out.at[:, :, pl.ds(pl.multiple_of(p * cols, cols), cols)]
    copies = []
    for k in range(1, size):
        q = lax.rem(p + k, size)
        copies.append(remote(src.at[:, q], here, ss.at[k], rs.at[k], (d, q)))
    for copy in copies:
        copy.start()
    mine = pltpu.make_async_copy(src.at[:, p], here, loc)
    mine.start()
    mine.wait()
    for copy in copies:
        copy.wait()


def to_rows(src, size, number):
    g, _, lat, cols = src.shape
    return pl.pallas_call(
        functools.partial(to_rows_kernel, size),
        name="to_rows",
        out_shape=struct((g, lat, size * cols), src.dtype),
        in_specs=[VMEM],
        out_specs=VMEM,
        scratch_shapes=[DMA, DMA((size,)), DMA((size,))],
        compiler_params=params(number),
    )(src)


def to_heads_kernel(size, src, out, loc, ss, rs):
    d, p = lax.axis_index("dp"), lax.axis_index("patch")
    cols = out.shape[3]
    meet(patch_peers(d, p, size))

    def part(q):
        return src.at[:, :, pl.ds(pl.multiple_of(q * cols, cols), cols)]

    copies = []
    for k in range(1, size):
        q = lax.rem(p + k, size)
        copies.append(remote(part(q), out.at[:, p], ss.at[k], rs.at[k], (d, q)))
    for copy in copies:
        copy.start()
    mine = pltpu.make_async_copy(part(p), out.at[:, p], loc)
    mine.start()
    mine.wait()
    for copy in copies:
        copy.wait()


def to_heads(src, size, number):
    g, lat, width = src.shape
    return pl.pallas_call(
        functools.partial(to_heads_kernel, size),
        name="to_heads",
        out_shape=struct((g, size, lat, width // size), src.dtype),
        in_specs=[VMEM],
        out_specs=VMEM,
        scratch_shapes=[DMA, DMA((size,)), DMA((size,))],
        compiler_params=params(number),
    )(src)


def join_rows_kernel(src, out, loc, ss, rs):
    d, p, z, y, x, c = place()
    x_dev, c_dev = (d, (1 - x) * 2 + c), (d, x * 2 + 1 - c)
    px = (1 - x) * 2 + c
    meet([x_dev, c_dev])
    to_x = remote(src, out.at[p], ss.at[0], rs.at[0], x_dev)
    to_c = remote(src, out.at[p], ss.at[1], rs.at[1], c_dev)
    on = remote(out.at[px], out.at[px], ss.at[2], rs.at[2], c_dev)
    to_x.start()
    to_c.start()
    mine = pltpu.make_async_copy(src, out.at[p], loc)
    mine.start()
    to_x.wait_recv()
    on.start()
    mine.wait()
    to_c.wait()
    on.wait()
    to_x.wait_send()


def join_rows(src, size, number):
    return pl.pallas_call(
        join_rows_kernel,
        name="join_rows",
        out_shape=struct((size,) + src.shape, src.dtype),
        in_specs=[VMEM],
        out_specs=VMEM,
        scratch_shapes=[DMA, DMA((3,)), DMA((3,))],
        compiler_params=params(number),
    )(src)


def split_rows_kernel(ins, src, out, half, mid, quarter, ss, rs):
    d, p, z, y, x, c = place()
    x_dev, c_dev = (d, (1 - x) * 2 + c), (d, x * 2 + 1 - c)
    meet([x_dev, c_dev])
    first = [remote(src.at[i, :, 1 - c], half.at[i], ss.at[i], rs.at[i], c_dev) for i in range(ins)]
    for copy in first:
        copy.start()
    second = []
    for i in range(ins):
        first[i].wait_recv()
        mid[i] = (half[i, 1 - x].astype(F32) + src[i, 1 - x, c].astype(F32)).astype(BF16)
        copy = remote(mid.at[i], quarter.at[i], ss.at[ins + i], rs.at[ins + i], x_dev)
        copy.start()
        second.append(copy)
    for i in range(ins):
        out[i] = half[i, x].astype(F32) + src[i, x, c].astype(F32)
    for i in range(ins):
        second[i].wait_recv()
        out[i] = out[i] + quarter[i].astype(F32)
    for copy in first + second:
        copy.wait_send()


def split_rows(src, number):
    ins, _, _, rows, width = src.shape
    return pl.pallas_call(
        functools.partial(split_rows_kernel, ins),
        name="split_rows",
        out_shape=struct((ins, rows, width), F32),
        in_specs=[VMEM],
        out_specs=VMEM,
        scratch_shapes=[
            pltpu.VMEM((ins, 2, rows, width), BF16),
            pltpu.VMEM((ins, rows, width), BF16),
            pltpu.VMEM((ins, rows, width), BF16),
            DMA((2 * ins,)), DMA((2 * ins,)),
        ],
        compiler_params=params(number),
    )(src)


def head_rows(q, hands):
    rows, cols = q.shape
    size = cols // hands
    lane = lax.broadcasted_iota(jnp.int32, (rows, cols), 1)
    zero = jnp.zeros_like(q)
    parts = [
        jnp.where(jnp.logical_and(lane >= h * size, lane < (h + 1) * size), q, zero)
        for h in range(hands)
    ]
    return jnp.concatenate(parts, axis=0)


def own_columns(full, hands):
    rows, cols = full.shape[0] // hands, full.shape[1]
    size = cols // hands
    lane = lax.broadcasted_iota(jnp.int32, (rows, cols), 1)
    out = jnp.zeros((rows, cols), F32)
    for h in range(hands):
        keep = jnp.logical_and(lane >= h * size, lane < (h + 1) * size)
        out = jnp.where(keep, full[h * rows : (h + 1) * rows], out)
    return out


def nt(a, b):
    return lax.dot_general(a, b, (((1,), (1,)), ((), ())), preferred_element_type=F32)


def nn(a, b):
    return lax.dot_general(a, b, (((1,), (0,)), ((), ())), preferred_element_type=F32)


def tn(a, b):
    return lax.dot_general(a, b, (((0,), (0,)), ((), ())), preferred_element_type=F32)


def soft(qb, kp, kl, real, scale):
    sp = nt(qb, kp) * scale
    sl = nt(qb, kl) * scale
    key = lax.broadcasted_iota(jnp.int32, sp.shape, 1).astype(F32)
    sp = jnp.where(key < real, sp, -1e30)
    peak = jnp.maximum(jnp.max(sp, axis=1, keepdims=True), jnp.max(sl, axis=1, keepdims=True))
    ep, el = jnp.exp(sp - peak), jnp.exp(sl - peak)
    total = jnp.sum(ep, axis=1, keepdims=True) + jnp.sum(el, axis=1, keepdims=True)
    return ep / total, el / total


def attend_kernel(hands, scale, real, q, kp, kl, vp, vl, out):
    g = pl.program_id(0)
    qb = head_rows(q[0], hands)
    pp, plat = soft(qb, kp[0], kl[0], real[g].astype(F32), scale)
    full = nn(pp.astype(BF16), vp[0]) + nn(plat.astype(BF16), vl[0])
    out[0] = own_columns(full, hands).astype(BF16)


def attend(real, q, kp, kl, vp, vl, hands, scale):
    g, lat, cols = q.shape
    patches = kp.shape[1]

    def spec(rows):
        return pl.BlockSpec((1, rows, cols), lambda i, real: (i, 0, 0))

    return pl.pallas_call(
        functools.partial(attend_kernel, hands, scale),
        name="attend",
        grid_spec=pltpu.PrefetchScalarGridSpec(
            num_scalar_prefetch=1,
            grid=(g,),
            in_specs=[spec(lat), spec(patches), spec(lat), spec(patches), spec(lat)],
            out_specs=spec(lat),
        ),
        out_shape=struct((g, lat, cols), BF16),
        compiler_params=pltpu.CompilerParams(dimension_semantics=("arbitrary",)),
    )(real, q, kp, kl, vp, vl)


def attend_back_kernel(hands, scale, real, q, kp, kl, vp, vl, da, dq, dkp, dkl, dvp, dvl):
    g = pl.program_id(0)
    qb = head_rows(q[0], hands)
    dab = head_rows(da[0], hands)
    pp, plat = soft(qb, kp[0], kl[0], real[g].astype(F32), scale)
    gp, gl = nt(dab, vp[0]), nt(dab, vl[0])
    delta = jnp.sum(pp * gp, axis=1, keepdims=True) + jnp.sum(plat * gl, axis=1, keepdims=True)
    sp, sl = (pp * (gp - delta)).astype(BF16), (plat * (gl - delta)).astype(BF16)
    dvp[0] = tn(pp.astype(BF16), dab).astype(BF16)
    dvl[0] = tn(plat.astype(BF16), dab).astype(BF16)
    dkp[0] = (tn(sp, qb) * scale).astype(BF16)
    dkl[0] = (tn(sl, qb) * scale).astype(BF16)
    full = nn(sp, kp[0]) + nn(sl, kl[0])
    dq[0] = (own_columns(full, hands) * scale).astype(BF16)


def attend_back(real, q, kp, kl, vp, vl, da, hands, scale):
    g, lat, cols = q.shape
    patches = kp.shape[1]

    def spec(rows):
        return pl.BlockSpec((1, rows, cols), lambda i, real: (i, 0, 0))

    return pl.pallas_call(
        functools.partial(attend_back_kernel, hands, scale),
        name="attend_back",
        grid_spec=pltpu.PrefetchScalarGridSpec(
            num_scalar_prefetch=1,
            grid=(g,),
            in_specs=[spec(lat), spec(patches), spec(lat), spec(patches), spec(lat), spec(lat)],
            out_specs=[spec(lat), spec(patches), spec(lat), spec(patches), spec(lat)],
        ),
        out_shape=(
            struct((g, lat, cols), BF16),
            struct((g, patches, cols), BF16),
            struct((g, lat, cols), BF16),
            struct((g, patches, cols), BF16),
            struct((g, lat, cols), BF16),
        ),
        compiler_params=pltpu.CompilerParams(dimension_semantics=("arbitrary",)),
    )(real, q, kp, kl, vp, vl, da)


def aligned(start, step, count=None):
    return pl.ds(pl.multiple_of(start * step, step), count or step)


def unit_of(x):
    mean = jnp.mean(x, axis=-1, keepdims=True)
    centred = x - mean
    spread_ = jnp.mean(centred * centred, axis=-1, keepdims=True)
    scaled = lax.rsqrt(spread_ + 1e-05)
    return centred * scaled, scaled


def matmul(a, b, tile=256):
    return jnp.concatenate([nn(a, b[:, k : k + tile]) for k in range(0, b.shape[1], tile)], axis=1)


def front_kernel(chain, size, hands, scale,
                 held, media, latents, cot, cns, norms,
                 wqkv, wo, up, dn, nm, nl, dy, cn, q, kp, kl, vp, vl, mixed, ab, hidden, nf,
                 dys, loc, a_s, a_r, su, sd, sy, rz, ry, ms, mr, mcs, mcr, xs, xr, cs, cr, ts, tr):
    d, p, z, y, x, c = place()
    r, width = held.shape[1], held.shape[2]
    cols = width // size
    ups = up.shape[0]
    images, patches, _ = media.shape
    lat = latents.shape[1]
    own = images * lat
    above, below = z + 1 < chain, z > 0
    up_dev, dn_dev = ((z + 1) * 2 + y, p), ((z - 1) * 2 + y, p)
    y_dev, x_dev, c_dev = (z * 2 + 1 - y, p), (d, (1 - x) * 2 + c), (d, x * 2 + 1 - c)
    px = (1 - x) * 2 + c
    meet(patch_peers(d, p, size) + [y_dev], [(above, up_dev), (below, dn_dev)])

    def lanes(k):
        return aligned(k, cols)

    def piece(i, dd):
        if i == 0:
            return wqkv.at[:, aligned(dd, size * r)]
        if i == 1:
            return wo.at[aligned(dd * size + p, r)]
        return (up, dn)[i - 2].at[:, aligned(dd, r)]

    first = (
        wqkv.at[:, aligned(d, size * r)], held.at[3], held.at[pl.ds(4, ups)],
        held.at[pl.ds(4 + ups, ups)],
    )
    here = wqkv.at[:, aligned(d * size + p, r)]
    swaps = []
    for k in range(1, size):
        to = lax.rem(p + k, size)
        swaps.append(
            remote(held.at[pl.ds(0, 3), :, lanes(to)], here, a_s.at[k], a_r.at[k], (d, to))
        )
    for copy in swaps:
        copy.start()
    local = [
        pltpu.make_async_copy(held.at[pl.ds(0, 3), :, lanes(p)], here, loc.at[0]),
        pltpu.make_async_copy(first[1], piece(1, d), loc.at[1]),
        pltpu.make_async_copy(first[2], piece(2, d), loc.at[2]),
        pltpu.make_async_copy(first[3], piece(3, d), loc.at[3]),
    ]
    for copy in local:
        copy.start()

    def hop(i, zz, sends, to, own_src=False):
        src = first[i] if own_src else piece(i, zz * 2 + y)
        return remote(src, piece(i, zz * 2 + y), sends.at[i, zz], rz.at[i, zz], to)

    def over(i, zz, own_src=False):
        src = first[i] if own_src else piece(i, zz * 2 + y)
        return remote(src, piece(i, zz * 2 + y), sy.at[i, zz], ry.at[i, zz], y_dev)

    def start_own(i):
        @pl.when(above)
        def _():
            hop(i, z, su, up_dev, True).start()

        @pl.when(below)
        def _():
            hop(i, z, sd, dn_dev, True).start()

        over(i, z, True).start()

    def forward(i):
        def step(s, carry):
            @pl.when(z - s >= 0)
            def _():
                hop(i, z - s, su, up_dev).wait_recv()

                @pl.when(above)
                def _():
                    hop(i, z - s, su, up_dev).start()

                over(i, z - s).start()

            @pl.when(z + s < chain)
            def _():
                hop(i, z + s, sd, dn_dev).wait_recv()

                @pl.when(below)
                def _():
                    hop(i, z + s, sd, dn_dev).start()

                over(i, z + s).start()

            return carry

        lax.fori_loop(1, chain, step, 0)

    def arrived(i):
        def step(zz, carry):
            src = piece(i, zz * 2 + 1 - y)
            remote(src, src, sy.at[i, zz], ry.at[i, zz], y_dev).wait_recv()
            return carry

        lax.fori_loop(0, chain, step, 0)

    def sent(i):
        def step(zz, carry):
            over(i, zz).wait_send()

            @pl.when(jnp.logical_and(above, zz <= z))
            def _():
                hop(i, zz, su, up_dev).wait_send()

            @pl.when(jnp.logical_and(below, zz >= z))
            def _():
                hop(i, zz, sd, dn_dev).wait_send()

            return carry

        lax.fori_loop(0, chain, step, 0)

    def slot(j, k):
        if j == 0:
            return nl.at[:, aligned(k, lat)]
        if j == 1:
            return cn.at[k]
        return (dy if j == 2 else nf).at[aligned(k, own)]

    def row_copies(j, src=None):
        src = slot(j, p) if src is None else src
        return (
            remote(src, slot(j, p), xs.at[j], xr.at[j], x_dev),
            remote(src, slot(j, p), cs.at[j, 0], cr.at[j, 0], c_dev),
            remote(slot(j, px), slot(j, px), cs.at[j, 1], cr.at[j, 1], c_dev),
        )

    def start_rows(j, src=None):
        to_x, to_c, _ = row_copies(j, src)
        to_x.start()
        to_c.start()

    def pass_rows(j):
        to_x, _, on = row_copies(j)
        to_x.wait_recv()
        on.start()

    def have_rows(j):
        _, to_c, on = row_copies(j)
        to_c.wait_recv()
        on.wait_recv()

    def end_rows(j):
        to_x, to_c, on = row_copies(j)
        to_x.wait_send()
        to_c.wait_send()
        on.wait_send()

    def wo_slot(dd, k):
        return wo.at[aligned(dd * size + k, r)]

    def wo_copies(dd):
        return (
            remote(wo_slot(dd, p), wo_slot(dd, p), ws_x(dd), wr_x(dd), x_dev),
            remote(wo_slot(dd, p), wo_slot(dd, p), ws_c(dd, 0), wr_c(dd, 0), c_dev),
            remote(wo_slot(dd, px), wo_slot(dd, px), ws_c(dd, 1), wr_c(dd, 1), c_dev),
        )

    ws_x = lambda dd: ms.at[images + dd]
    wr_x = lambda dd: mr.at[images + dd]
    ws_c = lambda dd, e: mcs.at[images + dd, e]
    wr_c = lambda dd, e: mcr.at[images + dd, e]

    def each(lo, hi, body):
        def step(k, carry):
            body(k)
            return carry

        lax.fori_loop(lo, hi, step, 0)

    def wo_start(dd):
        to_x, to_c, _ = wo_copies(dd)
        to_x.start()
        to_c.start()

    def wo_pass(dd):
        to_x, _, on = wo_copies(dd)
        to_x.wait_recv()
        on.start()

    def wo_have(dd):
        _, to_c, on = wo_copies(dd)
        to_c.wait_recv()
        on.wait_recv()

    def wo_end(dd):
        for copy in wo_copies(dd):
            copy.wait_send()

    def media_slot(g, k):
        return nm.at[g, aligned(k, patches)]

    def media_copies(g):
        return (
            remote(media_slot(g, p), media_slot(g, p), ms.at[g], mr.at[g], x_dev),
            remote(media_slot(g, p), media_slot(g, p), mcs.at[g, 0], mcr.at[g, 0], c_dev),
            remote(media_slot(g, px), media_slot(g, px), mcs.at[g, 1], mcr.at[g, 1], c_dev),
        )

    def media_start(g):
        to_x, to_c, _ = media_copies(g)
        to_x.start()
        to_c.start()

    def media_pass(g):
        to_x, _, on = media_copies(g)
        to_x.wait_recv()
        on.start()

    def media_have(g):
        _, to_c, on = media_copies(g)
        to_c.wait_recv()
        on.wait_recv()

    def media_end(g):
        for copy in media_copies(g):
            copy.wait_send()

    media_gain, media_shift = 1.0 + norms[0:1, :], norms[1:2, :]
    latent_gain, latent_shift = 1.0 + norms[2:3, :], norms[3:4, :]
    ffn_gain, ffn_shift = 1.0 + norms[4:5, :], norms[5:6, :]

    def latent_norm(g):
        unit, _ = unit_of(latents[g])
        nl[g, aligned(p, lat)] = (unit * latent_gain + latent_shift).astype(BF16)

    def media_norm(g):
        unit, _ = unit_of(media[g])
        nm[g, aligned(p, patches)] = (unit * media_gain + media_shift).astype(BF16)

    each(0, images, latent_norm)
    start_rows(0)
    cn[p] = cns[...]
    start_rows(1, cns)
    local[0].wait()
    for copy in swaps:
        copy.wait_recv()
    start_own(0)
    start_own(1)
    each(0, images, media_norm)
    each(0, images, media_start)
    dys[...] = cot[...].astype(BF16)
    dy[aligned(p, own)] = dys[...]
    forward(0)
    start_own(2)
    pass_rows(0)
    pass_rows(1)
    each(0, 2, media_pass)
    forward(1)
    start_own(3)
    start_rows(2, dys)
    arrived(0)
    have_rows(0)
    have_rows(1)

    flat_nl = nl[...].reshape(images * size * lat, width)
    for i, out in enumerate((q, kl, vl)):
        out[...] = nn(flat_nl, wqkv[i]).astype(BF16).reshape(images, size * lat, cols)

    def image(g):
        media_have(g)
        kp[g] = nn(nm[g], wqkv[1]).astype(BF16)
        vp[g] = nn(nm[g], wqkv[2]).astype(BF16)
        real = cn[0, pl.ds(g, 1), :]
        for k in range(1, size):
            real = real + cn[k, pl.ds(g, 1), :]
        pp, plat = soft(head_rows(q[g], hands), kp[g], kl[g], real, scale)
        full = nn(pp.astype(BF16), vp[g]) + nn(plat.astype(BF16), vl[g])
        mixed[g] = own_columns(full, hands).astype(BF16)

    def image_and_pass(g):
        media_pass(g + 2)
        image(g)

    each(0, 2, image_and_pass)
    arrived(1)
    local[1].wait()
    each(0, 2 * chain, wo_start)
    each(2, 4, image_and_pass)
    forward(2)
    each(4, images - 2, image_and_pass)
    pass_rows(2)
    each(images - 2, images, image)
    each(0, 2 * chain, wo_pass)

    def head_part(k):
        return ab.at[:, :, lanes(k)]

    turns = []
    for k in range(1, size):
        to = lax.rem(p + k, size)
        turns.append(
            remote(mixed.at[:, aligned(to, lat)], head_part(p), ts.at[k], tr.at[k], (d, to))
        )
    for copy in turns:
        copy.start()
    ab[:, :, lanes(p)] = mixed[:, aligned(p, lat)]
    forward(3)
    each(0, 2 * chain, wo_have)
    for copy in turns:
        copy.wait_recv()
    flat_ab = ab[...].reshape(own, width)
    hidden[...] = latents[...].reshape(own, width) + matmul(flat_ab, wo)
    unit, _ = unit_of(hidden[...])
    nf[aligned(p, own)] = (unit * ffn_gain + ffn_shift).astype(BF16)
    start_rows(4)
    have_rows(2)
    pass_rows(4)
    have_rows(4)
    arrived(2)
    arrived(3)
    for copy in local[2:]:
        copy.wait()
    for copy in swaps + turns:
        copy.wait_send()
    for j in (0, 1, 2, 4):
        end_rows(j)
    each(0, images, media_end)
    each(0, 2 * chain, wo_end)
    for i in range(4):
        sent(i)


def front(held, media, latents, cot, cns, norms, n, size, hands, scale, ups):
    _, r, width = held.shape
    cols = width // size
    chain = n // 2
    g, patches, _ = media.shape
    lat = latents.shape[1]
    own = g * lat
    heads_lat, heads_patch = struct((g, size * lat, cols), BF16), struct((g, size * patches, cols), BF16)
    return pl.pallas_call(
        functools.partial(front_kernel, chain, size, hands, scale),
        name="front",
        out_shape=(
            struct((3, width, cols), BF16),
            struct((width, width), BF16),
            struct((ups, n * r, width), BF16),
            struct((ups, n * r, width), BF16),
            struct((g, size * patches, width), BF16),
            struct((g, size * lat, width), BF16),
            struct((size * own, width), BF16),
            struct((size,) + cns.shape, F32),
            heads_lat, heads_patch, heads_lat, heads_patch, heads_lat, heads_lat,
            struct((g, lat, width), BF16),
            struct((own, width), F32),
            struct((size * own, width), BF16),
        ),
        in_specs=[VMEM] * 6,
        out_specs=(VMEM,) * 17,
        scratch_shapes=[
            pltpu.VMEM((own, width), BF16),
            DMA((4,)), DMA((size,)), DMA((size,)),
            DMA((4, chain)), DMA((4, chain)), DMA((4, chain)), DMA((4, chain)), DMA((4, chain)),
            DMA((g + n,)), DMA((g + n,)), DMA((g + n, 2)), DMA((g + n, 2)),
            DMA((5,)), DMA((5,)), DMA((5, 2)), DMA((5, 2)),
            DMA((size,)), DMA((size,)),
        ],
        compiler_params=params(8),
    )(held, media, latents, cot, cns, norms)


def collect_kernel(chain, size, gq, gw, gu, gd, kp, kl,
                   oq, ow, ou, od, okp, okl,
                   yq, yw, yu, yd, uq, uw, uu, ud, dq, dw, du, dd,
                   wc, wsum, wx, total, kc, kx, lc, lx, fin,
                   ys, yr, us, ur, ds, dr, ks, kr, qs, qr):
    d, p, z, y, x, c = place()
    above, below = z + 1 < chain, z > 0
    up_dev, dn_dev = ((z + 1) * 2 + y, p), ((z - 1) * 2 + y, p)
    y_dev, x_dev, c_dev = (z * 2 + 1 - y, p), (d, (1 - x) * 2 + c), (d, x * 2 + 1 - c)
    meet(patch_peers(d, p, size) + [y_dev], [(above, up_dev), (below, dn_dev)])

    mine = (
        lambda k: gq.at[:, k], lambda k: total.at[k], lambda k: gu.at[:, k], lambda k: gd.at[:, k]
    )
    land_y, land_u, land_d = (yq, yw, yu, yd), (uq, uw, uu, ud), (dq, dw, du, dd)

    def over(i, zz):
        return remote(
            mine[i](zz * 2 + 1 - y), land_y[i].at[zz], ys.at[i, zz], yr.at[i, zz], y_dev
        )

    def send_over(i):
        def step(zz, carry):
            over(i, zz).start()
            return carry

        lax.fori_loop(0, chain, step, 0)

    def add_over(i):
        def step(zz, carry):
            over(i, zz).wait_recv()
            have = mine[i](zz * 2 + y)
            land_y[i][zz] = (land_y[i][zz].astype(F32) + have[...].astype(F32)).astype(BF16)
            return carry

        lax.fori_loop(0, chain, step, 0)

    def rise(i, zz):
        return remote(land_y[i].at[zz], land_u[i].at[zz], us.at[i, zz], ur.at[i, zz], up_dev)

    def fall(i, zz):
        return remote(land_y[i].at[zz], land_d[i].at[zz], ds.at[i, zz], dr.at[i, zz], dn_dev)

    def gather(i, zz, land):
        land_y[i][zz] = (land_y[i][zz].astype(F32) + land[i][zz].astype(F32)).astype(BF16)

    def along(i):
        def step(k, carry):
            s = chain - k

            @pl.when(z + s < chain)
            def _():
                @pl.when(below)
                def _():
                    rise(i, z + s).wait_recv()
                    gather(i, z + s, land_u)

                rise(i, z + s).start()

            @pl.when(z - s >= 0)
            def _():
                @pl.when(above)
                def _():
                    fall(i, z - s).wait_recv()
                    gather(i, z - s, land_d)

                fall(i, z - s).start()

            return carry

        lax.fori_loop(1, chain, step, 0)

    def finish(i, write):
        write(land_y[i][z].astype(F32))

        @pl.when(below)
        def _():
            rise(i, z).wait_recv()
            write(land_u[i][z].astype(F32), True)

        @pl.when(above)
        def _():
            fall(i, z).wait_recv()
            write(land_d[i][z].astype(F32), True)

    def into(ref):
        def write(value, more=False):
            ref[...] = ref[...] + value if more else value

        return write

    def sent(i):
        def step(zz, carry):
            over(i, zz).wait_send()

            @pl.when(zz > z)
            def _():
                rise(i, zz).wait_send()

            @pl.when(zz < z)
            def _():
                fall(i, zz).wait_send()

            return carry

        lax.fori_loop(0, chain, step, 0)

    send_over(2)
    w_core = remote(gw.at[:, :, 1 - c], wc, ks.at[0], kr.at[0], c_dev)
    p_core = remote(kp.at[:, :, 1 - c], kc, ks.at[1], kr.at[1], c_dev)
    l_core = remote(kl.at[:, :, 1 - c], lc, ks.at[2], kr.at[2], c_dev)
    w_core.start()
    p_core.start()
    l_core.start()
    send_over(3)
    send_over(0)

    w_core.wait_recv()

    def w_add(k, carry):
        wsum[k] = (wc[k, 1 - x].astype(F32) + gw[k, 1 - x, c].astype(F32)).astype(BF16)
        return carry

    lax.fori_loop(0, 2 * chain, w_add, 0)
    w_x = remote(wsum, wx, ks.at[3], kr.at[3], x_dev)
    w_x.start()

    p_core.wait_recv()
    images = kp.shape[0]

    def p_add(k, carry):
        kc[k] = (kc[k].astype(F32) + kp[k, :, c].astype(F32)).astype(BF16)
        return carry

    lax.fori_loop(0, images, p_add, 0)
    p_x = remote(kc.at[:, 1 - x], kx, ks.at[4], kr.at[4], x_dev)
    p_x.start()
    l_core.wait_recv()

    def l_add(k, carry):
        lc[k] = (lc[k].astype(F32) + kl[k, :, c].astype(F32)).astype(BF16)
        return carry

    lax.fori_loop(0, images, l_add, 0)
    l_x = remote(lc.at[:, 1 - x], lx, ks.at[5], kr.at[5], x_dev)
    l_x.start()

    w_x.wait_recv()

    def w_last(k, carry):
        total[k] = (
            wc[k, x].astype(F32) + gw[k, x, c].astype(F32) + wx[k].astype(F32)
        ).astype(BF16)
        return carry

    lax.fori_loop(0, 2 * chain, w_last, 0)
    send_over(1)

    add_over(2)
    along(2)
    add_over(3)
    along(3)
    add_over(0)
    along(0)
    add_over(1)
    along(1)
    finish(2, into(ou))
    finish(3, into(od))
    finish(0, into(fin))
    swaps = []
    for k in range(1, size):
        q = lax.rem(p + k, size)
        swaps.append(remote(fin.at[:, q], oq.at[p], qs.at[k], qr.at[k], (d, q)))
    for copy in swaps:
        copy.start()
    finish(1, into(ow))
    oq[p] = fin[:, p]

    p_x.wait_recv()

    def p_last(k, carry):
        okp[k] = kc[k, x].astype(F32) + kx[k].astype(F32)
        return carry

    lax.fori_loop(0, images, p_last, 0)
    l_x.wait_recv()

    def l_last(k, carry):
        okl[k] = lc[k, x].astype(F32) + lx[k].astype(F32)
        return carry

    lax.fori_loop(0, images, l_last, 0)
    for copy in swaps:
        copy.wait()
    for i in range(4):
        sent(i)
    for copy in (w_core, p_core, l_core, w_x, p_x, l_x):
        copy.wait_send()


def collect(gq, gw, gu, gd, kp, kl, n, size):
    chain = n // 2
    three, _, _, r, cols = gq.shape
    width = gw.shape[-1]
    fu, fd = gu.shape[0], gd.shape[0]
    g, two, _, patches, _ = kp.shape
    lat = kl.shape[3]
    lands = [
        ((three, size, r, cols)), ((r, width)), ((fu, r, width)), ((fd, r, width)),
    ]
    stage = [pltpu.VMEM((chain,) + s, BF16) for s in lands]
    return pl.pallas_call(
        functools.partial(collect_kernel, chain, size),
        name="collect",
        out_shape=(
            struct((size, three, r, cols), F32),
            struct((r, width), F32),
            struct((fu, r, width), F32),
            struct((fd, r, width), F32),
            struct((g, patches, width), F32),
            struct((g, lat, width), F32),
        ),
        in_specs=[VMEM] * 6,
        out_specs=(VMEM,) * 6,
        scratch_shapes=stage * 3
        + [
            pltpu.VMEM((n, two, r, width), BF16),
            pltpu.VMEM((n, r, width), BF16),
            pltpu.VMEM((n, r, width), BF16),
            pltpu.VMEM((n, r, width), BF16),
            pltpu.VMEM((g, two, patches, width), BF16),
            pltpu.VMEM((g, patches, width), BF16),
            pltpu.VMEM((g, two, lat, width), BF16),
            pltpu.VMEM((g, lat, width), BF16),
            pltpu.VMEM((three, size, r, cols), F32),
        ]
        + [DMA((4, chain))] * 6
        + [DMA((6,)), DMA((6,)), DMA((size,)), DMA((size,))],
        compiler_params=params(6),
    )(gq, gw, gu, gd, kp, kl)


def total_kernel(hops, src, out, hold, land, ss, rs):
    d, p = lax.axis_index("dp"), lax.axis_index("patch")

    def flip(v, bit):
        return v + bit - 2 * bit * lax.rem(lax.div(v, bit), 2)

    to = [(d, flip(p, b)) if kind else (flip(d, b), p) for kind, b in hops]
    meet(to)
    sends = []
    for i, who in enumerate(to):
        copy = remote(src if i == 0 else hold.at[i], land.at[i], ss.at[i], rs.at[i], who)
        copy.start()
        copy.wait_recv()
        sends.append(copy)
        value = (src[...] if i == 0 else hold[i]) + land[i]
        if i + 1 < len(to):
            hold[i + 1] = value
        else:
            out[...] = value
    for copy in sends:
        copy.wait_send()


def total(src, n, size):
    hops = [(True, 1 << b) for b in range(size.bit_length() - 1)]
    hops += [(False, 1 << b) for b in range(n.bit_length() - 1)]
    return pl.pallas_call(
        functools.partial(total_kernel, hops),
        name="total",
        out_shape=struct(src.shape, F32),
        in_specs=[VMEM],
        out_specs=VMEM,
        scratch_shapes=[
            pltpu.VMEM((len(hops),) + src.shape, F32),
            pltpu.VMEM((len(hops),) + src.shape, F32),
            DMA((len(hops),)), DMA((len(hops),)),
        ],
        compiler_params=params(7),
    )(src)


def norm_parts(values, gain_row, shift_row):
    average = jnp.mean(values, axis=-1, keepdims=True)
    centred = values - average
    spread_ = jnp.mean(centred * centred, axis=-1, keepdims=True)
    scaled = lax.rsqrt(spread_ + 1e-05)
    unit_rows = centred * scaled
    return (unit_rows * gain_row + shift_row, unit_rows, scaled)


def norm_back(grad_out, unit_rows, scaled, gain_row):
    inner_grad = grad_out * gain_row
    plain_mean = jnp.mean(inner_grad, axis=-1, keepdims=True)
    cross_mean = jnp.mean(inner_grad * unit_rows, axis=-1, keepdims=True)
    return scaled * (inner_grad - plain_mean - unit_rows * cross_mean)


def gain_terms(grad_out, unit_rows):
    width = grad_out.shape[-1]
    flat_grad = grad_out.reshape(-1, width)
    flat_unit = unit_rows.reshape(-1, width)
    return [jnp.sum(flat_grad * flat_unit, axis=0), jnp.sum(flat_grad, axis=0)]


def exact_gelu(values):
    return jax.nn.gelu(values, approximate=False)


def adamw_update(parameter, first_m, second_m, average, gradient, factor, decay_rate):
    clipped = gradient * factor
    new_first = 0.9 * first_m + 0.1 * clipped
    new_second = 0.999 * second_m + 0.001 * clipped * clipped
    first_hat = new_first / (1.0 - 0.9**STEP)
    second_hat = new_second / (1.0 - 0.999**STEP)
    new_param = parameter - 0.02 * (
        first_hat / (jnp.sqrt(second_hat) + 1e-08) + decay_rate * parameter
    )
    new_avg = 0.8 * average + 0.2 * new_param
    return (new_param, new_first, new_second, new_avg)


def dot32(spec, a, b):
    return jnp.einsum(spec, a, b, preferred_element_type=F32)


def on_device(n, size, media_tokens, patch_mask, latents, cotangent, weights, weights_first,
              weights_second, weights_average, norm_params, norm_first, norm_second, norm_average):
    g, patches, width = media_tokens.shape
    lat = latents.shape[1]
    blocks = weights.shape[0]
    r = width // (n * size)
    cols = width // size
    hands = HEADS // size
    scale = 1.0 / math.sqrt(width // HEADS)
    ups = FF // width
    own = g * lat
    media_gain, latent_gain, ffn_gain = 1.0 + norm_params[0], 1.0 + norm_params[2], 1.0 + norm_params[4]

    cot = cotangent.reshape(own, width)
    media_norm, media_unit, media_scale = norm_parts(media_tokens, media_gain, norm_params[1])
    latent_norm, latent_unit, latent_scale = norm_parts(latents, latent_gain, norm_params[3])
    held = weights.astype(BF16).reshape(blocks, r, width)
    count_rows = (g + 15) // 16 * 16
    counts = jnp.sum((patch_mask > 0).astype(F32), axis=1)
    counts = jnp.broadcast_to(jnp.pad(counts, (0, count_rows - g))[:, None], (count_rows, size * patches))
    wqkv, wo, up, dn, nm, nl, dy, cn, q, kp, kl, vp, vl, mixed, ab, hidden, nf = front(
        held, media_tokens, latents, cot, counts, norm_params, n, size, hands, scale, ups
    )
    ab = ab.reshape(own, width)
    up = up.reshape(-1, width)
    dn = dn.reshape(-1, width)
    nm = nm.reshape(g * size * patches, width)
    nl = nl.reshape(g * size * lat, width)
    real = jnp.sum(cn[:, :g, 0], axis=0).astype(jnp.int32)
    _, ffn_unit, ffn_scale = norm_parts(hidden, ffn_gain, norm_params[5])
    u = dot32("rd,fd->rf", nf, up)
    active, pull = jax.vjp(exact_gelu, u)
    gb = active.astype(BF16)
    y_part = dot32("rf,fd->rd", gb, dn).astype(BF16)
    du = pull(dot32("rd,fd->rf", dy, dn))[0].astype(BF16)
    f_part = dot32("rf,fd->rd", du, up).astype(BF16)
    g_dn = dot32("rf,rd->fd", gb, dy).astype(BF16)
    g_up = dot32("rf,rd->fd", du, nf).astype(BF16)
    both = split_rows(jnp.stack([y_part, f_part]).reshape(2, 2, 2, own, width), 3)
    latents_out = (hidden + both[0]).reshape(g, lat, width)
    d_ffn = both[1]
    ffn_terms = gain_terms(d_ffn, ffn_unit)
    d_hidden = cot + norm_back(d_ffn, ffn_unit, ffn_scale, ffn_gain)

    do = d_hidden.astype(BF16)
    g_wo = dot32("rd,re->de", ab, do).astype(BF16)
    da = dot32("re,de->rd", do, wo).astype(BF16).reshape(g, lat, width)
    da = to_heads(da, size, 4).reshape(g, size * lat, cols)
    dq, dkp, dkl, dvp, dvl = attend_back(real, q, kp, kl, vp, vl, da, hands, scale)

    def flat(a):
        return a.reshape(-1, cols)

    dq, dkp, dkl, dvp, dvl = flat(dq), flat(dkp), flat(dkl), flat(dvp), flat(dvl)
    g_qkv = jnp.stack([
        dot32("rd,re->de", nl, dq),
        dot32("rd,re->de", nm, dkp) + dot32("rd,re->de", nl, dkl),
        dot32("rd,re->de", nm, dvp) + dot32("rd,re->de", nl, dvl),
    ]).astype(BF16)
    d_nm = (dot32("re,de->rd", dkp, wqkv[1]) + dot32("re,de->rd", dvp, wqkv[2])).astype(BF16)
    d_nl = (
        dot32("re,de->rd", dkl, wqkv[1]) + dot32("re,de->rd", dvl, wqkv[2])
        + dot32("re,de->rd", dq, wqkv[0])
    ).astype(BF16)

    oq, ow, ou, od, d_media, d_latent = collect(
        g_qkv.reshape(3, n, size, r, cols), g_wo.reshape(n, 2, 2, r, width),
        g_up.reshape(ups, n, r, width), g_dn.reshape(ups, n, r, width),
        d_nm.reshape(g, 2, 2, patches, width), d_nl.reshape(g, 2, 2, lat, width), n, size,
    )
    media_grad = norm_back(d_media, media_unit, media_scale, media_gain)
    latents_grad = d_hidden.reshape(g, lat, width) + norm_back(
        d_latent, latent_unit, latent_scale, latent_gain
    )
    grads = jnp.concatenate([
        oq.transpose(1, 2, 0, 3).reshape(3, r, width), ow[None], ou, od,
    ])
    square = jnp.broadcast_to(jnp.sum(grads * grads), (width,))
    rows = jnp.stack(
        gain_terms(d_media, media_unit) + gain_terms(d_latent, latent_unit) + ffn_terms
        + [square, jnp.zeros_like(square)]
    )
    sums = total(rows, n, size)
    norm_grads = sums[:6]
    grad_norm = jnp.sqrt(sums[6, 0] + jnp.sum(norm_grads * norm_grads))
    clip = jnp.minimum(1.0, 1.0 / (grad_norm + 1e-06))
    new_w, new_first, new_second, new_avg = adamw_update(
        weights, weights_first, weights_second, weights_average,
        grads.reshape(weights.shape), clip, 0.1,
    )
    new_n, new_nf, new_ns, new_na = adamw_update(
        norm_params, norm_first, norm_second, norm_average, norm_grads, clip, 0.0
    )
    return (
        latents_out, media_grad, latents_grad, grad_norm, new_w, new_w.astype(BF16), new_first,
        new_second, new_avg, new_n, new_nf, new_ns, new_na, norm_grads[4:6],
    )


def solution(mesh):
    n, size = mesh.shape["dp"], mesh.shape["patch"]
    rows, weight = P("dp", "patch", None), P(None, ("dp", "patch"))
    return jax.shard_map(
        functools.partial(on_device, n, size),
        mesh=mesh,
        in_specs=(rows, P("dp", "patch"), rows, rows) + (weight,) * 4 + (P(),) * 4,
        out_specs=(rows, rows, rows, P()) + (weight,) * 5 + (P(),) * 5,
        check_vma=False,
    )
```

```python
import functools
import math

import jax
import jax.numpy as jnp
from jax import lax
from jax.experimental import pallas as pl
from jax.experimental.pallas import tpu as pltpu
from jax.sharding import PartitionSpec as P

HEADS = 16
FF = 4096
STEP = 7
MESH = pl.DeviceIdType.MESH
F32 = jnp.float32
BF16 = jnp.bfloat16
ANY = pl.BlockSpec(memory_space=pl.ANY)
VMEM = pl.BlockSpec(memory_space=pltpu.VMEM)
DMA = pltpu.SemaphoreType.DMA
VMEM_LIMIT = 64 * 1024 * 1024 - 65536


def struct(shape, kind):
    return jax.ShapeDtypeStruct(shape, kind)


def place():
    d, p = lax.axis_index("dp"), lax.axis_index("patch")
    return d, p, lax.div(d, 2), lax.rem(d, 2), lax.div(p, 2), lax.rem(p, 2)


def remote(src, dst, send, recv, to):
    return pltpu.make_async_remote_copy(
        src_ref=src, dst_ref=dst, send_sem=send, recv_sem=recv, device_id=to, device_id_type=MESH
    )


def meet(always, maybe=()):
    barrier = pltpu.get_barrier_semaphore()
    count = len(always)
    for to in always:
        pl.semaphore_signal(barrier, inc=1, device_id=to, device_id_type=MESH)
    for there, to in maybe:

        @pl.when(there)
        def _(to=to):
            pl.semaphore_signal(barrier, inc=1, device_id=to, device_id_type=MESH)

        count = count + there.astype(jnp.int32)
    pl.semaphore_wait(barrier, count)


def patch_peers(d, p, size):
    return [(d, lax.rem(p + k, size)) for k in range(1, size)]


def params(number):
    return pltpu.CompilerParams(
        collective_id=number, has_side_effects=True, vmem_limit_bytes=VMEM_LIMIT
    )


def spread_kernel(chain, size, qs, wos, ups, dns, nms, nls, dys, cns,
                  wqkv, wo, up, dn, nm, nl, dy, cn,
                  loc, a_s, a_r, su, sd, sy, rz, ry, xs, xr, cs, cr):
    d, p, z, y, x, c = place()
    above, below = z + 1 < chain, z > 0
    up_dev, dn_dev = ((z + 1) * 2 + y, p), ((z - 1) * 2 + y, p)
    y_dev, x_dev, c_dev = (z * 2 + 1 - y, p), (d, (1 - x) * 2 + c), (d, x * 2 + 1 - c)
    px, pc = (1 - x) * 2 + c, x * 2 + 1 - c
    pd = (1 - x) * 2 + 1 - c
    meet(patch_peers(d, p, size) + [y_dev], [(above, up_dev), (below, dn_dev)])

    own = [
        (qs.at[p], wqkv.at[:, d, p]), (wos, wo.at[d, p]), (ups, up.at[:, d]), (dns, dn.at[:, d]),
        (nms, nm.at[:, p]), (nls, nl.at[:, p]), (dys, dy.at[p]), (cns, cn.at[p]),
    ]
    local = [pltpu.make_async_copy(a, b, loc.at[i]) for i, (a, b) in enumerate(own)]
    for copy in local:
        copy.start()
    swaps = []
    for k in range(1, size):
        q = lax.rem(p + k, size)
        swaps.append(remote(qs.at[q], wqkv.at[:, d, p], a_s.at[k], a_r.at[k], (d, q)))
    for copy in swaps:
        copy.start()

    rows = [(nms, nm), (nls, nl), (cns, cn), (dys, dy)]

    def slot(j, q):
        ref = rows[j][1] if j < 4 else wo
        return ref.at[q] if j in (2, 3) else ref.at[:, q]

    def row_copies(j):
        src = rows[j][0] if j < 4 else slot(j, p)
        return (
            remote(src, slot(j, p), xs.at[j], xr.at[j], x_dev),
            remote(src, slot(j, p), cs.at[j, 0], cr.at[j, 0], c_dev),
            remote(slot(j, px), slot(j, px), cs.at[j, 1], cr.at[j, 1], c_dev),
        )

    def start_rows(j):
        to_x, to_c, _ = row_copies(j)
        to_x.start()
        to_c.start()

    def pass_rows(j):
        to_x, _, on = row_copies(j)
        to_x.wait_recv()
        on.start()

    def end_rows(j):
        to_x, to_c, on = row_copies(j)
        to_c.wait_recv()
        on.wait_recv()
        to_x.wait_send()
        to_c.wait_send()
        on.wait_send()

    for j in range(4):
        start_rows(j)

    def piece(i, dd):
        return (wqkv.at[:, dd], wo.at[dd, p], up.at[:, dd], dn.at[:, dd])[i]

    first = (wqkv.at[:, d], wos, ups, dns)

    def hop(i, zz, sends, to, own_src=False):
        src = first[i] if own_src else piece(i, zz * 2 + y)
        return remote(src, piece(i, zz * 2 + y), sends.at[i, zz], rz.at[i, zz], to)

    def over(i, zz, own_src=False):
        src = first[i] if own_src else piece(i, zz * 2 + y)
        return remote(src, piece(i, zz * 2 + y), sy.at[i, zz], ry.at[i, zz], y_dev)

    def start_own(i):
        @pl.when(above)
        def _():
            hop(i, z, su, up_dev, True).start()

        @pl.when(below)
        def _():
            hop(i, z, sd, dn_dev, True).start()

        over(i, z, True).start()

    def forward(i):
        def step(s, carry):
            @pl.when(z - s >= 0)
            def _():
                hop(i, z - s, su, up_dev).wait_recv()

                @pl.when(above)
                def _():
                    hop(i, z - s, su, up_dev).start()

                over(i, z - s).start()

            @pl.when(z + s < chain)
            def _():
                hop(i, z + s, sd, dn_dev).wait_recv()

                @pl.when(below)
                def _():
                    hop(i, z + s, sd, dn_dev).start()

                over(i, z + s).start()

            return carry

        lax.fori_loop(1, chain, step, 0)

    def arrived(i):
        def step(zz, carry):
            src = piece(i, zz * 2 + 1 - y)
            remote(src, src, sy.at[i, zz], ry.at[i, zz], y_dev).wait_recv()
            return carry

        lax.fori_loop(0, chain, step, 0)

    def sent(i):
        def step(zz, carry):
            over(i, zz).wait_send()

            @pl.when(jnp.logical_and(above, zz <= z))
            def _():
                hop(i, zz, su, up_dev).wait_send()

            @pl.when(jnp.logical_and(below, zz >= z))
            def _():
                hop(i, zz, sd, dn_dev).wait_send()

            return carry

        lax.fori_loop(0, chain, step, 0)

    local[0].wait()
    for copy in swaps:
        copy.wait_recv()
    start_own(0)
    start_own(1)
    forward(0)
    start_own(2)
    forward(1)
    start_own(3)
    local[1].wait()
    arrived(1)
    start_rows(4)
    forward(2)
    for j in range(5):
        pass_rows(j)
    forward(3)
    arrived(0)
    arrived(2)
    arrived(3)
    for j in range(5):
        end_rows(j)
    for copy in swaps:
        copy.wait_send()
    for i in range(4):
        sent(i)
    for copy in local[2:]:
        copy.wait()


def spread(qs, wos, ups, dns, nms, nls, dys, cns, n, size):
    _, three, r, cols = qs.shape
    width = wos.shape[1]
    chain = n // 2
    g, patches, _ = nms.shape
    lat = nls.shape[1]
    return pl.pallas_call(
        functools.partial(spread_kernel, chain, size),
        name="spread",
        out_shape=(
            struct((three, n, size, r, cols), BF16),
            struct((n, size, r, width), BF16),
            struct((ups.shape[0], n, r, width), BF16),
            struct((dns.shape[0], n, r, width), BF16),
            struct((g, size, patches, width), BF16),
            struct((g, size, lat, width), BF16),
            struct((size,) + dys.shape, BF16),
            struct((size,) + cns.shape, F32),
        ),
        in_specs=[VMEM] * 8,
        out_specs=(ANY,) * 8,
        scratch_shapes=[
            DMA((8,)), DMA((size,)), DMA((size,)),
            DMA((4, chain)), DMA((4, chain)), DMA((4, chain)), DMA((4, chain)), DMA((4, chain)),
            DMA((5,)), DMA((5,)), DMA((5, 2)), DMA((5, 2)),
        ],
        compiler_params=params(0),
    )(qs, wos, ups, dns, nms, nls, dys, cns)


def to_rows_kernel(size, src, out, loc, ss, rs):
    d, p = lax.axis_index("dp"), lax.axis_index("patch")
    cols = src.shape[3]
    meet(patch_peers(d, p, size))
    here = out.at[:, :, pl.ds(pl.multiple_of(p * cols, cols), cols)]
    copies = []
    for k in range(1, size):
        q = lax.rem(p + k, size)
        copies.append(remote(src.at[:, q], here, ss.at[k], rs.at[k], (d, q)))
    for copy in copies:
        copy.start()
    mine = pltpu.make_async_copy(src.at[:, p], here, loc)
    mine.start()
    mine.wait()
    for copy in copies:
        copy.wait()


def to_rows(src, size, number):
    g, _, lat, cols = src.shape
    return pl.pallas_call(
        functools.partial(to_rows_kernel, size),
        name="to_rows",
        out_shape=struct((g, lat, size * cols), src.dtype),
        in_specs=[VMEM],
        out_specs=VMEM,
        scratch_shapes=[DMA, DMA((size,)), DMA((size,))],
        compiler_params=params(number),
    )(src)


def to_heads_kernel(size, src, out, loc, ss, rs):
    d, p = lax.axis_index("dp"), lax.axis_index("patch")
    cols = out.shape[3]
    meet(patch_peers(d, p, size))

    def part(q):
        return src.at[:, :, pl.ds(pl.multiple_of(q * cols, cols), cols)]

    copies = []
    for k in range(1, size):
        q = lax.rem(p + k, size)
        copies.append(remote(part(q), out.at[:, p], ss.at[k], rs.at[k], (d, q)))
    for copy in copies:
        copy.start()
    mine = pltpu.make_async_copy(part(p), out.at[:, p], loc)
    mine.start()
    mine.wait()
    for copy in copies:
        copy.wait()


def to_heads(src, size, number):
    g, lat, width = src.shape
    return pl.pallas_call(
        functools.partial(to_heads_kernel, size),
        name="to_heads",
        out_shape=struct((g, size, lat, width // size), src.dtype),
        in_specs=[VMEM],
        out_specs=VMEM,
        scratch_shapes=[DMA, DMA((size,)), DMA((size,))],
        compiler_params=params(number),
    )(src)


def join_rows_kernel(src, out, loc, ss, rs):
    d, p, z, y, x, c = place()
    x_dev, c_dev = (d, (1 - x) * 2 + c), (d, x * 2 + 1 - c)
    px = (1 - x) * 2 + c
    meet([x_dev, c_dev])
    to_x = remote(src, out.at[p], ss.at[0], rs.at[0], x_dev)
    to_c = remote(src, out.at[p], ss.at[1], rs.at[1], c_dev)
    on = remote(out.at[px], out.at[px], ss.at[2], rs.at[2], c_dev)
    to_x.start()
    to_c.start()
    mine = pltpu.make_async_copy(src, out.at[p], loc)
    mine.start()
    to_x.wait_recv()
    on.start()
    mine.wait()
    to_c.wait()
    on.wait()
    to_x.wait_send()


def join_rows(src, size, number):
    return pl.pallas_call(
        join_rows_kernel,
        name="join_rows",
        out_shape=struct((size,) + src.shape, src.dtype),
        in_specs=[VMEM],
        out_specs=VMEM,
        scratch_shapes=[DMA, DMA((3,)), DMA((3,))],
        compiler_params=params(number),
    )(src)


def split_rows_kernel(ins, src, out, half, mid, quarter, ss, rs):
    d, p, z, y, x, c = place()
    x_dev, c_dev = (d, (1 - x) * 2 + c), (d, x * 2 + 1 - c)
    meet([x_dev, c_dev])
    first = [remote(src.at[i, :, 1 - c], half.at[i], ss.at[i], rs.at[i], c_dev) for i in range(ins)]
    for copy in first:
        copy.start()
    second = []
    for i in range(ins):
        first[i].wait_recv()
        mid[i] = (half[i, 1 - x].astype(F32) + src[i, 1 - x, c].astype(F32)).astype(BF16)
        copy = remote(mid.at[i], quarter.at[i], ss.at[ins + i], rs.at[ins + i], x_dev)
        copy.start()
        second.append(copy)
    for i in range(ins):
        out[i] = half[i, x].astype(F32) + src[i, x, c].astype(F32)
    for i in range(ins):
        second[i].wait_recv()
        out[i] = out[i] + quarter[i].astype(F32)
    for copy in first + second:
        copy.wait_send()


def split_rows(src, number):
    ins, _, _, rows, width = src.shape
    return pl.pallas_call(
        functools.partial(split_rows_kernel, ins),
        name="split_rows",
        out_shape=struct((ins, rows, width), F32),
        in_specs=[VMEM],
        out_specs=VMEM,
        scratch_shapes=[
            pltpu.VMEM((ins, 2, rows, width), BF16),
            pltpu.VMEM((ins, rows, width), BF16),
            pltpu.VMEM((ins, rows, width), BF16),
            DMA((2 * ins,)), DMA((2 * ins,)),
        ],
        compiler_params=params(number),
    )(src)


def head_rows(q, hands):
    rows, cols = q.shape
    size = cols // hands
    lane = lax.broadcasted_iota(jnp.int32, (rows, cols), 1)
    zero = jnp.zeros_like(q)
    parts = [
        jnp.where(jnp.logical_and(lane >= h * size, lane < (h + 1) * size), q, zero)
        for h in range(hands)
    ]
    return jnp.concatenate(parts, axis=0)


def own_columns(full, hands):
    rows, cols = full.shape[0] // hands, full.shape[1]
    size = cols // hands
    lane = lax.broadcasted_iota(jnp.int32, (rows, cols), 1)
    out = jnp.zeros((rows, cols), F32)
    for h in range(hands):
        keep = jnp.logical_and(lane >= h * size, lane < (h + 1) * size)
        out = jnp.where(keep, full[h * rows : (h + 1) * rows], out)
    return out


def nt(a, b):
    return lax.dot_general(a, b, (((1,), (1,)), ((), ())), preferred_element_type=F32)


def nn(a, b):
    return lax.dot_general(a, b, (((1,), (0,)), ((), ())), preferred_element_type=F32)


def tn(a, b):
    return lax.dot_general(a, b, (((0,), (0,)), ((), ())), preferred_element_type=F32)


def soft(qb, kp, kl, real, scale):
    sp = nt(qb, kp) * scale
    sl = nt(qb, kl) * scale
    key = lax.broadcasted_iota(jnp.int32, sp.shape, 1).astype(F32)
    sp = jnp.where(key < real, sp, -1e30)
    peak = jnp.maximum(jnp.max(sp, axis=1, keepdims=True), jnp.max(sl, axis=1, keepdims=True))
    ep, el = jnp.exp(sp - peak), jnp.exp(sl - peak)
    total = jnp.sum(ep, axis=1, keepdims=True) + jnp.sum(el, axis=1, keepdims=True)
    return ep / total, el / total


def attend_kernel(hands, scale, real, q, kp, kl, vp, vl, out):
    g = pl.program_id(0)
    qb = head_rows(q[0], hands)
    pp, plat = soft(qb, kp[0], kl[0], real[g].astype(F32), scale)
    full = nn(pp.astype(BF16), vp[0]) + nn(plat.astype(BF16), vl[0])
    out[0] = own_columns(full, hands).astype(BF16)


def attend(real, q, kp, kl, vp, vl, hands, scale):
    g, lat, cols = q.shape
    patches = kp.shape[1]

    def spec(rows):
        return pl.BlockSpec((1, rows, cols), lambda i, real: (i, 0, 0))

    return pl.pallas_call(
        functools.partial(attend_kernel, hands, scale),
        name="attend",
        grid_spec=pltpu.PrefetchScalarGridSpec(
            num_scalar_prefetch=1,
            grid=(g,),
            in_specs=[spec(lat), spec(patches), spec(lat), spec(patches), spec(lat)],
            out_specs=spec(lat),
        ),
        out_shape=struct((g, lat, cols), BF16),
        compiler_params=pltpu.CompilerParams(dimension_semantics=("arbitrary",)),
    )(real, q, kp, kl, vp, vl)


def attend_back_kernel(hands, scale, real, q, kp, kl, vp, vl, da, dq, dkp, dkl, dvp, dvl):
    g = pl.program_id(0)
    qb = head_rows(q[0], hands)
    dab = head_rows(da[0], hands)
    pp, plat = soft(qb, kp[0], kl[0], real[g].astype(F32), scale)
    gp, gl = nt(dab, vp[0]), nt(dab, vl[0])
    delta = jnp.sum(pp * gp, axis=1, keepdims=True) + jnp.sum(plat * gl, axis=1, keepdims=True)
    sp, sl = (pp * (gp - delta)).astype(BF16), (plat * (gl - delta)).astype(BF16)
    dvp[0] = tn(pp.astype(BF16), dab).astype(BF16)
    dvl[0] = tn(plat.astype(BF16), dab).astype(BF16)
    dkp[0] = (tn(sp, qb) * scale).astype(BF16)
    dkl[0] = (tn(sl, qb) * scale).astype(BF16)
    full = nn(sp, kp[0]) + nn(sl, kl[0])
    dq[0] = (own_columns(full, hands) * scale).astype(BF16)


def attend_back(real, q, kp, kl, vp, vl, da, hands, scale):
    g, lat, cols = q.shape
    patches = kp.shape[1]

    def spec(rows):
        return pl.BlockSpec((1, rows, cols), lambda i, real: (i, 0, 0))

    return pl.pallas_call(
        functools.partial(attend_back_kernel, hands, scale),
        name="attend_back",
        grid_spec=pltpu.PrefetchScalarGridSpec(
            num_scalar_prefetch=1,
            grid=(g,),
            in_specs=[spec(lat), spec(patches), spec(lat), spec(patches), spec(lat), spec(lat)],
            out_specs=[spec(lat), spec(patches), spec(lat), spec(patches), spec(lat)],
        ),
        out_shape=(
            struct((g, lat, cols), BF16),
            struct((g, patches, cols), BF16),
            struct((g, lat, cols), BF16),
            struct((g, patches, cols), BF16),
            struct((g, lat, cols), BF16),
        ),
        compiler_params=pltpu.CompilerParams(dimension_semantics=("arbitrary",)),
    )(real, q, kp, kl, vp, vl, da)


def collect_kernel(chain, size, gq, gw, gu, gd, kp, kl,
                   oq, ow, ou, od, okp, okl,
                   yq, yw, yu, yd, uq, uw, uu, ud, dq, dw, du, dd,
                   wc, wsum, wx, total, kc, kx, lc, lx, fin,
                   ys, yr, us, ur, ds, dr, ks, kr, qs, qr):
    d, p, z, y, x, c = place()
    above, below = z + 1 < chain, z > 0
    up_dev, dn_dev = ((z + 1) * 2 + y, p), ((z - 1) * 2 + y, p)
    y_dev, x_dev, c_dev = (z * 2 + 1 - y, p), (d, (1 - x) * 2 + c), (d, x * 2 + 1 - c)
    meet(patch_peers(d, p, size) + [y_dev], [(above, up_dev), (below, dn_dev)])

    mine = (
        lambda k: gq.at[:, k], lambda k: total.at[k], lambda k: gu.at[:, k], lambda k: gd.at[:, k]
    )
    land_y, land_u, land_d = (yq, yw, yu, yd), (uq, uw, uu, ud), (dq, dw, du, dd)

    def over(i, zz):
        return remote(
            mine[i](zz * 2 + 1 - y), land_y[i].at[zz], ys.at[i, zz], yr.at[i, zz], y_dev
        )

    def send_over(i):
        def step(zz, carry):
            over(i, zz).start()
            return carry

        lax.fori_loop(0, chain, step, 0)

    def add_over(i):
        def step(zz, carry):
            over(i, zz).wait_recv()
            have = mine[i](zz * 2 + y)
            land_y[i][zz] = (land_y[i][zz].astype(F32) + have[...].astype(F32)).astype(BF16)
            return carry

        lax.fori_loop(0, chain, step, 0)

    def rise(i, zz):
        return remote(land_y[i].at[zz], land_u[i].at[zz], us.at[i, zz], ur.at[i, zz], up_dev)

    def fall(i, zz):
        return remote(land_y[i].at[zz], land_d[i].at[zz], ds.at[i, zz], dr.at[i, zz], dn_dev)

    def gather(i, zz, land):
        land_y[i][zz] = (land_y[i][zz].astype(F32) + land[i][zz].astype(F32)).astype(BF16)

    def along(i):
        def step(k, carry):
            s = chain - k

            @pl.when(z + s < chain)
            def _():
                @pl.when(below)
                def _():
                    rise(i, z + s).wait_recv()
                    gather(i, z + s, land_u)

                rise(i, z + s).start()

            @pl.when(z - s >= 0)
            def _():
                @pl.when(above)
                def _():
                    fall(i, z - s).wait_recv()
                    gather(i, z - s, land_d)

                fall(i, z - s).start()

            return carry

        lax.fori_loop(1, chain, step, 0)

    def finish(i, write):
        write(land_y[i][z].astype(F32))

        @pl.when(below)
        def _():
            rise(i, z).wait_recv()
            write(land_u[i][z].astype(F32), True)

        @pl.when(above)
        def _():
            fall(i, z).wait_recv()
            write(land_d[i][z].astype(F32), True)

    def into(ref):
        def write(value, more=False):
            ref[...] = ref[...] + value if more else value

        return write

    def sent(i):
        def step(zz, carry):
            over(i, zz).wait_send()

            @pl.when(zz > z)
            def _():
                rise(i, zz).wait_send()

            @pl.when(zz < z)
            def _():
                fall(i, zz).wait_send()

            return carry

        lax.fori_loop(0, chain, step, 0)

    send_over(2)
    w_core = remote(gw.at[:, :, 1 - c], wc, ks.at[0], kr.at[0], c_dev)
    p_core = remote(kp.at[:, :, 1 - c], kc, ks.at[1], kr.at[1], c_dev)
    l_core = remote(kl.at[:, :, 1 - c], lc, ks.at[2], kr.at[2], c_dev)
    w_core.start()
    p_core.start()
    l_core.start()
    send_over(3)
    send_over(0)

    w_core.wait_recv()

    def w_add(k, carry):
        wsum[k] = (wc[k, 1 - x].astype(F32) + gw[k, 1 - x, c].astype(F32)).astype(BF16)
        return carry

    lax.fori_loop(0, 2 * chain, w_add, 0)
    w_x = remote(wsum, wx, ks.at[3], kr.at[3], x_dev)
    w_x.start()

    p_core.wait_recv()
    images = kp.shape[0]

    def p_add(k, carry):
        kc[k] = (kc[k].astype(F32) + kp[k, :, c].astype(F32)).astype(BF16)
        return carry

    lax.fori_loop(0, images, p_add, 0)
    p_x = remote(kc.at[:, 1 - x], kx, ks.at[4], kr.at[4], x_dev)
    p_x.start()
    l_core.wait_recv()

    def l_add(k, carry):
        lc[k] = (lc[k].astype(F32) + kl[k, :, c].astype(F32)).astype(BF16)
        return carry

    lax.fori_loop(0, images, l_add, 0)
    l_x = remote(lc.at[:, 1 - x], lx, ks.at[5], kr.at[5], x_dev)
    l_x.start()

    w_x.wait_recv()

    def w_last(k, carry):
        total[k] = (
            wc[k, x].astype(F32) + gw[k, x, c].astype(F32) + wx[k].astype(F32)
        ).astype(BF16)
        return carry

    lax.fori_loop(0, 2 * chain, w_last, 0)
    send_over(1)

    add_over(2)
    along(2)
    add_over(3)
    along(3)
    add_over(0)
    along(0)
    add_over(1)
    along(1)
    finish(2, into(ou))
    finish(3, into(od))
    finish(0, into(fin))
    swaps = []
    for k in range(1, size):
        q = lax.rem(p + k, size)
        swaps.append(remote(fin.at[:, q], oq.at[p], qs.at[k], qr.at[k], (d, q)))
    for copy in swaps:
        copy.start()
    finish(1, into(ow))
    oq[p] = fin[:, p]

    p_x.wait_recv()

    def p_last(k, carry):
        okp[k] = kc[k, x].astype(F32) + kx[k].astype(F32)
        return carry

    lax.fori_loop(0, images, p_last, 0)
    l_x.wait_recv()

    def l_last(k, carry):
        okl[k] = lc[k, x].astype(F32) + lx[k].astype(F32)
        return carry

    lax.fori_loop(0, images, l_last, 0)
    for copy in swaps:
        copy.wait()
    for i in range(4):
        sent(i)
    for copy in (w_core, p_core, l_core, w_x, p_x, l_x):
        copy.wait_send()


def collect(gq, gw, gu, gd, kp, kl, n, size):
    chain = n // 2
    three, _, _, r, cols = gq.shape
    width = gw.shape[-1]
    fu, fd = gu.shape[0], gd.shape[0]
    g, two, _, patches, _ = kp.shape
    lat = kl.shape[3]
    lands = [
        ((three, size, r, cols)), ((r, width)), ((fu, r, width)), ((fd, r, width)),
    ]
    stage = [pltpu.VMEM((chain,) + s, BF16) for s in lands]
    return pl.pallas_call(
        functools.partial(collect_kernel, chain, size),
        name="collect",
        out_shape=(
            struct((size, three, r, cols), F32),
            struct((r, width), F32),
            struct((fu, r, width), F32),
            struct((fd, r, width), F32),
            struct((g, patches, width), F32),
            struct((g, lat, width), F32),
        ),
        in_specs=[VMEM] * 6,
        out_specs=(VMEM,) * 6,
        scratch_shapes=stage * 3
        + [
            pltpu.VMEM((n, two, r, width), BF16),
            pltpu.VMEM((n, r, width), BF16),
            pltpu.VMEM((n, r, width), BF16),
            pltpu.VMEM((n, r, width), BF16),
            pltpu.VMEM((g, two, patches, width), BF16),
            pltpu.VMEM((g, patches, width), BF16),
            pltpu.VMEM((g, two, lat, width), BF16),
            pltpu.VMEM((g, lat, width), BF16),
            pltpu.VMEM((three, size, r, cols), F32),
        ]
        + [DMA((4, chain))] * 6
        + [DMA((6,)), DMA((6,)), DMA((size,)), DMA((size,))],
        compiler_params=params(6),
    )(gq, gw, gu, gd, kp, kl)


def total_kernel(hops, src, out, hold, land, ss, rs):
    d, p = lax.axis_index("dp"), lax.axis_index("patch")

    def flip(v, bit):
        return v + bit - 2 * bit * lax.rem(lax.div(v, bit), 2)

    to = [(d, flip(p, b)) if kind else (flip(d, b), p) for kind, b in hops]
    meet(to)
    sends = []
    for i, who in enumerate(to):
        copy = remote(src if i == 0 else hold.at[i], land.at[i], ss.at[i], rs.at[i], who)
        copy.start()
        copy.wait_recv()
        sends.append(copy)
        value = (src[...] if i == 0 else hold[i]) + land[i]
        if i + 1 < len(to):
            hold[i + 1] = value
        else:
            out[...] = value
    for copy in sends:
        copy.wait_send()


def total(src, n, size):
    hops = [(True, 1 << b) for b in range(size.bit_length() - 1)]
    hops += [(False, 1 << b) for b in range(n.bit_length() - 1)]
    return pl.pallas_call(
        functools.partial(total_kernel, hops),
        name="total",
        out_shape=struct(src.shape, F32),
        in_specs=[VMEM],
        out_specs=VMEM,
        scratch_shapes=[
            pltpu.VMEM((len(hops),) + src.shape, F32),
            pltpu.VMEM((len(hops),) + src.shape, F32),
            DMA((len(hops),)), DMA((len(hops),)),
        ],
        compiler_params=params(7),
    )(src)


class Names:
    def __init__(self, pairs):
        self.__dict__.update(pairs)


def aligned(start, step, count=None):
    return pl.ds(pl.multiple_of(start * step, step), count or step)


def each(lo, hi, body):
    def step(k, carry):
        body(k)
        return carry

    lax.fori_loop(lo, hi, step, 0)


def unit_of(x):
    mean = jnp.mean(x, axis=-1, keepdims=True)
    centred = x - mean
    spread_ = jnp.mean(centred * centred, axis=-1, keepdims=True)
    scaled = lax.rsqrt(spread_ + 1e-05)
    return centred * scaled, scaled


def column_sum(a):
    return jnp.sum(a, axis=0, keepdims=True)


INPUTS = ("held", "media", "latents", "cot", "cns", "norms")
OUTPUTS = ("media_grad", "latents_grad", "latents_out", "grads", "sums", "squares")


def buffers(n, size, g, patches, lat, width, ups, r):
    chain, cols, own = n // 2, width // size, g * lat
    keys, rows, tiles = size * (patches + lat), patches + lat, width // 256
    low = {
        "wqkv": (3, width, cols), "wo": (width, width), "ud": (2, ups, n * r, width),
        "nm": (g, size * patches, width), "nl": (g, size * lat, width), "dy": (size * own, width),
        "q": (g, size * lat, cols), "k": (g, keys, cols), "v": (g, keys, cols),
        "mixed": (g, size * lat, cols), "ab": (g, lat, width), "nf": (size * own, width),
        "gb": (ups, size * own, n * r), "du": (ups, size * own, n * r),
        "part": (2, tiles, 2, 2, own, 256), "half": (2, tiles, 2, own, 256),
        "mid": (2, tiles, own, 256), "quart": (2, tiles, own, 256),
        "da": (g, lat, width), "dah": (g, size * lat, cols), "gwo": (n, 2, 2, r, width),
        "yq": (chain, 3, size * r, cols), "zq": (chain + 1, 3, size * r, cols),
        "yw": (chain, r, width), "zw": (chain + 1, r, width),
        "yf": (2, chain, ups, r, width), "zf": (2, chain + 1, ups, r, width),
        "wc": (n, 2, r, width), "wsum": (n, r, width), "wx": (n, r, width), "total": (n, r, width),
        "kall": (2, 2, 2, rows, width), "kland": (g, 2, rows, width), "kx": (g, rows, width),
    }
    full = {
        "media": (g, patches, width), "latents": (g, lat, width), "cot": (g, lat, width),
        "norms": (6, width), "hidden": (own, width), "dhid": (own, width),
        "fin": (3, size * r, cols), "grads": (3 + 1 + 2 * ups, r, width), "gsum": (8, width),
        "cn": (size, (g + 15) // 16 * 16, size * patches),
        "nland": (size, 8, width), "nhold": (8, width), "dland": (n, 8, width),
        "sland": (size, 8, 128), "shold": (8, 128), "tland": (n, 8, 128), "sqr": (8, 128),
    }
    sems = {
        "loc": (4,), "ins": (5,), "outs": (4,), "mouts": (g,),
        "a_s": (size,), "a_r": (size,), "su": (4, chain), "sd": (4, chain), "sy": (4, chain),
        "rz": (4, chain), "ry": (4, chain),
        "ms": (g,), "mr": (g,), "mcs": (g, 2), "mcr": (g, 2),
        "os": (n,), "or_": (n,), "ocs": (n, 2), "ocr": (n, 2),
        "xs": (5,), "xr": (5,), "cs": (5, 2), "cr": (5, 2), "ts": (size,), "tr": (size,),
        "hs": (size,), "hr": (size,), "ps": (2, tiles), "pr": (2, tiles), "qs": (2, tiles),
        "qr": (2, tiles), "ws": (2,), "wr": (2,), "ks": (g,), "kr": (g,), "lxs": (g,), "lxr": (g,),
        "gys": (4, chain), "gyr": (4, chain), "gzs": (4, chain), "gzr": (4, chain + 1),
        "fs": (size,), "fr": (size,),
        "n1s": (size,), "n1r": (size,), "n2s": (n,), "n2r": (n,),
        "s1s": (size,), "s1r": (size,), "s2s": (n,), "s2r": (n,),
    }
    scratch = [(k, pltpu.VMEM(s, BF16)) for k, s in low.items()]
    scratch += [(k, pltpu.VMEM(s, F32)) for k, s in full.items()]
    scratch += [("held", pltpu.VMEM((4 + 2 * ups, r, width), BF16))]
    scratch += [(k, DMA(s)) for k, s in sems.items()]
    return scratch


def step_kernel(n, size, hands, scale, names, *refs):
    chain = n // 2
    count = len(INPUTS) + len(OUTPUTS)
    into = Names(zip(INPUTS, refs[: len(INPUTS)]))
    out = Names(zip(OUTPUTS, refs[len(INPUTS) : count]))
    b = Names(zip(names, refs[count:]))
    d, p, z, y, x, c = place()
    held, media, latents, cot, norms = b.held, b.media, b.latents, b.cot, b.norms
    wqkv, wo, ud, nm, nl, dy, cn = b.wqkv, b.wo, b.ud, b.nm, b.nl, b.dy, b.cn
    q, k_, v_, mixed, ab, hidden, nf = b.q, b.k, b.v, b.mixed, b.ab, b.hidden, b.nf
    r, width = held.shape[1], held.shape[2]
    cols, ups = width // size, ud.shape[1]
    images, patches, _ = media.shape
    lat = latents.shape[1]
    own, keys, reals = images * lat, size * (patches + lat), size * patches
    tiles = width // 256
    above, below = z + 1 < chain, z > 0
    up_dev, dn_dev = ((z + 1) * 2 + y, p), ((z - 1) * 2 + y, p)
    y_dev, x_dev, c_dev = (z * 2 + 1 - y, p), (d, (1 - x) * 2 + c), (d, x * 2 + 1 - c)
    px = (1 - x) * 2 + c
    dp_peers = [(lax.rem(d + s, n), p) for s in range(1, n)]

    loads = [
        pltpu.make_async_copy(src, dst, b.ins.at[i])
        for i, (src, dst) in enumerate(
            ((into.held, held), (into.latents, latents), (into.norms, norms),
             (into.media, media), (into.cot, cot))
        )
    ]
    for copy in loads:
        copy.start()
    meet(patch_peers(d, p, size) + dp_peers)

    def lanes(k):
        return aligned(k, cols)

    def piece(i, dd):
        if i == 0:
            return wqkv.at[:, aligned(dd, size * r)]
        if i == 1:
            return wo.at[aligned(dd * size + p, r)]
        return ud.at[i - 2, :, aligned(dd, r)]

    first = (
        wqkv.at[:, aligned(d, size * r)], held.at[3], held.at[pl.ds(4, ups)],
        held.at[pl.ds(4 + ups, ups)],
    )
    here = wqkv.at[:, aligned(d * size + p, r)]
    loads[0].wait()
    swaps = []
    for k in range(1, size):
        to = lax.rem(p + k, size)
        swaps.append(
            remote(held.at[pl.ds(0, 3), :, lanes(to)], here, b.a_s.at[k], b.a_r.at[k], (d, to))
        )
    for copy in swaps:
        copy.start()
    local = [pltpu.make_async_copy(held.at[pl.ds(0, 3), :, lanes(p)], here, b.loc.at[0])]
    local += [pltpu.make_async_copy(first[i], piece(i, d), b.loc.at[i]) for i in (1, 2, 3)]
    for copy in local:
        copy.start()

    def hop(i, zz, sends, to, own_src=False):
        src = first[i] if own_src else piece(i, zz * 2 + y)
        return remote(src, piece(i, zz * 2 + y), sends.at[i, zz], b.rz.at[i, zz], to)

    def over(i, zz, own_src=False):
        src = first[i] if own_src else piece(i, zz * 2 + y)
        return remote(src, piece(i, zz * 2 + y), b.sy.at[i, zz], b.ry.at[i, zz], y_dev)

    def start_own(i):
        @pl.when(above)
        def _():
            hop(i, z, b.su, up_dev, True).start()

        @pl.when(below)
        def _():
            hop(i, z, b.sd, dn_dev, True).start()

        over(i, z, True).start()

    def forward(i):
        def step(s):
            @pl.when(z - s >= 0)
            def _():
                hop(i, z - s, b.su, up_dev).wait_recv()

                @pl.when(above)
                def _():
                    hop(i, z - s, b.su, up_dev).start()

                over(i, z - s).start()

            @pl.when(z + s < chain)
            def _():
                hop(i, z + s, b.sd, dn_dev).wait_recv()

                @pl.when(below)
                def _():
                    hop(i, z + s, b.sd, dn_dev).start()

                over(i, z + s).start()

        each(1, chain, step)

    def arrived(i):
        def step(zz):
            src = piece(i, zz * 2 + 1 - y)
            remote(src, src, b.sy.at[i, zz], b.ry.at[i, zz], y_dev).wait_recv()

        each(0, chain, step)

    def sent(i):
        def step(zz):
            over(i, zz).wait_send()

            @pl.when(jnp.logical_and(above, zz <= z))
            def _():
                hop(i, zz, b.su, up_dev).wait_send()

            @pl.when(jnp.logical_and(below, zz >= z))
            def _():
                hop(i, zz, b.sd, dn_dev).wait_send()

        each(0, chain, step)

    class Rows:
        def __init__(self, slot, xs, xr, cs, cr, at, src=None):
            src = slot(p) if src is None else src
            self.to_x = remote(src, slot(p), xs.at[at], xr.at[at], x_dev)
            self.to_c = remote(src, slot(p), cs.at[at, 0], cr.at[at, 0], c_dev)
            self.on = remote(slot(px), slot(px), cs.at[at, 1], cr.at[at, 1], c_dev)

        def start(self):
            self.to_x.start()
            self.to_c.start()

        def forward(self):
            self.to_x.wait_recv()
            self.on.start()

        def have(self):
            self.to_c.wait_recv()
            self.on.wait_recv()

        def end(self):
            self.to_x.wait_send()
            self.to_c.wait_send()
            self.on.wait_send()

    def group(slot, j, src=None):
        return Rows(slot, b.xs, b.xr, b.cs, b.cr, j, src)

    lat_rows = group(lambda k: nl.at[:, aligned(k, lat)], 0)
    cn_rows = group(lambda k: cn.at[k], 1, into.cns)
    dy_rows = group(lambda k: dy.at[aligned(k, own)], 2)
    nf_rows = group(lambda k: nf.at[aligned(k, own)], 3)

    def wo_rows(dd):
        return Rows(lambda k: wo.at[aligned(dd * size + k, r)], b.os, b.or_, b.ocs, b.ocr, dd)

    def media_rows(g):
        return Rows(lambda k: nm.at[g, aligned(k, patches)], b.ms, b.mr, b.mcs, b.mcr, g)

    loads[1].wait()
    loads[2].wait()
    media_gain, media_shift = 1.0 + norms[0:1, :], norms[1:2, :]
    latent_gain, latent_shift = 1.0 + norms[2:3, :], norms[3:4, :]
    ffn_gain, ffn_shift = 1.0 + norms[4:5, :], norms[5:6, :]

    def latent_norm(g):
        unit, _ = unit_of(latents[g])
        nl[g, aligned(p, lat)] = (unit * latent_gain + latent_shift).astype(BF16)

    def media_norm(g):
        unit, _ = unit_of(media[g])
        nm[g, aligned(p, patches)] = (unit * media_gain + media_shift).astype(BF16)

    each(0, images, latent_norm)
    lat_rows.start()
    cn_rows.start()
    mine = pltpu.make_async_copy(into.cns, cn.at[p], b.ins.at[0])
    mine.start()
    local[0].wait()
    for copy in swaps:
        copy.wait_recv()
    start_own(0)
    start_own(1)
    loads[3].wait()
    each(0, images, media_norm)
    each(0, images, lambda g: media_rows(g).start())
    loads[4].wait()
    dy[aligned(p, own)] = cot[...].reshape(own, width).astype(BF16)
    forward(0)
    start_own(2)
    lat_rows.forward()
    cn_rows.forward()
    each(0, 2, lambda g: media_rows(g).forward())
    forward(1)
    start_own(3)
    dy_rows.start()
    arrived(0)
    lat_rows.have()
    cn_rows.have()
    mine.wait()

    flat_nl = nl[...].reshape(images * size * lat, width)
    q[...] = nn(flat_nl, wqkv[0]).astype(BF16).reshape(images, size * lat, cols)
    k_[:, reals:] = nn(flat_nl, wqkv[1]).astype(BF16).reshape(images, size * lat, cols)
    v_[:, reals:] = nn(flat_nl, wqkv[2]).astype(BF16).reshape(images, size * lat, cols)

    def real_keys(g):
        real = cn[0, pl.ds(g, 1), :]
        for k in range(1, size):
            real = real + cn[k, pl.ds(g, 1), :]
        return real

    def image(g):
        media_rows(g).have()
        k_[g, :reals] = nn(nm[g], wqkv[1]).astype(BF16)
        v_[g, :reals] = nn(nm[g], wqkv[2]).astype(BF16)
        pp, plat = soft(
            head_rows(q[g], hands), k_[g, :reals], k_[g, reals:], real_keys(g), scale
        )
        full = nn(pp.astype(BF16), v_[g, :reals]) + nn(plat.astype(BF16), v_[g, reals:])
        mixed[g] = own_columns(full, hands).astype(BF16)

    def image_and_pass(g):
        media_rows(g + 2).forward()
        image(g)

    each(0, 2, image_and_pass)
    arrived(1)
    local[1].wait()
    each(0, n, lambda dd: wo_rows(dd).start())
    each(2, 4, image_and_pass)
    forward(2)
    each(4, images - 2, image_and_pass)
    dy_rows.forward()
    each(images - 2, images, image)
    each(0, n, lambda dd: wo_rows(dd).forward())

    turns = []
    for k in range(1, size):
        to = lax.rem(p + k, size)
        turns.append(
            remote(mixed.at[:, aligned(to, lat)], ab.at[:, :, lanes(p)],
                   b.ts.at[k], b.tr.at[k], (d, to))
        )
    for copy in turns:
        copy.start()
    ab[:, :, lanes(p)] = mixed[:, aligned(p, lat)]
    forward(3)
    each(0, n, lambda dd: wo_rows(dd).have())
    for copy in turns:
        copy.wait_recv()
    flat_ab = ab[...].reshape(own, width)
    for t in range(tiles):
        span = pl.ds(256 * t, 256)
        hidden[:, span] = latents[:, :, span].reshape(own, 256) + nn(flat_ab, wo[:, span])
    unit, _ = unit_of(hidden[...])
    nf[aligned(p, own)] = (unit * ffn_gain + ffn_shift).astype(BF16)
    nf_rows.start()
    dy_rows.have()
    nf_rows.forward()
    nf_rows.have()
    for copy in local[2:]:
        copy.wait()
    arrived(2)
    arrived(3)

    def hidden_block(e):
        u = nt(nf[...], ud[0, e])
        into_active = nt(dy[...], ud[1, e])
        chance = 0.5 * (1.0 + lax.erf(u * math.sqrt(0.5)))
        slope = chance + u * jnp.exp(-0.5 * u * u) * (1.0 / math.sqrt(2.0 * math.pi))
        b.gb[e] = (u * chance).astype(BF16)
        b.du[e] = (into_active * slope).astype(BF16)

    each(0, ups, hidden_block)

    def part_core(i, t):
        return remote(
            b.part.at[i, t, :, 1 - c], b.half.at[i, t], b.ps.at[i, t], b.pr.at[i, t], c_dev
        )

    def part_x(i, t):
        return remote(b.mid.at[i, t], b.quart.at[i, t], b.qs.at[i, t], b.qr.at[i, t], x_dev)

    def part_of(i, acts):
        def tile(t):
            span = aligned(t, 256)
            acc = nn(acts[0], ud[i, 0, :, span])
            for e in range(1, ups):
                acc = acc + nn(acts[e], ud[i, e, :, span])
            b.part[i, t] = acc.astype(BF16).reshape(2, 2, own, 256)
            part_core(i, t).start()

        each(0, tiles, tile)

    def part_pass(i):
        def tile(t):
            part_core(i, t).wait_recv()
            b.mid[i, t] = (
                b.half[i, t, 1 - x].astype(F32) + b.part[i, t, 1 - x, c].astype(F32)
            ).astype(BF16)
            part_x(i, t).start()

        each(0, tiles, tile)

    def part_end(i, write):
        def tile(t):
            part_x(i, t).wait_recv()
            write(
                aligned(t, 256),
                b.half[i, t, x].astype(F32) + b.part[i, t, x, c].astype(F32)
                + b.quart[i, t].astype(F32),
            )

        each(0, tiles, tile)

    def parts_sent(i):
        def tile(t):
            part_core(i, t).wait_send()
            part_x(i, t).wait_send()

        each(0, tiles, tile)

    part_of(0, b.du)
    part_pass(0)
    part_of(1, b.gb)
    for i in range(4):
        sent(i)

    def own_part(i, k):
        if i == 0:
            return wqkv.at[:, aligned(k, size * r)]
        if i == 1:
            return b.total.at[k]
        return ud.at[i - 2, :, aligned(k, r)]

    def land_y(i):
        return b.yq if i == 0 else b.yw if i == 1 else b.yf.at[i - 2]

    def land_z(i):
        return b.zq if i == 0 else b.zw if i == 1 else b.zf.at[i - 2]

    class Sum:
        def __init__(self, i, kind=None):
            self.i, kind = i, i if kind is None else kind
            self.mine = lambda k: own_part(i, k) if kind < 2 else ud.at[i - 2, :, aligned(k, r)]
            self.ly = land_y(kind) if kind < 2 else b.yf.at[i - 2]
            self.lz = land_z(kind) if kind < 2 else b.zf.at[i - 2]

        def over(self, zt):
            return remote(
                self.mine(zt * 2 + 1 - y), self.ly.at[zt], b.gys.at[self.i, zt],
                b.gyr.at[self.i, zt], y_dev,
            )

        def along(self, zt, slot, to):
            return remote(
                self.ly.at[zt], self.lz.at[slot], b.gzs.at[self.i, zt], b.gzr.at[self.i, slot], to
            )

        def send(self):
            def step(k):
                s = chain - 1 - k

                @pl.when(z + s < chain)
                def _():
                    self.over(z + s).start()

                @pl.when(jnp.logical_and(z - s >= 0, s > 0))
                def _():
                    self.over(z - s).start()

            each(0, chain, step)

        def pair(self, zt):
            return self.ly[zt].astype(F32) + self.mine(zt * 2 + y)[...].astype(F32)

        def move(self, zt, more, slot, to):
            self.over(zt).wait_recv()

            @pl.when(more)
            def _():
                self.along(zt, slot, to).wait_recv()
                self.ly[zt] = (self.pair(zt) + self.lz[slot].astype(F32)).astype(BF16)

            @pl.when(jnp.logical_not(more))
            def _():
                self.ly[zt] = self.pair(zt).astype(BF16)

            self.along(zt, slot, to).start()

        def step(self, s):
            @pl.when(z + s < chain)
            def _():
                self.move(z + s, below, z + s + 1, up_dev)

            @pl.when(z - s >= 0)
            def _():
                self.move(z - s, above, z - s, dn_dev)

        def last(self, dst):
            self.over(z).wait_recv()
            dst[...] = self.pair(z)

            @pl.when(below)
            def _():
                self.along(z, z + 1, up_dev).wait_recv()
                dst[...] = dst[...] + self.lz[z + 1].astype(F32)

            @pl.when(above)
            def _():
                self.along(z, z, dn_dev).wait_recv()
                dst[...] = dst[...] + self.lz[z].astype(F32)

        def steps(self):
            each(0, chain - 1, lambda k: self.step(chain - 1 - k))

        def sent(self):
            def step(zt):
                self.over(zt).wait_send()

                @pl.when(zt != z)
                def _():
                    self.along(zt, 0, up_dev).wait_send()

            each(0, chain, step)

    sums = [Sum(0), Sum(1)]

    def ffn_sum(j):
        return Sum(2 + j, 2)

    def down_grad(e):
        for t in range(0, width, 512):
            ud[1, e, :, t : t + 512] = tn(b.gb[e], dy[:, t : t + 512]).astype(BF16)

    def up_grad(e):
        for t in range(0, width, 512):
            ud[0, e, :, t : t + 512] = tn(b.du[e], nf[:, t : t + 512]).astype(BF16)

    each(0, ups, down_grad)
    ffn_sum(1).send()
    each(0, ups, up_grad)
    ffn_sum(0).send()

    def write_dhid(span, value):
        b.dhid[:, span] = value

    part_end(0, write_dhid)
    part_pass(1)
    dn = b.dhid[...]
    unit, scaled = unit_of(hidden[...])
    b.gsum[...] = jnp.zeros_like(b.gsum)
    b.gsum[4:5, :] = column_sum(dn * unit)
    b.gsum[5:6, :] = column_sum(dn)
    b.dhid[...] = cot[...].reshape(own, width) + norm_back(dn, unit, scaled, ffn_gain)
    do = b.dhid[...].astype(BF16)
    for t in range(tiles):
        span = pl.ds(256 * t, 256)
        b.da[:, :, span] = nt(do, wo[span, :]).astype(BF16).reshape(images, lat, 256)
    turns_back = []
    for k in range(1, size):
        to = lax.rem(p + k, size)
        turns_back.append(
            remote(b.da.at[:, :, lanes(to)], b.dah.at[:, aligned(p, lat)],
                   b.hs.at[k], b.hr.at[k], (d, to))
        )
    for copy in turns_back:
        copy.start()
    b.dah[:, aligned(p, lat)] = b.da[:, :, lanes(p)]
    for t in range(tiles):
        span = pl.ds(256 * t, 256)
        b.gwo[:, :, :, :, span] = (
            tn(ab[...].reshape(own, width), do[:, 256 * t : 256 * t + 256])
            .astype(BF16).reshape(n, 2, 2, r, 256)
        )
    w_core = remote(b.gwo.at[:, :, 1 - c], b.wc, b.ws.at[0], b.wr.at[0], c_dev)
    w_x = remote(b.wsum, b.wx, b.ws.at[1], b.wr.at[1], x_dev)
    w_core.start()

    def write_out(span, value):
        hidden[:, span] = hidden[:, span] + value

    part_end(1, write_out)
    out_copy = pltpu.make_async_copy(hidden, out.latents_out, b.outs.at[0])
    out_copy.start()
    w_core.wait_recv()

    def w_add(k):
        b.wsum[k] = (b.wc[k, 1 - x].astype(F32) + b.gwo[k, 1 - x, c].astype(F32)).astype(BF16)

    each(0, n, w_add)
    w_x.start()
    for copy in turns_back:
        copy.wait_recv()

    def kin_core(g):
        return remote(
            b.kall.at[lax.rem(g, 2), 1 - c], b.kland.at[g], b.ks.at[g], b.kr.at[g], c_dev
        )

    def kin_x(g):
        return remote(b.kland.at[g, 1 - x], b.kx.at[g], b.lxs.at[g], b.lxr.at[g], x_dev)

    def image_back(g):
        slot = lax.rem(g, 2)
        qb, dab = head_rows(q[g], hands), head_rows(b.dah[g], hands)
        kp, kl, vp, vl = k_[g, :reals], k_[g, reals:], v_[g, :reals], v_[g, reals:]
        pp, plat = soft(qb, kp, kl, real_keys(g), scale)
        gp, gl = nt(dab, vp), nt(dab, vl)
        delta = column_of(pp * gp) + column_of(plat * gl)
        sp, sl = (pp * (gp - delta)).astype(BF16), (plat * (gl - delta)).astype(BF16)
        v_[g, :reals] = tn(pp.astype(BF16), dab).astype(BF16)
        v_[g, reals:] = tn(plat.astype(BF16), dab).astype(BF16)
        k_[g, :reals] = (tn(sp, qb) * scale).astype(BF16)
        k_[g, reals:] = (tn(sl, qb) * scale).astype(BF16)
        q[g] = (own_columns(nn(sp, kp) + nn(sl, kl), hands) * scale).astype(BF16)
        for t in range(tiles):
            span = pl.ds(256 * t, 256)
            rows = nt(k_[g], wqkv[1, span, :]) + nt(v_[g], wqkv[2, span, :])
            tail = rows[reals:] + nt(q[g], wqkv[0, span, :])
            for e in range(size):
                b.kall[slot, e % 2, e // 2, :patches, span] = (
                    rows[e * patches : (e + 1) * patches].astype(BF16)
                )
                b.kall[slot, e % 2, e // 2, patches:, span] = (
                    tail[e * lat : (e + 1) * lat].astype(BF16)
                )
        kin_core(g).start()

    def kin_mid(g):
        kin_core(g).wait_recv()
        b.kland[g] = (
            b.kland[g].astype(F32) + b.kall[lax.rem(g, 2), c].astype(F32)
        ).astype(BF16)
        kin_x(g).start()

    def media_out(g):
        return pltpu.make_async_copy(media.at[g], out.media_grad.at[g], b.mouts.at[g])

    def kin_last(g):
        kin_x(g).wait_recv()
        total_ = b.kland[g, x].astype(F32) + b.kx[g].astype(F32)
        grad = total_[:patches]
        unit, scaled = unit_of(media[g])
        b.gsum[0:1, :] = b.gsum[0:1, :] + column_sum(grad * unit)
        b.gsum[1:2, :] = b.gsum[1:2, :] + column_sum(grad)
        media[g] = norm_back(grad, unit, scaled, media_gain)
        media_out(g).start()
        grad = total_[patches:]
        unit, scaled = unit_of(latents[g])
        b.gsum[2:3, :] = b.gsum[2:3, :] + column_sum(grad * unit)
        b.gsum[3:4, :] = b.gsum[3:4, :] + column_sum(grad)
        latents[g] = b.dhid[aligned(g, lat)] + norm_back(grad, unit, scaled, latent_gain)

    moves = 2 * (chain - 1)

    def ffn_step(k):
        ffn_sum(1 - lax.div(k, chain - 1)).step(chain - 1 - lax.rem(k, chain - 1))

    def back(g):
        @pl.when(g >= 2)
        def _():
            kin_core(g - 2).wait_send()

        image_back(g)

        @pl.when(g >= 1)
        def _():
            kin_mid(g - 1)

        @pl.when(g >= 3)
        def _():
            kin_last(g - 3)

        @pl.when(jnp.logical_and(g >= 1, g < 1 + moves))
        def _():
            ffn_step(g - 1)

    def w_last(k):
        b.total[k] = (
            b.wc[k, x].astype(F32) + b.gwo[k, x, c].astype(F32) + b.wx[k].astype(F32)
        ).astype(BF16)

    half_way = min(5, images)
    each(0, half_way, back)
    w_x.wait_recv()
    each(0, n, w_last)
    sums[1].send()
    each(half_way, images, back)
    each(min(images - 1, moves), moves, ffn_step)
    kin_mid(images - 1)

    def qkv_grad(t):
        span = aligned(t, 256)
        rows_m = nm[:, :, span].reshape(images * reals, 256)
        rows_l = nl[:, :, span].reshape(images * size * lat, 256)

        def flat(a, n_rows):
            return a.reshape(images * n_rows, cols)

        wqkv[0, span, :] = tn(rows_l, flat(q[...], size * lat)).astype(BF16)
        for j, ref in ((1, k_), (2, v_)):
            wqkv[j, span, :] = (
                tn(rows_m, flat(ref[:, :reals], reals))
                + tn(rows_l, flat(ref[:, reals:], size * lat))
            ).astype(BF16)

    each(0, tiles, qkv_grad)
    sums[0].send()
    ffn_sum(1).last(b.grads.at[pl.ds(4 + ups, ups)])
    ffn_sum(0).last(b.grads.at[pl.ds(4, ups)])
    sums[1].steps()
    each(max(images - 3, 0), images, kin_last)
    lat_copy = pltpu.make_async_copy(latents, out.latents_grad, b.outs.at[1])
    lat_copy.start()

    def share(src, land, hold, s1, r1, total_to, land2, s2, r2):
        land[p] = src[...]
        near = []
        for k in range(1, size):
            to = lax.rem(p + k, size)
            near.append(remote(src, land.at[p], s1.at[to], r1.at[p], (d, to)))
        for copy in near:
            copy.start()
        for k in range(1, size):
            who = lax.rem(p + k, size)
            remote(src, land.at[who], s1.at[who], r1.at[who], (d, who)).wait_recv()
        value = land[0]
        for k in range(1, size):
            value = value + land[k]
        hold[...] = value
        land2[d] = value
        far = []
        for k in range(1, n):
            to = lax.rem(d + k, n)
            far.append(remote(hold, land2.at[d], s2.at[to], r2.at[d], (to, p)))
        for copy in far:
            copy.start()

        def finish():
            for k in range(1, n):
                who = lax.rem(d + k, n)
                remote(hold, land2.at[who], s2.at[who], r2.at[who], (who, p)).wait_recv()
            value = land2[0]
            for k in range(1, n):
                value = value + land2[k]
            total_to[...] = value
            for copy in near + far:
                copy.wait_send()

        return finish

    norms_done = share(b.gsum, b.nland, b.nhold, b.n1s, b.n1r, out.sums, b.dland, b.n2s, b.n2r)
    sums[0].steps()
    sums[1].last(b.grads.at[3])
    sums[0].last(b.fin)
    ends = []
    for k in range(1, size):
        to = lax.rem(p + k, size)
        ends.append(
            remote(b.fin.at[:, aligned(to, r)], b.grads.at[pl.ds(0, 3), :, lanes(p)],
                   b.fs.at[k], b.fr.at[k], (d, to))
        )
    for copy in ends:
        copy.start()
    b.grads[0:3, :, lanes(p)] = b.fin[:, aligned(p, r)]
    for copy in ends:
        copy.wait_recv()
    grads_copy = pltpu.make_async_copy(b.grads, out.grads, b.outs.at[2])
    grads_copy.start()
    squares = jnp.zeros((8, 128), F32)
    for i in range(b.grads.shape[0]):
        for t in range(0, width, 128):
            tile = b.grads[i, :, t : t + 128]
            squares = squares + jnp.sum((tile * tile).reshape(r // 8, 8, 128), axis=0)
    b.sqr[...] = squares
    squares_done = share(
        b.sqr, b.sland, b.shold, b.s1s, b.s1r, out.squares, b.tland, b.s2s, b.s2r
    )
    norms_done()
    for copy in swaps + turns + turns_back + ends:
        copy.wait_send()
    for rows in (lat_rows, cn_rows, dy_rows, nf_rows):
        rows.end()
    each(0, images, lambda g: media_rows(g).end())
    each(0, n, lambda dd: wo_rows(dd).end())
    parts_sent(0)
    parts_sent(1)
    w_core.wait_send()
    w_x.wait_send()
    each(max(images - 2, 0), images, lambda g: kin_core(g).wait_send())
    each(0, images, lambda g: kin_x(g).wait_send())
    for i in (0, 1):
        sums[i].sent()
    for j in (0, 1):
        ffn_sum(j).sent()
    each(0, images, lambda g: media_out(g).wait())
    out_copy.wait()
    lat_copy.wait()
    grads_copy.wait()
    squares_done()


def column_of(a):
    return jnp.sum(a, axis=1, keepdims=True)


def whole_step(held, media, latents, cot, cns, norms, n, size, hands, scale):
    blocks, r, width = held.shape
    g, patches, _ = media.shape
    lat = latents.shape[1]
    scratch = buffers(n, size, g, patches, lat, width, FF // width, r)
    return pl.pallas_call(
        functools.partial(step_kernel, n, size, hands, scale, [k for k, _ in scratch]),
        name="whole_step",
        out_shape=(
            struct((g, patches, width), F32),
            struct((g, lat, width), F32),
            struct((g * lat, width), F32),
            struct((blocks, r, width), F32),
            struct((8, width), F32),
            struct((8, 128), F32),
        ),
        in_specs=[ANY] * 4 + [VMEM] + [ANY],
        out_specs=(ANY,) * 4 + (VMEM,) * 2,
        scratch_shapes=[s for _, s in scratch],
        compiler_params=params(8),
    )(held, media, latents, cot, cns, norms)


def norm_parts(values, gain_row, shift_row):
    average = jnp.mean(values, axis=-1, keepdims=True)
    centred = values - average
    spread_ = jnp.mean(centred * centred, axis=-1, keepdims=True)
    scaled = lax.rsqrt(spread_ + 1e-05)
    unit_rows = centred * scaled
    return (unit_rows * gain_row + shift_row, unit_rows, scaled)


def norm_back(grad_out, unit_rows, scaled, gain_row):
    inner_grad = grad_out * gain_row
    plain_mean = jnp.mean(inner_grad, axis=-1, keepdims=True)
    cross_mean = jnp.mean(inner_grad * unit_rows, axis=-1, keepdims=True)
    return scaled * (inner_grad - plain_mean - unit_rows * cross_mean)


def gain_terms(grad_out, unit_rows):
    width = grad_out.shape[-1]
    flat_grad = grad_out.reshape(-1, width)
    flat_unit = unit_rows.reshape(-1, width)
    return [jnp.sum(flat_grad * flat_unit, axis=0), jnp.sum(flat_grad, axis=0)]


def exact_gelu(values):
    return jax.nn.gelu(values, approximate=False)


def adamw_update(parameter, first_m, second_m, average, gradient, factor, decay_rate):
    clipped = gradient * factor
    new_first = 0.9 * first_m + 0.1 * clipped
    new_second = 0.999 * second_m + 0.001 * clipped * clipped
    first_hat = new_first / (1.0 - 0.9**STEP)
    second_hat = new_second / (1.0 - 0.999**STEP)
    new_param = parameter - 0.02 * (
        first_hat / (jnp.sqrt(second_hat) + 1e-08) + decay_rate * parameter
    )
    new_avg = 0.8 * average + 0.2 * new_param
    return (new_param, new_first, new_second, new_avg)


def dot32(spec, a, b):
    return jnp.einsum(spec, a, b, preferred_element_type=F32)


def general_step(n, size, media_tokens, patch_mask, latents, cotangent, weights, weights_first,
              weights_second, weights_average, norm_params, norm_first, norm_second, norm_average):
    g, patches, width = media_tokens.shape
    lat = latents.shape[1]
    blocks = weights.shape[0]
    r = width // (n * size)
    cols = width // size
    hands = HEADS // size
    scale = 1.0 / math.sqrt(width // HEADS)
    ups = FF // width
    own = g * lat
    media_gain, latent_gain, ffn_gain = 1.0 + norm_params[0], 1.0 + norm_params[2], 1.0 + norm_params[4]

    held = weights.astype(BF16).reshape(blocks, r, width)
    qs = held[:3].reshape(3, r, size, cols).transpose(2, 0, 1, 3)
    media_norm, media_unit, media_scale = norm_parts(media_tokens, media_gain, norm_params[1])
    latent_norm, latent_unit, latent_scale = norm_parts(latents, latent_gain, norm_params[3])
    cot = cotangent.reshape(own, width)
    count_rows = (g + 15) // 16 * 16
    counts = jnp.sum((patch_mask > 0).astype(F32), axis=1)
    counts = jnp.broadcast_to(jnp.pad(counts, (0, count_rows - g))[:, None], (count_rows, 128))

    wqkv, wo, up, dn, nm, nl, dy, cn = spread(
        qs, held[3], held[4 : 4 + ups], held[4 + ups :],
        media_norm.astype(BF16), latent_norm.astype(BF16), cot.astype(BF16), counts, n, size,
    )
    wqkv = wqkv.reshape(3, width, cols)
    wo = wo.reshape(width, width)
    up = up.reshape(-1, width)
    dn = dn.reshape(-1, width)
    nm = nm.reshape(g * size * patches, width)
    nl = nl.reshape(g * size * lat, width)
    dy = dy.reshape(size * own, width)
    real = jnp.sum(cn[:, :g, 0], axis=0).astype(jnp.int32)

    def by_image(a):
        return a.astype(BF16).reshape(g, -1, cols)

    q = by_image(dot32("rd,de->re", nl, wqkv[0]))
    kp, kl = by_image(dot32("rd,de->re", nm, wqkv[1])), by_image(dot32("rd,de->re", nl, wqkv[1]))
    vp, vl = by_image(dot32("rd,de->re", nm, wqkv[2])), by_image(dot32("rd,de->re", nl, wqkv[2]))
    mixed = attend(real, q, kp, kl, vp, vl, hands, scale)
    ab = to_rows(mixed.reshape(g, size, lat, cols), size, 1).reshape(own, width)

    hidden = latents.reshape(own, width) + dot32("rd,de->re", ab, wo)
    ffn_norm, ffn_unit, ffn_scale = norm_parts(hidden, ffn_gain, norm_params[5])
    nf = join_rows(ffn_norm.astype(BF16), size, 2).reshape(size * own, width)
    u = dot32("rd,fd->rf", nf, up)
    active, pull = jax.vjp(exact_gelu, u)
    gb = active.astype(BF16)
    y_part = dot32("rf,fd->rd", gb, dn).astype(BF16)
    du = pull(dot32("rd,fd->rf", dy, dn))[0].astype(BF16)
    f_part = dot32("rf,fd->rd", du, up).astype(BF16)
    g_dn = dot32("rf,rd->fd", gb, dy).astype(BF16)
    g_up = dot32("rf,rd->fd", du, nf).astype(BF16)
    both = split_rows(jnp.stack([y_part, f_part]).reshape(2, 2, 2, own, width), 3)
    latents_out = (hidden + both[0]).reshape(g, lat, width)
    d_ffn = both[1]
    ffn_terms = gain_terms(d_ffn, ffn_unit)
    d_hidden = cot + norm_back(d_ffn, ffn_unit, ffn_scale, ffn_gain)

    do = d_hidden.astype(BF16)
    g_wo = dot32("rd,re->de", ab, do).astype(BF16)
    da = dot32("re,de->rd", do, wo).astype(BF16).reshape(g, lat, width)
    da = to_heads(da, size, 4).reshape(g, size * lat, cols)
    dq, dkp, dkl, dvp, dvl = attend_back(real, q, kp, kl, vp, vl, da, hands, scale)

    def flat(a):
        return a.reshape(-1, cols)

    dq, dkp, dkl, dvp, dvl = flat(dq), flat(dkp), flat(dkl), flat(dvp), flat(dvl)
    g_qkv = jnp.stack([
        dot32("rd,re->de", nl, dq),
        dot32("rd,re->de", nm, dkp) + dot32("rd,re->de", nl, dkl),
        dot32("rd,re->de", nm, dvp) + dot32("rd,re->de", nl, dvl),
    ]).astype(BF16)
    d_nm = (dot32("re,de->rd", dkp, wqkv[1]) + dot32("re,de->rd", dvp, wqkv[2])).astype(BF16)
    d_nl = (
        dot32("re,de->rd", dkl, wqkv[1]) + dot32("re,de->rd", dvl, wqkv[2])
        + dot32("re,de->rd", dq, wqkv[0])
    ).astype(BF16)

    oq, ow, ou, od, d_media, d_latent = collect(
        g_qkv.reshape(3, n, size, r, cols), g_wo.reshape(n, 2, 2, r, width),
        g_up.reshape(ups, n, r, width), g_dn.reshape(ups, n, r, width),
        d_nm.reshape(g, 2, 2, patches, width), d_nl.reshape(g, 2, 2, lat, width), n, size,
    )
    media_grad = norm_back(d_media, media_unit, media_scale, media_gain)
    latents_grad = d_hidden.reshape(g, lat, width) + norm_back(
        d_latent, latent_unit, latent_scale, latent_gain
    )
    grads = jnp.concatenate([
        oq.transpose(1, 2, 0, 3).reshape(3, r, width), ow[None], ou, od,
    ])
    square = jnp.broadcast_to(jnp.sum(grads * grads), (width,))
    rows = jnp.stack(
        gain_terms(d_media, media_unit) + gain_terms(d_latent, latent_unit) + ffn_terms
        + [square, jnp.zeros_like(square)]
    )
    sums = total(rows, n, size)
    return latents_out, media_grad, latents_grad, grads, sums[:6], sums[6, 0]


def on_device(n, size, media_tokens, patch_mask, latents, cotangent, weights, weights_first,
              weights_second, weights_average, norm_params, norm_first, norm_second, norm_average):
    g, patches, width = media_tokens.shape
    lat = latents.shape[1]
    r = width // (n * size)
    arrays = (
        media_tokens, patch_mask, latents, cotangent, weights, weights_first, weights_second,
        weights_average, norm_params, norm_first, norm_second, norm_average,
    )
    if r % 16 or lat % 16 or size != 4:
        latents_out, media_grad, latents_grad, grads, norm_grads, square = general_step(
            n, size, *arrays
        )
    else:
        held = weights.astype(BF16).reshape(weights.shape[0], r, width)
        count_rows = (g + 15) // 16 * 16
        counts = jnp.sum((patch_mask > 0).astype(F32), axis=1)
        counts = jnp.broadcast_to(
            jnp.pad(counts, (0, count_rows - g))[:, None], (count_rows, size * patches)
        )
        media_grad, latents_grad, latents_out, grads, sums, squares = whole_step(
            held, media_tokens, latents, cotangent, counts, norm_params,
            n, size, HEADS // size, 1.0 / math.sqrt(width // HEADS),
        )
        latents_out = latents_out.reshape(g, lat, width)
        norm_grads, square = sums[:6], jnp.sum(squares)
    grad_norm = jnp.sqrt(square + jnp.sum(norm_grads * norm_grads))
    clip = jnp.minimum(1.0, 1.0 / (grad_norm + 1e-06))
    new_w, new_first, new_second, new_avg = adamw_update(
        weights, weights_first, weights_second, weights_average,
        grads.reshape(weights.shape), clip, 0.1,
    )
    new_n, new_nf, new_ns, new_na = adamw_update(
        norm_params, norm_first, norm_second, norm_average, norm_grads, clip, 0.0
    )
    return (
        latents_out, media_grad, latents_grad, grad_norm, new_w, new_w.astype(BF16), new_first,
        new_second, new_avg, new_n, new_nf, new_ns, new_na, norm_grads[4:6],
    )


def solution(mesh):
    n, size = mesh.shape["dp"], mesh.shape["patch"]
    rows, weight = P("dp", "patch", None), P(None, ("dp", "patch"))
    return jax.shard_map(
        functools.partial(on_device, n, size),
        mesh=mesh,
        in_specs=(rows, P("dp", "patch"), rows, rows) + (weight,) * 4 + (P(),) * 4,
        out_specs=(rows, rows, rows, P()) + (weight,) * 5 + (P(),) * 5,
        check_vma=False,
    )
```

```python
import functools
import math

import jax
import jax.numpy as jnp
from jax import lax
from jax.experimental import pallas as pl
from jax.experimental.pallas import tpu as pltpu
from jax.sharding import PartitionSpec as P

HEADS = 16
FF = 4096
STEP = 7
MESH = pl.DeviceIdType.MESH
F32 = jnp.float32
BF16 = jnp.bfloat16
ANY = pl.BlockSpec(memory_space=pl.ANY)
VMEM = pl.BlockSpec(memory_space=pltpu.VMEM)
DMA = pltpu.SemaphoreType.DMA
VMEM_LIMIT = 64 * 1024 * 1024 - 65536


def struct(shape, kind):
    return jax.ShapeDtypeStruct(shape, kind)


def place():
    d, p = lax.axis_index("dp"), lax.axis_index("patch")
    return d, p, lax.div(d, 2), lax.rem(d, 2), lax.div(p, 2), lax.rem(p, 2)


def remote(src, dst, send, recv, to):
    return pltpu.make_async_remote_copy(
        src_ref=src, dst_ref=dst, send_sem=send, recv_sem=recv, device_id=to, device_id_type=MESH
    )


def greet(peers):
    barrier = pltpu.get_barrier_semaphore()
    for to in peers:
        pl.semaphore_signal(barrier, inc=1, device_id=to, device_id_type=MESH)
    return functools.partial(pl.semaphore_wait, barrier, len(peers))


def meet(always, maybe=()):
    barrier = pltpu.get_barrier_semaphore()
    count = len(always)
    for to in always:
        pl.semaphore_signal(barrier, inc=1, device_id=to, device_id_type=MESH)
    for there, to in maybe:

        @pl.when(there)
        def _(to=to):
            pl.semaphore_signal(barrier, inc=1, device_id=to, device_id_type=MESH)

        count = count + there.astype(jnp.int32)
    pl.semaphore_wait(barrier, count)


def patch_peers(d, p, size):
    return [(d, lax.rem(p + k, size)) for k in range(1, size)]


def params(number):
    return pltpu.CompilerParams(
        collective_id=number, has_side_effects=True, vmem_limit_bytes=VMEM_LIMIT
    )


def spread_kernel(chain, size, qs, wos, ups, dns, nms, nls, dys, cns,
                  wqkv, wo, up, dn, nm, nl, dy, cn,
                  loc, a_s, a_r, su, sd, sy, rz, ry, xs, xr, cs, cr):
    d, p, z, y, x, c = place()
    above, below = z + 1 < chain, z > 0
    up_dev, dn_dev = ((z + 1) * 2 + y, p), ((z - 1) * 2 + y, p)
    y_dev, x_dev, c_dev = (z * 2 + 1 - y, p), (d, (1 - x) * 2 + c), (d, x * 2 + 1 - c)
    px, pc = (1 - x) * 2 + c, x * 2 + 1 - c
    pd = (1 - x) * 2 + 1 - c
    meet(patch_peers(d, p, size) + [y_dev], [(above, up_dev), (below, dn_dev)])

    own = [
        (qs.at[p], wqkv.at[:, d, p]), (wos, wo.at[d, p]), (ups, up.at[:, d]), (dns, dn.at[:, d]),
        (nms, nm.at[:, p]), (nls, nl.at[:, p]), (dys, dy.at[p]), (cns, cn.at[p]),
    ]
    local = [pltpu.make_async_copy(a, b, loc.at[i]) for i, (a, b) in enumerate(own)]
    for copy in local:
        copy.start()
    swaps = []
    for k in range(1, size):
        q = lax.rem(p + k, size)
        swaps.append(remote(qs.at[q], wqkv.at[:, d, p], a_s.at[k], a_r.at[k], (d, q)))
    for copy in swaps:
        copy.start()

    rows = [(nms, nm), (nls, nl), (cns, cn), (dys, dy)]

    def slot(j, q):
        ref = rows[j][1] if j < 4 else wo
        return ref.at[q] if j in (2, 3) else ref.at[:, q]

    def row_copies(j):
        src = rows[j][0] if j < 4 else slot(j, p)
        return (
            remote(src, slot(j, p), xs.at[j], xr.at[j], x_dev),
            remote(src, slot(j, p), cs.at[j, 0], cr.at[j, 0], c_dev),
            remote(slot(j, px), slot(j, px), cs.at[j, 1], cr.at[j, 1], c_dev),
        )

    def start_rows(j):
        to_x, to_c, _ = row_copies(j)
        to_x.start()
        to_c.start()

    def pass_rows(j):
        to_x, _, on = row_copies(j)
        to_x.wait_recv()
        on.start()

    def end_rows(j):
        to_x, to_c, on = row_copies(j)
        to_c.wait_recv()
        on.wait_recv()
        to_x.wait_send()
        to_c.wait_send()
        on.wait_send()

    for j in range(4):
        start_rows(j)

    def piece(i, dd):
        return (wqkv.at[:, dd], wo.at[dd, p], up.at[:, dd], dn.at[:, dd])[i]

    first = (wqkv.at[:, d], wos, ups, dns)

    def hop(i, zz, sends, to, own_src=False):
        src = first[i] if own_src else piece(i, zz * 2 + y)
        return remote(src, piece(i, zz * 2 + y), sends.at[i, zz], rz.at[i, zz], to)

    def over(i, zz, own_src=False):
        src = first[i] if own_src else piece(i, zz * 2 + y)
        return remote(src, piece(i, zz * 2 + y), sy.at[i, zz], ry.at[i, zz], y_dev)

    def start_own(i):
        @pl.when(above)
        def _():
            hop(i, z, su, up_dev, True).start()

        @pl.when(below)
        def _():
            hop(i, z, sd, dn_dev, True).start()

        over(i, z, True).start()

    def forward(i):
        def step(s, carry):
            @pl.when(z - s >= 0)
            def _():
                hop(i, z - s, su, up_dev).wait_recv()

                @pl.when(above)
                def _():
                    hop(i, z - s, su, up_dev).start()

                over(i, z - s).start()

            @pl.when(z + s < chain)
            def _():
                hop(i, z + s, sd, dn_dev).wait_recv()

                @pl.when(below)
                def _():
                    hop(i, z + s, sd, dn_dev).start()

                over(i, z + s).start()

            return carry

        lax.fori_loop(1, chain, step, 0)

    def arrived(i):
        def step(zz, carry):
            src = piece(i, zz * 2 + 1 - y)
            remote(src, src, sy.at[i, zz], ry.at[i, zz], y_dev).wait_recv()
            return carry

        lax.fori_loop(0, chain, step, 0)

    def sent(i):
        def step(zz, carry):
            over(i, zz).wait_send()

            @pl.when(jnp.logical_and(above, zz <= z))
            def _():
                hop(i, zz, su, up_dev).wait_send()

            @pl.when(jnp.logical_and(below, zz >= z))
            def _():
                hop(i, zz, sd, dn_dev).wait_send()

            return carry

        lax.fori_loop(0, chain, step, 0)

    local[0].wait()
    for copy in swaps:
        copy.wait_recv()
    start_own(0)
    start_own(1)
    forward(0)
    start_own(2)
    forward(1)
    start_own(3)
    local[1].wait()
    arrived(1)
    start_rows(4)
    forward(2)
    for j in range(5):
        pass_rows(j)
    forward(3)
    arrived(0)
    arrived(2)
    arrived(3)
    for j in range(5):
        end_rows(j)
    for copy in swaps:
        copy.wait_send()
    for i in range(4):
        sent(i)
    for copy in local[2:]:
        copy.wait()


def spread(qs, wos, ups, dns, nms, nls, dys, cns, n, size):
    _, three, r, cols = qs.shape
    width = wos.shape[1]
    chain = n // 2
    g, patches, _ = nms.shape
    lat = nls.shape[1]
    return pl.pallas_call(
        functools.partial(spread_kernel, chain, size),
        name="spread",
        out_shape=(
            struct((three, n, size, r, cols), BF16),
            struct((n, size, r, width), BF16),
            struct((ups.shape[0], n, r, width), BF16),
            struct((dns.shape[0], n, r, width), BF16),
            struct((g, size, patches, width), BF16),
            struct((g, size, lat, width), BF16),
            struct((size,) + dys.shape, BF16),
            struct((size,) + cns.shape, F32),
        ),
        in_specs=[VMEM] * 8,
        out_specs=(ANY,) * 8,
        scratch_shapes=[
            DMA((8,)), DMA((size,)), DMA((size,)),
            DMA((4, chain)), DMA((4, chain)), DMA((4, chain)), DMA((4, chain)), DMA((4, chain)),
            DMA((5,)), DMA((5,)), DMA((5, 2)), DMA((5, 2)),
        ],
        compiler_params=params(0),
    )(qs, wos, ups, dns, nms, nls, dys, cns)


def to_rows_kernel(size, src, out, loc, ss, rs):
    d, p = lax.axis_index("dp"), lax.axis_index("patch")
    cols = src.shape[3]
    meet(patch_peers(d, p, size))
    here = out.at[:, :, pl.ds(pl.multiple_of(p * cols, cols), cols)]
    copies = []
    for k in range(1, size):
        q = lax.rem(p + k, size)
        copies.append(remote(src.at[:, q], here, ss.at[k], rs.at[k], (d, q)))
    for copy in copies:
        copy.start()
    mine = pltpu.make_async_copy(src.at[:, p], here, loc)
    mine.start()
    mine.wait()
    for copy in copies:
        copy.wait()


def to_rows(src, size, number):
    g, _, lat, cols = src.shape
    return pl.pallas_call(
        functools.partial(to_rows_kernel, size),
        name="to_rows",
        out_shape=struct((g, lat, size * cols), src.dtype),
        in_specs=[VMEM],
        out_specs=VMEM,
        scratch_shapes=[DMA, DMA((size,)), DMA((size,))],
        compiler_params=params(number),
    )(src)


def to_heads_kernel(size, src, out, loc, ss, rs):
    d, p = lax.axis_index("dp"), lax.axis_index("patch")
    cols = out.shape[3]
    meet(patch_peers(d, p, size))

    def part(q):
        return src.at[:, :, pl.ds(pl.multiple_of(q * cols, cols), cols)]

    copies = []
    for k in range(1, size):
        q = lax.rem(p + k, size)
        copies.append(remote(part(q), out.at[:, p], ss.at[k], rs.at[k], (d, q)))
    for copy in copies:
        copy.start()
    mine = pltpu.make_async_copy(part(p), out.at[:, p], loc)
    mine.start()
    mine.wait()
    for copy in copies:
        copy.wait()


def to_heads(src, size, number):
    g, lat, width = src.shape
    return pl.pallas_call(
        functools.partial(to_heads_kernel, size),
        name="to_heads",
        out_shape=struct((g, size, lat, width // size), src.dtype),
        in_specs=[VMEM],
        out_specs=VMEM,
        scratch_shapes=[DMA, DMA((size,)), DMA((size,))],
        compiler_params=params(number),
    )(src)


def join_rows_kernel(src, out, loc, ss, rs):
    d, p, z, y, x, c = place()
    x_dev, c_dev = (d, (1 - x) * 2 + c), (d, x * 2 + 1 - c)
    px = (1 - x) * 2 + c
    meet([x_dev, c_dev])
    to_x = remote(src, out.at[p], ss.at[0], rs.at[0], x_dev)
    to_c = remote(src, out.at[p], ss.at[1], rs.at[1], c_dev)
    on = remote(out.at[px], out.at[px], ss.at[2], rs.at[2], c_dev)
    to_x.start()
    to_c.start()
    mine = pltpu.make_async_copy(src, out.at[p], loc)
    mine.start()
    to_x.wait_recv()
    on.start()
    mine.wait()
    to_c.wait()
    on.wait()
    to_x.wait_send()


def join_rows(src, size, number):
    return pl.pallas_call(
        join_rows_kernel,
        name="join_rows",
        out_shape=struct((size,) + src.shape, src.dtype),
        in_specs=[VMEM],
        out_specs=VMEM,
        scratch_shapes=[DMA, DMA((3,)), DMA((3,))],
        compiler_params=params(number),
    )(src)


def split_rows_kernel(ins, src, out, half, mid, quarter, ss, rs):
    d, p, z, y, x, c = place()
    x_dev, c_dev = (d, (1 - x) * 2 + c), (d, x * 2 + 1 - c)
    meet([x_dev, c_dev])
    first = [remote(src.at[i, :, 1 - c], half.at[i], ss.at[i], rs.at[i], c_dev) for i in range(ins)]
    for copy in first:
        copy.start()
    second = []
    for i in range(ins):
        first[i].wait_recv()
        mid[i] = (half[i, 1 - x].astype(F32) + src[i, 1 - x, c].astype(F32)).astype(BF16)
        copy = remote(mid.at[i], quarter.at[i], ss.at[ins + i], rs.at[ins + i], x_dev)
        copy.start()
        second.append(copy)
    for i in range(ins):
        out[i] = half[i, x].astype(F32) + src[i, x, c].astype(F32)
    for i in range(ins):
        second[i].wait_recv()
        out[i] = out[i] + quarter[i].astype(F32)
    for copy in first + second:
        copy.wait_send()


def split_rows(src, number):
    ins, _, _, rows, width = src.shape
    return pl.pallas_call(
        functools.partial(split_rows_kernel, ins),
        name="split_rows",
        out_shape=struct((ins, rows, width), F32),
        in_specs=[VMEM],
        out_specs=VMEM,
        scratch_shapes=[
            pltpu.VMEM((ins, 2, rows, width), BF16),
            pltpu.VMEM((ins, rows, width), BF16),
            pltpu.VMEM((ins, rows, width), BF16),
            DMA((2 * ins,)), DMA((2 * ins,)),
        ],
        compiler_params=params(number),
    )(src)


def head_rows(q, hands):
    rows, cols = q.shape
    size = cols // hands
    lane = lax.broadcasted_iota(jnp.int32, (rows, cols), 1)
    zero = jnp.zeros_like(q)
    parts = [
        jnp.where(jnp.logical_and(lane >= h * size, lane < (h + 1) * size), q, zero)
        for h in range(hands)
    ]
    return jnp.concatenate(parts, axis=0)


def own_columns(full, hands):
    rows, cols = full.shape[0] // hands, full.shape[1]
    size = cols // hands
    lane = lax.broadcasted_iota(jnp.int32, (rows, cols), 1)
    out = jnp.zeros((rows, cols), F32)
    for h in range(hands):
        keep = jnp.logical_and(lane >= h * size, lane < (h + 1) * size)
        out = jnp.where(keep, full[h * rows : (h + 1) * rows], out)
    return out


def nt(a, b):
    return lax.dot_general(a, b, (((1,), (1,)), ((), ())), preferred_element_type=F32)


def nn(a, b):
    return lax.dot_general(a, b, (((1,), (0,)), ((), ())), preferred_element_type=F32)


def tn(a, b):
    return lax.dot_general(a, b, (((0,), (0,)), ((), ())), preferred_element_type=F32)


def soft(qb, kp, kl, real, scale):
    sp = nt(qb, kp) * scale
    sl = nt(qb, kl) * scale
    key = lax.broadcasted_iota(jnp.int32, sp.shape, 1).astype(F32)
    sp = jnp.where(key < real, sp, -1e30)
    peak = jnp.maximum(jnp.max(sp, axis=1, keepdims=True), jnp.max(sl, axis=1, keepdims=True))
    ep, el = jnp.exp(sp - peak), jnp.exp(sl - peak)
    total = jnp.sum(ep, axis=1, keepdims=True) + jnp.sum(el, axis=1, keepdims=True)
    return ep / total, el / total


def attend_kernel(hands, scale, real, q, kp, kl, vp, vl, out):
    g = pl.program_id(0)
    qb = head_rows(q[0], hands)
    pp, plat = soft(qb, kp[0], kl[0], real[g].astype(F32), scale)
    full = nn(pp.astype(BF16), vp[0]) + nn(plat.astype(BF16), vl[0])
    out[0] = own_columns(full, hands).astype(BF16)


def attend(real, q, kp, kl, vp, vl, hands, scale):
    g, lat, cols = q.shape
    patches = kp.shape[1]

    def spec(rows):
        return pl.BlockSpec((1, rows, cols), lambda i, real: (i, 0, 0))

    return pl.pallas_call(
        functools.partial(attend_kernel, hands, scale),
        name="attend",
        grid_spec=pltpu.PrefetchScalarGridSpec(
            num_scalar_prefetch=1,
            grid=(g,),
            in_specs=[spec(lat), spec(patches), spec(lat), spec(patches), spec(lat)],
            out_specs=spec(lat),
        ),
        out_shape=struct((g, lat, cols), BF16),
        compiler_params=pltpu.CompilerParams(dimension_semantics=("arbitrary",)),
    )(real, q, kp, kl, vp, vl)


def attend_back_kernel(hands, scale, real, q, kp, kl, vp, vl, da, dq, dkp, dkl, dvp, dvl):
    g = pl.program_id(0)
    qb = head_rows(q[0], hands)
    dab = head_rows(da[0], hands)
    pp, plat = soft(qb, kp[0], kl[0], real[g].astype(F32), scale)
    gp, gl = nt(dab, vp[0]), nt(dab, vl[0])
    delta = jnp.sum(pp * gp, axis=1, keepdims=True) + jnp.sum(plat * gl, axis=1, keepdims=True)
    sp, sl = (pp * (gp - delta)).astype(BF16), (plat * (gl - delta)).astype(BF16)
    dvp[0] = tn(pp.astype(BF16), dab).astype(BF16)
    dvl[0] = tn(plat.astype(BF16), dab).astype(BF16)
    dkp[0] = (tn(sp, qb) * scale).astype(BF16)
    dkl[0] = (tn(sl, qb) * scale).astype(BF16)
    full = nn(sp, kp[0]) + nn(sl, kl[0])
    dq[0] = (own_columns(full, hands) * scale).astype(BF16)


def attend_back(real, q, kp, kl, vp, vl, da, hands, scale):
    g, lat, cols = q.shape
    patches = kp.shape[1]

    def spec(rows):
        return pl.BlockSpec((1, rows, cols), lambda i, real: (i, 0, 0))

    return pl.pallas_call(
        functools.partial(attend_back_kernel, hands, scale),
        name="attend_back",
        grid_spec=pltpu.PrefetchScalarGridSpec(
            num_scalar_prefetch=1,
            grid=(g,),
            in_specs=[spec(lat), spec(patches), spec(lat), spec(patches), spec(lat), spec(lat)],
            out_specs=[spec(lat), spec(patches), spec(lat), spec(patches), spec(lat)],
        ),
        out_shape=(
            struct((g, lat, cols), BF16),
            struct((g, patches, cols), BF16),
            struct((g, lat, cols), BF16),
            struct((g, patches, cols), BF16),
            struct((g, lat, cols), BF16),
        ),
        compiler_params=pltpu.CompilerParams(dimension_semantics=("arbitrary",)),
    )(real, q, kp, kl, vp, vl, da)


def collect_kernel(chain, size, gq, gw, gu, gd, kp, kl,
                   oq, ow, ou, od, okp, okl,
                   yq, yw, yu, yd, uq, uw, uu, ud, dq, dw, du, dd,
                   wc, wsum, wx, total, kc, kx, lc, lx, fin,
                   ys, yr, us, ur, ds, dr, ks, kr, qs, qr):
    d, p, z, y, x, c = place()
    above, below = z + 1 < chain, z > 0
    up_dev, dn_dev = ((z + 1) * 2 + y, p), ((z - 1) * 2 + y, p)
    y_dev, x_dev, c_dev = (z * 2 + 1 - y, p), (d, (1 - x) * 2 + c), (d, x * 2 + 1 - c)
    meet(patch_peers(d, p, size) + [y_dev], [(above, up_dev), (below, dn_dev)])

    mine = (
        lambda k: gq.at[:, k], lambda k: total.at[k], lambda k: gu.at[:, k], lambda k: gd.at[:, k]
    )
    land_y, land_u, land_d = (yq, yw, yu, yd), (uq, uw, uu, ud), (dq, dw, du, dd)

    def over(i, zz):
        return remote(
            mine[i](zz * 2 + 1 - y), land_y[i].at[zz], ys.at[i, zz], yr.at[i, zz], y_dev
        )

    def send_over(i):
        def step(zz, carry):
            over(i, zz).start()
            return carry

        lax.fori_loop(0, chain, step, 0)

    def add_over(i):
        def step(zz, carry):
            over(i, zz).wait_recv()
            have = mine[i](zz * 2 + y)
            land_y[i][zz] = (land_y[i][zz].astype(F32) + have[...].astype(F32)).astype(BF16)
            return carry

        lax.fori_loop(0, chain, step, 0)

    def rise(i, zz):
        return remote(land_y[i].at[zz], land_u[i].at[zz], us.at[i, zz], ur.at[i, zz], up_dev)

    def fall(i, zz):
        return remote(land_y[i].at[zz], land_d[i].at[zz], ds.at[i, zz], dr.at[i, zz], dn_dev)

    def gather(i, zz, land):
        land_y[i][zz] = (land_y[i][zz].astype(F32) + land[i][zz].astype(F32)).astype(BF16)

    def along(i):
        def step(k, carry):
            s = chain - k

            @pl.when(z + s < chain)
            def _():
                @pl.when(below)
                def _():
                    rise(i, z + s).wait_recv()
                    gather(i, z + s, land_u)

                rise(i, z + s).start()

            @pl.when(z - s >= 0)
            def _():
                @pl.when(above)
                def _():
                    fall(i, z - s).wait_recv()
                    gather(i, z - s, land_d)

                fall(i, z - s).start()

            return carry

        lax.fori_loop(1, chain, step, 0)

    def finish(i, write):
        write(land_y[i][z].astype(F32))

        @pl.when(below)
        def _():
            rise(i, z).wait_recv()
            write(land_u[i][z].astype(F32), True)

        @pl.when(above)
        def _():
            fall(i, z).wait_recv()
            write(land_d[i][z].astype(F32), True)

    def into(ref):
        def write(value, more=False):
            ref[...] = ref[...] + value if more else value

        return write

    def sent(i):
        def step(zz, carry):
            over(i, zz).wait_send()

            @pl.when(zz > z)
            def _():
                rise(i, zz).wait_send()

            @pl.when(zz < z)
            def _():
                fall(i, zz).wait_send()

            return carry

        lax.fori_loop(0, chain, step, 0)

    send_over(2)
    w_core = remote(gw.at[:, :, 1 - c], wc, ks.at[0], kr.at[0], c_dev)
    p_core = remote(kp.at[:, :, 1 - c], kc, ks.at[1], kr.at[1], c_dev)
    l_core = remote(kl.at[:, :, 1 - c], lc, ks.at[2], kr.at[2], c_dev)
    w_core.start()
    p_core.start()
    l_core.start()
    send_over(3)
    send_over(0)

    w_core.wait_recv()

    def w_add(k, carry):
        wsum[k] = (wc[k, 1 - x].astype(F32) + gw[k, 1 - x, c].astype(F32)).astype(BF16)
        return carry

    lax.fori_loop(0, 2 * chain, w_add, 0)
    w_x = remote(wsum, wx, ks.at[3], kr.at[3], x_dev)
    w_x.start()

    p_core.wait_recv()
    images = kp.shape[0]

    def p_add(k, carry):
        kc[k] = (kc[k].astype(F32) + kp[k, :, c].astype(F32)).astype(BF16)
        return carry

    lax.fori_loop(0, images, p_add, 0)
    p_x = remote(kc.at[:, 1 - x], kx, ks.at[4], kr.at[4], x_dev)
    p_x.start()
    l_core.wait_recv()

    def l_add(k, carry):
        lc[k] = (lc[k].astype(F32) + kl[k, :, c].astype(F32)).astype(BF16)
        return carry

    lax.fori_loop(0, images, l_add, 0)
    l_x = remote(lc.at[:, 1 - x], lx, ks.at[5], kr.at[5], x_dev)
    l_x.start()

    w_x.wait_recv()

    def w_last(k, carry):
        total[k] = (
            wc[k, x].astype(F32) + gw[k, x, c].astype(F32) + wx[k].astype(F32)
        ).astype(BF16)
        return carry

    lax.fori_loop(0, 2 * chain, w_last, 0)
    send_over(1)

    add_over(2)
    along(2)
    add_over(3)
    along(3)
    add_over(0)
    along(0)
    add_over(1)
    along(1)
    finish(2, into(ou))
    finish(3, into(od))
    finish(0, into(fin))
    swaps = []
    for k in range(1, size):
        q = lax.rem(p + k, size)
        swaps.append(remote(fin.at[:, q], oq.at[p], qs.at[k], qr.at[k], (d, q)))
    for copy in swaps:
        copy.start()
    finish(1, into(ow))
    oq[p] = fin[:, p]

    p_x.wait_recv()

    def p_last(k, carry):
        okp[k] = kc[k, x].astype(F32) + kx[k].astype(F32)
        return carry

    lax.fori_loop(0, images, p_last, 0)
    l_x.wait_recv()

    def l_last(k, carry):
        okl[k] = lc[k, x].astype(F32) + lx[k].astype(F32)
        return carry

    lax.fori_loop(0, images, l_last, 0)
    for copy in swaps:
        copy.wait()
    for i in range(4):
        sent(i)
    for copy in (w_core, p_core, l_core, w_x, p_x, l_x):
        copy.wait_send()


def collect(gq, gw, gu, gd, kp, kl, n, size):
    chain = n // 2
    three, _, _, r, cols = gq.shape
    width = gw.shape[-1]
    fu, fd = gu.shape[0], gd.shape[0]
    g, two, _, patches, _ = kp.shape
    lat = kl.shape[3]
    lands = [
        ((three, size, r, cols)), ((r, width)), ((fu, r, width)), ((fd, r, width)),
    ]
    stage = [pltpu.VMEM((chain,) + s, BF16) for s in lands]
    return pl.pallas_call(
        functools.partial(collect_kernel, chain, size),
        name="collect",
        out_shape=(
            struct((size, three, r, cols), F32),
            struct((r, width), F32),
            struct((fu, r, width), F32),
            struct((fd, r, width), F32),
            struct((g, patches, width), F32),
            struct((g, lat, width), F32),
        ),
        in_specs=[VMEM] * 6,
        out_specs=(VMEM,) * 6,
        scratch_shapes=stage * 3
        + [
            pltpu.VMEM((n, two, r, width), BF16),
            pltpu.VMEM((n, r, width), BF16),
            pltpu.VMEM((n, r, width), BF16),
            pltpu.VMEM((n, r, width), BF16),
            pltpu.VMEM((g, two, patches, width), BF16),
            pltpu.VMEM((g, patches, width), BF16),
            pltpu.VMEM((g, two, lat, width), BF16),
            pltpu.VMEM((g, lat, width), BF16),
            pltpu.VMEM((three, size, r, cols), F32),
        ]
        + [DMA((4, chain))] * 6
        + [DMA((6,)), DMA((6,)), DMA((size,)), DMA((size,))],
        compiler_params=params(6),
    )(gq, gw, gu, gd, kp, kl)


def total_kernel(hops, src, out, hold, land, ss, rs):
    d, p = lax.axis_index("dp"), lax.axis_index("patch")

    def flip(v, bit):
        return v + bit - 2 * bit * lax.rem(lax.div(v, bit), 2)

    to = [(d, flip(p, b)) if kind else (flip(d, b), p) for kind, b in hops]
    meet(to)
    sends = []
    for i, who in enumerate(to):
        copy = remote(src if i == 0 else hold.at[i], land.at[i], ss.at[i], rs.at[i], who)
        copy.start()
        copy.wait_recv()
        sends.append(copy)
        value = (src[...] if i == 0 else hold[i]) + land[i]
        if i + 1 < len(to):
            hold[i + 1] = value
        else:
            out[...] = value
    for copy in sends:
        copy.wait_send()


def total(src, n, size):
    hops = [(True, 1 << b) for b in range(size.bit_length() - 1)]
    hops += [(False, 1 << b) for b in range(n.bit_length() - 1)]
    return pl.pallas_call(
        functools.partial(total_kernel, hops),
        name="total",
        out_shape=struct(src.shape, F32),
        in_specs=[VMEM],
        out_specs=VMEM,
        scratch_shapes=[
            pltpu.VMEM((len(hops),) + src.shape, F32),
            pltpu.VMEM((len(hops),) + src.shape, F32),
            DMA((len(hops),)), DMA((len(hops),)),
        ],
        compiler_params=params(7),
    )(src)


class Names:
    def __init__(self, pairs):
        self.__dict__.update(pairs)


def aligned(start, step, count=None):
    return pl.ds(pl.multiple_of(start * step, step), count or step)


def each(lo, hi, body):
    def step(k, carry):
        body(k)
        return carry

    lax.fori_loop(lo, hi, step, 0)


def unit_of(x):
    mean = jnp.mean(x, axis=-1, keepdims=True)
    centred = x - mean
    spread_ = jnp.mean(centred * centred, axis=-1, keepdims=True)
    scaled = lax.rsqrt(spread_ + 1e-05)
    return centred * scaled, scaled


def column_sum(a):
    return jnp.sum(a, axis=0, keepdims=True)


INPUTS = ("weights", "media", "latents", "cot", "mask", "norms")
OUTPUTS = ("media_grad", "latents_grad", "latents_out", "grads", "sums", "squares")


def crowd_of(images):
    return 3 if images % 3 == 0 else 1


def buffers(n, size, g, patches, lat, width, ups, r):
    chain, cols, own = n // 2, width // size, g * lat
    keys, rows, tiles = size * (patches + lat), patches + lat, width // 256
    crowds = g // crowd_of(g)
    low = {
        "wqkv": (3, width, cols), "wo": (n, size, r, width), "ud": (3, ups, n * r, width),
        "nm": (g, size * patches, width), "nl": (g, size * lat, width), "dy": (size * own, width),
        "q": (g, size * lat, cols), "k": (g, keys, cols), "v": (g, keys, cols),
        "mixed": (g, size * lat, cols), "ab": (g, lat, width), "nf": (size * own, width),
        "gb": (ups, size * own, n * r), "du": (ups, size * own, n * r),
        "part": (2, tiles, 2, 2, own, 256), "half": (2, tiles, 2, own, 256),
        "mid": (2, tiles, own, 256), "quart": (2, tiles, own, 256),
        "da": (g, lat, width), "dah": (g, size * lat, cols), "gwo": (n, 2, 2, r, width),
        "yq": (3, chain, size * r, cols), "zq": (3, chain + 1, size * r, cols),
        "yw": (chain, r, width), "zw": (chain + 1, r, width),
        "yf": (3, chain, ups // 2, r, width), "zf": (3, chain + 1, ups // 2, r, width),
        "zb": (chain + 1, ups // 2, 2 * r, width), "yb": (ups // 2, r, width),
        "wc": (n, 2, r, width), "wsum": (n, r, width), "wx": (n, r, width), "total": (n, r, width),
        "kall": (2, 2, 2, rows, width), "kland": (g, 2, rows, width), "kx": (g, rows, width),
    }
    full = {
        "media": (g, patches, width), "latents": (g, lat, width), "cot": (g, lat, width),
        "norms": (6, width), "hidden": (own, width), "dhid": (own, width),
        "fin": (3, size * r, cols), "grads": (3 + 1 + 2 * ups, r, width), "gsum": (8, width),
        "flat": (3 + 1 + 2 * ups, r * width),
        "turn": (width // 128, (3 + 1 + 2 * ups) * r, 128),
        "cn": (size, (g + 15) // 16 * 16, size * patches),
        "nland": (size, 8, width), "nhold": (8, width), "dland": (n, 8, width),
        "sland": (size, 8, 128), "shold": (8, 128), "tland": (n, 8, 128), "sqr": (8, 128),
    }
    sems = {
        "loc": (5,), "ins": (5,), "outs": (3,), "mouts": (2,),
        "a_s": (size,), "a_r": (size,), "su": (5, chain), "sd": (5, chain), "sy": (5, chain),
        "rz": (5, chain), "ry": (5, chain),
        "ms": (crowds,), "mr": (crowds,), "mcs": (crowds, 2), "mcr": (crowds, 2),
        "xs": (5,), "xr": (5,), "cs": (5, 2), "cr": (5, 2), "ts": (size,), "tr": (size,),
        "hs": (size,), "hr": (size,), "ps": (2, tiles), "pr": (2, tiles), "qs": (2, tiles),
        "qr": (2, tiles), "ws": (2,), "wr": (2,), "ks": (2,), "kr": (g,), "lxs": (g,), "lxr": (g,),
        "gys": (7, chain), "gyr": (7, chain), "gzs": (7, chain), "gzr": (7, chain + 1),
        "bzs": (chain,), "bzr": (chain + 1,), "bys": (1,), "byr": (1,),
        "fs": (3, size), "fr": (3, size),
        "n1s": (size,), "n1r": (size,), "n2s": (n,), "n2r": (n,),
        "s1s": (size,), "s1r": (size,), "s2s": (n,), "s2r": (n,),
    }
    scratch = [(k, pltpu.VMEM(s, BF16)) for k, s in low.items()]
    scratch += [(k, pltpu.VMEM(s, F32)) for k, s in full.items()]
    scratch += [("held", pltpu.VMEM((4 + 2 * ups, r, width), BF16))]
    scratch += [(k, DMA(s)) for k, s in sems.items()]
    return scratch


def step_kernel(n, size, hands, scale, names, *refs):
    chain = n // 2
    count = len(INPUTS) + len(OUTPUTS)
    into = Names(zip(INPUTS, refs[: len(INPUTS)]))
    out = Names(zip(OUTPUTS, refs[len(INPUTS) : count]))
    b = Names(zip(names, refs[count:]))
    d, p, z, y, x, c = place()
    held, media, latents, cot, norms = b.held, b.media, b.latents, b.cot, b.norms
    wqkv, wo, ud, nm, nl, dy, cn = b.wqkv, b.wo, b.ud, b.nm, b.nl, b.dy, b.cn
    q, k_, v_, mixed, ab, hidden, nf = b.q, b.k, b.v, b.mixed, b.ab, b.hidden, b.nf
    r, width = held.shape[1], held.shape[2]
    cols, ups = width // size, ud.shape[1]
    images, patches, _ = media.shape
    lat = latents.shape[1]
    own, keys, reals = images * lat, size * (patches + lat), size * patches
    tiles = width // 256
    above, below = z + 1 < chain, z > 0
    up_dev, dn_dev = ((z + 1) * 2 + y, p), ((z - 1) * 2 + y, p)
    y_dev, x_dev, c_dev = (z * 2 + 1 - y, p), (d, (1 - x) * 2 + c), (d, x * 2 + 1 - c)
    px = (1 - x) * 2 + c
    dp_peers = [(lax.rem(d + s, n), p) for s in range(1, n)]

    loads = [
        pltpu.make_async_copy(src, dst, b.ins.at[i])
        for i, (src, dst) in enumerate(
            ((into.weights, b.flat), (into.latents, latents), (into.norms, norms),
             (into.media, media), (into.cot, cot))
        )
    ]
    for copy in loads:
        copy.start()
    everyone_here = greet(patch_peers(d, p, size) + dp_peers)
    blocks = held.shape[0]
    loads[0].wait()
    for t in range(width // 128):
        for k in range(r):
            at = k * width + t * 128
            b.turn[t, pl.ds(k, blocks, stride=r), :] = b.flat[:, at : at + 128]
        held[:, :, t * 128 : (t + 1) * 128] = (
            b.turn[t].reshape(blocks, r, 128).astype(BF16)
        )
    everyone_here()

    def lanes(k):
        return aligned(k, cols)

    half = ups // 2
    def piece(i, dd):
        if i == 0:
            return wqkv.at[:, aligned(dd, size * r)]
        if i == 1:
            return wo.at[dd, p]
        if i == 2:
            return ud.at[0, :, aligned(dd, r)]
        return ud.at[1, pl.ds((i - 3) * half, half), aligned(dd, r)]

    first = (
        wqkv.at[:, aligned(d, size * r)], held.at[3], held.at[pl.ds(4, ups)],
        held.at[pl.ds(4 + ups, half)], held.at[pl.ds(4 + ups + half, half)],
    )
    here = wqkv.at[:, aligned(d * size + p, r)]
    def hop(i, zz, sends, to, own_src=False):
        src = first[i] if own_src else piece(i, zz * 2 + y)
        return remote(src, piece(i, zz * 2 + y), sends.at[i, zz], b.rz.at[i, zz], to)

    def over(i, zz, own_src=False):
        src = first[i] if own_src else piece(i, zz * 2 + y)
        return remote(src, piece(i, zz * 2 + y), b.sy.at[i, zz], b.ry.at[i, zz], y_dev)

    def start_own(i):
        @pl.when(above)
        def _():
            hop(i, z, b.su, up_dev, True).start()

        @pl.when(below)
        def _():
            hop(i, z, b.sd, dn_dev, True).start()

        over(i, z, True).start()

    swaps = []
    for k in range(1, size):
        to = lax.rem(p + k, size)
        swaps.append(
            remote(held.at[pl.ds(0, 3), :, lanes(to)], here, b.a_s.at[k], b.a_r.at[k], (d, to))
        )
    for copy in swaps:
        copy.start()
    start_own(2)
    over(4, z, True).start()
    local = [pltpu.make_async_copy(held.at[pl.ds(0, 3), :, lanes(p)], here, b.loc.at[0])]
    local += [pltpu.make_async_copy(first[i], piece(i, d), b.loc.at[i]) for i in (1, 2, 3, 4)]
    for copy in local:
        copy.start()

    def forward(i):
        def step(s):
            @pl.when(z - s >= 0)
            def _():
                hop(i, z - s, b.su, up_dev).wait_recv()

                @pl.when(above)
                def _():
                    hop(i, z - s, b.su, up_dev).start()

                over(i, z - s).start()

            @pl.when(z + s < chain)
            def _():
                hop(i, z + s, b.sd, dn_dev).wait_recv()

                @pl.when(below)
                def _():
                    hop(i, z + s, b.sd, dn_dev).start()

                over(i, z + s).start()

        each(1, chain, step)

    def pair(zz):
        return ud.at[1, pl.ds(half, half), aligned(zz, 2 * r)]

    def pair_hop(zz, sends, to):
        return remote(pair(zz), pair(zz), sends.at[4, zz], b.rz.at[4, zz], to)

    def pair_start():
        src = piece(4, z * 2 + 1 - y)
        local[4].wait()
        remote(src, src, b.sy.at[4, z], b.ry.at[4, z], y_dev).wait_recv()

        @pl.when(above)
        def _():
            pair_hop(z, b.su, up_dev).start()

        @pl.when(below)
        def _():
            pair_hop(z, b.sd, dn_dev).start()

    def pair_forward(s):
        @pl.when(z - s >= 0)
        def _():
            pair_hop(z - s, b.su, up_dev).wait_recv()

            @pl.when(above)
            def _():
                pair_hop(z - s, b.su, up_dev).start()

        @pl.when(z + s < chain)
        def _():
            pair_hop(z + s, b.sd, dn_dev).wait_recv()

            @pl.when(below)
            def _():
                pair_hop(z + s, b.sd, dn_dev).start()

    def pair_sent():
        over(4, z).wait_send()

        def step(zz):
            @pl.when(jnp.logical_and(above, zz <= z))
            def _():
                pair_hop(zz, b.su, up_dev).wait_send()

            @pl.when(jnp.logical_and(below, zz >= z))
            def _():
                pair_hop(zz, b.sd, dn_dev).wait_send()

        each(0, chain, step)

    def arrived(i):
        def step(zz):
            src = piece(i, zz * 2 + 1 - y)
            remote(src, src, b.sy.at[i, zz], b.ry.at[i, zz], y_dev).wait_recv()

        each(0, chain, step)

    def sent(i):
        def step(zz):
            over(i, zz).wait_send()

            @pl.when(jnp.logical_and(above, zz <= z))
            def _():
                hop(i, zz, b.su, up_dev).wait_send()

            @pl.when(jnp.logical_and(below, zz >= z))
            def _():
                hop(i, zz, b.sd, dn_dev).wait_send()

        each(0, chain, step)

    class Rows:
        def __init__(self, slot, xs, xr, cs, cr, at, src=None):
            src = slot(p) if src is None else src
            self.to_x = remote(src, slot(p), xs.at[at], xr.at[at], x_dev)
            self.to_c = remote(src, slot(p), cs.at[at, 0], cr.at[at, 0], c_dev)
            self.on = remote(slot(px), slot(px), cs.at[at, 1], cr.at[at, 1], c_dev)

        def start(self):
            self.to_x.start()
            self.to_c.start()

        def forward(self):
            self.to_x.wait_recv()
            self.on.start()

        def have(self):
            self.to_c.wait_recv()
            self.on.wait_recv()

        def end(self):
            self.to_x.wait_send()
            self.to_c.wait_send()
            self.on.wait_send()

    def group(slot, j, src=None):
        return Rows(slot, b.xs, b.xr, b.cs, b.cr, j, src)

    lat_rows = group(lambda k: nl.at[:, aligned(k, lat)], 0)
    cn_rows = group(lambda k: cn.at[k], 1)
    dy_rows = group(lambda k: dy.at[aligned(k, own)], 2)
    nf_rows = group(lambda k: nf.at[aligned(k, own)], 3)

    wo_rows = group(lambda k: wo.at[:, k], 4)
    crowd = crowd_of(images)
    crowds = images // crowd

    def media_rows(j):
        return Rows(
            lambda k: nm.at[aligned(j, crowd), aligned(k, patches)],
            b.ms, b.mr, b.mcs, b.mcr, j,
        )

    loads[1].wait()
    loads[2].wait()
    media_gain, media_shift = 1.0 + norms[0:1, :], norms[1:2, :]
    latent_gain, latent_shift = 1.0 + norms[2:3, :], norms[3:4, :]
    ffn_gain, ffn_shift = 1.0 + norms[4:5, :], norms[5:6, :]

    def latent_norm(g):
        unit, _ = unit_of(latents[g])
        nl[g, aligned(p, lat)] = (unit * latent_gain + latent_shift).astype(BF16)

    def media_norm(g):
        unit, _ = unit_of(media[g])
        nm[g, aligned(p, patches)] = (unit * media_gain + media_shift).astype(BF16)

    cn[p] = jnp.zeros(cn.shape[1:], F32)
    counts = column_of((into.mask[...] > 0).astype(F32))
    cn[p, :images, :] = jnp.broadcast_to(counts, (images, cn.shape[2]))
    each(0, images, latent_norm)
    cn_rows.start()
    lat_rows.start()
    local[0].wait()
    for copy in swaps:
        copy.wait_recv()
    start_own(0)
    start_own(1)
    loads[3].wait()
    each(0, images, media_norm)
    each(0, crowds, lambda j: media_rows(j).start())
    loads[4].wait()
    dy[aligned(p, own)] = cot[...].reshape(own, width).astype(BF16)
    forward(0)
    start_own(3)
    cn_rows.forward()
    lat_rows.forward()
    forward(1)
    pair_start()
    dy_rows.start()
    media_rows(0).forward()
    arrived(0)
    lat_rows.have()
    cn_rows.have()

    flat_nl = nl[...].reshape(images * size * lat, width)
    q[...] = nn(flat_nl, wqkv[0]).astype(BF16).reshape(images, size * lat, cols)
    k_[:, reals:] = nn(flat_nl, wqkv[1]).astype(BF16).reshape(images, size * lat, cols)
    v_[:, reals:] = nn(flat_nl, wqkv[2]).astype(BF16).reshape(images, size * lat, cols)

    def real_keys(g):
        real = cn[0, pl.ds(g, 1), :]
        for k in range(1, size):
            real = real + cn[k, pl.ds(g, 1), :]
        return real

    def image(g):
        k_[g, :reals] = nn(nm[g], wqkv[1]).astype(BF16)
        v_[g, :reals] = nn(nm[g], wqkv[2]).astype(BF16)
        pp, plat = soft(
            head_rows(q[g], hands), k_[g, :reals], k_[g, reals:], real_keys(g), scale
        )
        full = nn(pp.astype(BF16), v_[g, :reals]) + nn(plat.astype(BF16), v_[g, reals:])
        mixed[g] = own_columns(full, hands).astype(BF16)

    media_rows(0).have()
    each(0, crowd, image)
    forward(2)
    arrived(1)
    local[1].wait()
    wo_rows.start()
    for j in range(1, crowds):
        media_rows(j).forward()
        media_rows(j).have()
        each(j * crowd, (j + 1) * crowd, image)
    dy_rows.forward()

    turns = []
    for k in range(1, size):
        to = lax.rem(p + k, size)
        turns.append(
            remote(mixed.at[:, aligned(to, lat)], ab.at[:, :, lanes(p)],
                   b.ts.at[k], b.tr.at[k], (d, to))
        )
    for copy in turns:
        copy.start()
    ab[:, :, lanes(p)] = mixed[:, aligned(p, lat)]
    forward(3)
    wo_rows.forward()
    wo_rows.have()
    for copy in turns:
        copy.wait_recv()
    flat_ab = ab[...].reshape(own, width)
    for t in range(tiles):
        span = pl.ds(256 * t, 256)
        hidden[:, span] = latents[:, :, span].reshape(own, 256) + nn(
            flat_ab, wo[:, :, :, span].reshape(width, 256)
        )
    unit, _ = unit_of(hidden[...])
    nf[aligned(p, own)] = (unit * ffn_gain + ffn_shift).astype(BF16)
    nf_rows.start()
    dy_rows.have()
    for s in range(1, chain - 1):
        pair_forward(s)
    arrived(2)
    arrived(3)
    for copy in local[2:4]:
        copy.wait()
    nf_rows.forward()
    nf_rows.have()

    def hidden_block(e):
        u = nt(nf[...], ud[0, e])
        into_active = nt(dy[...], ud[1, e])
        chance = 0.5 * (1.0 + lax.erf(u * math.sqrt(0.5)))
        slope = chance + u * jnp.exp(-0.5 * u * u) * (1.0 / math.sqrt(2.0 * math.pi))
        b.gb[e] = (u * chance).astype(BF16)
        b.du[e] = (into_active * slope).astype(BF16)

    def down_grad(e):
        for t in range(0, width, 512):
            ud[2, e, :, t : t + 512] = tn(b.gb[e], dy[:, t : t + 512]).astype(BF16)

    def up_grad(e):
        for t in range(0, width, 512):
            ud[0, e, :, t : t + 512] = tn(b.du[e], nf[:, t : t + 512]).astype(BF16)

    def part_core(i, t):
        return remote(
            b.part.at[i, t, :, 1 - c], b.half.at[i, t], b.ps.at[i, t], b.pr.at[i, t], c_dev
        )

    def part_x(i, t):
        return remote(b.mid.at[i, t], b.quart.at[i, t], b.qs.at[i, t], b.qr.at[i, t], x_dev)

    def part_of(i, acts):
        def tile(t):
            span = aligned(t, 256)
            acc = nn(acts[0], ud[i, 0, :, span])
            for e in range(1, ups):
                acc = acc + nn(acts[e], ud[i, e, :, span])
            b.part[i, t] = acc.astype(BF16).reshape(2, 2, own, 256)
            part_core(i, t).start()

        each(0, tiles, tile)

    def part_pass(i):
        def tile(t):
            part_core(i, t).wait_recv()
            b.mid[i, t] = (
                b.half[i, t, 1 - x].astype(F32) + b.part[i, t, 1 - x, c].astype(F32)
            ).astype(BF16)
            part_x(i, t).start()

        each(0, tiles, tile)

    def part_end(i, write):
        def tile(t):
            part_x(i, t).wait_recv()
            write(
                aligned(t, 256),
                b.half[i, t, x].astype(F32) + b.part[i, t, x, c].astype(F32)
                + b.quart[i, t].astype(F32),
            )

        each(0, tiles, tile)

    def parts_sent(i):
        def tile(t):
            part_core(i, t).wait_send()
            part_x(i, t).wait_send()

        each(0, tiles, tile)

    def ffn_part(i, k):
        late = lax.div(i - 3, 2) if not isinstance(i, int) else (i - 3) // 2
        plane = 2 * (1 - late)
        start = half * lax.max(i - 5, 0) if not isinstance(i, int) else half * max(i - 5, 0)
        return ud.at[plane, pl.ds(start, half), aligned(k, r)]

    class Sum:
        def __init__(self, i, kind):
            self.i = i
            if kind == 0:
                self.mine = lambda k: wqkv.at[i, aligned(k, size * r)]
                self.ly, self.lz = b.yq.at[i], b.zq.at[i]
            elif kind == 1:
                self.mine = lambda k: b.total.at[k]
                self.ly, self.lz = b.yw, b.zw
            else:
                self.mine = lambda k: ffn_part(i, k)
                self.ly, self.lz = b.yf.at[i - 4], b.zf.at[i - 4]

        def over(self, zt):
            return remote(
                self.mine(zt * 2 + 1 - y), self.ly.at[zt], b.gys.at[self.i, zt],
                b.gyr.at[self.i, zt], y_dev,
            )

        def along(self, zt, slot, to):
            return remote(
                self.ly.at[zt], self.lz.at[slot], b.gzs.at[self.i, zt], b.gzr.at[self.i, slot], to
            )

        def send(self):
            def step(k):
                s = chain - 1 - k

                @pl.when(z + s < chain)
                def _():
                    self.over(z + s).start()

                @pl.when(jnp.logical_and(z - s >= 0, s > 0))
                def _():
                    self.over(z - s).start()

            each(0, chain, step)

        def pair(self, zt):
            return self.ly[zt].astype(F32) + self.mine(zt * 2 + y)[...].astype(F32)

        def move(self, zt, more, slot, to):
            self.over(zt).wait_recv()

            @pl.when(more)
            def _():
                self.along(zt, slot, to).wait_recv()
                self.ly[zt] = (self.pair(zt) + self.lz[slot].astype(F32)).astype(BF16)

            @pl.when(jnp.logical_not(more))
            def _():
                self.ly[zt] = self.pair(zt).astype(BF16)

            self.along(zt, slot, to).start()

        def step(self, s):
            @pl.when(z + s < chain)
            def _():
                self.move(z + s, below, z + s + 1, up_dev)

            @pl.when(z - s >= 0)
            def _():
                self.move(z - s, above, z - s, dn_dev)

        def last(self, dst):
            self.over(z).wait_recv()
            dst[...] = self.pair(z)

            @pl.when(below)
            def _():
                self.along(z, z + 1, up_dev).wait_recv()
                dst[...] = dst[...] + self.lz[z + 1].astype(F32)

            @pl.when(above)
            def _():
                self.along(z, z, dn_dev).wait_recv()
                dst[...] = dst[...] + self.lz[z].astype(F32)

        def steps(self):
            each(0, chain - 1, lambda k: self.step(chain - 1 - k))

        def sent(self):
            def step(zt):
                self.over(zt).wait_send()

                @pl.when(zt != z)
                def _():
                    self.along(zt, 0, up_dev).wait_send()

            each(0, chain, step)

    class Cross:
        def pair(self, zt):
            return ud.at[2, pl.ds(half, half), aligned(zt, 2 * r)]

        def along(self, zt, slot, to):
            return remote(self.pair(zt), b.zb.at[slot], b.bzs.at[zt], b.bzr.at[slot], to)

        def move(self, zt, more, slot, to):
            @pl.when(more)
            def _():
                self.along(zt, slot, to).wait_recv()
                self.pair(zt)[...] = (
                    self.pair(zt)[...].astype(F32) + b.zb[slot].astype(F32)
                ).astype(BF16)

            self.along(zt, slot, to).start()

        def step(self, s):
            @pl.when(z + s < chain)
            def _():
                self.move(z + s, below, z + s + 1, up_dev)

            @pl.when(z - s >= 0)
            def _():
                self.move(z - s, above, z - s, dn_dev)

        def over(self):
            src = ud.at[2, pl.ds(half, half), aligned(z * 2 + 1 - y, r)]
            return remote(src, b.yb, b.bys.at[0], b.byr.at[0], y_dev)

        def meet(self, dst):
            theirs, ours = aligned(1 - y, r), aligned(y, r)
            far = ud.at[2, pl.ds(half, half), aligned(z * 2 + 1 - y, r)]
            near = ud.at[2, pl.ds(half, half), aligned(z * 2 + y, r)]
            dst[...] = near[...].astype(F32)

            def add(slot):
                dst[...] = dst[...] + b.zb[slot, :, ours].astype(F32)
                far[...] = (
                    far[...].astype(F32) + b.zb[slot, :, theirs].astype(F32)
                ).astype(BF16)

            @pl.when(below)
            def _():
                self.along(z, z + 1, up_dev).wait_recv()
                add(z + 1)

            @pl.when(above)
            def _():
                self.along(z, z, dn_dev).wait_recv()
                add(z)

            self.over().start()

        def last(self, dst):
            self.over().wait_recv()
            dst[...] = dst[...] + b.yb[...].astype(F32)

        def sent(self):
            self.over().wait_send()

            def step(zt):
                @pl.when(zt != z)
                def _():
                    self.along(zt, 0, up_dev).wait_send()

            each(0, chain, step)

    cross = Cross()
    qkv_sums, wo_sum = [Sum(i, 0) for i in range(3)], Sum(3, 1)

    def ffn_sum(i):
        return Sum(i, 2)

    each(0, half, hidden_block)
    each(0, half, down_grad)
    ffn_sum(4).send()
    pair_forward(chain - 1)
    each(half, ups, hidden_block)
    part_of(0, b.du)
    each(half, ups, down_grad)
    cross.step(chain - 1)
    part_pass(0)
    for i in range(4):
        sent(i)
    pair_sent()
    each(0, ups, up_grad)
    ffn_sum(5).send()
    ffn_sum(6).send()
    for s in range(chain - 2, 1, -1):
        cross.step(s)

    def write_dhid(span, value):
        b.dhid[:, span] = value

    part_end(0, write_dhid)
    dn = b.dhid[...]
    unit, scaled = unit_of(hidden[...])
    b.gsum[...] = jnp.zeros_like(b.gsum)
    b.gsum[4:5, :] = column_sum(dn * unit)
    b.gsum[5:6, :] = column_sum(dn)
    b.dhid[...] = cot[...].reshape(own, width) + norm_back(dn, unit, scaled, ffn_gain)
    do = b.dhid[...].astype(BF16)
    step_rows = 256 // (size * r)

    def wo_block(t):
        return wo[t * step_rows : (t + 1) * step_rows].reshape(256, width)

    for t in range(tiles):
        span = pl.ds(256 * t, 256)
        b.da[:, :, span] = nt(do, wo_block(t)).astype(BF16).reshape(images, lat, 256)
    turns_back = []
    for k in range(1, size):
        to = lax.rem(p + k, size)
        turns_back.append(
            remote(b.da.at[:, :, lanes(to)], b.dah.at[:, aligned(p, lat)],
                   b.hs.at[k], b.hr.at[k], (d, to))
        )
    for copy in turns_back:
        copy.start()
    b.dah[:, aligned(p, lat)] = b.da[:, :, lanes(p)]
    for t in range(tiles):
        span = pl.ds(256 * t, 256)
        b.gwo[:, :, :, :, span] = (
            tn(ab[...].reshape(own, width), do[:, 256 * t : 256 * t + 256])
            .astype(BF16).reshape(n, 2, 2, r, 256)
        )
    w_core = remote(b.gwo.at[:, :, 1 - c], b.wc, b.ws.at[0], b.wr.at[0], c_dev)
    w_x = remote(b.wsum, b.wx, b.ws.at[1], b.wr.at[1], x_dev)
    w_core.start()
    cross.step(1)
    part_of(1, b.gb)
    w_core.wait_recv()

    def w_add(k):
        b.wsum[k] = (b.wc[k, 1 - x].astype(F32) + b.gwo[k, 1 - x, c].astype(F32)).astype(BF16)

    each(0, n, w_add)
    w_x.start()
    for copy in turns_back:
        copy.wait_recv()

    def kin_core(g):
        return remote(
            b.kall.at[lax.rem(g, 2), 1 - c], b.kland.at[g], b.ks.at[lax.rem(g, 2)], b.kr.at[g], c_dev
        )

    def kin_x(g):
        return remote(b.kland.at[g, 1 - x], b.kx.at[g], b.lxs.at[g], b.lxr.at[g], x_dev)

    def image_back(g):
        slot = lax.rem(g, 2)
        qb, dab = head_rows(q[g], hands), head_rows(b.dah[g], hands)
        kp, kl, vp, vl = k_[g, :reals], k_[g, reals:], v_[g, :reals], v_[g, reals:]
        pp, plat = soft(qb, kp, kl, real_keys(g), scale)
        gp, gl = nt(dab, vp), nt(dab, vl)
        delta = column_of(pp * gp) + column_of(plat * gl)
        sp, sl = (pp * (gp - delta)).astype(BF16), (plat * (gl - delta)).astype(BF16)
        v_[g, :reals] = tn(pp.astype(BF16), dab).astype(BF16)
        v_[g, reals:] = tn(plat.astype(BF16), dab).astype(BF16)
        k_[g, :reals] = (tn(sp, qb) * scale).astype(BF16)
        k_[g, reals:] = (tn(sl, qb) * scale).astype(BF16)
        q[g] = (own_columns(nn(sp, kp) + nn(sl, kl), hands) * scale).astype(BF16)
        for t in range(tiles):
            span = pl.ds(256 * t, 256)
            rows = nt(k_[g], wqkv[1, span, :]) + nt(v_[g], wqkv[2, span, :])
            tail = rows[reals:] + nt(q[g], wqkv[0, span, :])
            for e in range(size):
                b.kall[slot, e % 2, e // 2, :patches, span] = (
                    rows[e * patches : (e + 1) * patches].astype(BF16)
                )
                b.kall[slot, e % 2, e // 2, patches:, span] = (
                    tail[e * lat : (e + 1) * lat].astype(BF16)
                )
        kin_core(g).start()

    def kin_mid(g):
        kin_core(g).wait_recv()
        b.kland[g] = (
            b.kland[g].astype(F32) + b.kall[lax.rem(g, 2), c].astype(F32)
        ).astype(BF16)
        kin_x(g).start()

    def media_out(g):
        return pltpu.make_async_copy(media.at[g], out.media_grad.at[g], b.mouts.at[lax.rem(g, 2)])

    def kin_last(g):
        kin_x(g).wait_recv()
        total_ = b.kland[g, x].astype(F32) + b.kx[g].astype(F32)
        grad = total_[:patches]
        unit, scaled = unit_of(media[g])
        b.gsum[0:1, :] = b.gsum[0:1, :] + column_sum(grad * unit)
        b.gsum[1:2, :] = b.gsum[1:2, :] + column_sum(grad)
        media[g] = norm_back(grad, unit, scaled, media_gain)

        @pl.when(g >= 2)
        def _():
            media_out(g - 2).wait()

        media_out(g).start()
        grad = total_[patches:]
        unit, scaled = unit_of(latents[g])
        b.gsum[2:3, :] = b.gsum[2:3, :] + column_sum(grad * unit)
        b.gsum[3:4, :] = b.gsum[3:4, :] + column_sum(grad)
        latents[g] = b.dhid[aligned(g, lat)] + norm_back(grad, unit, scaled, latent_gain)

    moves = min(2 * (chain - 1), images)

    def ffn_step(k):
        ffn_sum(4 + lax.div(k, chain - 1)).step(chain - 1 - lax.rem(k, chain - 1))

    def back(g):
        @pl.when(g >= 2)
        def _():
            kin_core(g - 2).wait_send()

        image_back(g)

        @pl.when(g >= 1)
        def _():
            kin_mid(g - 1)

        @pl.when(g < moves)
        def _():
            ffn_step(g)

    def w_last(k):
        b.total[k] = (
            b.wc[k, x].astype(F32) + b.gwo[k, x, c].astype(F32) + b.wx[k].astype(F32)
        ).astype(BF16)

    each(0, images, back)
    kin_mid(images - 1)

    def flat(a, n_rows):
        return a.reshape(images * n_rows, cols)

    def qkv_grad(j):
        def tile(t):
            span = aligned(t, 256)
            rows_l = nl[:, :, span].reshape(images * size * lat, 256)
            if j == 0:
                wqkv[0, span, :] = tn(rows_l, flat(q[...], size * lat)).astype(BF16)
                return
            rows_m = nm[:, :, span].reshape(images * reals, 256)
            ref = (k_, v_)[j - 1]
            wqkv[j, span, :] = (
                tn(rows_m, flat(ref[:, :reals], reals))
                + tn(rows_l, flat(ref[:, reals:], size * lat))
            ).astype(BF16)

        each(0, tiles, tile)
        qkv_sums[j].send()

    qkv_grad(0)
    qkv_grad(2)
    qkv_grad(1)
    w_x.wait_recv()
    each(0, n, w_last)
    wo_sum.send()
    part_pass(1)
    each(moves, 3 * (chain - 1), ffn_step)
    down_rows = b.grads.at[pl.ds(4 + ups + half, half)]
    cross.meet(down_rows)
    ffn_sum(4).last(b.grads.at[pl.ds(4 + ups, half)])
    ffn_sum(5).last(b.grads.at[pl.ds(4, half)])
    ffn_sum(6).last(b.grads.at[pl.ds(4 + half, half)])
    third = (images + 2) // 3
    qkv_sums[0].steps()
    each(0, third, kin_last)
    qkv_sums[2].steps()
    each(third, 2 * third, kin_last)
    qkv_sums[1].steps()
    each(2 * third, images, kin_last)
    lat_copy = pltpu.make_async_copy(latents, out.latents_grad, b.outs.at[1])
    lat_copy.start()
    cross.last(down_rows)
    wo_sum.steps()

    def write_out(span, value):
        hidden[:, span] = hidden[:, span] + value

    part_end(1, write_out)
    out_copy = pltpu.make_async_copy(hidden, out.latents_out, b.outs.at[0])
    out_copy.start()

    def share(src, land, hold, s1, r1, total_to, land2, s2, r2):
        land[p] = src[...]
        near = []
        for k in range(1, size):
            to = lax.rem(p + k, size)
            near.append(remote(src, land.at[p], s1.at[to], r1.at[p], (d, to)))
        for copy in near:
            copy.start()
        for k in range(1, size):
            who = lax.rem(p + k, size)
            remote(src, land.at[who], s1.at[who], r1.at[who], (d, who)).wait_recv()
        value = land[0]
        for k in range(1, size):
            value = value + land[k]
        hold[...] = value
        land2[d] = value
        far = []
        for k in range(1, n):
            to = lax.rem(d + k, n)
            far.append(remote(hold, land2.at[d], s2.at[to], r2.at[d], (to, p)))
        for copy in far:
            copy.start()

        def finish():
            for k in range(1, n):
                who = lax.rem(d + k, n)
                remote(hold, land2.at[who], s2.at[who], r2.at[who], (who, p)).wait_recv()
            value = land2[0]
            for k in range(1, n):
                value = value + land2[k]
            total_to[...] = value
            for copy in near + far:
                copy.wait_send()

        return finish

    norms_done = share(b.gsum, b.nland, b.nhold, b.n1s, b.n1r, out.sums, b.dland, b.n2s, b.n2r)
    ends = []
    for j in (0, 2, 1):
        qkv_sums[j].last(b.fin.at[j])
        for k in range(1, size):
            to = lax.rem(p + k, size)
            copy = remote(
                b.fin.at[j, aligned(to, r)], b.grads.at[j, :, lanes(p)],
                b.fs.at[j, k], b.fr.at[j, k], (d, to),
            )
            copy.start()
            ends.append(copy)
        b.grads[j, :, lanes(p)] = b.fin[j, aligned(p, r)]
    wo_sum.last(b.grads.at[3])
    for copy in ends:
        copy.wait_recv()
    for t in range(width // 128):
        b.turn[t] = b.grads[:, :, t * 128 : (t + 1) * 128].reshape(blocks * r, 128)
        for k in range(r):
            at = k * width + t * 128
            b.flat[:, at : at + 128] = b.turn[t, pl.ds(k, blocks, stride=r), :]
    grads_copy = pltpu.make_async_copy(b.flat, out.grads, b.outs.at[2])
    grads_copy.start()
    squares = jnp.zeros((8, 128), F32)
    for i in range(b.grads.shape[0]):
        for t in range(0, width, 128):
            tile = b.grads[i, :, t : t + 128]
            squares = squares + jnp.sum((tile * tile).reshape(r // 8, 8, 128), axis=0)
    b.sqr[...] = squares
    squares_done = share(
        b.sqr, b.sland, b.shold, b.s1s, b.s1r, out.squares, b.tland, b.s2s, b.s2r
    )
    norms_done()
    for copy in swaps + turns + turns_back + ends:
        copy.wait_send()
    for rows in (lat_rows, cn_rows, dy_rows, nf_rows):
        rows.end()
    wo_rows.end()
    each(0, crowds, lambda j: media_rows(j).end())
    parts_sent(0)
    parts_sent(1)
    w_core.wait_send()
    w_x.wait_send()
    each(max(images - 2, 0), images, lambda g: kin_core(g).wait_send())
    each(0, images, lambda g: kin_x(g).wait_send())
    for item in qkv_sums:
        item.sent()
    wo_sum.sent()
    each(4, 7, lambda i: ffn_sum(i).sent())
    cross.sent()
    each(max(images - 2, 0), images, lambda g: media_out(g).wait())
    out_copy.wait()
    lat_copy.wait()
    grads_copy.wait()
    squares_done()


def column_of(a):
    return jnp.sum(a, axis=1, keepdims=True)


def whole_step(weights, media, latents, cot, mask, norms, n, size, hands, scale):
    g, patches, width = media.shape
    blocks, r = weights.shape[0], weights.shape[1] // width
    lat = latents.shape[1]
    scratch = buffers(n, size, g, patches, lat, width, FF // width, r)
    return pl.pallas_call(
        functools.partial(step_kernel, n, size, hands, scale, [k for k, _ in scratch]),
        name="whole_step",
        out_shape=(
            struct((g, patches, width), F32),
            struct((g, lat, width), F32),
            struct((g * lat, width), F32),
            struct(weights.shape, F32),
            struct((8, width), F32),
            struct((8, 128), F32),
        ),
        in_specs=[ANY] * 4 + [VMEM] + [ANY],
        out_specs=(ANY,) * 4 + (VMEM,) * 2,
        scratch_shapes=[s for _, s in scratch],
        compiler_params=params(8),
    )(weights, media, latents, cot, mask, norms)


def finish_kernel(sums, squares, *refs):
    weights, grads, norms = refs[:4], refs[4], refs[5:9]
    passed, outs = refs[9:12], refs[12:]
    grad_norm, new_weights, new_low, new_norms, ffn, passed_out = (
        outs[0], outs[1:5], outs[5], outs[6:10], outs[10], outs[11:14]
    )
    norm_grads = sums[:6, :]
    square = jnp.sum(squares[...], axis=0, keepdims=True)
    square = jnp.sum(square, axis=1, keepdims=True)
    rest = jnp.sum(norm_grads * norm_grads, axis=0, keepdims=True)
    length = jnp.sqrt(square + jnp.sum(rest, axis=1, keepdims=True))
    clip = jnp.minimum(1.0, 1.0 / (length + 1e-06))
    new = adamw_update(*(ref[...] for ref in weights), grads[...], clip, 0.1)
    for ref, value in zip(new_weights, new):
        ref[...] = value
    new_low[...] = new[0].astype(BF16)
    for src, dst in zip(passed, passed_out):
        dst[...] = src[...]

    @pl.when(pl.program_id(0) == 0)
    def _():
        grad_norm[...] = jnp.broadcast_to(length, grad_norm.shape)
        for ref, value in zip(
            new_norms, adamw_update(*(ref[...] for ref in norms), norm_grads, clip, 0.0)
        ):
            ref[...] = value
        ffn[...] = norm_grads[4:6]


def finish(sums, squares, weights, grads, norms, passed):
    steps = 4
    rows, flat = grads.shape
    six, width = norms[0].shape

    def whole(shape):
        return pl.BlockSpec(shape, lambda i: (0,) * len(shape))

    wide = pl.BlockSpec((rows, flat // steps), lambda i: (0, i))
    through = [
        pl.BlockSpec(a.shape[:2] + (width // steps,), lambda i: (0, 0, i)) for a in passed
    ]
    return pl.pallas_call(
        finish_kernel,
        name="finish",
        grid=(steps,),
        in_specs=[whole(sums.shape), whole(squares.shape)] + [wide] * 5
        + [whole((six, width))] * 4 + through,
        out_specs=[whole((1, 128))] + [wide] * 5 + [whole((six, width))] * 4
        + [whole((2, width))] + through,
        out_shape=[struct((1, 128), F32)] + [struct(grads.shape, F32)] * 4
        + [struct(grads.shape, BF16)] + [struct((six, width), F32)] * 4
        + [struct((2, width), F32)] + [struct(a.shape, F32) for a in passed],
        compiler_params=pltpu.CompilerParams(
            dimension_semantics=("arbitrary",), vmem_limit_bytes=VMEM_LIMIT
        ),
    )(sums, squares, *weights, grads, *norms, *passed)


def norm_parts(values, gain_row, shift_row):
    average = jnp.mean(values, axis=-1, keepdims=True)
    centred = values - average
    spread_ = jnp.mean(centred * centred, axis=-1, keepdims=True)
    scaled = lax.rsqrt(spread_ + 1e-05)
    unit_rows = centred * scaled
    return (unit_rows * gain_row + shift_row, unit_rows, scaled)


def norm_back(grad_out, unit_rows, scaled, gain_row):
    inner_grad = grad_out * gain_row
    plain_mean = jnp.mean(inner_grad, axis=-1, keepdims=True)
    cross_mean = jnp.mean(inner_grad * unit_rows, axis=-1, keepdims=True)
    return scaled * (inner_grad - plain_mean - unit_rows * cross_mean)


def gain_terms(grad_out, unit_rows):
    width = grad_out.shape[-1]
    flat_grad = grad_out.reshape(-1, width)
    flat_unit = unit_rows.reshape(-1, width)
    return [jnp.sum(flat_grad * flat_unit, axis=0), jnp.sum(flat_grad, axis=0)]


def exact_gelu(values):
    return jax.nn.gelu(values, approximate=False)


def adamw_update(parameter, first_m, second_m, average, gradient, factor, decay_rate):
    clipped = gradient * factor
    new_first = 0.9 * first_m + 0.1 * clipped
    new_second = 0.999 * second_m + 0.001 * clipped * clipped
    first_hat = new_first / (1.0 - 0.9**STEP)
    second_hat = new_second / (1.0 - 0.999**STEP)
    new_param = parameter - 0.02 * (
        first_hat / (jnp.sqrt(second_hat) + 1e-08) + decay_rate * parameter
    )
    new_avg = 0.8 * average + 0.2 * new_param
    return (new_param, new_first, new_second, new_avg)


def dot32(spec, a, b):
    return jnp.einsum(spec, a, b, preferred_element_type=F32)


def general_step(n, size, media_tokens, patch_mask, latents, cotangent, weights, weights_first,
              weights_second, weights_average, norm_params, norm_first, norm_second, norm_average):
    g, patches, width = media_tokens.shape
    lat = latents.shape[1]
    blocks = weights.shape[0]
    r = width // (n * size)
    cols = width // size
    hands = HEADS // size
    scale = 1.0 / math.sqrt(width // HEADS)
    ups = FF // width
    own = g * lat
    media_gain, latent_gain, ffn_gain = 1.0 + norm_params[0], 1.0 + norm_params[2], 1.0 + norm_params[4]

    held = weights.astype(BF16).reshape(blocks, r, width)
    qs = held[:3].reshape(3, r, size, cols).transpose(2, 0, 1, 3)
    media_norm, media_unit, media_scale = norm_parts(media_tokens, media_gain, norm_params[1])
    latent_norm, latent_unit, latent_scale = norm_parts(latents, latent_gain, norm_params[3])
    cot = cotangent.reshape(own, width)
    count_rows = (g + 15) // 16 * 16
    counts = jnp.sum((patch_mask > 0).astype(F32), axis=1)
    counts = jnp.broadcast_to(jnp.pad(counts, (0, count_rows - g))[:, None], (count_rows, 128))

    wqkv, wo, up, dn, nm, nl, dy, cn = spread(
        qs, held[3], held[4 : 4 + ups], held[4 + ups :],
        media_norm.astype(BF16), latent_norm.astype(BF16), cot.astype(BF16), counts, n, size,
    )
    wqkv = wqkv.reshape(3, width, cols)
    wo = wo.reshape(width, width)
    up = up.reshape(-1, width)
    dn = dn.reshape(-1, width)
    nm = nm.reshape(g * size * patches, width)
    nl = nl.reshape(g * size * lat, width)
    dy = dy.reshape(size * own, width)
    real = jnp.sum(cn[:, :g, 0], axis=0).astype(jnp.int32)

    def by_image(a):
        return a.astype(BF16).reshape(g, -1, cols)

    q = by_image(dot32("rd,de->re", nl, wqkv[0]))
    kp, kl = by_image(dot32("rd,de->re", nm, wqkv[1])), by_image(dot32("rd,de->re", nl, wqkv[1]))
    vp, vl = by_image(dot32("rd,de->re", nm, wqkv[2])), by_image(dot32("rd,de->re", nl, wqkv[2]))
    mixed = attend(real, q, kp, kl, vp, vl, hands, scale)
    ab = to_rows(mixed.reshape(g, size, lat, cols), size, 1).reshape(own, width)

    hidden = latents.reshape(own, width) + dot32("rd,de->re", ab, wo)
    ffn_norm, ffn_unit, ffn_scale = norm_parts(hidden, ffn_gain, norm_params[5])
    nf = join_rows(ffn_norm.astype(BF16), size, 2).reshape(size * own, width)
    u = dot32("rd,fd->rf", nf, up)
    active, pull = jax.vjp(exact_gelu, u)
    gb = active.astype(BF16)
    y_part = dot32("rf,fd->rd", gb, dn).astype(BF16)
    du = pull(dot32("rd,fd->rf", dy, dn))[0].astype(BF16)
    f_part = dot32("rf,fd->rd", du, up).astype(BF16)
    g_dn = dot32("rf,rd->fd", gb, dy).astype(BF16)
    g_up = dot32("rf,rd->fd", du, nf).astype(BF16)
    both = split_rows(jnp.stack([y_part, f_part]).reshape(2, 2, 2, own, width), 3)
    latents_out = (hidden + both[0]).reshape(g, lat, width)
    d_ffn = both[1]
    ffn_terms = gain_terms(d_ffn, ffn_unit)
    d_hidden = cot + norm_back(d_ffn, ffn_unit, ffn_scale, ffn_gain)

    do = d_hidden.astype(BF16)
    g_wo = dot32("rd,re->de", ab, do).astype(BF16)
    da = dot32("re,de->rd", do, wo).astype(BF16).reshape(g, lat, width)
    da = to_heads(da, size, 4).reshape(g, size * lat, cols)
    dq, dkp, dkl, dvp, dvl = attend_back(real, q, kp, kl, vp, vl, da, hands, scale)

    def flat(a):
        return a.reshape(-1, cols)

    dq, dkp, dkl, dvp, dvl = flat(dq), flat(dkp), flat(dkl), flat(dvp), flat(dvl)
    g_qkv = jnp.stack([
        dot32("rd,re->de", nl, dq),
        dot32("rd,re->de", nm, dkp) + dot32("rd,re->de", nl, dkl),
        dot32("rd,re->de", nm, dvp) + dot32("rd,re->de", nl, dvl),
    ]).astype(BF16)
    d_nm = (dot32("re,de->rd", dkp, wqkv[1]) + dot32("re,de->rd", dvp, wqkv[2])).astype(BF16)
    d_nl = (
        dot32("re,de->rd", dkl, wqkv[1]) + dot32("re,de->rd", dvl, wqkv[2])
        + dot32("re,de->rd", dq, wqkv[0])
    ).astype(BF16)

    oq, ow, ou, od, d_media, d_latent = collect(
        g_qkv.reshape(3, n, size, r, cols), g_wo.reshape(n, 2, 2, r, width),
        g_up.reshape(ups, n, r, width), g_dn.reshape(ups, n, r, width),
        d_nm.reshape(g, 2, 2, patches, width), d_nl.reshape(g, 2, 2, lat, width), n, size,
    )
    media_grad = norm_back(d_media, media_unit, media_scale, media_gain)
    latents_grad = d_hidden.reshape(g, lat, width) + norm_back(
        d_latent, latent_unit, latent_scale, latent_gain
    )
    grads = jnp.concatenate([
        oq.transpose(1, 2, 0, 3).reshape(3, r, width), ow[None], ou, od,
    ])
    square = jnp.broadcast_to(jnp.sum(grads * grads), (width,))
    rows = jnp.stack(
        gain_terms(d_media, media_unit) + gain_terms(d_latent, latent_unit) + ffn_terms
        + [square, jnp.zeros_like(square)]
    )
    sums = total(rows, n, size)
    return latents_out, media_grad, latents_grad, grads, sums[:6], sums[6, 0]


def on_device(n, size, media_tokens, patch_mask, latents, cotangent, weights, weights_first,
              weights_second, weights_average, norm_params, norm_first, norm_second, norm_average):
    g, patches, width = media_tokens.shape
    lat = latents.shape[1]
    r = width // (n * size)
    arrays = (
        media_tokens, patch_mask, latents, cotangent, weights, weights_first, weights_second,
        weights_average, norm_params, norm_first, norm_second, norm_average,
    )
    if r % 16 or lat % 16 or size != 4:
        latents_out, media_grad, latents_grad, grads, norm_grads, square = general_step(
            n, size, *arrays
        )
    else:
        media_grad, latents_grad, latents_out, grads, sums, squares = whole_step(
            weights, media_tokens, latents, cotangent, patch_mask, norm_params,
            n, size, HEADS // size, 1.0 / math.sqrt(width // HEADS),
        )
        done = finish(
            sums, squares, (weights, weights_first, weights_second, weights_average), grads,
            (norm_params, norm_first, norm_second, norm_average),
            (latents_out.reshape(g, lat, width), media_grad, latents_grad),
        )
        return (
            *done[11:14], done[0][0, 0], done[1], done[5], *done[2:5], *done[6:11],
        )
    grad_norm = jnp.sqrt(square + jnp.sum(norm_grads * norm_grads))
    clip = jnp.minimum(1.0, 1.0 / (grad_norm + 1e-06))
    new_w, new_first, new_second, new_avg = adamw_update(
        weights, weights_first, weights_second, weights_average,
        grads.reshape(weights.shape), clip, 0.1,
    )
    new_n, new_nf, new_ns, new_na = adamw_update(
        norm_params, norm_first, norm_second, norm_average, norm_grads, clip, 0.0
    )
    return (
        latents_out, media_grad, latents_grad, grad_norm, new_w, new_w.astype(BF16), new_first,
        new_second, new_avg, new_n, new_nf, new_ns, new_na, norm_grads[4:6],
    )


def solution(mesh):
    n, size = mesh.shape["dp"], mesh.shape["patch"]
    rows, weight = P("dp", "patch", None), P(None, ("dp", "patch"))
    return jax.shard_map(
        functools.partial(on_device, n, size),
        mesh=mesh,
        in_specs=(rows, P("dp", "patch"), rows, rows) + (weight,) * 4 + (P(),) * 4,
        out_specs=(rows, rows, rows, P()) + (weight,) * 5 + (P(),) * 5,
        check_vma=False,
    )
```

```python
import functools
import math

import jax
import jax.numpy as jnp
from jax import lax
from jax.experimental import pallas as pl
from jax.experimental.pallas import tpu as pltpu
from jax.sharding import PartitionSpec as P

HEADS = 16
FF = 4096
STEP = 7
MESH = pl.DeviceIdType.MESH
F32 = jnp.float32
BF16 = jnp.bfloat16
ANY = pl.BlockSpec(memory_space=pl.ANY)
VMEM = pl.BlockSpec(memory_space=pltpu.VMEM)
DMA = pltpu.SemaphoreType.DMA
VMEM_LIMIT = 64 * 1024 * 1024 - 65536


def struct(shape, kind):
    return jax.ShapeDtypeStruct(shape, kind)


def place():
    d, p = lax.axis_index("dp"), lax.axis_index("patch")
    return d, p, lax.div(d, 2), lax.rem(d, 2), lax.div(p, 2), lax.rem(p, 2)


def remote(src, dst, send, recv, to):
    return pltpu.make_async_remote_copy(
        src_ref=src, dst_ref=dst, send_sem=send, recv_sem=recv, device_id=to, device_id_type=MESH
    )


def greet(peers):
    barrier = pltpu.get_barrier_semaphore()
    for to in peers:
        pl.semaphore_signal(barrier, inc=1, device_id=to, device_id_type=MESH)
    return functools.partial(pl.semaphore_wait, barrier, len(peers))


def meet(always, maybe=()):
    barrier = pltpu.get_barrier_semaphore()
    count = len(always)
    for to in always:
        pl.semaphore_signal(barrier, inc=1, device_id=to, device_id_type=MESH)
    for there, to in maybe:

        @pl.when(there)
        def _(to=to):
            pl.semaphore_signal(barrier, inc=1, device_id=to, device_id_type=MESH)

        count = count + there.astype(jnp.int32)
    pl.semaphore_wait(barrier, count)


def patch_peers(d, p, size):
    return [(d, lax.rem(p + k, size)) for k in range(1, size)]


def params(number):
    return pltpu.CompilerParams(
        collective_id=number, has_side_effects=True, vmem_limit_bytes=VMEM_LIMIT
    )


def spread_kernel(chain, size, qs, wos, ups, dns, nms, nls, dys, cns,
                  wqkv, wo, up, dn, nm, nl, dy, cn,
                  loc, a_s, a_r, su, sd, sy, rz, ry, xs, xr, cs, cr):
    d, p, z, y, x, c = place()
    above, below = z + 1 < chain, z > 0
    up_dev, dn_dev = ((z + 1) * 2 + y, p), ((z - 1) * 2 + y, p)
    y_dev, x_dev, c_dev = (z * 2 + 1 - y, p), (d, (1 - x) * 2 + c), (d, x * 2 + 1 - c)
    px, pc = (1 - x) * 2 + c, x * 2 + 1 - c
    pd = (1 - x) * 2 + 1 - c
    meet(patch_peers(d, p, size) + [y_dev], [(above, up_dev), (below, dn_dev)])

    own = [
        (qs.at[p], wqkv.at[:, d, p]), (wos, wo.at[d, p]), (ups, up.at[:, d]), (dns, dn.at[:, d]),
        (nms, nm.at[:, p]), (nls, nl.at[:, p]), (dys, dy.at[p]), (cns, cn.at[p]),
    ]
    local = [pltpu.make_async_copy(a, b, loc.at[i]) for i, (a, b) in enumerate(own)]
    for copy in local:
        copy.start()
    swaps = []
    for k in range(1, size):
        q = lax.rem(p + k, size)
        swaps.append(remote(qs.at[q], wqkv.at[:, d, p], a_s.at[k], a_r.at[k], (d, q)))
    for copy in swaps:
        copy.start()

    rows = [(nms, nm), (nls, nl), (cns, cn), (dys, dy)]

    def slot(j, q):
        ref = rows[j][1] if j < 4 else wo
        return ref.at[q] if j in (2, 3) else ref.at[:, q]

    def row_copies(j):
        src = rows[j][0] if j < 4 else slot(j, p)
        return (
            remote(src, slot(j, p), xs.at[j], xr.at[j], x_dev),
            remote(src, slot(j, p), cs.at[j, 0], cr.at[j, 0], c_dev),
            remote(slot(j, px), slot(j, px), cs.at[j, 1], cr.at[j, 1], c_dev),
        )

    def start_rows(j):
        to_x, to_c, _ = row_copies(j)
        to_x.start()
        to_c.start()

    def pass_rows(j):
        to_x, _, on = row_copies(j)
        to_x.wait_recv()
        on.start()

    def end_rows(j):
        to_x, to_c, on = row_copies(j)
        to_c.wait_recv()
        on.wait_recv()
        to_x.wait_send()
        to_c.wait_send()
        on.wait_send()

    for j in range(4):
        start_rows(j)

    def piece(i, dd):
        return (wqkv.at[:, dd], wo.at[dd, p], up.at[:, dd], dn.at[:, dd])[i]

    first = (wqkv.at[:, d], wos, ups, dns)

    def hop(i, zz, sends, to, own_src=False):
        src = first[i] if own_src else piece(i, zz * 2 + y)
        return remote(src, piece(i, zz * 2 + y), sends.at[i, zz], rz.at[i, zz], to)

    def over(i, zz, own_src=False):
        src = first[i] if own_src else piece(i, zz * 2 + y)
        return remote(src, piece(i, zz * 2 + y), sy.at[i, zz], ry.at[i, zz], y_dev)

    def start_own(i):
        @pl.when(above)
        def _():
            hop(i, z, su, up_dev, True).start()

        @pl.when(below)
        def _():
            hop(i, z, sd, dn_dev, True).start()

        over(i, z, True).start()

    def forward(i):
        def step(s, carry):
            @pl.when(z - s >= 0)
            def _():
                hop(i, z - s, su, up_dev).wait_recv()

                @pl.when(above)
                def _():
                    hop(i, z - s, su, up_dev).start()

                over(i, z - s).start()

            @pl.when(z + s < chain)
            def _():
                hop(i, z + s, sd, dn_dev).wait_recv()

                @pl.when(below)
                def _():
                    hop(i, z + s, sd, dn_dev).start()

                over(i, z + s).start()

            return carry

        lax.fori_loop(1, chain, step, 0)

    def arrived(i):
        def step(zz, carry):
            src = piece(i, zz * 2 + 1 - y)
            remote(src, src, sy.at[i, zz], ry.at[i, zz], y_dev).wait_recv()
            return carry

        lax.fori_loop(0, chain, step, 0)

    def sent(i):
        def step(zz, carry):
            over(i, zz).wait_send()

            @pl.when(jnp.logical_and(above, zz <= z))
            def _():
                hop(i, zz, su, up_dev).wait_send()

            @pl.when(jnp.logical_and(below, zz >= z))
            def _():
                hop(i, zz, sd, dn_dev).wait_send()

            return carry

        lax.fori_loop(0, chain, step, 0)

    local[0].wait()
    for copy in swaps:
        copy.wait_recv()
    start_own(0)
    start_own(1)
    forward(0)
    start_own(2)
    forward(1)
    start_own(3)
    local[1].wait()
    arrived(1)
    start_rows(4)
    forward(2)
    for j in range(5):
        pass_rows(j)
    forward(3)
    arrived(0)
    arrived(2)
    arrived(3)
    for j in range(5):
        end_rows(j)
    for copy in swaps:
        copy.wait_send()
    for i in range(4):
        sent(i)
    for copy in local[2:]:
        copy.wait()


def spread(qs, wos, ups, dns, nms, nls, dys, cns, n, size):
    _, three, r, cols = qs.shape
    width = wos.shape[1]
    chain = n // 2
    g, patches, _ = nms.shape
    lat = nls.shape[1]
    return pl.pallas_call(
        functools.partial(spread_kernel, chain, size),
        name="spread",
        out_shape=(
            struct((three, n, size, r, cols), BF16),
            struct((n, size, r, width), BF16),
            struct((ups.shape[0], n, r, width), BF16),
            struct((dns.shape[0], n, r, width), BF16),
            struct((g, size, patches, width), BF16),
            struct((g, size, lat, width), BF16),
            struct((size,) + dys.shape, BF16),
            struct((size,) + cns.shape, F32),
        ),
        in_specs=[VMEM] * 8,
        out_specs=(ANY,) * 8,
        scratch_shapes=[
            DMA((8,)), DMA((size,)), DMA((size,)),
            DMA((4, chain)), DMA((4, chain)), DMA((4, chain)), DMA((4, chain)), DMA((4, chain)),
            DMA((5,)), DMA((5,)), DMA((5, 2)), DMA((5, 2)),
        ],
        compiler_params=params(0),
    )(qs, wos, ups, dns, nms, nls, dys, cns)


def to_rows_kernel(size, src, out, loc, ss, rs):
    d, p = lax.axis_index("dp"), lax.axis_index("patch")
    cols = src.shape[3]
    meet(patch_peers(d, p, size))
    here = out.at[:, :, pl.ds(pl.multiple_of(p * cols, cols), cols)]
    copies = []
    for k in range(1, size):
        q = lax.rem(p + k, size)
        copies.append(remote(src.at[:, q], here, ss.at[k], rs.at[k], (d, q)))
    for copy in copies:
        copy.start()
    mine = pltpu.make_async_copy(src.at[:, p], here, loc)
    mine.start()
    mine.wait()
    for copy in copies:
        copy.wait()


def to_rows(src, size, number):
    g, _, lat, cols = src.shape
    return pl.pallas_call(
        functools.partial(to_rows_kernel, size),
        name="to_rows",
        out_shape=struct((g, lat, size * cols), src.dtype),
        in_specs=[VMEM],
        out_specs=VMEM,
        scratch_shapes=[DMA, DMA((size,)), DMA((size,))],
        compiler_params=params(number),
    )(src)


def to_heads_kernel(size, src, out, loc, ss, rs):
    d, p = lax.axis_index("dp"), lax.axis_index("patch")
    cols = out.shape[3]
    meet(patch_peers(d, p, size))

    def part(q):
        return src.at[:, :, pl.ds(pl.multiple_of(q * cols, cols), cols)]

    copies = []
    for k in range(1, size):
        q = lax.rem(p + k, size)
        copies.append(remote(part(q), out.at[:, p], ss.at[k], rs.at[k], (d, q)))
    for copy in copies:
        copy.start()
    mine = pltpu.make_async_copy(part(p), out.at[:, p], loc)
    mine.start()
    mine.wait()
    for copy in copies:
        copy.wait()


def to_heads(src, size, number):
    g, lat, width = src.shape
    return pl.pallas_call(
        functools.partial(to_heads_kernel, size),
        name="to_heads",
        out_shape=struct((g, size, lat, width // size), src.dtype),
        in_specs=[VMEM],
        out_specs=VMEM,
        scratch_shapes=[DMA, DMA((size,)), DMA((size,))],
        compiler_params=params(number),
    )(src)


def join_rows_kernel(src, out, loc, ss, rs):
    d, p, z, y, x, c = place()
    x_dev, c_dev = (d, (1 - x) * 2 + c), (d, x * 2 + 1 - c)
    px = (1 - x) * 2 + c
    meet([x_dev, c_dev])
    to_x = remote(src, out.at[p], ss.at[0], rs.at[0], x_dev)
    to_c = remote(src, out.at[p], ss.at[1], rs.at[1], c_dev)
    on = remote(out.at[px], out.at[px], ss.at[2], rs.at[2], c_dev)
    to_x.start()
    to_c.start()
    mine = pltpu.make_async_copy(src, out.at[p], loc)
    mine.start()
    to_x.wait_recv()
    on.start()
    mine.wait()
    to_c.wait()
    on.wait()
    to_x.wait_send()


def join_rows(src, size, number):
    return pl.pallas_call(
        join_rows_kernel,
        name="join_rows",
        out_shape=struct((size,) + src.shape, src.dtype),
        in_specs=[VMEM],
        out_specs=VMEM,
        scratch_shapes=[DMA, DMA((3,)), DMA((3,))],
        compiler_params=params(number),
    )(src)


def split_rows_kernel(ins, src, out, half, mid, quarter, ss, rs):
    d, p, z, y, x, c = place()
    x_dev, c_dev = (d, (1 - x) * 2 + c), (d, x * 2 + 1 - c)
    meet([x_dev, c_dev])
    first = [remote(src.at[i, :, 1 - c], half.at[i], ss.at[i], rs.at[i], c_dev) for i in range(ins)]
    for copy in first:
        copy.start()
    second = []
    for i in range(ins):
        first[i].wait_recv()
        mid[i] = (half[i, 1 - x].astype(F32) + src[i, 1 - x, c].astype(F32)).astype(BF16)
        copy = remote(mid.at[i], quarter.at[i], ss.at[ins + i], rs.at[ins + i], x_dev)
        copy.start()
        second.append(copy)
    for i in range(ins):
        out[i] = half[i, x].astype(F32) + src[i, x, c].astype(F32)
    for i in range(ins):
        second[i].wait_recv()
        out[i] = out[i] + quarter[i].astype(F32)
    for copy in first + second:
        copy.wait_send()


def split_rows(src, number):
    ins, _, _, rows, width = src.shape
    return pl.pallas_call(
        functools.partial(split_rows_kernel, ins),
        name="split_rows",
        out_shape=struct((ins, rows, width), F32),
        in_specs=[VMEM],
        out_specs=VMEM,
        scratch_shapes=[
            pltpu.VMEM((ins, 2, rows, width), BF16),
            pltpu.VMEM((ins, rows, width), BF16),
            pltpu.VMEM((ins, rows, width), BF16),
            DMA((2 * ins,)), DMA((2 * ins,)),
        ],
        compiler_params=params(number),
    )(src)


def head_rows(q, hands):
    rows, cols = q.shape
    size = cols // hands
    lane = lax.broadcasted_iota(jnp.int32, (rows, cols), 1)
    zero = jnp.zeros_like(q)
    parts = [
        jnp.where(jnp.logical_and(lane >= h * size, lane < (h + 1) * size), q, zero)
        for h in range(hands)
    ]
    return jnp.concatenate(parts, axis=0)


def own_columns(full, hands):
    rows, cols = full.shape[0] // hands, full.shape[1]
    size = cols // hands
    lane = lax.broadcasted_iota(jnp.int32, (rows, cols), 1)
    out = jnp.zeros((rows, cols), F32)
    for h in range(hands):
        keep = jnp.logical_and(lane >= h * size, lane < (h + 1) * size)
        out = jnp.where(keep, full[h * rows : (h + 1) * rows], out)
    return out


def nt(a, b):
    return lax.dot_general(a, b, (((1,), (1,)), ((), ())), preferred_element_type=F32)


def nn(a, b):
    return lax.dot_general(a, b, (((1,), (0,)), ((), ())), preferred_element_type=F32)


def tn(a, b):
    return lax.dot_general(a, b, (((0,), (0,)), ((), ())), preferred_element_type=F32)


def soft(qb, kp, kl, real, scale):
    sp = nt(qb, kp) * scale
    sl = nt(qb, kl) * scale
    key = lax.broadcasted_iota(jnp.int32, sp.shape, 1).astype(F32)
    sp = jnp.where(key < real, sp, -1e30)
    peak = jnp.maximum(jnp.max(sp, axis=1, keepdims=True), jnp.max(sl, axis=1, keepdims=True))
    ep, el = jnp.exp(sp - peak), jnp.exp(sl - peak)
    total = jnp.sum(ep, axis=1, keepdims=True) + jnp.sum(el, axis=1, keepdims=True)
    return ep / total, el / total


def attend_kernel(hands, scale, real, q, kp, kl, vp, vl, out):
    g = pl.program_id(0)
    qb = head_rows(q[0], hands)
    pp, plat = soft(qb, kp[0], kl[0], real[g].astype(F32), scale)
    full = nn(pp.astype(BF16), vp[0]) + nn(plat.astype(BF16), vl[0])
    out[0] = own_columns(full, hands).astype(BF16)


def attend(real, q, kp, kl, vp, vl, hands, scale):
    g, lat, cols = q.shape
    patches = kp.shape[1]

    def spec(rows):
        return pl.BlockSpec((1, rows, cols), lambda i, real: (i, 0, 0))

    return pl.pallas_call(
        functools.partial(attend_kernel, hands, scale),
        name="attend",
        grid_spec=pltpu.PrefetchScalarGridSpec(
            num_scalar_prefetch=1,
            grid=(g,),
            in_specs=[spec(lat), spec(patches), spec(lat), spec(patches), spec(lat)],
            out_specs=spec(lat),
        ),
        out_shape=struct((g, lat, cols), BF16),
        compiler_params=pltpu.CompilerParams(dimension_semantics=("arbitrary",)),
    )(real, q, kp, kl, vp, vl)


def attend_back_kernel(hands, scale, real, q, kp, kl, vp, vl, da, dq, dkp, dkl, dvp, dvl):
    g = pl.program_id(0)
    qb = head_rows(q[0], hands)
    dab = head_rows(da[0], hands)
    pp, plat = soft(qb, kp[0], kl[0], real[g].astype(F32), scale)
    gp, gl = nt(dab, vp[0]), nt(dab, vl[0])
    delta = jnp.sum(pp * gp, axis=1, keepdims=True) + jnp.sum(plat * gl, axis=1, keepdims=True)
    sp, sl = (pp * (gp - delta)).astype(BF16), (plat * (gl - delta)).astype(BF16)
    dvp[0] = tn(pp.astype(BF16), dab).astype(BF16)
    dvl[0] = tn(plat.astype(BF16), dab).astype(BF16)
    dkp[0] = (tn(sp, qb) * scale).astype(BF16)
    dkl[0] = (tn(sl, qb) * scale).astype(BF16)
    full = nn(sp, kp[0]) + nn(sl, kl[0])
    dq[0] = (own_columns(full, hands) * scale).astype(BF16)


def attend_back(real, q, kp, kl, vp, vl, da, hands, scale):
    g, lat, cols = q.shape
    patches = kp.shape[1]

    def spec(rows):
        return pl.BlockSpec((1, rows, cols), lambda i, real: (i, 0, 0))

    return pl.pallas_call(
        functools.partial(attend_back_kernel, hands, scale),
        name="attend_back",
        grid_spec=pltpu.PrefetchScalarGridSpec(
            num_scalar_prefetch=1,
            grid=(g,),
            in_specs=[spec(lat), spec(patches), spec(lat), spec(patches), spec(lat), spec(lat)],
            out_specs=[spec(lat), spec(patches), spec(lat), spec(patches), spec(lat)],
        ),
        out_shape=(
            struct((g, lat, cols), BF16),
            struct((g, patches, cols), BF16),
            struct((g, lat, cols), BF16),
            struct((g, patches, cols), BF16),
            struct((g, lat, cols), BF16),
        ),
        compiler_params=pltpu.CompilerParams(dimension_semantics=("arbitrary",)),
    )(real, q, kp, kl, vp, vl, da)


def collect_kernel(chain, size, gq, gw, gu, gd, kp, kl,
                   oq, ow, ou, od, okp, okl,
                   yq, yw, yu, yd, uq, uw, uu, ud, dq, dw, du, dd,
                   wc, wsum, wx, total, kc, kx, lc, lx, fin,
                   ys, yr, us, ur, ds, dr, ks, kr, qs, qr):
    d, p, z, y, x, c = place()
    above, below = z + 1 < chain, z > 0
    up_dev, dn_dev = ((z + 1) * 2 + y, p), ((z - 1) * 2 + y, p)
    y_dev, x_dev, c_dev = (z * 2 + 1 - y, p), (d, (1 - x) * 2 + c), (d, x * 2 + 1 - c)
    meet(patch_peers(d, p, size) + [y_dev], [(above, up_dev), (below, dn_dev)])

    mine = (
        lambda k: gq.at[:, k], lambda k: total.at[k], lambda k: gu.at[:, k], lambda k: gd.at[:, k]
    )
    land_y, land_u, land_d = (yq, yw, yu, yd), (uq, uw, uu, ud), (dq, dw, du, dd)

    def over(i, zz):
        return remote(
            mine[i](zz * 2 + 1 - y), land_y[i].at[zz], ys.at[i, zz], yr.at[i, zz], y_dev
        )

    def send_over(i):
        def step(zz, carry):
            over(i, zz).start()
            return carry

        lax.fori_loop(0, chain, step, 0)

    def add_over(i):
        def step(zz, carry):
            over(i, zz).wait_recv()
            have = mine[i](zz * 2 + y)
            land_y[i][zz] = (land_y[i][zz].astype(F32) + have[...].astype(F32)).astype(BF16)
            return carry

        lax.fori_loop(0, chain, step, 0)

    def rise(i, zz):
        return remote(land_y[i].at[zz], land_u[i].at[zz], us.at[i, zz], ur.at[i, zz], up_dev)

    def fall(i, zz):
        return remote(land_y[i].at[zz], land_d[i].at[zz], ds.at[i, zz], dr.at[i, zz], dn_dev)

    def gather(i, zz, land):
        land_y[i][zz] = (land_y[i][zz].astype(F32) + land[i][zz].astype(F32)).astype(BF16)

    def along(i):
        def step(k, carry):
            s = chain - k

            @pl.when(z + s < chain)
            def _():
                @pl.when(below)
                def _():
                    rise(i, z + s).wait_recv()
                    gather(i, z + s, land_u)

                rise(i, z + s).start()

            @pl.when(z - s >= 0)
            def _():
                @pl.when(above)
                def _():
                    fall(i, z - s).wait_recv()
                    gather(i, z - s, land_d)

                fall(i, z - s).start()

            return carry

        lax.fori_loop(1, chain, step, 0)

    def finish(i, write):
        write(land_y[i][z].astype(F32))

        @pl.when(below)
        def _():
            rise(i, z).wait_recv()
            write(land_u[i][z].astype(F32), True)

        @pl.when(above)
        def _():
            fall(i, z).wait_recv()
            write(land_d[i][z].astype(F32), True)

    def into(ref):
        def write(value, more=False):
            ref[...] = ref[...] + value if more else value

        return write

    def sent(i):
        def step(zz, carry):
            over(i, zz).wait_send()

            @pl.when(zz > z)
            def _():
                rise(i, zz).wait_send()

            @pl.when(zz < z)
            def _():
                fall(i, zz).wait_send()

            return carry

        lax.fori_loop(0, chain, step, 0)

    send_over(2)
    w_core = remote(gw.at[:, :, 1 - c], wc, ks.at[0], kr.at[0], c_dev)
    p_core = remote(kp.at[:, :, 1 - c], kc, ks.at[1], kr.at[1], c_dev)
    l_core = remote(kl.at[:, :, 1 - c], lc, ks.at[2], kr.at[2], c_dev)
    w_core.start()
    p_core.start()
    l_core.start()
    send_over(3)
    send_over(0)

    w_core.wait_recv()

    def w_add(k, carry):
        wsum[k] = (wc[k, 1 - x].astype(F32) + gw[k, 1 - x, c].astype(F32)).astype(BF16)
        return carry

    lax.fori_loop(0, 2 * chain, w_add, 0)
    w_x = remote(wsum, wx, ks.at[3], kr.at[3], x_dev)
    w_x.start()

    p_core.wait_recv()
    images = kp.shape[0]

    def p_add(k, carry):
        kc[k] = (kc[k].astype(F32) + kp[k, :, c].astype(F32)).astype(BF16)
        return carry

    lax.fori_loop(0, images, p_add, 0)
    p_x = remote(kc.at[:, 1 - x], kx, ks.at[4], kr.at[4], x_dev)
    p_x.start()
    l_core.wait_recv()

    def l_add(k, carry):
        lc[k] = (lc[k].astype(F32) + kl[k, :, c].astype(F32)).astype(BF16)
        return carry

    lax.fori_loop(0, images, l_add, 0)
    l_x = remote(lc.at[:, 1 - x], lx, ks.at[5], kr.at[5], x_dev)
    l_x.start()

    w_x.wait_recv()

    def w_last(k, carry):
        total[k] = (
            wc[k, x].astype(F32) + gw[k, x, c].astype(F32) + wx[k].astype(F32)
        ).astype(BF16)
        return carry

    lax.fori_loop(0, 2 * chain, w_last, 0)
    send_over(1)

    add_over(2)
    along(2)
    add_over(3)
    along(3)
    add_over(0)
    along(0)
    add_over(1)
    along(1)
    finish(2, into(ou))
    finish(3, into(od))
    finish(0, into(fin))
    swaps = []
    for k in range(1, size):
        q = lax.rem(p + k, size)
        swaps.append(remote(fin.at[:, q], oq.at[p], qs.at[k], qr.at[k], (d, q)))
    for copy in swaps:
        copy.start()
    finish(1, into(ow))
    oq[p] = fin[:, p]

    p_x.wait_recv()

    def p_last(k, carry):
        okp[k] = kc[k, x].astype(F32) + kx[k].astype(F32)
        return carry

    lax.fori_loop(0, images, p_last, 0)
    l_x.wait_recv()

    def l_last(k, carry):
        okl[k] = lc[k, x].astype(F32) + lx[k].astype(F32)
        return carry

    lax.fori_loop(0, images, l_last, 0)
    for copy in swaps:
        copy.wait()
    for i in range(4):
        sent(i)
    for copy in (w_core, p_core, l_core, w_x, p_x, l_x):
        copy.wait_send()


def collect(gq, gw, gu, gd, kp, kl, n, size):
    chain = n // 2
    three, _, _, r, cols = gq.shape
    width = gw.shape[-1]
    fu, fd = gu.shape[0], gd.shape[0]
    g, two, _, patches, _ = kp.shape
    lat = kl.shape[3]
    lands = [
        ((three, size, r, cols)), ((r, width)), ((fu, r, width)), ((fd, r, width)),
    ]
    stage = [pltpu.VMEM((chain,) + s, BF16) for s in lands]
    return pl.pallas_call(
        functools.partial(collect_kernel, chain, size),
        name="collect",
        out_shape=(
            struct((size, three, r, cols), F32),
            struct((r, width), F32),
            struct((fu, r, width), F32),
            struct((fd, r, width), F32),
            struct((g, patches, width), F32),
            struct((g, lat, width), F32),
        ),
        in_specs=[VMEM] * 6,
        out_specs=(VMEM,) * 6,
        scratch_shapes=stage * 3
        + [
            pltpu.VMEM((n, two, r, width), BF16),
            pltpu.VMEM((n, r, width), BF16),
            pltpu.VMEM((n, r, width), BF16),
            pltpu.VMEM((n, r, width), BF16),
            pltpu.VMEM((g, two, patches, width), BF16),
            pltpu.VMEM((g, patches, width), BF16),
            pltpu.VMEM((g, two, lat, width), BF16),
            pltpu.VMEM((g, lat, width), BF16),
            pltpu.VMEM((three, size, r, cols), F32),
        ]
        + [DMA((4, chain))] * 6
        + [DMA((6,)), DMA((6,)), DMA((size,)), DMA((size,))],
        compiler_params=params(6),
    )(gq, gw, gu, gd, kp, kl)


def total_kernel(hops, src, out, hold, land, ss, rs):
    d, p = lax.axis_index("dp"), lax.axis_index("patch")

    def flip(v, bit):
        return v + bit - 2 * bit * lax.rem(lax.div(v, bit), 2)

    to = [(d, flip(p, b)) if kind else (flip(d, b), p) for kind, b in hops]
    meet(to)
    sends = []
    for i, who in enumerate(to):
        copy = remote(src if i == 0 else hold.at[i], land.at[i], ss.at[i], rs.at[i], who)
        copy.start()
        copy.wait_recv()
        sends.append(copy)
        value = (src[...] if i == 0 else hold[i]) + land[i]
        if i + 1 < len(to):
            hold[i + 1] = value
        else:
            out[...] = value
    for copy in sends:
        copy.wait_send()


def total(src, n, size):
    hops = [(True, 1 << b) for b in range(size.bit_length() - 1)]
    hops += [(False, 1 << b) for b in range(n.bit_length() - 1)]
    return pl.pallas_call(
        functools.partial(total_kernel, hops),
        name="total",
        out_shape=struct(src.shape, F32),
        in_specs=[VMEM],
        out_specs=VMEM,
        scratch_shapes=[
            pltpu.VMEM((len(hops),) + src.shape, F32),
            pltpu.VMEM((len(hops),) + src.shape, F32),
            DMA((len(hops),)), DMA((len(hops),)),
        ],
        compiler_params=params(7),
    )(src)


class Names:
    def __init__(self, pairs):
        self.__dict__.update(pairs)


def aligned(start, step, count=None):
    return pl.ds(pl.multiple_of(start * step, step), count or step)


def each(lo, hi, body):
    def step(k, carry):
        body(k)
        return carry

    lax.fori_loop(lo, hi, step, 0)


def unit_of(x):
    mean = jnp.mean(x, axis=-1, keepdims=True)
    centred = x - mean
    spread_ = jnp.mean(centred * centred, axis=-1, keepdims=True)
    scaled = lax.rsqrt(spread_ + 1e-05)
    return centred * scaled, scaled


def column_sum(a):
    return jnp.sum(a, axis=0, keepdims=True)


INPUTS = ("weights", "media", "latents", "cot", "mask", "norms")
OUTPUTS = ("media_grad", "latents_grad", "latents_out", "grads", "sums", "squares")


def crowd_of(images):
    return 3 if images % 3 == 0 else 1


def buffers(n, size, g, patches, lat, width, ups, r):
    chain, cols, own = n // 2, width // size, g * lat
    keys, rows, tiles = size * (patches + lat), patches + lat, width // 256
    crowd = crowd_of(g)
    crowds = g // crowd
    low = {
        "wqkv": (3, width, cols), "wo": (width // size, width), "ud": (3, ups, n * r, width),
        "nm": (g, size * patches, width), "nl": (g, size * lat, width), "dy": (size * own, width), "doa": (g, size * lat, width),
        "q": (g, size * lat, cols), "k": (g, keys, cols), "v": (g, keys, cols),
        "mixed": (g, size * lat, cols), "nf": (size * own, width),
        "hpart": (crowds, 2, 2, crowd * lat, width), "hhalf": (crowds, 2, crowd * lat, width),
        "hmid": (crowds, crowd * lat, width), "hquart": (crowds, crowd * lat, width),
        "gb": (ups, size * own, n * r), "du": (ups, size * own, n * r),
        "part": (2, tiles, 2, 2, own, 256), "half": (2, tiles, 2, own, 256),
        "mid": (2, tiles, own, 256), "quart": (2, tiles, own, 256),
        "dah": (g, size * lat, cols), "gwo": (2, size * r, width),
        "yq": (3, chain, size * r, cols), "zq": (3, chain + 1, size * r, cols),
        "yw": (size * r, width), "zw": (2, size * r, width),
        "yf": (3, chain, ups // 2, r, width), "zf": (3, chain + 1, ups // 2, r, width),
        "zb": (2, chain + 1, ups // 4, 2 * r, width), "yb": (2, ups // 4, r, width),
        "kall": (2, 2, 2, rows, width), "kland": (g, 2, rows, width), "kx": (g, rows, width),
    }
    full = {
        "media": (g, patches, width), "latents": (g, lat, width), "cot": (g, lat, width),
        "norms": (6, width), "hidden": (own, width), "dhid": (own, width),
        "fin": (3, size * r, cols), "wfin": (size * r, width), "grads": (3 + 1 + 2 * ups, r, width), "gsum": (8, width),
        "flat": (3 + 1 + 2 * ups, r * width),
        "turn": (width // 128, (3 + 1 + 2 * ups) * r, 128),
        "cn": (size, (g + 15) // 16 * 16, size * patches),
        "nland": (size, 8, width), "nhold": (8, width), "dland": (n, 8, width),
        "sland": (size, 8, 128), "shold": (8, 128), "tland": (n, 8, 128), "sqr": (8, 128),
    }
    sems = {
        "loc": (8,), "ins": (5,), "outs": (3,), "mouts": (2,),
        "a_s": (size,), "a_r": (size,), "su": (8, chain), "sd": (8, chain), "sy": (8, chain),
        "rz": (8, chain), "ry": (8, chain), "was": (1,), "war": (size,), "ww": (5,),
        "hcs": (crowds,), "hcr": (crowds,), "hxs": (crowds,), "hxr": (crowds,),
        "nxs": (crowds,), "nxr": (crowds,), "ncs": (crowds, 2), "ncr": (crowds, 2),
        "dxs": (crowds,), "dxr": (crowds,), "dcs": (crowds, 2), "dcr": (crowds, 2),
        "ms": (crowds,), "mr": (crowds,), "mcs": (crowds, 2), "mcr": (crowds, 2),
        "xs": (3,), "xr": (3,), "cs": (3, 2), "cr": (3, 2),
        "ps": (2, tiles), "pr": (2, tiles), "qs": (2, tiles),
        "qr": (2, tiles), "gws": (3,), "gwr": (3,), "ks": (2,), "kr": (g,), "lxs": (g,), "lxr": (g,),
        "gys": (6, chain), "gyr": (6, chain), "gzs": (6, chain), "gzr": (6, chain + 1),
        "es": (size,), "er": (size,),
        "bzs": (2, chain), "bzr": (2, chain + 1), "bys": (2,), "byr": (2,),
        "fs": (3, size), "fr": (3, size),
        "n1s": (size,), "n1r": (size,), "n2s": (n,), "n2r": (n,),
        "s1s": (size,), "s1r": (size,), "s2s": (n,), "s2r": (n,),
    }
    scratch = [(k, pltpu.VMEM(s, BF16)) for k, s in low.items()]
    scratch += [(k, pltpu.VMEM(s, F32)) for k, s in full.items()]
    scratch += [("held", pltpu.VMEM((4 + 2 * ups, r, width), BF16))]
    scratch += [(k, DMA(s)) for k, s in sems.items()]
    return scratch


def step_kernel(n, size, hands, scale, names, *refs):
    chain = n // 2
    count = len(INPUTS) + len(OUTPUTS)
    into = Names(zip(INPUTS, refs[: len(INPUTS)]))
    out = Names(zip(OUTPUTS, refs[len(INPUTS) : count]))
    b = Names(zip(names, refs[count:]))
    d, p, z, y, x, c = place()
    held, media, latents, cot, norms = b.held, b.media, b.latents, b.cot, b.norms
    wqkv, wo, ud, nm, nl, dy, cn = b.wqkv, b.wo, b.ud, b.nm, b.nl, b.dy, b.cn
    q, k_, v_, mixed, hidden, nf, doa = b.q, b.k, b.v, b.mixed, b.hidden, b.nf, b.doa
    r, width = held.shape[1], held.shape[2]
    cols, ups = width // size, ud.shape[1]
    images, patches, _ = media.shape
    lat = latents.shape[1]
    own, keys, reals = images * lat, size * (patches + lat), size * patches
    tiles = width // 256
    above, below = z + 1 < chain, z > 0
    up_dev, dn_dev = ((z + 1) * 2 + y, p), ((z - 1) * 2 + y, p)
    y_dev, x_dev, c_dev = (z * 2 + 1 - y, p), (d, (1 - x) * 2 + c), (d, x * 2 + 1 - c)
    px = (1 - x) * 2 + c
    dp_peers = [(lax.rem(d + s, n), p) for s in range(1, n)]

    loads = [
        pltpu.make_async_copy(src, dst, b.ins.at[i])
        for i, (src, dst) in enumerate(
            ((into.weights, b.flat), (into.cot, cot), (into.norms, norms),
             (into.latents, latents), (into.media, media))
        )
    ]
    for copy in loads:
        copy.start()
    everyone_here = greet(patch_peers(d, p, size) + dp_peers)
    blocks = held.shape[0]
    loads[0].wait()
    for t in range(width // 128):
        for k in range(r):
            at = k * width + t * 128
            b.turn[t, pl.ds(k, blocks, stride=r), :] = b.flat[:, at : at + 128]
        held[:, :, t * 128 : (t + 1) * 128] = (
            b.turn[t].reshape(blocks, r, 128).astype(BF16)
        )
    loads[1].wait()
    dy[aligned(p, own)] = cot[...].reshape(own, width).astype(BF16)
    everyone_here()

    def lanes(k):
        return aligned(k, cols)

    half, quarter = ups // 2, ups // 4
    blocks_of = {
        3: (0, 0, half), 4: (0, half, half), 5: (1, 0, half),
        6: (1, half, quarter), 7: (1, half + quarter, quarter),
    }
    def piece(i, dd):
        if i < 3:
            return wqkv.at[i, aligned(dd, size * r)]
        return ud.at[blocks_of[i][0], pl.ds(*blocks_of[i][1:]), aligned(dd, r)]

    first = [wqkv.at[i, aligned(d, size * r)] for i in range(3)]
    for i in range(3, 8):
        plane, start, many = blocks_of[i]
        first.append(held.at[pl.ds(4 + plane * ups + start, many)])
    here = wqkv.at[:, aligned(d * size + p, r)]
    def hop(i, zz, sends, to, own_src=False):
        src = first[i] if own_src else piece(i, zz * 2 + y)
        return remote(src, piece(i, zz * 2 + y), sends.at[i, zz], b.rz.at[i, zz], to)

    def over(i, zz, own_src=False):
        src = first[i] if own_src else piece(i, zz * 2 + y)
        return remote(src, piece(i, zz * 2 + y), b.sy.at[i, zz], b.ry.at[i, zz], y_dev)

    def start_own(i):
        @pl.when(above)
        def _():
            hop(i, z, b.su, up_dev, True).start()

        @pl.when(below)
        def _():
            hop(i, z, b.sd, dn_dev, True).start()

        over(i, z, True).start()

    swaps = []
    for k in range(1, size):
        to = lax.rem(p + k, size)
        swaps.append(
            remote(held.at[pl.ds(0, 3), :, lanes(to)], here, b.a_s.at[k], b.a_r.at[k], (d, to))
        )
    for copy in swaps:
        copy.start()
    wo_near = remote(
        held.at[3], wo.at[aligned(y * size + p, r)], b.was.at[0], b.war.at[p], (d, z)
    )
    wo_own = pltpu.make_async_copy(held.at[3], wo.at[aligned(y * size + p, r)], b.loc.at[1])

    @pl.when(z != p)
    def _():
        wo_near.start()

    @pl.when(z == p)
    def _():
        wo_own.start()

    start_own(3)
    over(6, z, True).start()
    over(7, z, True).start()
    local = [pltpu.make_async_copy(held.at[pl.ds(0, 3), :, lanes(p)], here, b.loc.at[0])]
    local += [pltpu.make_async_copy(first[i], piece(i, d), b.loc.at[i]) for i in range(3, 8)]
    for copy in local:
        copy.start()

    def forward(i, s):
        @pl.when(z - s >= 0)
        def _():
            hop(i, z - s, b.su, up_dev).wait_recv()

            @pl.when(above)
            def _():
                hop(i, z - s, b.su, up_dev).start()

            over(i, z - s).start()

        @pl.when(z + s < chain)
        def _():
            hop(i, z + s, b.sd, dn_dev).wait_recv()

            @pl.when(below)
            def _():
                hop(i, z + s, b.sd, dn_dev).start()

            over(i, z + s).start()

    def pair(k, zz):
        return ud.at[1, pl.ds(half + k * quarter, quarter), aligned(zz, 2 * r)]

    def pair_hop(k, zz, sends, to):
        return remote(pair(k, zz), pair(k, zz), sends.at[6 + k, zz], b.rz.at[6 + k, zz], to)

    def pair_start():
        for k in range(2):
            src = piece(6 + k, z * 2 + 1 - y)
            local[4 + k].wait()
            remote(src, src, b.sy.at[6 + k, z], b.ry.at[6 + k, z], y_dev).wait_recv()

            @pl.when(above)
            def _():
                pair_hop(k, z, b.su, up_dev).start()

            @pl.when(below)
            def _():
                pair_hop(k, z, b.sd, dn_dev).start()

    def pair_forward(s):
        for k in range(2):

            @pl.when(z - s >= 0)
            def _():
                pair_hop(k, z - s, b.su, up_dev).wait_recv()

                @pl.when(above)
                def _():
                    pair_hop(k, z - s, b.su, up_dev).start()

            @pl.when(z + s < chain)
            def _():
                pair_hop(k, z + s, b.sd, dn_dev).wait_recv()

                @pl.when(below)
                def _():
                    pair_hop(k, z + s, b.sd, dn_dev).start()

    def pair_sent():
        for k in range(2):
            over(6 + k, z).wait_send()

            def step(zz):
                @pl.when(jnp.logical_and(above, zz <= z))
                def _():
                    pair_hop(k, zz, b.su, up_dev).wait_send()

                @pl.when(jnp.logical_and(below, zz >= z))
                def _():
                    pair_hop(k, zz, b.sd, dn_dev).wait_send()

            each(0, chain, step)

    def arrived(i):
        def step(zz):
            src = piece(i, zz * 2 + 1 - y)
            remote(src, src, b.sy.at[i, zz], b.ry.at[i, zz], y_dev).wait_recv()

        each(0, chain, step)

    def sent(i):
        def step(zz):
            over(i, zz).wait_send()

            @pl.when(jnp.logical_and(above, zz <= z))
            def _():
                hop(i, zz, b.su, up_dev).wait_send()

            @pl.when(jnp.logical_and(below, zz >= z))
            def _():
                hop(i, zz, b.sd, dn_dev).wait_send()

        each(0, chain, step)

    class Rows:
        def __init__(self, slot, xs, xr, cs, cr, at, src=None):
            src = slot(p) if src is None else src
            self.to_x = remote(src, slot(p), xs.at[at], xr.at[at], x_dev)
            self.to_c = remote(src, slot(p), cs.at[at, 0], cr.at[at, 0], c_dev)
            self.on = remote(slot(px), slot(px), cs.at[at, 1], cr.at[at, 1], c_dev)

        def start(self):
            self.to_x.start()
            self.to_c.start()

        def forward(self):
            self.to_x.wait_recv()
            self.on.start()

        def have(self):
            self.to_c.wait_recv()
            self.on.wait_recv()

        def end(self):
            self.to_x.wait_send()
            self.to_c.wait_send()
            self.on.wait_send()

    def group(slot, j, src=None):
        return Rows(slot, b.xs, b.xr, b.cs, b.cr, j, src)

    lat_rows = group(lambda k: nl.at[:, aligned(k, lat)], 0)
    cn_rows = group(lambda k: cn.at[k], 1)
    dy_rows = group(lambda k: dy.at[aligned(k, own)], 2)

    def wo_block(k):
        return wo.at[aligned(k, size * r)]

    def wo_hop(e, to, k):
        return remote(wo_block(k), wo_block(k), b.ww.at[e], b.ww.at[3 + e // 2], to)

    def wo_pass(first_end, second_end):
        @pl.when(first_end)
        def _():
            wo_hop(0, up_dev, y).start()

        @pl.when(second_end)
        def _():
            wo_hop(1, dn_dev, y).start()

        wo_hop(2, y_dev, y).start()

    def wo_source():
        @pl.when(z == p)
        def _():
            for k in range(1, size):
                who = lax.rem(p + k, size)
                part = wo.at[aligned(y * size + who, r)]
                remote(part, part, b.was.at[0], b.war.at[who], (d, who)).wait_recv()
            wo_own.wait()
            wo_pass(above, below)

    def wo_rest():
        @pl.when(z > p)
        def _():
            wo_hop(0, up_dev, y).wait_recv()
            wo_pass(above, z < 0)

        @pl.when(z < p)
        def _():
            wo_hop(0, dn_dev, y).wait_recv()
            wo_pass(z < 0, below)

    def wo_have():
        wo_hop(2, y_dev, 1 - y).wait_recv()

    def wo_sent():
        @pl.when(jnp.logical_and(z >= p, above))
        def _():
            wo_hop(0, up_dev, y).wait_send()

        @pl.when(jnp.logical_and(z <= p, below))
        def _():
            wo_hop(1, dn_dev, y).wait_send()

        wo_hop(2, y_dev, y).wait_send()

        @pl.when(z != p)
        def _():
            wo_near.wait_send()

    crowd = crowd_of(images)
    crowds = images // crowd

    def media_rows(j):
        return Rows(
            lambda k: nm.at[aligned(j, crowd), aligned(k, patches)],
            b.ms, b.mr, b.mcs, b.mcr, j,
        )

    fold = crowd * lat

    def nf_rows(j):
        return Rows(
            lambda k: nf.at[pl.ds(pl.multiple_of(k * own + j * fold, fold), fold)],
            b.nxs, b.nxr, b.ncs, b.ncr, j,
        )

    def do_rows(j):
        return Rows(
            lambda k: doa.at[aligned(j, crowd), aligned(k, lat)],
            b.dxs, b.dxr, b.dcs, b.dcr, j,
        )

    loads[2].wait()
    loads[3].wait()
    media_gain, media_shift = 1.0 + norms[0:1, :], norms[1:2, :]
    latent_gain, latent_shift = 1.0 + norms[2:3, :], norms[3:4, :]
    ffn_gain, ffn_shift = 1.0 + norms[4:5, :], norms[5:6, :]

    def latent_norm(g):
        unit, _ = unit_of(latents[g])
        nl[g, aligned(p, lat)] = (unit * latent_gain + latent_shift).astype(BF16)

    def media_norm(g):
        unit, _ = unit_of(media[g])
        nm[g, aligned(p, patches)] = (unit * media_gain + media_shift).astype(BF16)

    dy_rows.start()
    cn[p] = jnp.zeros(cn.shape[1:], F32)
    counts = column_of((into.mask[...] > 0).astype(F32))
    cn[p, :images, :] = jnp.broadcast_to(counts, (images, cn.shape[2]))
    each(0, images, latent_norm)
    cn_rows.start()
    lat_rows.start()
    local[0].wait()
    for copy in swaps:
        copy.wait_recv()
    for i in range(3):
        start_own(i)
    loads[4].wait()
    each(0, images, media_norm)
    each(0, crowds, lambda j: media_rows(j).start())
    wo_source()
    for s in range(1, chain):
        for i in range(3):
            forward(i, s)
        if s == 1:
            start_own(4)
            dy_rows.forward()
            cn_rows.forward()
    lat_rows.forward()
    wo_rest()
    start_own(5)
    for s in range(1, chain - 1):
        forward(3, s)
    pair_start()
    for i in range(3):
        arrived(i)
    lat_rows.have()
    cn_rows.have()

    flat_nl = nl[...].reshape(images * size * lat, width)
    q[...] = nn(flat_nl, wqkv[0]).astype(BF16).reshape(images, size * lat, cols)
    k_[:, reals:] = nn(flat_nl, wqkv[1]).astype(BF16).reshape(images, size * lat, cols)
    v_[:, reals:] = nn(flat_nl, wqkv[2]).astype(BF16).reshape(images, size * lat, cols)

    def real_keys(g):
        real = cn[0, pl.ds(g, 1), :]
        for k in range(1, size):
            real = real + cn[k, pl.ds(g, 1), :]
        return real

    def image(g):
        k_[g, :reals] = nn(nm[g], wqkv[1]).astype(BF16)
        v_[g, :reals] = nn(nm[g], wqkv[2]).astype(BF16)
        pp, plat = soft(
            head_rows(q[g], hands), k_[g, :reals], k_[g, reals:], real_keys(g), scale
        )
        full = nn(pp.astype(BF16), v_[g, :reals]) + nn(plat.astype(BF16), v_[g, reals:])
        mixed[g] = own_columns(full, hands).astype(BF16)

    def hid_core(j):
        return remote(b.hpart.at[j, :, 1 - c], b.hhalf.at[j], b.hcs.at[j], b.hcr.at[j], c_dev)

    def hid_x(j):
        return remote(b.hmid.at[j], b.hquart.at[j], b.hxs.at[j], b.hxr.at[j], x_dev)

    def hid_part(j):
        rows = mixed[j * crowd : (j + 1) * crowd].reshape(crowd * size * lat, cols)
        for t in range(tiles):
            span = pl.ds(256 * t, 256)
            value = nn(rows, wo[:, span]).astype(BF16)
            for i in range(crowd):
                for e in range(size):
                    at = (i * size + e) * lat
                    b.hpart[j, e // 2, e % 2, i * lat : (i + 1) * lat, span] = value[at : at + lat]
        hid_core(j).start()

    def hid_pass(j):
        hid_core(j).wait_recv()
        b.hmid[j] = (b.hhalf[j, 1 - x].astype(F32) + b.hpart[j, 1 - x, c].astype(F32)).astype(BF16)
        hid_x(j).start()

    def hid_end(j):
        hid_x(j).wait_recv()
        value = (
            latents[j * crowd : (j + 1) * crowd].reshape(fold, width)
            + b.hhalf[j, x].astype(F32) + b.hpart[j, x, c].astype(F32) + b.hquart[j].astype(F32)
        )
        hidden[j * fold : (j + 1) * fold] = value
        unit, _ = unit_of(value)
        nf[pl.ds(pl.multiple_of(p * own + j * fold, fold), fold)] = (
            unit * ffn_gain + ffn_shift
        ).astype(BF16)
        nf_rows(j).start()

    pending = [(3, chain - 1)] + [(i, s) for i in (4, 5) for s in range(1, chain)]

    def forward_some(count):
        for _ in range(count):
            if pending:
                forward(*pending.pop(0))

    for j in range(crowds):
        media_rows(j).forward()
        if j:
            forward_some(1)
        media_rows(j).have()
        each(j * crowd, (j + 1) * crowd, image)
        if j == 0:
            wo_have()
        hid_part(j)
        if j > 0:
            hid_end(j - 1)
        forward_some(1)
        hid_pass(j)
        forward_some(1)
    forward_some(len(pending))
    for j in range(crowds - 1):
        nf_rows(j).forward()
    hid_end(crowds - 1)
    for s in range(1, chain - 1):
        pair_forward(s)
    dy_rows.have()
    for i in (3, 4, 5):
        arrived(i)
    for copy in local[1:4]:
        copy.wait()
    nf_rows(crowds - 1).forward()
    for j in range(crowds):
        nf_rows(j).have()

    def hidden_block(e):
        u = nt(nf[...], ud[0, e])
        into_active = nt(dy[...], ud[1, e])
        chance = 0.5 * (1.0 + lax.erf(u * math.sqrt(0.5)))
        slope = chance + u * jnp.exp(-0.5 * u * u) * (1.0 / math.sqrt(2.0 * math.pi))
        b.gb[e] = (u * chance).astype(BF16)
        b.du[e] = (into_active * slope).astype(BF16)

    def down_grad(e):
        for t in range(0, width, 512):
            ud[2, e, :, t : t + 512] = tn(b.gb[e], dy[:, t : t + 512]).astype(BF16)

    def up_grad(e):
        for t in range(0, width, 512):
            ud[0, e, :, t : t + 512] = tn(b.du[e], nf[:, t : t + 512]).astype(BF16)

    def part_core(i, t):
        return remote(
            b.part.at[i, t, :, 1 - c], b.half.at[i, t], b.ps.at[i, t], b.pr.at[i, t], c_dev
        )

    def part_x(i, t):
        return remote(b.mid.at[i, t], b.quart.at[i, t], b.qs.at[i, t], b.qr.at[i, t], x_dev)

    def part_of(i, acts):
        def tile(t):
            span = aligned(t, 256)
            acc = nn(acts[0], ud[i, 0, :, span])
            for e in range(1, ups):
                acc = acc + nn(acts[e], ud[i, e, :, span])
            b.part[i, t] = acc.astype(BF16).reshape(2, 2, own, 256)
            part_core(i, t).start()

        each(0, tiles, tile)

    def part_pass(i):
        def tile(t):
            part_core(i, t).wait_recv()
            b.mid[i, t] = (
                b.half[i, t, 1 - x].astype(F32) + b.part[i, t, 1 - x, c].astype(F32)
            ).astype(BF16)
            part_x(i, t).start()

        each(0, tiles, tile)

    def part_end(i, write):
        def tile(t):
            part_x(i, t).wait_recv()
            write(
                aligned(t, 256),
                b.half[i, t, x].astype(F32) + b.part[i, t, x, c].astype(F32)
                + b.quart[i, t].astype(F32),
            )

        each(0, tiles, tile)

    def parts_sent(i):
        def tile(t):
            part_core(i, t).wait_send()
            part_x(i, t).wait_send()

        each(0, tiles, tile)

    def ffn_part(i, k):
        plane, start = (2 if i == 3 else 0), half * (i == 5)
        return ud.at[plane, pl.ds(start, half), aligned(k, r)]

    class Staged:
        def stage(self, k):
            @pl.when(z == k)
            def _():
                each(0, chain - 1 - k, lambda t: self.move(
                    chain - 1 - t, k > 0, chain - t, up_dev
                ))

            @pl.when(chain - 1 - z == k)
            def _():
                each(0, chain - 1 - k, lambda t: self.move(t, k > 0, t, dn_dev))

    class Sum(Staged):
        def __init__(self, i, kind):
            self.i = i
            if kind == 0:
                self.mine = lambda k: wqkv.at[i, aligned(k, size * r)]
                self.ly, self.lz = b.yq.at[i], b.zq.at[i]
            else:
                self.mine = lambda k: ffn_part(i, k)
                self.ly, self.lz = b.yf.at[i - 3], b.zf.at[i - 3]

        def over(self, zt):
            return remote(
                self.mine(zt * 2 + 1 - y), self.ly.at[zt], b.gys.at[self.i, zt],
                b.gyr.at[self.i, zt], y_dev,
            )

        def along(self, zt, slot, to):
            return remote(
                self.ly.at[zt], self.lz.at[slot], b.gzs.at[self.i, zt], b.gzr.at[self.i, slot], to
            )

        def send(self):
            def step(k):
                s = chain - 1 - k

                @pl.when(z + s < chain)
                def _():
                    self.over(z + s).start()

                @pl.when(jnp.logical_and(z - s >= 0, s > 0))
                def _():
                    self.over(z - s).start()

            each(0, chain, step)

        def pair(self, zt):
            return self.ly[zt].astype(F32) + self.mine(zt * 2 + y)[...].astype(F32)

        def move(self, zt, more, slot, to):
            self.over(zt).wait_recv()
            if more:
                self.along(zt, slot, to).wait_recv()
                self.ly[zt] = (self.pair(zt) + self.lz[slot].astype(F32)).astype(BF16)
            else:
                self.ly[zt] = self.pair(zt).astype(BF16)
            self.along(zt, slot, to).start()

        def last(self, dst):
            self.over(z).wait_recv()
            dst[...] = self.pair(z)

            @pl.when(below)
            def _():
                self.along(z, z + 1, up_dev).wait_recv()
                dst[...] = dst[...] + self.lz[z + 1].astype(F32)

            @pl.when(above)
            def _():
                self.along(z, z, dn_dev).wait_recv()
                dst[...] = dst[...] + self.lz[z].astype(F32)

        def sent(self):
            def step(zt):
                self.over(zt).wait_send()

                @pl.when(zt != z)
                def _():
                    self.along(zt, 0, up_dev).wait_send()

            each(0, chain, step)

    class Cross(Staged):
        def __init__(self, k):
            self.k, self.blocks = k, pl.ds(half + k * quarter, quarter)
            self.lz, self.ly = b.zb.at[k], b.yb.at[k]

        def pair(self, zt):
            return ud.at[2, self.blocks, aligned(zt, 2 * r)]

        def along(self, zt, slot, to):
            return remote(
                self.pair(zt), self.lz.at[slot], b.bzs.at[self.k, zt], b.bzr.at[self.k, slot], to
            )

        def move(self, zt, more, slot, to):
            if more:
                self.along(zt, slot, to).wait_recv()
                self.pair(zt)[...] = (
                    self.pair(zt)[...].astype(F32) + self.lz[slot].astype(F32)
                ).astype(BF16)
            self.along(zt, slot, to).start()

        def over(self):
            src = ud.at[2, self.blocks, aligned(z * 2 + 1 - y, r)]
            return remote(src, self.ly, b.bys.at[self.k], b.byr.at[self.k], y_dev)

        def meet(self, dst):
            theirs, ours = aligned(1 - y, r), aligned(y, r)
            far = ud.at[2, self.blocks, aligned(z * 2 + 1 - y, r)]
            near = ud.at[2, self.blocks, aligned(z * 2 + y, r)]
            dst[...] = near[...].astype(F32)

            def add(slot):
                dst[...] = dst[...] + self.lz[slot, :, ours].astype(F32)
                far[...] = (
                    far[...].astype(F32) + self.lz[slot, :, theirs].astype(F32)
                ).astype(BF16)

            @pl.when(below)
            def _():
                self.along(z, z + 1, up_dev).wait_recv()
                add(z + 1)

            @pl.when(above)
            def _():
                self.along(z, z, dn_dev).wait_recv()
                add(z)

            self.over().start()

        def last(self, dst):
            self.over().wait_recv()
            dst[...] = dst[...] + self.ly[...].astype(F32)

        def sent(self):
            self.over().wait_send()

            def step(zt):
                @pl.when(zt != z)
                def _():
                    self.along(zt, 0, up_dev).wait_send()

            each(0, chain, step)

    class Gather:
        def over(self):
            return remote(b.gwo.at[1 - y], b.yw, b.gws.at[0], b.gwr.at[0], y_dev)

        def rise(self):
            return remote(b.gwo.at[y], b.zw.at[0], b.gws.at[1], b.gwr.at[1], up_dev)

        def fall(self):
            return remote(b.gwo.at[y], b.zw.at[1], b.gws.at[2], b.gwr.at[2], dn_dev)

        def send(self):
            self.over().start()

        def add(self, k):
            b.gwo[y] = (b.gwo[y].astype(F32) + b.zw[k].astype(F32)).astype(BF16)

        def step(self, k):
            @pl.when(jnp.logical_or(
                jnp.logical_and(z < p, z == k), jnp.logical_and(z > p, chain - 1 - z == k)
            ))
            def _():
                self.over().wait_recv()
                b.gwo[y] = (b.gwo[y].astype(F32) + b.yw[...].astype(F32)).astype(BF16)

                @pl.when(z < p)
                def _():
                    if k:
                        self.rise().wait_recv()
                        self.add(0)
                    self.rise().start()

                @pl.when(z > p)
                def _():
                    if k:
                        self.fall().wait_recv()
                        self.add(1)
                    self.fall().start()

        def part(self, k, to):
            return remote(
                b.wfin.at[aligned(k, r)], b.grads.at[3], b.es.at[k], b.er.at[0], to
            )

        def last(self):
            @pl.when(z == p)
            def _():
                self.over().wait_recv()
                b.wfin[...] = b.gwo[y].astype(F32) + b.yw[...].astype(F32)

                @pl.when(below)
                def _():
                    self.rise().wait_recv()
                    b.wfin[...] = b.wfin[...] + b.zw[0].astype(F32)

                @pl.when(above)
                def _():
                    self.fall().wait_recv()
                    b.wfin[...] = b.wfin[...] + b.zw[1].astype(F32)

                for k in range(1, size):
                    to = lax.rem(p + k, size)
                    self.part(to, (d, to)).start()
                b.grads[3] = b.wfin[aligned(p, r)]

        def have(self):
            @pl.when(z != p)
            def _():
                self.part(0, (d, z)).wait_recv()

        def sent(self):
            self.over().wait_send()

            @pl.when(z < p)
            def _():
                self.rise().wait_send()

            @pl.when(z > p)
            def _():
                self.fall().wait_send()

            @pl.when(z == p)
            def _():
                for k in range(1, size):
                    to = lax.rem(p + k, size)
                    self.part(to, (d, to)).wait_send()

    crosses = [Cross(0), Cross(1)]

    qkv_sums, wo_sum = [Sum(i, 0) for i in range(3)], Gather()

    ffn_sums = {i: Sum(i, 2) for i in (3, 4, 5)}

    each(0, half, hidden_block)
    each(0, half, down_grad)
    ffn_sums[3].send()
    pair_forward(chain - 1)
    each(half, ups, hidden_block)
    part_of(0, b.du)
    each(half, ups, down_grad)
    for item in crosses:
        item.stage(0)
    part_pass(0)
    for i in range(6):
        sent(i)
    pair_sent()
    wo_sent()
    each(0, ups, up_grad)
    ffn_sums[4].send()
    ffn_sums[5].send()
    part_of(1, b.gb)

    def write_dhid(span, value):
        b.dhid[:, span] = value

    part_end(0, write_dhid)
    dn = b.dhid[...]
    unit, scaled = unit_of(hidden[...])
    b.gsum[...] = jnp.zeros_like(b.gsum)
    b.gsum[4:5, :] = column_sum(dn * unit)
    b.gsum[5:6, :] = column_sum(dn)
    b.dhid[...] = cot[...].reshape(own, width) + norm_back(dn, unit, scaled, ffn_gain)
    for j in range(crowds):
        doa[j * crowd : (j + 1) * crowd, aligned(p, lat)] = (
            b.dhid[j * fold : (j + 1) * fold].astype(BF16).reshape(crowd, lat, width)
        )
        do_rows(j).start()
    def stages(*pairs):
        for item, k in pairs:
            if k < chain - 1:
                item.stage(k)

    def head_grads(j):
        do_rows(j).have()
        rows = doa[j * crowd : (j + 1) * crowd].reshape(crowd * size * lat, width)
        b.dah[j * crowd : (j + 1) * crowd] = (
            nt(rows, wo[...]).astype(BF16).reshape(crowd, size * lat, cols)
        )

    def out_grad():
        for t in range(tiles):
            span = pl.ds(256 * t, 256)
            b.gwo[:, :, span] = tn(
                mixed[...].reshape(images * size * lat, cols),
                doa[:, :, span].reshape(images * size * lat, 256),
            ).astype(BF16).reshape(2, size * r, 256)

    def kin_core(g):
        return remote(
            b.kall.at[lax.rem(g, 2), 1 - c], b.kland.at[g], b.ks.at[lax.rem(g, 2)], b.kr.at[g], c_dev
        )

    def kin_x(g):
        return remote(b.kland.at[g, 1 - x], b.kx.at[g], b.lxs.at[g], b.lxr.at[g], x_dev)

    def image_back(g):
        slot = lax.rem(g, 2)
        qb, dab = head_rows(q[g], hands), head_rows(b.dah[g], hands)
        kp, kl, vp, vl = k_[g, :reals], k_[g, reals:], v_[g, :reals], v_[g, reals:]
        pp, plat = soft(qb, kp, kl, real_keys(g), scale)
        gp, gl = nt(dab, vp), nt(dab, vl)
        delta = column_of(pp * gp) + column_of(plat * gl)
        sp, sl = (pp * (gp - delta)).astype(BF16), (plat * (gl - delta)).astype(BF16)
        v_[g, :reals] = tn(pp.astype(BF16), dab).astype(BF16)
        v_[g, reals:] = tn(plat.astype(BF16), dab).astype(BF16)
        k_[g, :reals] = (tn(sp, qb) * scale).astype(BF16)
        k_[g, reals:] = (tn(sl, qb) * scale).astype(BF16)
        q[g] = (own_columns(nn(sp, kp) + nn(sl, kl), hands) * scale).astype(BF16)
        for t in range(tiles):
            span = pl.ds(256 * t, 256)
            rows = nt(k_[g], wqkv[1, span, :]) + nt(v_[g], wqkv[2, span, :])
            tail = rows[reals:] + nt(q[g], wqkv[0, span, :])
            for e in range(size):
                b.kall[slot, e % 2, e // 2, :patches, span] = (
                    rows[e * patches : (e + 1) * patches].astype(BF16)
                )
                b.kall[slot, e % 2, e // 2, patches:, span] = (
                    tail[e * lat : (e + 1) * lat].astype(BF16)
                )
        kin_core(g).start()

    def kin_mid(g):
        kin_core(g).wait_recv()
        b.kland[g] = (
            b.kland[g].astype(F32) + b.kall[lax.rem(g, 2), c].astype(F32)
        ).astype(BF16)
        kin_x(g).start()

    def media_out(g):
        return pltpu.make_async_copy(media.at[g], out.media_grad.at[g], b.mouts.at[lax.rem(g, 2)])

    def kin_last(g):
        kin_x(g).wait_recv()
        total_ = b.kland[g, x].astype(F32) + b.kx[g].astype(F32)
        grad = total_[:patches]
        unit, scaled = unit_of(media[g])
        b.gsum[0:1, :] = b.gsum[0:1, :] + column_sum(grad * unit)
        b.gsum[1:2, :] = b.gsum[1:2, :] + column_sum(grad)
        media[g] = norm_back(grad, unit, scaled, media_gain)

        @pl.when(g >= 2)
        def _():
            media_out(g - 2).wait()

        media_out(g).start()
        grad = total_[patches:]
        unit, scaled = unit_of(latents[g])
        b.gsum[2:3, :] = b.gsum[2:3, :] + column_sum(grad * unit)
        b.gsum[3:4, :] = b.gsum[3:4, :] + column_sum(grad)
        latents[g] = b.dhid[aligned(g, lat)] + norm_back(grad, unit, scaled, latent_gain)

    def back(g):
        @pl.when(g >= 2)
        def _():
            kin_core(g - 2).wait_send()

        image_back(g)

        @pl.when(g >= 1)
        def _():
            kin_mid(g - 1)

    down, first_up, last_up = (ffn_sums[i] for i in (3, 4, 5))
    between = [
        [(crosses[1], 1), (first_up, 0)],
        [(crosses[0], 2), (crosses[1], 2), (down, 1)],
        [(last_up, 0)],
    ]
    stages((down, 0), (crosses[0], 1))
    do_rows(0).forward()
    for j in range(crowds):
        head_grads(j)
        if j + 1 < crowds:
            do_rows(j + 1).forward()
        else:
            out_grad()
            wo_sum.send()
        each(j * crowd, (j + 1) * crowd, back)
        if between:
            stages(*between.pop(0))
    kin_mid(images - 1)
    for pairs in between:
        stages(*pairs)
    for k in range(3, chain - 1):
        stages((crosses[0], k), (crosses[1], k))
    wo_sum.step(0)
    cross_rows = [
        b.grads.at[pl.ds(4 + ups + half + k * quarter, quarter)] for k in range(2)
    ]

    def flat(a, n_rows):
        return a.reshape(images * n_rows, cols)

    def qkv_grad(j):
        def tile(t):
            span = aligned(t, 256)
            rows_l = nl[:, :, span].reshape(images * size * lat, 256)
            if j == 0:
                wqkv[0, span, :] = tn(rows_l, flat(q[...], size * lat)).astype(BF16)
                return
            rows_m = nm[:, :, span].reshape(images * reals, 256)
            ref = (k_, v_)[j - 1]
            wqkv[j, span, :] = (
                tn(rows_m, flat(ref[:, :reals], reals))
                + tn(rows_l, flat(ref[:, reals:], size * lat))
            ).astype(BF16)

        each(0, tiles, tile)
        qkv_sums[j].send()

    for item, rows in zip(crosses, cross_rows):
        item.meet(rows)
    qkv_grad(0)
    qkv_grad(2)
    qkv_grad(1)
    part_pass(1)
    waiting = [(0, (images + 2) // 3)]
    waiting += [(waiting[0][1], 2 * waiting[0][1]), (2 * waiting[0][1], images)]

    def last_keys():
        if waiting:
            each(*waiting.pop(0), kin_last)

    q_sum, k_sum, v_sum = qkv_sums
    stages((first_up, 1), (q_sum, 0), (down, 2))
    wo_sum.step(1)
    last_keys()
    stages((v_sum, 0), (last_up, 1), (first_up, 2))
    last_keys()
    stages((k_sum, 0), (q_sum, 1))
    wo_sum.step(2)
    stages((last_up, 2), (v_sum, 1), (k_sum, 1))
    last_keys()
    for k in range(2, chain - 1):
        stages((q_sum, k), (v_sum, k), (k_sum, k))
        if k > 2:
            stages((down, k), (first_up, k), (last_up, k))
            wo_sum.step(k)
    down.last(b.grads.at[pl.ds(4 + ups, half)])
    first_up.last(b.grads.at[pl.ds(4, half)])
    last_up.last(b.grads.at[pl.ds(4 + half, half)])
    for span in waiting:
        each(*span, kin_last)
    for item, rows in zip(crosses, cross_rows):
        item.last(rows)
    lat_copy = pltpu.make_async_copy(latents, out.latents_grad, b.outs.at[1])
    lat_copy.start()

    def write_out(span, value):
        hidden[:, span] = hidden[:, span] + value

    part_end(1, write_out)
    out_copy = pltpu.make_async_copy(hidden, out.latents_out, b.outs.at[0])
    out_copy.start()

    def share(src, land, hold, s1, r1, total_to, land2, s2, r2):
        land[p] = src[...]
        near = []
        for k in range(1, size):
            to = lax.rem(p + k, size)
            near.append(remote(src, land.at[p], s1.at[to], r1.at[p], (d, to)))
        for copy in near:
            copy.start()
        for k in range(1, size):
            who = lax.rem(p + k, size)
            remote(src, land.at[who], s1.at[who], r1.at[who], (d, who)).wait_recv()
        value = land[0]
        for k in range(1, size):
            value = value + land[k]
        hold[...] = value
        land2[d] = value
        far = []
        for k in range(1, n):
            to = lax.rem(d + k, n)
            far.append(remote(hold, land2.at[d], s2.at[to], r2.at[d], (to, p)))
        for copy in far:
            copy.start()

        def finish():
            for k in range(1, n):
                who = lax.rem(d + k, n)
                remote(hold, land2.at[who], s2.at[who], r2.at[who], (who, p)).wait_recv()
            value = land2[0]
            for k in range(1, n):
                value = value + land2[k]
            total_to[...] = value
            for copy in near + far:
                copy.wait_send()

        return finish

    norms_done = share(b.gsum, b.nland, b.nhold, b.n1s, b.n1r, out.sums, b.dland, b.n2s, b.n2r)
    ends = []
    for j in (0, 2, 1):
        qkv_sums[j].last(b.fin.at[j])
        for k in range(1, size):
            to = lax.rem(p + k, size)
            copy = remote(
                b.fin.at[j, aligned(to, r)], b.grads.at[j, :, lanes(p)],
                b.fs.at[j, k], b.fr.at[j, k], (d, to),
            )
            copy.start()
            ends.append(copy)
        b.grads[j, :, lanes(p)] = b.fin[j, aligned(p, r)]
    wo_sum.last()
    squares = jnp.zeros((8, 128), F32)

    def squares_of(i, squares):
        for t in range(0, width, 128):
            tile = b.grads[i, :, t : t + 128]
            squares = squares + jnp.sum((tile * tile).reshape(r // 8, 8, 128), axis=0)
        return squares

    for i in range(4, 4 + 2 * ups):
        squares = squares_of(i, squares)
    wo_sum.have()
    for copy in ends:
        copy.wait_recv()
    for t in range(width // 128):
        b.turn[t] = b.grads[:, :, t * 128 : (t + 1) * 128].reshape(blocks * r, 128)
        for k in range(r):
            at = k * width + t * 128
            b.flat[:, at : at + 128] = b.turn[t, pl.ds(k, blocks, stride=r), :]
    grads_copy = pltpu.make_async_copy(b.flat, out.grads, b.outs.at[2])
    grads_copy.start()
    for i in range(4):
        squares = squares_of(i, squares)
    b.sqr[...] = squares
    squares_done = share(
        b.sqr, b.sland, b.shold, b.s1s, b.s1r, out.squares, b.tland, b.s2s, b.s2r
    )
    norms_done()
    for copy in swaps + ends:
        copy.wait_send()
    for rows in (lat_rows, cn_rows, dy_rows):
        rows.end()
    for j in range(crowds):
        media_rows(j).end()
        nf_rows(j).end()
        do_rows(j).end()
        hid_core(j).wait_send()
        hid_x(j).wait_send()
    parts_sent(0)
    parts_sent(1)
    each(max(images - 2, 0), images, lambda g: kin_core(g).wait_send())
    each(0, images, lambda g: kin_x(g).wait_send())
    for item in qkv_sums:
        item.sent()
    wo_sum.sent()
    for item in ffn_sums.values():
        item.sent()
    for item in crosses:
        item.sent()
    each(max(images - 2, 0), images, lambda g: media_out(g).wait())
    out_copy.wait()
    lat_copy.wait()
    grads_copy.wait()
    squares_done()


def column_of(a):
    return jnp.sum(a, axis=1, keepdims=True)


def whole_step(weights, media, latents, cot, mask, norms, n, size, hands, scale):
    g, patches, width = media.shape
    blocks, r = weights.shape[0], weights.shape[1] // width
    lat = latents.shape[1]
    scratch = buffers(n, size, g, patches, lat, width, FF // width, r)
    return pl.pallas_call(
        functools.partial(step_kernel, n, size, hands, scale, [k for k, _ in scratch]),
        name="whole_step",
        out_shape=(
            struct((g, patches, width), F32),
            struct((g, lat, width), F32),
            struct((g * lat, width), F32),
            struct(weights.shape, F32),
            struct((8, width), F32),
            struct((8, 128), F32),
        ),
        in_specs=[ANY] * 4 + [VMEM] + [ANY],
        out_specs=(ANY,) * 4 + (VMEM,) * 2,
        scratch_shapes=[s for _, s in scratch],
        compiler_params=params(8),
    )(weights, media, latents, cot, mask, norms)


def finish_kernel(sums, squares, *refs):
    weights, grads, norms = refs[:4], refs[4], refs[5:9]
    passed, outs = refs[9:12], refs[12:]
    grad_norm, new_weights, new_low, new_norms, ffn, passed_out = (
        outs[0], outs[1:5], outs[5], outs[6:10], outs[10], outs[11:14]
    )
    norm_grads = sums[:6, :]
    square = jnp.sum(squares[...], axis=0, keepdims=True)
    square = jnp.sum(square, axis=1, keepdims=True)
    rest = jnp.sum(norm_grads * norm_grads, axis=0, keepdims=True)
    length = jnp.sqrt(square + jnp.sum(rest, axis=1, keepdims=True))
    clip = jnp.minimum(1.0, 1.0 / (length + 1e-06))
    new = adamw_update(*(ref[...] for ref in weights), grads[...], clip, 0.1)
    for ref, value in zip(new_weights, new):
        ref[...] = value
    new_low[...] = new[0].astype(BF16)
    for src, dst in zip(passed, passed_out):
        dst[...] = src[...]

    @pl.when(pl.program_id(0) == 0)
    def _():
        grad_norm[...] = jnp.broadcast_to(length, grad_norm.shape)
        for ref, value in zip(
            new_norms, adamw_update(*(ref[...] for ref in norms), norm_grads, clip, 0.0)
        ):
            ref[...] = value
        ffn[...] = norm_grads[4:6]


def finish(sums, squares, weights, grads, norms, passed):
    steps = 4
    rows, flat = grads.shape
    six, width = norms[0].shape

    def whole(shape):
        return pl.BlockSpec(shape, lambda i: (0,) * len(shape))

    wide = pl.BlockSpec((rows, flat // steps), lambda i: (0, i))
    through = [
        pl.BlockSpec(a.shape[:2] + (width // steps,), lambda i: (0, 0, i)) for a in passed
    ]
    return pl.pallas_call(
        finish_kernel,
        name="finish",
        grid=(steps,),
        in_specs=[whole(sums.shape), whole(squares.shape)] + [wide] * 5
        + [whole((six, width))] * 4 + through,
        out_specs=[whole((1, 128))] + [wide] * 5 + [whole((six, width))] * 4
        + [whole((2, width))] + through,
        out_shape=[struct((1, 128), F32)] + [struct(grads.shape, F32)] * 4
        + [struct(grads.shape, BF16)] + [struct((six, width), F32)] * 4
        + [struct((2, width), F32)] + [struct(a.shape, F32) for a in passed],
        compiler_params=pltpu.CompilerParams(
            dimension_semantics=("arbitrary",), vmem_limit_bytes=VMEM_LIMIT
        ),
    )(sums, squares, *weights, grads, *norms, *passed)


def norm_parts(values, gain_row, shift_row):
    average = jnp.mean(values, axis=-1, keepdims=True)
    centred = values - average
    spread_ = jnp.mean(centred * centred, axis=-1, keepdims=True)
    scaled = lax.rsqrt(spread_ + 1e-05)
    unit_rows = centred * scaled
    return (unit_rows * gain_row + shift_row, unit_rows, scaled)


def norm_back(grad_out, unit_rows, scaled, gain_row):
    inner_grad = grad_out * gain_row
    plain_mean = jnp.mean(inner_grad, axis=-1, keepdims=True)
    cross_mean = jnp.mean(inner_grad * unit_rows, axis=-1, keepdims=True)
    return scaled * (inner_grad - plain_mean - unit_rows * cross_mean)


def gain_terms(grad_out, unit_rows):
    width = grad_out.shape[-1]
    flat_grad = grad_out.reshape(-1, width)
    flat_unit = unit_rows.reshape(-1, width)
    return [jnp.sum(flat_grad * flat_unit, axis=0), jnp.sum(flat_grad, axis=0)]


def exact_gelu(values):
    return jax.nn.gelu(values, approximate=False)


def adamw_update(parameter, first_m, second_m, average, gradient, factor, decay_rate):
    clipped = gradient * factor
    new_first = 0.9 * first_m + 0.1 * clipped
    new_second = 0.999 * second_m + 0.001 * clipped * clipped
    first_hat = new_first / (1.0 - 0.9**STEP)
    second_hat = new_second / (1.0 - 0.999**STEP)
    new_param = parameter - 0.02 * (
        first_hat / (jnp.sqrt(second_hat) + 1e-08) + decay_rate * parameter
    )
    new_avg = 0.8 * average + 0.2 * new_param
    return (new_param, new_first, new_second, new_avg)


def dot32(spec, a, b):
    return jnp.einsum(spec, a, b, preferred_element_type=F32)


def general_step(n, size, media_tokens, patch_mask, latents, cotangent, weights, weights_first,
              weights_second, weights_average, norm_params, norm_first, norm_second, norm_average):
    g, patches, width = media_tokens.shape
    lat = latents.shape[1]
    blocks = weights.shape[0]
    r = width // (n * size)
    cols = width // size
    hands = HEADS // size
    scale = 1.0 / math.sqrt(width // HEADS)
    ups = FF // width
    own = g * lat
    media_gain, latent_gain, ffn_gain = 1.0 + norm_params[0], 1.0 + norm_params[2], 1.0 + norm_params[4]

    held = weights.astype(BF16).reshape(blocks, r, width)
    qs = held[:3].reshape(3, r, size, cols).transpose(2, 0, 1, 3)
    media_norm, media_unit, media_scale = norm_parts(media_tokens, media_gain, norm_params[1])
    latent_norm, latent_unit, latent_scale = norm_parts(latents, latent_gain, norm_params[3])
    cot = cotangent.reshape(own, width)
    count_rows = (g + 15) // 16 * 16
    counts = jnp.sum((patch_mask > 0).astype(F32), axis=1)
    counts = jnp.broadcast_to(jnp.pad(counts, (0, count_rows - g))[:, None], (count_rows, 128))

    wqkv, wo, up, dn, nm, nl, dy, cn = spread(
        qs, held[3], held[4 : 4 + ups], held[4 + ups :],
        media_norm.astype(BF16), latent_norm.astype(BF16), cot.astype(BF16), counts, n, size,
    )
    wqkv = wqkv.reshape(3, width, cols)
    wo = wo.reshape(width, width)
    up = up.reshape(-1, width)
    dn = dn.reshape(-1, width)
    nm = nm.reshape(g * size * patches, width)
    nl = nl.reshape(g * size * lat, width)
    dy = dy.reshape(size * own, width)
    real = jnp.sum(cn[:, :g, 0], axis=0).astype(jnp.int32)

    def by_image(a):
        return a.astype(BF16).reshape(g, -1, cols)

    q = by_image(dot32("rd,de->re", nl, wqkv[0]))
    kp, kl = by_image(dot32("rd,de->re", nm, wqkv[1])), by_image(dot32("rd,de->re", nl, wqkv[1]))
    vp, vl = by_image(dot32("rd,de->re", nm, wqkv[2])), by_image(dot32("rd,de->re", nl, wqkv[2]))
    mixed = attend(real, q, kp, kl, vp, vl, hands, scale)
    ab = to_rows(mixed.reshape(g, size, lat, cols), size, 1).reshape(own, width)

    hidden = latents.reshape(own, width) + dot32("rd,de->re", ab, wo)
    ffn_norm, ffn_unit, ffn_scale = norm_parts(hidden, ffn_gain, norm_params[5])
    nf = join_rows(ffn_norm.astype(BF16), size, 2).reshape(size * own, width)
    u = dot32("rd,fd->rf", nf, up)
    active, pull = jax.vjp(exact_gelu, u)
    gb = active.astype(BF16)
    y_part = dot32("rf,fd->rd", gb, dn).astype(BF16)
    du = pull(dot32("rd,fd->rf", dy, dn))[0].astype(BF16)
    f_part = dot32("rf,fd->rd", du, up).astype(BF16)
    g_dn = dot32("rf,rd->fd", gb, dy).astype(BF16)
    g_up = dot32("rf,rd->fd", du, nf).astype(BF16)
    both = split_rows(jnp.stack([y_part, f_part]).reshape(2, 2, 2, own, width), 3)
    latents_out = (hidden + both[0]).reshape(g, lat, width)
    d_ffn = both[1]
    ffn_terms = gain_terms(d_ffn, ffn_unit)
    d_hidden = cot + norm_back(d_ffn, ffn_unit, ffn_scale, ffn_gain)

    do = d_hidden.astype(BF16)
    g_wo = dot32("rd,re->de", ab, do).astype(BF16)
    da = dot32("re,de->rd", do, wo).astype(BF16).reshape(g, lat, width)
    da = to_heads(da, size, 4).reshape(g, size * lat, cols)
    dq, dkp, dkl, dvp, dvl = attend_back(real, q, kp, kl, vp, vl, da, hands, scale)

    def flat(a):
        return a.reshape(-1, cols)

    dq, dkp, dkl, dvp, dvl = flat(dq), flat(dkp), flat(dkl), flat(dvp), flat(dvl)
    g_qkv = jnp.stack([
        dot32("rd,re->de", nl, dq),
        dot32("rd,re->de", nm, dkp) + dot32("rd,re->de", nl, dkl),
        dot32("rd,re->de", nm, dvp) + dot32("rd,re->de", nl, dvl),
    ]).astype(BF16)
    d_nm = (dot32("re,de->rd", dkp, wqkv[1]) + dot32("re,de->rd", dvp, wqkv[2])).astype(BF16)
    d_nl = (
        dot32("re,de->rd", dkl, wqkv[1]) + dot32("re,de->rd", dvl, wqkv[2])
        + dot32("re,de->rd", dq, wqkv[0])
    ).astype(BF16)

    oq, ow, ou, od, d_media, d_latent = collect(
        g_qkv.reshape(3, n, size, r, cols), g_wo.reshape(n, 2, 2, r, width),
        g_up.reshape(ups, n, r, width), g_dn.reshape(ups, n, r, width),
        d_nm.reshape(g, 2, 2, patches, width), d_nl.reshape(g, 2, 2, lat, width), n, size,
    )
    media_grad = norm_back(d_media, media_unit, media_scale, media_gain)
    latents_grad = d_hidden.reshape(g, lat, width) + norm_back(
        d_latent, latent_unit, latent_scale, latent_gain
    )
    grads = jnp.concatenate([
        oq.transpose(1, 2, 0, 3).reshape(3, r, width), ow[None], ou, od,
    ])
    square = jnp.broadcast_to(jnp.sum(grads * grads), (width,))
    rows = jnp.stack(
        gain_terms(d_media, media_unit) + gain_terms(d_latent, latent_unit) + ffn_terms
        + [square, jnp.zeros_like(square)]
    )
    sums = total(rows, n, size)
    return latents_out, media_grad, latents_grad, grads, sums[:6], sums[6, 0]


def on_device(n, size, media_tokens, patch_mask, latents, cotangent, weights, weights_first,
              weights_second, weights_average, norm_params, norm_first, norm_second, norm_average):
    g, patches, width = media_tokens.shape
    lat = latents.shape[1]
    r = width // (n * size)
    arrays = (
        media_tokens, patch_mask, latents, cotangent, weights, weights_first, weights_second,
        weights_average, norm_params, norm_first, norm_second, norm_average,
    )
    if r % 16 or lat % 16 or size != 4 or n != 2 * size or FF % (4 * width):
        latents_out, media_grad, latents_grad, grads, norm_grads, square = general_step(
            n, size, *arrays
        )
    else:
        media_grad, latents_grad, latents_out, grads, sums, squares = whole_step(
            weights, media_tokens, latents, cotangent, patch_mask, norm_params,
            n, size, HEADS // size, 1.0 / math.sqrt(width // HEADS),
        )
        done = finish(
            sums, squares, (weights, weights_first, weights_second, weights_average), grads,
            (norm_params, norm_first, norm_second, norm_average),
            (latents_out.reshape(g, lat, width), media_grad, latents_grad),
        )
        return (
            *done[11:14], done[0][0, 0], done[1], done[5], *done[2:5], *done[6:11],
        )
    grad_norm = jnp.sqrt(square + jnp.sum(norm_grads * norm_grads))
    clip = jnp.minimum(1.0, 1.0 / (grad_norm + 1e-06))
    new_w, new_first, new_second, new_avg = adamw_update(
        weights, weights_first, weights_second, weights_average,
        grads.reshape(weights.shape), clip, 0.1,
    )
    new_n, new_nf, new_ns, new_na = adamw_update(
        norm_params, norm_first, norm_second, norm_average, norm_grads, clip, 0.0
    )
    return (
        latents_out, media_grad, latents_grad, grad_norm, new_w, new_w.astype(BF16), new_first,
        new_second, new_avg, new_n, new_nf, new_ns, new_na, norm_grads[4:6],
    )


def solution(mesh):
    n, size = mesh.shape["dp"], mesh.shape["patch"]
    rows, weight = P("dp", "patch", None), P(None, ("dp", "patch"))
    return jax.shard_map(
        functools.partial(on_device, n, size),
        mesh=mesh,
        in_specs=(rows, P("dp", "patch"), rows, rows) + (weight,) * 4 + (P(),) * 4,
        out_specs=(rows, rows, rows, P()) + (weight,) * 5 + (P(),) * 5,
        check_vma=False,
    )
```

```python
import functools
import math

import jax
import jax.numpy as jnp
from jax import lax
from jax.experimental import pallas as pl
from jax.experimental.pallas import tpu as pltpu
from jax.sharding import PartitionSpec as P

HEADS = 16
FF = 4096
STEP = 7
MESH = pl.DeviceIdType.MESH
F32 = jnp.float32
BF16 = jnp.bfloat16
ANY = pl.BlockSpec(memory_space=pl.ANY)
VMEM = pl.BlockSpec(memory_space=pltpu.VMEM)
DMA = pltpu.SemaphoreType.DMA
VMEM_LIMIT = 64 * 1024 * 1024 - 65536


def struct(shape, kind):
    return jax.ShapeDtypeStruct(shape, kind)


def place():
    d, p = lax.axis_index("dp"), lax.axis_index("patch")
    return d, p, lax.div(d, 2), lax.rem(d, 2), lax.div(p, 2), lax.rem(p, 2)


def remote(src, dst, send, recv, to):
    return pltpu.make_async_remote_copy(
        src_ref=src, dst_ref=dst, send_sem=send, recv_sem=recv, device_id=to, device_id_type=MESH
    )


def greet(peers):
    barrier = pltpu.get_barrier_semaphore()
    for to in peers:
        pl.semaphore_signal(barrier, inc=1, device_id=to, device_id_type=MESH)
    return functools.partial(pl.semaphore_wait, barrier, len(peers))


def meet(always, maybe=()):
    barrier = pltpu.get_barrier_semaphore()
    count = len(always)
    for to in always:
        pl.semaphore_signal(barrier, inc=1, device_id=to, device_id_type=MESH)
    for there, to in maybe:

        @pl.when(there)
        def _(to=to):
            pl.semaphore_signal(barrier, inc=1, device_id=to, device_id_type=MESH)

        count = count + there.astype(jnp.int32)
    pl.semaphore_wait(barrier, count)


def patch_peers(d, p, size):
    return [(d, lax.rem(p + k, size)) for k in range(1, size)]


def params(number):
    return pltpu.CompilerParams(
        collective_id=number, has_side_effects=True, vmem_limit_bytes=VMEM_LIMIT
    )


def spread_kernel(chain, size, qs, wos, ups, dns, nms, nls, dys, cns,
                  wqkv, wo, up, dn, nm, nl, dy, cn,
                  loc, a_s, a_r, su, sd, sy, rz, ry, xs, xr, cs, cr):
    d, p, z, y, x, c = place()
    above, below = z + 1 < chain, z > 0
    up_dev, dn_dev = ((z + 1) * 2 + y, p), ((z - 1) * 2 + y, p)
    y_dev, x_dev, c_dev = (z * 2 + 1 - y, p), (d, (1 - x) * 2 + c), (d, x * 2 + 1 - c)
    px, pc = (1 - x) * 2 + c, x * 2 + 1 - c
    pd = (1 - x) * 2 + 1 - c
    meet(patch_peers(d, p, size) + [y_dev], [(above, up_dev), (below, dn_dev)])

    own = [
        (qs.at[p], wqkv.at[:, d, p]), (wos, wo.at[d, p]), (ups, up.at[:, d]), (dns, dn.at[:, d]),
        (nms, nm.at[:, p]), (nls, nl.at[:, p]), (dys, dy.at[p]), (cns, cn.at[p]),
    ]
    local = [pltpu.make_async_copy(a, b, loc.at[i]) for i, (a, b) in enumerate(own)]
    for copy in local:
        copy.start()
    swaps = []
    for k in range(1, size):
        q = lax.rem(p + k, size)
        swaps.append(remote(qs.at[q], wqkv.at[:, d, p], a_s.at[k], a_r.at[k], (d, q)))
    for copy in swaps:
        copy.start()

    rows = [(nms, nm), (nls, nl), (cns, cn), (dys, dy)]

    def slot(j, q):
        ref = rows[j][1] if j < 4 else wo
        return ref.at[q] if j in (2, 3) else ref.at[:, q]

    def row_copies(j):
        src = rows[j][0] if j < 4 else slot(j, p)
        return (
            remote(src, slot(j, p), xs.at[j], xr.at[j], x_dev),
            remote(src, slot(j, p), cs.at[j, 0], cr.at[j, 0], c_dev),
            remote(slot(j, px), slot(j, px), cs.at[j, 1], cr.at[j, 1], c_dev),
        )

    def start_rows(j):
        to_x, to_c, _ = row_copies(j)
        to_x.start()
        to_c.start()

    def pass_rows(j):
        to_x, _, on = row_copies(j)
        to_x.wait_recv()
        on.start()

    def end_rows(j):
        to_x, to_c, on = row_copies(j)
        to_c.wait_recv()
        on.wait_recv()
        to_x.wait_send()
        to_c.wait_send()
        on.wait_send()

    for j in range(4):
        start_rows(j)

    def piece(i, dd):
        return (wqkv.at[:, dd], wo.at[dd, p], up.at[:, dd], dn.at[:, dd])[i]

    first = (wqkv.at[:, d], wos, ups, dns)

    def hop(i, zz, sends, to, own_src=False):
        src = first[i] if own_src else piece(i, zz * 2 + y)
        return remote(src, piece(i, zz * 2 + y), sends.at[i, zz], rz.at[i, zz], to)

    def over(i, zz, own_src=False):
        src = first[i] if own_src else piece(i, zz * 2 + y)
        return remote(src, piece(i, zz * 2 + y), sy.at[i, zz], ry.at[i, zz], y_dev)

    def start_own(i):
        @pl.when(above)
        def _():
            hop(i, z, su, up_dev, True).start()

        @pl.when(below)
        def _():
            hop(i, z, sd, dn_dev, True).start()

        over(i, z, True).start()

    def forward(i):
        def step(s, carry):
            @pl.when(z - s >= 0)
            def _():
                hop(i, z - s, su, up_dev).wait_recv()

                @pl.when(above)
                def _():
                    hop(i, z - s, su, up_dev).start()

                over(i, z - s).start()

            @pl.when(z + s < chain)
            def _():
                hop(i, z + s, sd, dn_dev).wait_recv()

                @pl.when(below)
                def _():
                    hop(i, z + s, sd, dn_dev).start()

                over(i, z + s).start()

            return carry

        lax.fori_loop(1, chain, step, 0)

    def arrived(i):
        def step(zz, carry):
            src = piece(i, zz * 2 + 1 - y)
            remote(src, src, sy.at[i, zz], ry.at[i, zz], y_dev).wait_recv()
            return carry

        lax.fori_loop(0, chain, step, 0)

    def sent(i):
        def step(zz, carry):
            over(i, zz).wait_send()

            @pl.when(jnp.logical_and(above, zz <= z))
            def _():
                hop(i, zz, su, up_dev).wait_send()

            @pl.when(jnp.logical_and(below, zz >= z))
            def _():
                hop(i, zz, sd, dn_dev).wait_send()

            return carry

        lax.fori_loop(0, chain, step, 0)

    local[0].wait()
    for copy in swaps:
        copy.wait_recv()
    start_own(0)
    start_own(1)
    forward(0)
    start_own(2)
    forward(1)
    start_own(3)
    local[1].wait()
    arrived(1)
    start_rows(4)
    forward(2)
    for j in range(5):
        pass_rows(j)
    forward(3)
    arrived(0)
    arrived(2)
    arrived(3)
    for j in range(5):
        end_rows(j)
    for copy in swaps:
        copy.wait_send()
    for i in range(4):
        sent(i)
    for copy in local[2:]:
        copy.wait()


def spread(qs, wos, ups, dns, nms, nls, dys, cns, n, size):
    _, three, r, cols = qs.shape
    width = wos.shape[1]
    chain = n // 2
    g, patches, _ = nms.shape
    lat = nls.shape[1]
    return pl.pallas_call(
        functools.partial(spread_kernel, chain, size),
        name="spread",
        out_shape=(
            struct((three, n, size, r, cols), BF16),
            struct((n, size, r, width), BF16),
            struct((ups.shape[0], n, r, width), BF16),
            struct((dns.shape[0], n, r, width), BF16),
            struct((g, size, patches, width), BF16),
            struct((g, size, lat, width), BF16),
            struct((size,) + dys.shape, BF16),
            struct((size,) + cns.shape, F32),
        ),
        in_specs=[VMEM] * 8,
        out_specs=(ANY,) * 8,
        scratch_shapes=[
            DMA((8,)), DMA((size,)), DMA((size,)),
            DMA((4, chain)), DMA((4, chain)), DMA((4, chain)), DMA((4, chain)), DMA((4, chain)),
            DMA((5,)), DMA((5,)), DMA((5, 2)), DMA((5, 2)),
        ],
        compiler_params=params(0),
    )(qs, wos, ups, dns, nms, nls, dys, cns)


def to_rows_kernel(size, src, out, loc, ss, rs):
    d, p = lax.axis_index("dp"), lax.axis_index("patch")
    cols = src.shape[3]
    meet(patch_peers(d, p, size))
    here = out.at[:, :, pl.ds(pl.multiple_of(p * cols, cols), cols)]
    copies = []
    for k in range(1, size):
        q = lax.rem(p + k, size)
        copies.append(remote(src.at[:, q], here, ss.at[k], rs.at[k], (d, q)))
    for copy in copies:
        copy.start()
    mine = pltpu.make_async_copy(src.at[:, p], here, loc)
    mine.start()
    mine.wait()
    for copy in copies:
        copy.wait()


def to_rows(src, size, number):
    g, _, lat, cols = src.shape
    return pl.pallas_call(
        functools.partial(to_rows_kernel, size),
        name="to_rows",
        out_shape=struct((g, lat, size * cols), src.dtype),
        in_specs=[VMEM],
        out_specs=VMEM,
        scratch_shapes=[DMA, DMA((size,)), DMA((size,))],
        compiler_params=params(number),
    )(src)


def to_heads_kernel(size, src, out, loc, ss, rs):
    d, p = lax.axis_index("dp"), lax.axis_index("patch")
    cols = out.shape[3]
    meet(patch_peers(d, p, size))

    def part(q):
        return src.at[:, :, pl.ds(pl.multiple_of(q * cols, cols), cols)]

    copies = []
    for k in range(1, size):
        q = lax.rem(p + k, size)
        copies.append(remote(part(q), out.at[:, p], ss.at[k], rs.at[k], (d, q)))
    for copy in copies:
        copy.start()
    mine = pltpu.make_async_copy(part(p), out.at[:, p], loc)
    mine.start()
    mine.wait()
    for copy in copies:
        copy.wait()


def to_heads(src, size, number):
    g, lat, width = src.shape
    return pl.pallas_call(
        functools.partial(to_heads_kernel, size),
        name="to_heads",
        out_shape=struct((g, size, lat, width // size), src.dtype),
        in_specs=[VMEM],
        out_specs=VMEM,
        scratch_shapes=[DMA, DMA((size,)), DMA((size,))],
        compiler_params=params(number),
    )(src)


def join_rows_kernel(src, out, loc, ss, rs):
    d, p, z, y, x, c = place()
    x_dev, c_dev = (d, (1 - x) * 2 + c), (d, x * 2 + 1 - c)
    px = (1 - x) * 2 + c
    meet([x_dev, c_dev])
    to_x = remote(src, out.at[p], ss.at[0], rs.at[0], x_dev)
    to_c = remote(src, out.at[p], ss.at[1], rs.at[1], c_dev)
    on = remote(out.at[px], out.at[px], ss.at[2], rs.at[2], c_dev)
    to_x.start()
    to_c.start()
    mine = pltpu.make_async_copy(src, out.at[p], loc)
    mine.start()
    to_x.wait_recv()
    on.start()
    mine.wait()
    to_c.wait()
    on.wait()
    to_x.wait_send()


def join_rows(src, size, number):
    return pl.pallas_call(
        join_rows_kernel,
        name="join_rows",
        out_shape=struct((size,) + src.shape, src.dtype),
        in_specs=[VMEM],
        out_specs=VMEM,
        scratch_shapes=[DMA, DMA((3,)), DMA((3,))],
        compiler_params=params(number),
    )(src)


def split_rows_kernel(ins, src, out, half, mid, quarter, ss, rs):
    d, p, z, y, x, c = place()
    x_dev, c_dev = (d, (1 - x) * 2 + c), (d, x * 2 + 1 - c)
    meet([x_dev, c_dev])
    first = [remote(src.at[i, :, 1 - c], half.at[i], ss.at[i], rs.at[i], c_dev) for i in range(ins)]
    for copy in first:
        copy.start()
    second = []
    for i in range(ins):
        first[i].wait_recv()
        mid[i] = (half[i, 1 - x].astype(F32) + src[i, 1 - x, c].astype(F32)).astype(BF16)
        copy = remote(mid.at[i], quarter.at[i], ss.at[ins + i], rs.at[ins + i], x_dev)
        copy.start()
        second.append(copy)
    for i in range(ins):
        out[i] = half[i, x].astype(F32) + src[i, x, c].astype(F32)
    for i in range(ins):
        second[i].wait_recv()
        out[i] = out[i] + quarter[i].astype(F32)
    for copy in first + second:
        copy.wait_send()


def split_rows(src, number):
    ins, _, _, rows, width = src.shape
    return pl.pallas_call(
        functools.partial(split_rows_kernel, ins),
        name="split_rows",
        out_shape=struct((ins, rows, width), F32),
        in_specs=[VMEM],
        out_specs=VMEM,
        scratch_shapes=[
            pltpu.VMEM((ins, 2, rows, width), BF16),
            pltpu.VMEM((ins, rows, width), BF16),
            pltpu.VMEM((ins, rows, width), BF16),
            DMA((2 * ins,)), DMA((2 * ins,)),
        ],
        compiler_params=params(number),
    )(src)


def head_rows(q, hands):
    rows, cols = q.shape
    size = cols // hands
    lane = lax.broadcasted_iota(jnp.int32, (rows, cols), 1)
    zero = jnp.zeros_like(q)
    parts = [
        jnp.where(jnp.logical_and(lane >= h * size, lane < (h + 1) * size), q, zero)
        for h in range(hands)
    ]
    return jnp.concatenate(parts, axis=0)


def own_columns(full, hands):
    rows, cols = full.shape[0] // hands, full.shape[1]
    size = cols // hands
    lane = lax.broadcasted_iota(jnp.int32, (rows, cols), 1)
    out = jnp.zeros((rows, cols), F32)
    for h in range(hands):
        keep = jnp.logical_and(lane >= h * size, lane < (h + 1) * size)
        out = jnp.where(keep, full[h * rows : (h + 1) * rows], out)
    return out


def nt(a, b):
    return lax.dot_general(a, b, (((1,), (1,)), ((), ())), preferred_element_type=F32)


def nn(a, b):
    return lax.dot_general(a, b, (((1,), (0,)), ((), ())), preferred_element_type=F32)


def tn(a, b):
    return lax.dot_general(a, b, (((0,), (0,)), ((), ())), preferred_element_type=F32)


def soft(qb, kp, kl, real, scale):
    sp = nt(qb, kp) * scale
    sl = nt(qb, kl) * scale
    key = lax.broadcasted_iota(jnp.int32, sp.shape, 1).astype(F32)
    sp = jnp.where(key < real, sp, -1e30)
    peak = jnp.maximum(jnp.max(sp, axis=1, keepdims=True), jnp.max(sl, axis=1, keepdims=True))
    ep, el = jnp.exp(sp - peak), jnp.exp(sl - peak)
    total = jnp.sum(ep, axis=1, keepdims=True) + jnp.sum(el, axis=1, keepdims=True)
    return ep / total, el / total


def attend_kernel(hands, scale, real, q, kp, kl, vp, vl, out):
    g = pl.program_id(0)
    qb = head_rows(q[0], hands)
    pp, plat = soft(qb, kp[0], kl[0], real[g].astype(F32), scale)
    full = nn(pp.astype(BF16), vp[0]) + nn(plat.astype(BF16), vl[0])
    out[0] = own_columns(full, hands).astype(BF16)


def attend(real, q, kp, kl, vp, vl, hands, scale):
    g, lat, cols = q.shape
    patches = kp.shape[1]

    def spec(rows):
        return pl.BlockSpec((1, rows, cols), lambda i, real: (i, 0, 0))

    return pl.pallas_call(
        functools.partial(attend_kernel, hands, scale),
        name="attend",
        grid_spec=pltpu.PrefetchScalarGridSpec(
            num_scalar_prefetch=1,
            grid=(g,),
            in_specs=[spec(lat), spec(patches), spec(lat), spec(patches), spec(lat)],
            out_specs=spec(lat),
        ),
        out_shape=struct((g, lat, cols), BF16),
        compiler_params=pltpu.CompilerParams(dimension_semantics=("arbitrary",)),
    )(real, q, kp, kl, vp, vl)


def attend_back_kernel(hands, scale, real, q, kp, kl, vp, vl, da, dq, dkp, dkl, dvp, dvl):
    g = pl.program_id(0)
    qb = head_rows(q[0], hands)
    dab = head_rows(da[0], hands)
    pp, plat = soft(qb, kp[0], kl[0], real[g].astype(F32), scale)
    gp, gl = nt(dab, vp[0]), nt(dab, vl[0])
    delta = jnp.sum(pp * gp, axis=1, keepdims=True) + jnp.sum(plat * gl, axis=1, keepdims=True)
    sp, sl = (pp * (gp - delta)).astype(BF16), (plat * (gl - delta)).astype(BF16)
    dvp[0] = tn(pp.astype(BF16), dab).astype(BF16)
    dvl[0] = tn(plat.astype(BF16), dab).astype(BF16)
    dkp[0] = (tn(sp, qb) * scale).astype(BF16)
    dkl[0] = (tn(sl, qb) * scale).astype(BF16)
    full = nn(sp, kp[0]) + nn(sl, kl[0])
    dq[0] = (own_columns(full, hands) * scale).astype(BF16)


def attend_back(real, q, kp, kl, vp, vl, da, hands, scale):
    g, lat, cols = q.shape
    patches = kp.shape[1]

    def spec(rows):
        return pl.BlockSpec((1, rows, cols), lambda i, real: (i, 0, 0))

    return pl.pallas_call(
        functools.partial(attend_back_kernel, hands, scale),
        name="attend_back",
        grid_spec=pltpu.PrefetchScalarGridSpec(
            num_scalar_prefetch=1,
            grid=(g,),
            in_specs=[spec(lat), spec(patches), spec(lat), spec(patches), spec(lat), spec(lat)],
            out_specs=[spec(lat), spec(patches), spec(lat), spec(patches), spec(lat)],
        ),
        out_shape=(
            struct((g, lat, cols), BF16),
            struct((g, patches, cols), BF16),
            struct((g, lat, cols), BF16),
            struct((g, patches, cols), BF16),
            struct((g, lat, cols), BF16),
        ),
        compiler_params=pltpu.CompilerParams(dimension_semantics=("arbitrary",)),
    )(real, q, kp, kl, vp, vl, da)


def collect_kernel(chain, size, gq, gw, gu, gd, kp, kl,
                   oq, ow, ou, od, okp, okl,
                   yq, yw, yu, yd, uq, uw, uu, ud, dq, dw, du, dd,
                   wc, wsum, wx, total, kc, kx, lc, lx, fin,
                   ys, yr, us, ur, ds, dr, ks, kr, qs, qr):
    d, p, z, y, x, c = place()
    above, below = z + 1 < chain, z > 0
    up_dev, dn_dev = ((z + 1) * 2 + y, p), ((z - 1) * 2 + y, p)
    y_dev, x_dev, c_dev = (z * 2 + 1 - y, p), (d, (1 - x) * 2 + c), (d, x * 2 + 1 - c)
    meet(patch_peers(d, p, size) + [y_dev], [(above, up_dev), (below, dn_dev)])

    mine = (
        lambda k: gq.at[:, k], lambda k: total.at[k], lambda k: gu.at[:, k], lambda k: gd.at[:, k]
    )
    land_y, land_u, land_d = (yq, yw, yu, yd), (uq, uw, uu, ud), (dq, dw, du, dd)

    def over(i, zz):
        return remote(
            mine[i](zz * 2 + 1 - y), land_y[i].at[zz], ys.at[i, zz], yr.at[i, zz], y_dev
        )

    def send_over(i):
        def step(zz, carry):
            over(i, zz).start()
            return carry

        lax.fori_loop(0, chain, step, 0)

    def add_over(i):
        def step(zz, carry):
            over(i, zz).wait_recv()
            have = mine[i](zz * 2 + y)
            land_y[i][zz] = (land_y[i][zz].astype(F32) + have[...].astype(F32)).astype(BF16)
            return carry

        lax.fori_loop(0, chain, step, 0)

    def rise(i, zz):
        return remote(land_y[i].at[zz], land_u[i].at[zz], us.at[i, zz], ur.at[i, zz], up_dev)

    def fall(i, zz):
        return remote(land_y[i].at[zz], land_d[i].at[zz], ds.at[i, zz], dr.at[i, zz], dn_dev)

    def gather(i, zz, land):
        land_y[i][zz] = (land_y[i][zz].astype(F32) + land[i][zz].astype(F32)).astype(BF16)

    def along(i):
        def step(k, carry):
            s = chain - k

            @pl.when(z + s < chain)
            def _():
                @pl.when(below)
                def _():
                    rise(i, z + s).wait_recv()
                    gather(i, z + s, land_u)

                rise(i, z + s).start()

            @pl.when(z - s >= 0)
            def _():
                @pl.when(above)
                def _():
                    fall(i, z - s).wait_recv()
                    gather(i, z - s, land_d)

                fall(i, z - s).start()

            return carry

        lax.fori_loop(1, chain, step, 0)

    def finish(i, write):
        write(land_y[i][z].astype(F32))

        @pl.when(below)
        def _():
            rise(i, z).wait_recv()
            write(land_u[i][z].astype(F32), True)

        @pl.when(above)
        def _():
            fall(i, z).wait_recv()
            write(land_d[i][z].astype(F32), True)

    def into(ref):
        def write(value, more=False):
            ref[...] = ref[...] + value if more else value

        return write

    def sent(i):
        def step(zz, carry):
            over(i, zz).wait_send()

            @pl.when(zz > z)
            def _():
                rise(i, zz).wait_send()

            @pl.when(zz < z)
            def _():
                fall(i, zz).wait_send()

            return carry

        lax.fori_loop(0, chain, step, 0)

    send_over(2)
    w_core = remote(gw.at[:, :, 1 - c], wc, ks.at[0], kr.at[0], c_dev)
    p_core = remote(kp.at[:, :, 1 - c], kc, ks.at[1], kr.at[1], c_dev)
    l_core = remote(kl.at[:, :, 1 - c], lc, ks.at[2], kr.at[2], c_dev)
    w_core.start()
    p_core.start()
    l_core.start()
    send_over(3)
    send_over(0)

    w_core.wait_recv()

    def w_add(k, carry):
        wsum[k] = (wc[k, 1 - x].astype(F32) + gw[k, 1 - x, c].astype(F32)).astype(BF16)
        return carry

    lax.fori_loop(0, 2 * chain, w_add, 0)
    w_x = remote(wsum, wx, ks.at[3], kr.at[3], x_dev)
    w_x.start()

    p_core.wait_recv()
    images = kp.shape[0]

    def p_add(k, carry):
        kc[k] = (kc[k].astype(F32) + kp[k, :, c].astype(F32)).astype(BF16)
        return carry

    lax.fori_loop(0, images, p_add, 0)
    p_x = remote(kc.at[:, 1 - x], kx, ks.at[4], kr.at[4], x_dev)
    p_x.start()
    l_core.wait_recv()

    def l_add(k, carry):
        lc[k] = (lc[k].astype(F32) + kl[k, :, c].astype(F32)).astype(BF16)
        return carry

    lax.fori_loop(0, images, l_add, 0)
    l_x = remote(lc.at[:, 1 - x], lx, ks.at[5], kr.at[5], x_dev)
    l_x.start()

    w_x.wait_recv()

    def w_last(k, carry):
        total[k] = (
            wc[k, x].astype(F32) + gw[k, x, c].astype(F32) + wx[k].astype(F32)
        ).astype(BF16)
        return carry

    lax.fori_loop(0, 2 * chain, w_last, 0)
    send_over(1)

    add_over(2)
    along(2)
    add_over(3)
    along(3)
    add_over(0)
    along(0)
    add_over(1)
    along(1)
    finish(2, into(ou))
    finish(3, into(od))
    finish(0, into(fin))
    swaps = []
    for k in range(1, size):
        q = lax.rem(p + k, size)
        swaps.append(remote(fin.at[:, q], oq.at[p], qs.at[k], qr.at[k], (d, q)))
    for copy in swaps:
        copy.start()
    finish(1, into(ow))
    oq[p] = fin[:, p]

    p_x.wait_recv()

    def p_last(k, carry):
        okp[k] = kc[k, x].astype(F32) + kx[k].astype(F32)
        return carry

    lax.fori_loop(0, images, p_last, 0)
    l_x.wait_recv()

    def l_last(k, carry):
        okl[k] = lc[k, x].astype(F32) + lx[k].astype(F32)
        return carry

    lax.fori_loop(0, images, l_last, 0)
    for copy in swaps:
        copy.wait()
    for i in range(4):
        sent(i)
    for copy in (w_core, p_core, l_core, w_x, p_x, l_x):
        copy.wait_send()


def collect(gq, gw, gu, gd, kp, kl, n, size):
    chain = n // 2
    three, _, _, r, cols = gq.shape
    width = gw.shape[-1]
    fu, fd = gu.shape[0], gd.shape[0]
    g, two, _, patches, _ = kp.shape
    lat = kl.shape[3]
    lands = [
        ((three, size, r, cols)), ((r, width)), ((fu, r, width)), ((fd, r, width)),
    ]
    stage = [pltpu.VMEM((chain,) + s, BF16) for s in lands]
    return pl.pallas_call(
        functools.partial(collect_kernel, chain, size),
        name="collect",
        out_shape=(
            struct((size, three, r, cols), F32),
            struct((r, width), F32),
            struct((fu, r, width), F32),
            struct((fd, r, width), F32),
            struct((g, patches, width), F32),
            struct((g, lat, width), F32),
        ),
        in_specs=[VMEM] * 6,
        out_specs=(VMEM,) * 6,
        scratch_shapes=stage * 3
        + [
            pltpu.VMEM((n, two, r, width), BF16),
            pltpu.VMEM((n, r, width), BF16),
            pltpu.VMEM((n, r, width), BF16),
            pltpu.VMEM((n, r, width), BF16),
            pltpu.VMEM((g, two, patches, width), BF16),
            pltpu.VMEM((g, patches, width), BF16),
            pltpu.VMEM((g, two, lat, width), BF16),
            pltpu.VMEM((g, lat, width), BF16),
            pltpu.VMEM((three, size, r, cols), F32),
        ]
        + [DMA((4, chain))] * 6
        + [DMA((6,)), DMA((6,)), DMA((size,)), DMA((size,))],
        compiler_params=params(6),
    )(gq, gw, gu, gd, kp, kl)


def total_kernel(hops, src, out, hold, land, ss, rs):
    d, p = lax.axis_index("dp"), lax.axis_index("patch")

    def flip(v, bit):
        return v + bit - 2 * bit * lax.rem(lax.div(v, bit), 2)

    to = [(d, flip(p, b)) if kind else (flip(d, b), p) for kind, b in hops]
    meet(to)
    sends = []
    for i, who in enumerate(to):
        copy = remote(src if i == 0 else hold.at[i], land.at[i], ss.at[i], rs.at[i], who)
        copy.start()
        copy.wait_recv()
        sends.append(copy)
        value = (src[...] if i == 0 else hold[i]) + land[i]
        if i + 1 < len(to):
            hold[i + 1] = value
        else:
            out[...] = value
    for copy in sends:
        copy.wait_send()


def total(src, n, size):
    hops = [(True, 1 << b) for b in range(size.bit_length() - 1)]
    hops += [(False, 1 << b) for b in range(n.bit_length() - 1)]
    return pl.pallas_call(
        functools.partial(total_kernel, hops),
        name="total",
        out_shape=struct(src.shape, F32),
        in_specs=[VMEM],
        out_specs=VMEM,
        scratch_shapes=[
            pltpu.VMEM((len(hops),) + src.shape, F32),
            pltpu.VMEM((len(hops),) + src.shape, F32),
            DMA((len(hops),)), DMA((len(hops),)),
        ],
        compiler_params=params(7),
    )(src)


class Names:
    def __init__(self, pairs):
        self.__dict__.update(pairs)


def aligned(start, step, count=None):
    return pl.ds(pl.multiple_of(start * step, step), count or step)


def each(lo, hi, body):
    def step(k, carry):
        body(k)
        return carry

    lax.fori_loop(lo, hi, step, 0)


def unit_of(x):
    mean = jnp.mean(x, axis=-1, keepdims=True)
    centred = x - mean
    spread_ = jnp.mean(centred * centred, axis=-1, keepdims=True)
    scaled = lax.rsqrt(spread_ + 1e-05)
    return centred * scaled, scaled


def column_sum(a):
    return jnp.sum(a, axis=0, keepdims=True)


INPUTS = ("weights", "media", "latents", "cot", "mask", "norms")
OUTPUTS = ("media_grad", "latents_grad", "latents_out", "grads", "sums", "squares")


def crowd_of(images):
    return 3 if images % 3 == 0 else 1


def buffers(n, size, g, patches, lat, width, ups, r):
    chain, cols, own = n // 2, width // size, g * lat
    keys, rows, tiles = size * (patches + lat), patches + lat, width // 256
    crowd = crowd_of(g)
    crowds = g // crowd
    low = {
        "wqkv": (3, width, cols), "wo": (width // size, width), "ud": (3, ups, n * r, width),
        "nm": (g, size * patches, width), "nl": (g, size * lat, width), "dy": (size * own, width), "doa": (g, size * lat, width),
        "q": (g, size * lat, cols), "k": (g, keys, cols), "v": (g, keys, cols),
        "mixed": (g, size * lat, cols), "nf": (size * own, width),
        "hpart": (crowds, 2, 2, crowd * lat, width), "hhalf": (crowds, 2, crowd * lat, width),
        "hmid": (crowds, crowd * lat, width), "hquart": (crowds, crowd * lat, width),
        "gb": (ups, size * own, n * r), "du": (ups, size * own, n * r),
        "part": (2, tiles, 2, 2, own, 256), "half": (2, tiles, 2, own, 256),
        "mid": (2, tiles, own, 256), "quart": (2, tiles, own, 256),
        "dah": (g, size * lat, cols), "gwo": (2, size * r, width),
        "yq": (3, chain, size * r, cols), "zq": (3, chain + 1, size * r, cols),
        "yw": (size * r, width), "zw": (2, size * r, width),
        "yf": (2, chain, ups // 2, r, width), "zf": (2, chain + 1, ups // 2, r, width),
        "zb": (2, chain + 1, ups // 4, 2 * r, width), "yb": (2, ups // 4, r, width),
        "yn": (2, chain, ups // 4, r, width), "zn": (2, chain + 1, ups // 4, r, width),
        "kall": (2, 2, 2, rows, width), "kland": (g, 2, rows, width), "kx": (g, rows, width),
    }
    full = {
        "media": (g, patches, width), "latents": (g, lat, width), "cot": (g, lat, width),
        "norms": (6, width), "hidden": (own, width), "dhid": (own, width),
        "fin": (3, size * r, cols), "wfin": (size * r, width), "grads": (3 + 1 + 2 * ups, r, width), "gsum": (8, width),
        "flat": (3 + 1 + 2 * ups, r * width),
        "turn": (width // 128, (3 + 1 + 2 * ups) * r, 128),
        "cn": (size, (g + 15) // 16 * 16, size * patches),
        "nland": (size, 8, width), "nhold": (8, width), "dland": (n, 8, width),
        "sland": (size, 8, 128), "shold": (8, 128), "tland": (n, 8, 128), "sqr": (8, 128),
    }
    sems = {
        "loc": (7,), "ins": (5,), "outs": (3,), "mouts": (2,),
        "a_s": (size,), "a_r": (size,), "su": (7, chain), "sd": (7, chain), "sy": (7, chain),
        "rz": (7, chain), "ry": (7, chain), "was": (1,), "war": (size,), "ww": (5,),
        "hcs": (crowds,), "hcr": (crowds,), "hxs": (crowds,), "hxr": (crowds,),
        "nxs": (crowds,), "nxr": (crowds,), "ncs": (crowds, 2), "ncr": (crowds, 2),
        "dxs": (crowds,), "dxr": (crowds,), "dcs": (crowds, 2), "dcr": (crowds, 2),
        "ms": (crowds,), "mr": (crowds,), "mcs": (crowds, 2), "mcr": (crowds, 2),
        "xs": (3,), "xr": (3,), "cs": (3, 2), "cr": (3, 2),
        "ps": (2, tiles), "pr": (2, tiles), "qs": (2, tiles),
        "qr": (2, tiles), "gws": (3,), "gwr": (3,), "ks": (2,), "kr": (g,), "lxs": (g,), "lxr": (g,),
        "gyr": (7, chain), "gzr": (7, chain + 1),
        "es": (size,), "er": (size,),
        "bzr": (2, chain + 1), "bys": (2,), "byr": (2,),
        "fs": (3, size), "fr": (3, size),
        "n1s": (size,), "n1r": (size,), "n2s": (n,), "n2r": (n,), "s1r": (size,), "s2r": (n,), "s1s": (size,), "s2s": (n,),
    }
    scratch = [(k, pltpu.VMEM(s, BF16)) for k, s in low.items()]
    scratch += [(k, pltpu.VMEM(s, F32)) for k, s in full.items()]
    scratch += [("held", pltpu.VMEM((4 + 2 * ups, r, width), BF16))]
    scratch += [(k, DMA(s)) for k, s in sems.items()]
    return scratch


def step_kernel(n, size, hands, scale, names, *refs):
    chain = n // 2
    count = len(INPUTS) + len(OUTPUTS)
    into = Names(zip(INPUTS, refs[: len(INPUTS)]))
    out = Names(zip(OUTPUTS, refs[len(INPUTS) : count]))
    b = Names(zip(names, refs[count:]))
    d, p, z, y, x, c = place()
    held, media, latents, cot, norms = b.held, b.media, b.latents, b.cot, b.norms
    wqkv, wo, ud, nm, nl, dy, cn = b.wqkv, b.wo, b.ud, b.nm, b.nl, b.dy, b.cn
    q, k_, v_, mixed, hidden, nf, doa = b.q, b.k, b.v, b.mixed, b.hidden, b.nf, b.doa
    r, width = held.shape[1], held.shape[2]
    cols, ups = width // size, ud.shape[1]
    images, patches, _ = media.shape
    lat = latents.shape[1]
    own, keys, reals = images * lat, size * (patches + lat), size * patches
    tiles = width // 256
    above, below = z + 1 < chain, z > 0
    up_dev, dn_dev = ((z + 1) * 2 + y, p), ((z - 1) * 2 + y, p)
    y_dev, x_dev, c_dev = (z * 2 + 1 - y, p), (d, (1 - x) * 2 + c), (d, x * 2 + 1 - c)
    px = (1 - x) * 2 + c
    dp_peers = [(lax.rem(d + s, n), p) for s in range(1, n)]

    loads = [
        pltpu.make_async_copy(src, dst, b.ins.at[i])
        for i, (src, dst) in enumerate(
            ((into.weights, b.flat), (into.cot, cot), (into.norms, norms),
             (into.latents, latents), (into.media, media))
        )
    ]
    for copy in loads:
        copy.start()
    everyone_here = greet(patch_peers(d, p, size) + dp_peers)
    blocks = held.shape[0]
    loads[0].wait()
    for t in range(width // 128):
        for k in range(r):
            at = k * width + t * 128
            b.turn[t, pl.ds(k, blocks, stride=r), :] = b.flat[:, at : at + 128]
        held[:, :, t * 128 : (t + 1) * 128] = (
            b.turn[t].reshape(blocks, r, 128).astype(BF16)
        )
    loads[1].wait()
    dy[aligned(p, own)] = cot[...].reshape(own, width).astype(BF16)
    everyone_here()

    def lanes(k):
        return aligned(k, cols)

    half, quarter = ups // 2, ups // 4
    most = ups - quarter
    blocks_of = {
        3: (0, 0, half), 4: (0, half, half), 5: (1, 0, most), 6: (1, most, quarter),
    }
    def piece(i, dd):
        if i < 3:
            return wqkv.at[i, aligned(dd, size * r)]
        return ud.at[blocks_of[i][0], pl.ds(*blocks_of[i][1:]), aligned(dd, r)]

    first = [wqkv.at[i, aligned(d, size * r)] for i in range(3)]
    for i in range(3, 7):
        plane, start, many = blocks_of[i]
        first.append(held.at[pl.ds(4 + plane * ups + start, many)])
    here = wqkv.at[:, aligned(d * size + p, r)]
    def hop(i, zz, sends, to, own_src=False):
        src = first[i] if own_src else piece(i, zz * 2 + y)
        return remote(src, piece(i, zz * 2 + y), sends.at[i, zz], b.rz.at[i, zz], to)

    def over(i, zz, own_src=False):
        src = first[i] if own_src else piece(i, zz * 2 + y)
        return remote(src, piece(i, zz * 2 + y), b.sy.at[i, zz], b.ry.at[i, zz], y_dev)

    def start_own(i):
        @pl.when(above)
        def _():
            hop(i, z, b.su, up_dev, True).start()

        @pl.when(below)
        def _():
            hop(i, z, b.sd, dn_dev, True).start()

        over(i, z, True).start()

    swaps = []
    for k in range(1, size):
        to = lax.rem(p + k, size)
        swaps.append(
            remote(held.at[pl.ds(0, 3), :, lanes(to)], here, b.a_s.at[k], b.a_r.at[k], (d, to))
        )
    for copy in swaps:
        copy.start()
    wo_near = remote(
        held.at[3], wo.at[aligned(y * size + p, r)], b.was.at[0], b.war.at[p], (d, z)
    )
    wo_own = pltpu.make_async_copy(held.at[3], wo.at[aligned(y * size + p, r)], b.loc.at[1])

    @pl.when(z != p)
    def _():
        wo_near.start()

    @pl.when(z == p)
    def _():
        wo_own.start()

    start_own(3)
    over(6, z, True).start()
    local = [pltpu.make_async_copy(held.at[pl.ds(0, 3), :, lanes(p)], here, b.loc.at[0])]
    local += [pltpu.make_async_copy(first[i], piece(i, d), b.loc.at[i]) for i in range(3, 7)]
    for copy in local:
        copy.start()

    def forward(i, s):
        @pl.when(z - s >= 0)
        def _():
            hop(i, z - s, b.su, up_dev).wait_recv()

            @pl.when(above)
            def _():
                hop(i, z - s, b.su, up_dev).start()

            over(i, z - s).start()

        @pl.when(z + s < chain)
        def _():
            hop(i, z + s, b.sd, dn_dev).wait_recv()

            @pl.when(below)
            def _():
                hop(i, z + s, b.sd, dn_dev).start()

            over(i, z + s).start()

    def pair(k, zz):
        return ud.at[1, pl.ds(most + k * quarter, quarter), aligned(zz, 2 * r)]

    def pair_hop(k, zz, sends, to):
        return remote(pair(k, zz), pair(k, zz), sends.at[6 + k, zz], b.rz.at[6 + k, zz], to)

    def pair_start():
        for k in range(1):
            src = piece(6 + k, z * 2 + 1 - y)
            local[4 + k].wait()
            remote(src, src, b.sy.at[6 + k, z], b.ry.at[6 + k, z], y_dev).wait_recv()

            @pl.when(above)
            def _():
                pair_hop(k, z, b.su, up_dev).start()

            @pl.when(below)
            def _():
                pair_hop(k, z, b.sd, dn_dev).start()

    def pair_forward(s):
        for k in range(1):

            @pl.when(z - s >= 0)
            def _():
                pair_hop(k, z - s, b.su, up_dev).wait_recv()

                @pl.when(above)
                def _():
                    pair_hop(k, z - s, b.su, up_dev).start()

            @pl.when(z + s < chain)
            def _():
                pair_hop(k, z + s, b.sd, dn_dev).wait_recv()

                @pl.when(below)
                def _():
                    pair_hop(k, z + s, b.sd, dn_dev).start()

    def pair_sent():
        for k in range(1):
            over(6 + k, z).wait_send()

            def step(zz):
                @pl.when(jnp.logical_and(above, zz <= z))
                def _():
                    pair_hop(k, zz, b.su, up_dev).wait_send()

                @pl.when(jnp.logical_and(below, zz >= z))
                def _():
                    pair_hop(k, zz, b.sd, dn_dev).wait_send()

            each(0, chain, step)

    def arrived(i):
        def step(zz):
            src = piece(i, zz * 2 + 1 - y)
            remote(src, src, b.sy.at[i, zz], b.ry.at[i, zz], y_dev).wait_recv()

        each(0, chain, step)

    def sent(i):
        def step(zz):
            over(i, zz).wait_send()

            @pl.when(jnp.logical_and(above, zz <= z))
            def _():
                hop(i, zz, b.su, up_dev).wait_send()

            @pl.when(jnp.logical_and(below, zz >= z))
            def _():
                hop(i, zz, b.sd, dn_dev).wait_send()

        each(0, chain, step)

    class Rows:
        def __init__(self, slot, xs, xr, cs, cr, at, src=None):
            src = slot(p) if src is None else src
            self.to_x = remote(src, slot(p), xs.at[at], xr.at[at], x_dev)
            self.to_c = remote(src, slot(p), cs.at[at, 0], cr.at[at, 0], c_dev)
            self.on = remote(slot(px), slot(px), cs.at[at, 1], cr.at[at, 1], c_dev)

        def start(self):
            self.to_x.start()
            self.to_c.start()

        def forward(self):
            self.to_x.wait_recv()
            self.on.start()

        def have(self):
            self.to_c.wait_recv()
            self.on.wait_recv()

        def end(self):
            self.to_x.wait_send()
            self.to_c.wait_send()
            self.on.wait_send()

    def group(slot, j, src=None):
        return Rows(slot, b.xs, b.xr, b.cs, b.cr, j, src)

    lat_rows = group(lambda k: nl.at[:, aligned(k, lat)], 0)
    cn_rows = group(lambda k: cn.at[k], 1)
    dy_rows = group(lambda k: dy.at[aligned(k, own)], 2)

    def wo_block(k):
        return wo.at[aligned(k, size * r)]

    def wo_hop(e, to, k):
        return remote(wo_block(k), wo_block(k), b.ww.at[e], b.ww.at[3 + e // 2], to)

    def wo_pass(first_end, second_end):
        @pl.when(first_end)
        def _():
            wo_hop(0, up_dev, y).start()

        @pl.when(second_end)
        def _():
            wo_hop(1, dn_dev, y).start()

        wo_hop(2, y_dev, y).start()

    def wo_source():
        @pl.when(z == p)
        def _():
            for k in range(1, size):
                who = lax.rem(p + k, size)
                part = wo.at[aligned(y * size + who, r)]
                remote(part, part, b.was.at[0], b.war.at[who], (d, who)).wait_recv()
            wo_own.wait()
            wo_pass(above, below)

    def wo_rest():
        @pl.when(z > p)
        def _():
            wo_hop(0, up_dev, y).wait_recv()
            wo_pass(above, z < 0)

        @pl.when(z < p)
        def _():
            wo_hop(0, dn_dev, y).wait_recv()
            wo_pass(z < 0, below)

    def wo_have():
        wo_hop(2, y_dev, 1 - y).wait_recv()

    def wo_sent():
        @pl.when(jnp.logical_and(z >= p, above))
        def _():
            wo_hop(0, up_dev, y).wait_send()

        @pl.when(jnp.logical_and(z <= p, below))
        def _():
            wo_hop(1, dn_dev, y).wait_send()

        wo_hop(2, y_dev, y).wait_send()

        @pl.when(z != p)
        def _():
            wo_near.wait_send()

    crowd = crowd_of(images)
    crowds = images // crowd

    def media_rows(j):
        return Rows(
            lambda k: nm.at[aligned(j, crowd), aligned(k, patches)],
            b.ms, b.mr, b.mcs, b.mcr, j,
        )

    fold = crowd * lat

    def nf_rows(j):
        return Rows(
            lambda k: nf.at[pl.ds(pl.multiple_of(k * own + j * fold, fold), fold)],
            b.nxs, b.nxr, b.ncs, b.ncr, j,
        )

    def do_rows(j):
        return Rows(
            lambda k: doa.at[aligned(j, crowd), aligned(k, lat)],
            b.dxs, b.dxr, b.dcs, b.dcr, j,
        )

    loads[2].wait()
    loads[3].wait()
    media_gain, media_shift = 1.0 + norms[0:1, :], norms[1:2, :]
    latent_gain, latent_shift = 1.0 + norms[2:3, :], norms[3:4, :]
    ffn_gain, ffn_shift = 1.0 + norms[4:5, :], norms[5:6, :]

    def latent_norm(g):
        unit, _ = unit_of(latents[g])
        nl[g, aligned(p, lat)] = (unit * latent_gain + latent_shift).astype(BF16)

    def media_norm(g):
        unit, _ = unit_of(media[g])
        nm[g, aligned(p, patches)] = (unit * media_gain + media_shift).astype(BF16)

    dy_rows.start()
    cn[p] = jnp.zeros(cn.shape[1:], F32)
    counts = column_of((into.mask[...] > 0).astype(F32))
    cn[p, :images, :] = jnp.broadcast_to(counts, (images, cn.shape[2]))
    each(0, images, latent_norm)
    cn_rows.start()
    lat_rows.start()
    local[0].wait()
    for copy in swaps:
        copy.wait_recv()
    for i in range(3):
        start_own(i)
    loads[4].wait()
    each(0, images, media_norm)
    each(0, crowds, lambda j: media_rows(j).start())
    wo_source()
    for s in range(1, chain):
        for i in range(3):
            forward(i, s)
        if s == 1:
            start_own(4)
            dy_rows.forward()
            cn_rows.forward()
    lat_rows.forward()
    wo_rest()
    start_own(5)
    for s in range(1, chain - 1):
        forward(3, s)
    pair_start()
    for i in range(3):
        arrived(i)
    lat_rows.have()
    cn_rows.have()

    flat_nl = nl[...].reshape(images * size * lat, width)
    q[...] = nn(flat_nl, wqkv[0]).astype(BF16).reshape(images, size * lat, cols)
    k_[:, reals:] = nn(flat_nl, wqkv[1]).astype(BF16).reshape(images, size * lat, cols)
    v_[:, reals:] = nn(flat_nl, wqkv[2]).astype(BF16).reshape(images, size * lat, cols)

    def real_keys(g):
        real = cn[0, pl.ds(g, 1), :]
        for k in range(1, size):
            real = real + cn[k, pl.ds(g, 1), :]
        return real

    def image(g):
        k_[g, :reals] = nn(nm[g], wqkv[1]).astype(BF16)
        v_[g, :reals] = nn(nm[g], wqkv[2]).astype(BF16)
        pp, plat = soft(
            head_rows(q[g], hands), k_[g, :reals], k_[g, reals:], real_keys(g), scale
        )
        full = nn(pp.astype(BF16), v_[g, :reals]) + nn(plat.astype(BF16), v_[g, reals:])
        mixed[g] = own_columns(full, hands).astype(BF16)

    def hid_core(j):
        return remote(b.hpart.at[j, :, 1 - c], b.hhalf.at[j], b.hcs.at[j], b.hcr.at[j], c_dev)

    def hid_x(j):
        return remote(b.hmid.at[j], b.hquart.at[j], b.hxs.at[j], b.hxr.at[j], x_dev)

    def hid_part(j):
        rows = mixed[j * crowd : (j + 1) * crowd].reshape(crowd * size * lat, cols)
        for t in range(tiles):
            span = pl.ds(256 * t, 256)
            value = nn(rows, wo[:, span]).astype(BF16)
            for i in range(crowd):
                for e in range(size):
                    at = (i * size + e) * lat
                    b.hpart[j, e // 2, e % 2, i * lat : (i + 1) * lat, span] = value[at : at + lat]
        hid_core(j).start()

    def hid_pass(j):
        hid_core(j).wait_recv()
        b.hmid[j] = (b.hhalf[j, 1 - x].astype(F32) + b.hpart[j, 1 - x, c].astype(F32)).astype(BF16)
        hid_x(j).start()

    def hid_end(j):
        hid_x(j).wait_recv()
        value = (
            latents[j * crowd : (j + 1) * crowd].reshape(fold, width)
            + b.hhalf[j, x].astype(F32) + b.hpart[j, x, c].astype(F32) + b.hquart[j].astype(F32)
        )
        hidden[j * fold : (j + 1) * fold] = value
        unit, _ = unit_of(value)
        nf[pl.ds(pl.multiple_of(p * own + j * fold, fold), fold)] = (
            unit * ffn_gain + ffn_shift
        ).astype(BF16)
        nf_rows(j).start()

    pending = [(3, chain - 1)] + [(i, s) for i in (4, 5) for s in range(1, chain)]

    def forward_some(count):
        for _ in range(count):
            if pending:
                forward(*pending.pop(0))

    for j in range(crowds):
        media_rows(j).forward()
        if j:
            forward_some(1)
        media_rows(j).have()
        each(j * crowd, (j + 1) * crowd, image)
        if j == 0:
            wo_have()
        hid_part(j)
        if j > 0:
            hid_end(j - 1)
        forward_some(1)
        hid_pass(j)
        forward_some(1)
    forward_some(len(pending))
    for j in range(crowds - 1):
        nf_rows(j).forward()
    hid_end(crowds - 1)
    for s in range(1, chain - 1):
        pair_forward(s)
    dy_rows.have()
    for i in (3, 4, 5):
        arrived(i)
    for copy in local[1:4]:
        copy.wait()
    nf_rows(crowds - 1).forward()
    for j in range(crowds):
        nf_rows(j).have()

    def hidden_block(e):
        u = nt(nf[...], ud[0, e])
        into_active = nt(dy[...], ud[1, e])
        chance = 0.5 * (1.0 + lax.erf(u * math.sqrt(0.5)))
        slope = chance + u * jnp.exp(-0.5 * u * u) * (1.0 / math.sqrt(2.0 * math.pi))
        b.gb[e] = (u * chance).astype(BF16)
        b.du[e] = (into_active * slope).astype(BF16)

    def down_grad(e):
        for t in range(0, width, 512):
            ud[2, e, :, t : t + 512] = tn(b.gb[e], dy[:, t : t + 512]).astype(BF16)

    def up_grad(e):
        for t in range(0, width, 512):
            ud[0, e, :, t : t + 512] = tn(b.du[e], nf[:, t : t + 512]).astype(BF16)

    def part_core(i, t):
        return remote(
            b.part.at[i, t, :, 1 - c], b.half.at[i, t], b.ps.at[i, t], b.pr.at[i, t], c_dev
        )

    def part_x(i, t):
        return remote(b.mid.at[i, t], b.quart.at[i, t], b.qs.at[i, t], b.qr.at[i, t], x_dev)

    def part_of(i, acts, passing=False):
        def tile(t):
            span = aligned(t, 256)
            acc = nn(acts[0], ud[i, 0, :, span])
            for e in range(1, ups):
                acc = acc + nn(acts[e], ud[i, e, :, span])
            b.part[i, t] = acc.astype(BF16).reshape(2, 2, own, 256)
            part_core(i, t).start()
            if passing:
                @pl.when(t > 1)
                def _():
                    pass_tile(i, t - 2)

        each(0, tiles, tile)
        if passing:
            each(max(tiles - 2, 0), tiles, lambda t: pass_tile(i, t))

    def part_pass(i):
        each(0, tiles, lambda t: pass_tile(i, t))

    def pass_tile(i, t):
        part_core(i, t).wait_recv()
        b.mid[i, t] = (
            b.half[i, t, 1 - x].astype(F32) + b.part[i, t, 1 - x, c].astype(F32)
        ).astype(BF16)
        part_x(i, t).start()

    def part_end(i, write):
        def tile(t):
            part_x(i, t).wait_recv()
            write(
                aligned(t, 256),
                b.half[i, t, x].astype(F32) + b.part[i, t, x, c].astype(F32)
                + b.quart[i, t].astype(F32),
            )

        each(0, tiles, tile)

    def parts_sent(i):
        def tile(t):
            part_core(i, t).wait_send()
            part_x(i, t).wait_send()

        each(0, tiles, tile)

    def ffn_part(i, k):
        plane, start, many = {
            3: (2, 0, quarter), 4: (0, 0, half), 5: (0, half, half), 6: (2, most, quarter)
        }[i]
        return ud.at[plane, pl.ds(start, many), aligned(k, r)]

    class Staged:
        def stage(self, k):
            @pl.when(z == k)
            def _():
                each(0, chain - 1 - k, lambda t: self.move(
                    chain - 1 - t, k > 0, chain - t, up_dev
                ))

            @pl.when(chain - 1 - z == k)
            def _():
                each(0, chain - 1 - k, lambda t: self.move(t, k > 0, t, dn_dev))

    class Sum(Staged):
        def __init__(self, i, kind):
            self.i = i
            if kind == 0:
                self.mine = lambda k: wqkv.at[i, aligned(k, size * r)]
                self.ly, self.lz = b.yq.at[i], b.zq.at[i]
            else:
                self.mine = lambda k: ffn_part(i, k)
                self.ly = b.yf.at[i - 4] if i in (4, 5) else b.yn.at[i // 6]
                self.lz = b.zf.at[i - 4] if i in (4, 5) else b.zn.at[i // 6]

        def over(self, zt):
            return remote(
                self.mine(zt * 2 + 1 - y), self.ly.at[zt], b.sy.at[self.i, zt],
                b.gyr.at[self.i, zt], y_dev,
            )

        def along(self, zt, slot, to):
            return remote(
                self.ly.at[zt], self.lz.at[slot], b.su.at[self.i, zt], b.gzr.at[self.i, slot], to
            )

        def send(self):
            def step(k):
                s = chain - 1 - k

                @pl.when(z + s < chain)
                def _():
                    self.over(z + s).start()

                @pl.when(jnp.logical_and(z - s >= 0, s > 0))
                def _():
                    self.over(z - s).start()

            each(0, chain, step)

        def pair(self, zt):
            return self.ly[zt].astype(F32) + self.mine(zt * 2 + y)[...].astype(F32)

        def move(self, zt, more, slot, to):
            self.over(zt).wait_recv()
            if more:
                self.along(zt, slot, to).wait_recv()
                self.ly[zt] = (self.pair(zt) + self.lz[slot].astype(F32)).astype(BF16)
            else:
                self.ly[zt] = self.pair(zt).astype(BF16)
            self.along(zt, slot, to).start()

        def last(self, dst):
            self.over(z).wait_recv()
            dst[...] = self.pair(z)

            @pl.when(below)
            def _():
                self.along(z, z + 1, up_dev).wait_recv()
                dst[...] = dst[...] + self.lz[z + 1].astype(F32)

            @pl.when(above)
            def _():
                self.along(z, z, dn_dev).wait_recv()
                dst[...] = dst[...] + self.lz[z].astype(F32)

        def sent(self):
            def step(zt):
                self.over(zt).wait_send()

                @pl.when(zt != z)
                def _():
                    self.along(zt, 0, up_dev).wait_send()

            each(0, chain, step)

    class Cross(Staged):
        def __init__(self, k):
            self.k, self.blocks = k, pl.ds((1 + k) * quarter, quarter)
            self.lz, self.ly = b.zb.at[k], b.yb.at[k]

        def pair(self, zt):
            return ud.at[2, self.blocks, aligned(zt, 2 * r)]

        def along(self, zt, slot, to):
            return remote(
                self.pair(zt), self.lz.at[slot], b.sd.at[self.k, zt], b.bzr.at[self.k, slot], to
            )

        def move(self, zt, more, slot, to):
            if more:
                self.along(zt, slot, to).wait_recv()
                self.pair(zt)[...] = (
                    self.pair(zt)[...].astype(F32) + self.lz[slot].astype(F32)
                ).astype(BF16)
            self.along(zt, slot, to).start()

        def over(self):
            src = ud.at[2, self.blocks, aligned(z * 2 + 1 - y, r)]
            return remote(src, self.ly, b.bys.at[self.k], b.byr.at[self.k], y_dev)

        def meet(self, dst):
            theirs, ours = aligned(1 - y, r), aligned(y, r)
            far = ud.at[2, self.blocks, aligned(z * 2 + 1 - y, r)]
            near = ud.at[2, self.blocks, aligned(z * 2 + y, r)]
            dst[...] = near[...].astype(F32)

            def add(slot):
                dst[...] = dst[...] + self.lz[slot, :, ours].astype(F32)
                far[...] = (
                    far[...].astype(F32) + self.lz[slot, :, theirs].astype(F32)
                ).astype(BF16)

            @pl.when(below)
            def _():
                self.along(z, z + 1, up_dev).wait_recv()
                add(z + 1)

            @pl.when(above)
            def _():
                self.along(z, z, dn_dev).wait_recv()
                add(z)

            self.over().start()

        def last(self, dst):
            self.over().wait_recv()
            dst[...] = dst[...] + self.ly[...].astype(F32)

        def sent(self):
            self.over().wait_send()

            def step(zt):
                @pl.when(zt != z)
                def _():
                    self.along(zt, 0, up_dev).wait_send()

            each(0, chain, step)

    class Gather:
        def over(self):
            return remote(b.gwo.at[1 - y], b.yw, b.gws.at[0], b.gwr.at[0], y_dev)

        def rise(self):
            return remote(b.gwo.at[y], b.zw.at[0], b.gws.at[1], b.gwr.at[1], up_dev)

        def fall(self):
            return remote(b.gwo.at[y], b.zw.at[1], b.gws.at[2], b.gwr.at[2], dn_dev)

        def send(self):
            self.over().start()

        def add(self, k):
            b.gwo[y] = (b.gwo[y].astype(F32) + b.zw[k].astype(F32)).astype(BF16)

        def step(self, k):
            @pl.when(jnp.logical_or(
                jnp.logical_and(z < p, z == k), jnp.logical_and(z > p, chain - 1 - z == k)
            ))
            def _():
                self.over().wait_recv()
                b.gwo[y] = (b.gwo[y].astype(F32) + b.yw[...].astype(F32)).astype(BF16)

                @pl.when(z < p)
                def _():
                    if k:
                        self.rise().wait_recv()
                        self.add(0)
                    self.rise().start()

                @pl.when(z > p)
                def _():
                    if k:
                        self.fall().wait_recv()
                        self.add(1)
                    self.fall().start()

        def part(self, k, to):
            return remote(
                b.wfin.at[aligned(k, r)], b.grads.at[3], b.es.at[k], b.er.at[0], to
            )

        def last(self):
            @pl.when(z == p)
            def _():
                self.over().wait_recv()
                b.wfin[...] = b.gwo[y].astype(F32) + b.yw[...].astype(F32)

                @pl.when(below)
                def _():
                    self.rise().wait_recv()
                    b.wfin[...] = b.wfin[...] + b.zw[0].astype(F32)

                @pl.when(above)
                def _():
                    self.fall().wait_recv()
                    b.wfin[...] = b.wfin[...] + b.zw[1].astype(F32)

                for k in range(1, size):
                    to = lax.rem(p + k, size)
                    self.part(to, (d, to)).start()
                b.grads[3] = b.wfin[aligned(p, r)]

        def have(self):
            @pl.when(z != p)
            def _():
                self.part(0, (d, z)).wait_recv()

        def sent(self):
            self.over().wait_send()

            @pl.when(z < p)
            def _():
                self.rise().wait_send()

            @pl.when(z > p)
            def _():
                self.fall().wait_send()

            @pl.when(z == p)
            def _():
                for k in range(1, size):
                    to = lax.rem(p + k, size)
                    self.part(to, (d, to)).wait_send()

    crosses = [Cross(0), Cross(1)]

    qkv_sums, wo_sum = [Sum(i, 0) for i in range(3)], Gather()

    ffn_sums = {i: Sum(i, 2) for i in (3, 4, 5, 6)}

    each(0, quarter, hidden_block)
    each(0, quarter, down_grad)
    for i in range(6):
        sent(i)
    pair_sent()
    wo_sent()
    ffn_sums[3].send()
    for k in range(2):
        each((1 + k) * quarter, (2 + k) * quarter, hidden_block)
        each((1 + k) * quarter, (2 + k) * quarter, down_grad)
        crosses[k].stage(0)
    pair_forward(chain - 1)
    each(most, ups, hidden_block)
    each(most, ups, down_grad)
    ffn_sums[6].send()
    part_of(0, b.du, True)
    each(0, ups, up_grad)
    ffn_sums[4].send()
    ffn_sums[5].send()
    part_of(1, b.gb)

    def write_dhid(span, value):
        b.dhid[:, span] = value

    part_end(0, write_dhid)
    dn = b.dhid[...]
    unit, scaled = unit_of(hidden[...])
    b.gsum[...] = jnp.zeros_like(b.gsum)
    b.gsum[4:5, :] = column_sum(dn * unit)
    b.gsum[5:6, :] = column_sum(dn)
    b.dhid[...] = cot[...].reshape(own, width) + norm_back(dn, unit, scaled, ffn_gain)
    for j in range(crowds):
        doa[j * crowd : (j + 1) * crowd, aligned(p, lat)] = (
            b.dhid[j * fold : (j + 1) * fold].astype(BF16).reshape(crowd, lat, width)
        )
        do_rows(j).start()
    def stages(*pairs):
        for item, k in pairs:
            if k < chain - 1:
                item.stage(k)

    def head_grads(j):
        do_rows(j).have()
        rows = doa[j * crowd : (j + 1) * crowd].reshape(crowd * size * lat, width)
        b.dah[j * crowd : (j + 1) * crowd] = (
            nt(rows, wo[...]).astype(BF16).reshape(crowd, size * lat, cols)
        )

    def out_grad():
        for t in range(tiles):
            span = pl.ds(256 * t, 256)
            b.gwo[:, :, span] = tn(
                mixed[...].reshape(images * size * lat, cols),
                doa[:, :, span].reshape(images * size * lat, 256),
            ).astype(BF16).reshape(2, size * r, 256)

    def kin_core(g):
        return remote(
            b.kall.at[lax.rem(g, 2), 1 - c], b.kland.at[g], b.ks.at[lax.rem(g, 2)], b.kr.at[g], c_dev
        )

    def kin_x(g):
        return remote(b.kland.at[g, 1 - x], b.kx.at[g], b.lxs.at[g], b.lxr.at[g], x_dev)

    def image_back(g):
        slot = lax.rem(g, 2)
        qb, dab = head_rows(q[g], hands), head_rows(b.dah[g], hands)
        kp, kl, vp, vl = k_[g, :reals], k_[g, reals:], v_[g, :reals], v_[g, reals:]
        pp, plat = soft(qb, kp, kl, real_keys(g), scale)
        gp, gl = nt(dab, vp), nt(dab, vl)
        delta = column_of(pp * gp) + column_of(plat * gl)
        sp, sl = (pp * (gp - delta)).astype(BF16), (plat * (gl - delta)).astype(BF16)
        v_[g, :reals] = tn(pp.astype(BF16), dab).astype(BF16)
        v_[g, reals:] = tn(plat.astype(BF16), dab).astype(BF16)
        k_[g, :reals] = (tn(sp, qb) * scale).astype(BF16)
        k_[g, reals:] = (tn(sl, qb) * scale).astype(BF16)
        q[g] = (own_columns(nn(sp, kp) + nn(sl, kl), hands) * scale).astype(BF16)
        for t in range(tiles):
            span = pl.ds(256 * t, 256)
            rows = nt(k_[g], wqkv[1, span, :]) + nt(v_[g], wqkv[2, span, :])
            tail = rows[reals:] + nt(q[g], wqkv[0, span, :])
            for e in range(size):
                b.kall[slot, e % 2, e // 2, :patches, span] = (
                    rows[e * patches : (e + 1) * patches].astype(BF16)
                )
                b.kall[slot, e % 2, e // 2, patches:, span] = (
                    tail[e * lat : (e + 1) * lat].astype(BF16)
                )
        kin_core(g).start()

    def kin_mid(g):
        kin_core(g).wait_recv()
        b.kland[g] = (
            b.kland[g].astype(F32) + b.kall[lax.rem(g, 2), c].astype(F32)
        ).astype(BF16)
        kin_x(g).start()

    def media_out(g):
        return pltpu.make_async_copy(media.at[g], out.media_grad.at[g], b.mouts.at[lax.rem(g, 2)])

    def kin_last(g):
        kin_x(g).wait_recv()
        total_ = b.kland[g, x].astype(F32) + b.kx[g].astype(F32)
        grad = total_[:patches]
        unit, scaled = unit_of(media[g])
        b.gsum[0:1, :] = b.gsum[0:1, :] + column_sum(grad * unit)
        b.gsum[1:2, :] = b.gsum[1:2, :] + column_sum(grad)
        media[g] = norm_back(grad, unit, scaled, media_gain)

        @pl.when(g >= 2)
        def _():
            media_out(g - 2).wait()

        media_out(g).start()
        grad = total_[patches:]
        unit, scaled = unit_of(latents[g])
        b.gsum[2:3, :] = b.gsum[2:3, :] + column_sum(grad * unit)
        b.gsum[3:4, :] = b.gsum[3:4, :] + column_sum(grad)
        latents[g] = b.dhid[aligned(g, lat)] + norm_back(grad, unit, scaled, latent_gain)

    def back(g):
        @pl.when(g >= 2)
        def _():
            kin_core(g - 2).wait_send()

        image_back(g)

        @pl.when(g >= 1)
        def _():
            kin_mid(g - 1)

    down, first_up, last_up, more_down = (ffn_sums[i] for i in (3, 4, 5, 6))
    between = [
        [(crosses[1], 1), (first_up, 0), (crosses[0], 2)],
        [(crosses[1], 2), (down, 1)],
        [(more_down, 1), (last_up, 0)],
    ]
    stages((down, 0), (crosses[0], 1), (more_down, 0))
    do_rows(0).forward()
    for j in range(crowds):
        head_grads(j)
        if j + 1 < crowds:
            do_rows(j + 1).forward()
        else:
            out_grad()
            wo_sum.send()
        each(j * crowd, (j + 1) * crowd, back)
        if between:
            stages(*between.pop(0))
    kin_mid(images - 1)
    for pairs in between:
        stages(*pairs)
    for k in range(3, chain - 1):
        stages((crosses[0], k), (crosses[1], k))
    cross_rows = [
        b.grads.at[pl.ds(4 + ups + (1 + k) * quarter, quarter)] for k in range(2)
    ]

    def flat(a, n_rows):
        return a.reshape(images * n_rows, cols)

    def qkv_grad(j):
        def tile(t):
            span = aligned(t, 256)
            rows_l = nl[:, :, span].reshape(images * size * lat, 256)
            if j == 0:
                wqkv[0, span, :] = tn(rows_l, flat(q[...], size * lat)).astype(BF16)
                return
            rows_m = nm[:, :, span].reshape(images * reals, 256)
            ref = (k_, v_)[j - 1]
            wqkv[j, span, :] = (
                tn(rows_m, flat(ref[:, :reals], reals))
                + tn(rows_l, flat(ref[:, reals:], size * lat))
            ).astype(BF16)

        each(0, tiles, tile)
        qkv_sums[j].send()

    for item, rows in zip(crosses, cross_rows):
        item.meet(rows)
    qkv_grad(0)
    qkv_grad(2)
    qkv_grad(1)
    part_pass(1)
    waiting = [(0, (images + 2) // 3)]
    waiting += [(waiting[0][1], 2 * waiting[0][1]), (2 * waiting[0][1], images)]

    def last_keys():
        if waiting:
            each(*waiting.pop(0), kin_last)

    q_sum, k_sum, v_sum = qkv_sums
    wo_sum.step(0)
    stages((down, 2), (more_down, 2), (first_up, 1))
    last_keys()
    stages((q_sum, 0), (last_up, 1), (first_up, 2))
    last_keys()
    stages((v_sum, 0))
    wo_sum.step(1)
    stages((last_up, 2), (q_sum, 1), (k_sum, 0))
    last_keys()
    stages((v_sum, 1), (q_sum, 2))
    wo_sum.step(2)
    stages((k_sum, 1), (v_sum, 2), (k_sum, 2))
    for k in range(3, chain - 1):
        stages((q_sum, k), (v_sum, k), (k_sum, k))
        if k > 2:
            stages((down, k), (more_down, k), (first_up, k), (last_up, k))
            wo_sum.step(k)
    down.last(b.grads.at[pl.ds(4 + ups, quarter)])
    more_down.last(b.grads.at[pl.ds(4 + ups + most, quarter)])
    first_up.last(b.grads.at[pl.ds(4, half)])
    last_up.last(b.grads.at[pl.ds(4 + half, half)])
    for span in waiting:
        each(*span, kin_last)
    for item, rows in zip(crosses, cross_rows):
        item.last(rows)
    lat_copy = pltpu.make_async_copy(latents, out.latents_grad, b.outs.at[1])
    lat_copy.start()

    def write_out(span, value):
        hidden[:, span] = hidden[:, span] + value

    part_end(1, write_out)
    out_copy = pltpu.make_async_copy(hidden, out.latents_out, b.outs.at[0])
    out_copy.start()

    def share(src, land, hold, s1, r1, total_to, land2, s2, r2):
        land[p] = src[...]
        near = []
        for k in range(1, size):
            to = lax.rem(p + k, size)
            near.append(remote(src, land.at[p], s1.at[to], r1.at[p], (d, to)))
        for copy in near:
            copy.start()
        for k in range(1, size):
            who = lax.rem(p + k, size)
            remote(src, land.at[who], s1.at[who], r1.at[who], (d, who)).wait_recv()
        value = land[0]
        for k in range(1, size):
            value = value + land[k]
        hold[...] = value
        land2[d] = value
        far = []
        for k in range(1, n):
            to = lax.rem(d + k, n)
            far.append(remote(hold, land2.at[d], s2.at[to], r2.at[d], (to, p)))
        for copy in far:
            copy.start()

        def finish():
            for k in range(1, n):
                who = lax.rem(d + k, n)
                remote(hold, land2.at[who], s2.at[who], r2.at[who], (who, p)).wait_recv()
            value = land2[0]
            for k in range(1, n):
                value = value + land2[k]
            total_to[...] = value
            for copy in near + far:
                copy.wait_send()

        return finish

    norms_done = share(b.gsum, b.nland, b.nhold, b.n1s, b.n1r, out.sums, b.dland, b.n2s, b.n2r)
    ends = []
    for j in (0, 2, 1):
        if j == 1:
            wo_sum.last()
        qkv_sums[j].last(b.fin.at[j])
        for k in range(1, size):
            to = lax.rem(p + k, size)
            copy = remote(
                b.fin.at[j, aligned(to, r)], b.grads.at[j, :, lanes(p)],
                b.fs.at[j, k], b.fr.at[j, k], (d, to),
            )
            copy.start()
            ends.append(copy)
        b.grads[j, :, lanes(p)] = b.fin[j, aligned(p, r)]
    squares = jnp.zeros((8, 128), F32)

    def squares_of(i, squares):
        for t in range(0, width, 128):
            tile = b.grads[i, :, t : t + 128]
            squares = squares + jnp.sum((tile * tile).reshape(r // 8, 8, 128), axis=0)
        return squares

    for i in range(4, 4 + 2 * ups):
        squares = squares_of(i, squares)
    wo_sum.have()
    for copy in ends:
        copy.wait_recv()
    for i in range(4):
        squares = squares_of(i, squares)
    b.sqr[...] = squares
    squares_done = share(
        b.sqr, b.sland, b.shold, b.s1s, b.s1r, out.squares, b.tland, b.s2s, b.s2r
    )
    for t in range(width // 128):
        b.turn[t] = b.grads[:, :, t * 128 : (t + 1) * 128].reshape(blocks * r, 128)
        for k in range(r):
            at = k * width + t * 128
            b.flat[:, at : at + 128] = b.turn[t, pl.ds(k, blocks, stride=r), :]
    grads_copy = pltpu.make_async_copy(b.flat, out.grads, b.outs.at[2])
    grads_copy.start()
    norms_done()
    for copy in swaps + ends:
        copy.wait_send()
    for rows in (lat_rows, cn_rows, dy_rows):
        rows.end()
    for j in range(crowds):
        media_rows(j).end()
        nf_rows(j).end()
        do_rows(j).end()
        hid_core(j).wait_send()
        hid_x(j).wait_send()
    parts_sent(0)
    parts_sent(1)
    each(max(images - 2, 0), images, lambda g: kin_core(g).wait_send())
    each(0, images, lambda g: kin_x(g).wait_send())
    for item in qkv_sums:
        item.sent()
    wo_sum.sent()
    for item in ffn_sums.values():
        item.sent()
    for item in crosses:
        item.sent()
    each(max(images - 2, 0), images, lambda g: media_out(g).wait())
    out_copy.wait()
    lat_copy.wait()
    grads_copy.wait()
    squares_done()


def column_of(a):
    return jnp.sum(a, axis=1, keepdims=True)


def whole_step(weights, media, latents, cot, mask, norms, n, size, hands, scale):
    g, patches, width = media.shape
    blocks, r = weights.shape[0], weights.shape[1] // width
    lat = latents.shape[1]
    scratch = buffers(n, size, g, patches, lat, width, FF // width, r)
    return pl.pallas_call(
        functools.partial(step_kernel, n, size, hands, scale, [k for k, _ in scratch]),
        name="whole_step",
        out_shape=(
            struct((g, patches, width), F32),
            struct((g, lat, width), F32),
            struct((g * lat, width), F32),
            struct(weights.shape, F32),
            struct((8, width), F32),
            struct((8, 128), F32),
        ),
        in_specs=[ANY] * 4 + [VMEM] + [ANY],
        out_specs=(ANY,) * 4 + (VMEM,) * 2,
        scratch_shapes=[s for _, s in scratch],
        compiler_params=params(8),
    )(weights, media, latents, cot, mask, norms)


def finish_kernel(steps, sums, squares, *refs):
    arrays, norms, passed = refs[:5], refs[5:9], refs[9:12]
    grad_norm, new_weights, new_norms, ffn, passed_out = (
        refs[12], refs[13:18], refs[18:22], refs[22], refs[23:26]
    )
    hold, low, through, load, store, moved = refs[26], refs[27], refs[28:31], refs[31], refs[32], refs[33]
    part = arrays[0].shape[1] // steps

    def span(c):
        return pl.ds(c * part, part)

    loads = [
        [
            pltpu.make_async_copy(src.at[:, span(c)], hold.at[i, :, span(c)], load.at[i, c])
            for i, src in enumerate(arrays)
        ]
        for c in range(steps)
    ]
    into = [pltpu.make_async_copy(a, t, moved.at[0, i]) for i, (a, t) in enumerate(zip(passed, through))]
    away = [
        pltpu.make_async_copy(t, a, moved.at[1, i]) for i, (t, a) in enumerate(zip(through, passed_out))
    ]
    for c in range(steps):
        for copy in loads[c]:
            copy.start()
    for copy in into:
        copy.start()
    norm_grads = sums[:6, :]
    square = jnp.sum(squares[...], axis=0, keepdims=True)
    square = jnp.sum(square, axis=1, keepdims=True)
    rest = jnp.sum(norm_grads * norm_grads, axis=0, keepdims=True)
    length = jnp.sqrt(square + jnp.sum(rest, axis=1, keepdims=True))
    clip = jnp.minimum(1.0, 1.0 / (length + 1e-06))
    grad_norm[...] = jnp.broadcast_to(length, grad_norm.shape)
    for ref, value in zip(
        new_norms, adamw_update(*(ref[...] for ref in norms), norm_grads, clip, 0.0)
    ):
        ref[...] = value
    ffn[...] = norm_grads[4:6]
    stores = []
    for c in range(steps):
        for copy in loads[c]:
            copy.wait()
        new = adamw_update(*(hold[i, :, span(c)] for i in range(5)), clip, 0.1)
        for i in range(4):
            hold[i, :, span(c)] = new[i]
        low[:, span(c)] = new[0].astype(BF16)
        for i, out in enumerate(new_weights):
            src = hold.at[i, :, span(c)] if i < 4 else low.at[:, span(c)]
            copy = pltpu.make_async_copy(src, out.at[:, span(c)], store.at[i, c])
            copy.start()
            stores.append(copy)
        if c < 3:
            into[c].wait()
            away[c].start()
    for copy in stores + away:
        copy.wait()


def finish(sums, squares, weights, grads, norms, passed):
    steps = 4
    rows, flat = grads.shape
    six, width = norms[0].shape
    return pl.pallas_call(
        functools.partial(finish_kernel, steps),
        name="finish",
        in_specs=[VMEM] * 2 + [ANY] * 5 + [VMEM] * 4 + [ANY] * 3,
        out_specs=[VMEM] + [ANY] * 5 + [VMEM] * 5 + [ANY] * 3,
        out_shape=[struct((1, 128), F32)] + [struct(grads.shape, F32)] * 4
        + [struct(grads.shape, BF16)] + [struct((six, width), F32)] * 4
        + [struct((2, width), F32)] + [struct(a.shape, F32) for a in passed],
        scratch_shapes=[
            pltpu.VMEM((5, rows, flat), F32), pltpu.VMEM((rows, flat), BF16),
        ] + [pltpu.VMEM(a.shape, F32) for a in passed]
        + [DMA((5, steps)), DMA((5, steps)), DMA((2, 3))],
        compiler_params=pltpu.CompilerParams(vmem_limit_bytes=VMEM_LIMIT),
    )(sums, squares, *weights, grads, *norms, *passed)


def norm_parts(values, gain_row, shift_row):
    average = jnp.mean(values, axis=-1, keepdims=True)
    centred = values - average
    spread_ = jnp.mean(centred * centred, axis=-1, keepdims=True)
    scaled = lax.rsqrt(spread_ + 1e-05)
    unit_rows = centred * scaled
    return (unit_rows * gain_row + shift_row, unit_rows, scaled)


def norm_back(grad_out, unit_rows, scaled, gain_row):
    inner_grad = grad_out * gain_row
    plain_mean = jnp.mean(inner_grad, axis=-1, keepdims=True)
    cross_mean = jnp.mean(inner_grad * unit_rows, axis=-1, keepdims=True)
    return scaled * (inner_grad - plain_mean - unit_rows * cross_mean)


def gain_terms(grad_out, unit_rows):
    width = grad_out.shape[-1]
    flat_grad = grad_out.reshape(-1, width)
    flat_unit = unit_rows.reshape(-1, width)
    return [jnp.sum(flat_grad * flat_unit, axis=0), jnp.sum(flat_grad, axis=0)]


def exact_gelu(values):
    return jax.nn.gelu(values, approximate=False)


def adamw_update(parameter, first_m, second_m, average, gradient, factor, decay_rate):
    clipped = gradient * factor
    new_first = 0.9 * first_m + 0.1 * clipped
    new_second = 0.999 * second_m + 0.001 * clipped * clipped
    first_hat = new_first / (1.0 - 0.9**STEP)
    second_hat = new_second / (1.0 - 0.999**STEP)
    new_param = parameter - 0.02 * (
        first_hat / (jnp.sqrt(second_hat) + 1e-08) + decay_rate * parameter
    )
    new_avg = 0.8 * average + 0.2 * new_param
    return (new_param, new_first, new_second, new_avg)


def dot32(spec, a, b):
    return jnp.einsum(spec, a, b, preferred_element_type=F32)


def general_step(n, size, media_tokens, patch_mask, latents, cotangent, weights, weights_first,
              weights_second, weights_average, norm_params, norm_first, norm_second, norm_average):
    g, patches, width = media_tokens.shape
    lat = latents.shape[1]
    blocks = weights.shape[0]
    r = width // (n * size)
    cols = width // size
    hands = HEADS // size
    scale = 1.0 / math.sqrt(width // HEADS)
    ups = FF // width
    own = g * lat
    media_gain, latent_gain, ffn_gain = 1.0 + norm_params[0], 1.0 + norm_params[2], 1.0 + norm_params[4]

    held = weights.astype(BF16).reshape(blocks, r, width)
    qs = held[:3].reshape(3, r, size, cols).transpose(2, 0, 1, 3)
    media_norm, media_unit, media_scale = norm_parts(media_tokens, media_gain, norm_params[1])
    latent_norm, latent_unit, latent_scale = norm_parts(latents, latent_gain, norm_params[3])
    cot = cotangent.reshape(own, width)
    count_rows = (g + 15) // 16 * 16
    counts = jnp.sum((patch_mask > 0).astype(F32), axis=1)
    counts = jnp.broadcast_to(jnp.pad(counts, (0, count_rows - g))[:, None], (count_rows, 128))

    wqkv, wo, up, dn, nm, nl, dy, cn = spread(
        qs, held[3], held[4 : 4 + ups], held[4 + ups :],
        media_norm.astype(BF16), latent_norm.astype(BF16), cot.astype(BF16), counts, n, size,
    )
    wqkv = wqkv.reshape(3, width, cols)
    wo = wo.reshape(width, width)
    up = up.reshape(-1, width)
    dn = dn.reshape(-1, width)
    nm = nm.reshape(g * size * patches, width)
    nl = nl.reshape(g * size * lat, width)
    dy = dy.reshape(size * own, width)
    real = jnp.sum(cn[:, :g, 0], axis=0).astype(jnp.int32)

    def by_image(a):
        return a.astype(BF16).reshape(g, -1, cols)

    q = by_image(dot32("rd,de->re", nl, wqkv[0]))
    kp, kl = by_image(dot32("rd,de->re", nm, wqkv[1])), by_image(dot32("rd,de->re", nl, wqkv[1]))
    vp, vl = by_image(dot32("rd,de->re", nm, wqkv[2])), by_image(dot32("rd,de->re", nl, wqkv[2]))
    mixed = attend(real, q, kp, kl, vp, vl, hands, scale)
    ab = to_rows(mixed.reshape(g, size, lat, cols), size, 1).reshape(own, width)

    hidden = latents.reshape(own, width) + dot32("rd,de->re", ab, wo)
    ffn_norm, ffn_unit, ffn_scale = norm_parts(hidden, ffn_gain, norm_params[5])
    nf = join_rows(ffn_norm.astype(BF16), size, 2).reshape(size * own, width)
    u = dot32("rd,fd->rf", nf, up)
    active, pull = jax.vjp(exact_gelu, u)
    gb = active.astype(BF16)
    y_part = dot32("rf,fd->rd", gb, dn).astype(BF16)
    du = pull(dot32("rd,fd->rf", dy, dn))[0].astype(BF16)
    f_part = dot32("rf,fd->rd", du, up).astype(BF16)
    g_dn = dot32("rf,rd->fd", gb, dy).astype(BF16)
    g_up = dot32("rf,rd->fd", du, nf).astype(BF16)
    both = split_rows(jnp.stack([y_part, f_part]).reshape(2, 2, 2, own, width), 3)
    latents_out = (hidden + both[0]).reshape(g, lat, width)
    d_ffn = both[1]
    ffn_terms = gain_terms(d_ffn, ffn_unit)
    d_hidden = cot + norm_back(d_ffn, ffn_unit, ffn_scale, ffn_gain)

    do = d_hidden.astype(BF16)
    g_wo = dot32("rd,re->de", ab, do).astype(BF16)
    da = dot32("re,de->rd", do, wo).astype(BF16).reshape(g, lat, width)
    da = to_heads(da, size, 4).reshape(g, size * lat, cols)
    dq, dkp, dkl, dvp, dvl = attend_back(real, q, kp, kl, vp, vl, da, hands, scale)

    def flat(a):
        return a.reshape(-1, cols)

    dq, dkp, dkl, dvp, dvl = flat(dq), flat(dkp), flat(dkl), flat(dvp), flat(dvl)
    g_qkv = jnp.stack([
        dot32("rd,re->de", nl, dq),
        dot32("rd,re->de", nm, dkp) + dot32("rd,re->de", nl, dkl),
        dot32("rd,re->de", nm, dvp) + dot32("rd,re->de", nl, dvl),
    ]).astype(BF16)
    d_nm = (dot32("re,de->rd", dkp, wqkv[1]) + dot32("re,de->rd", dvp, wqkv[2])).astype(BF16)
    d_nl = (
        dot32("re,de->rd", dkl, wqkv[1]) + dot32("re,de->rd", dvl, wqkv[2])
        + dot32("re,de->rd", dq, wqkv[0])
    ).astype(BF16)

    oq, ow, ou, od, d_media, d_latent = collect(
        g_qkv.reshape(3, n, size, r, cols), g_wo.reshape(n, 2, 2, r, width),
        g_up.reshape(ups, n, r, width), g_dn.reshape(ups, n, r, width),
        d_nm.reshape(g, 2, 2, patches, width), d_nl.reshape(g, 2, 2, lat, width), n, size,
    )
    media_grad = norm_back(d_media, media_unit, media_scale, media_gain)
    latents_grad = d_hidden.reshape(g, lat, width) + norm_back(
        d_latent, latent_unit, latent_scale, latent_gain
    )
    grads = jnp.concatenate([
        oq.transpose(1, 2, 0, 3).reshape(3, r, width), ow[None], ou, od,
    ])
    square = jnp.broadcast_to(jnp.sum(grads * grads), (width,))
    rows = jnp.stack(
        gain_terms(d_media, media_unit) + gain_terms(d_latent, latent_unit) + ffn_terms
        + [square, jnp.zeros_like(square)]
    )
    sums = total(rows, n, size)
    return latents_out, media_grad, latents_grad, grads, sums[:6], sums[6, 0]


def on_device(n, size, media_tokens, patch_mask, latents, cotangent, weights, weights_first,
              weights_second, weights_average, norm_params, norm_first, norm_second, norm_average):
    g, patches, width = media_tokens.shape
    lat = latents.shape[1]
    r = width // (n * size)
    arrays = (
        media_tokens, patch_mask, latents, cotangent, weights, weights_first, weights_second,
        weights_average, norm_params, norm_first, norm_second, norm_average,
    )
    if r % 16 or lat % 16 or size != 4 or n != 2 * size or FF != 4 * width:
        latents_out, media_grad, latents_grad, grads, norm_grads, square = general_step(
            n, size, *arrays
        )
    else:
        media_grad, latents_grad, latents_out, grads, sums, squares = whole_step(
            weights, media_tokens, latents, cotangent, patch_mask, norm_params,
            n, size, HEADS // size, 1.0 / math.sqrt(width // HEADS),
        )
        done = finish(
            sums, squares, (weights, weights_first, weights_second, weights_average), grads,
            (norm_params, norm_first, norm_second, norm_average),
            (latents_out.reshape(g, lat, width), media_grad, latents_grad),
        )
        return (
            *done[11:14], done[0][0, 0], done[1], done[5], *done[2:5], *done[6:11],
        )
    grad_norm = jnp.sqrt(square + jnp.sum(norm_grads * norm_grads))
    clip = jnp.minimum(1.0, 1.0 / (grad_norm + 1e-06))
    new_w, new_first, new_second, new_avg = adamw_update(
        weights, weights_first, weights_second, weights_average,
        grads.reshape(weights.shape), clip, 0.1,
    )
    new_n, new_nf, new_ns, new_na = adamw_update(
        norm_params, norm_first, norm_second, norm_average, norm_grads, clip, 0.0
    )
    return (
        latents_out, media_grad, latents_grad, grad_norm, new_w, new_w.astype(BF16), new_first,
        new_second, new_avg, new_n, new_nf, new_ns, new_na, norm_grads[4:6],
    )


def solution(mesh):
    n, size = mesh.shape["dp"], mesh.shape["patch"]
    rows, weight = P("dp", "patch", None), P(None, ("dp", "patch"))
    return jax.shard_map(
        functools.partial(on_device, n, size),
        mesh=mesh,
        in_specs=(rows, P("dp", "patch"), rows, rows) + (weight,) * 4 + (P(),) * 4,
        out_specs=(rows, rows, rows, P()) + (weight,) * 5 + (P(),) * 5,
        check_vma=False,
    )
```

```python
import functools
import math

import jax
import jax.numpy as jnp
from jax import lax
from jax.experimental import pallas as pl
from jax.experimental.pallas import tpu as pltpu
from jax.sharding import PartitionSpec as P

HEADS = 16
FF = 4096
STEP = 7
MESH = pl.DeviceIdType.MESH
F32 = jnp.float32
BF16 = jnp.bfloat16
ANY = pl.BlockSpec(memory_space=pl.ANY)
VMEM = pl.BlockSpec(memory_space=pltpu.VMEM)
DMA = pltpu.SemaphoreType.DMA
VMEM_LIMIT = 64 * 1024 * 1024 - 65536


def struct(shape, kind):
    return jax.ShapeDtypeStruct(shape, kind)


def place():
    d, p = lax.axis_index("dp"), lax.axis_index("patch")
    return d, p, lax.div(d, 2), lax.rem(d, 2), lax.div(p, 2), lax.rem(p, 2)


def remote(src, dst, send, recv, to):
    return pltpu.make_async_remote_copy(
        src_ref=src, dst_ref=dst, send_sem=send, recv_sem=recv, device_id=to, device_id_type=MESH
    )


def greet(peers):
    barrier = pltpu.get_barrier_semaphore()
    for to in peers:
        pl.semaphore_signal(barrier, inc=1, device_id=to, device_id_type=MESH)
    return functools.partial(pl.semaphore_wait, barrier, len(peers))


def meet(always, maybe=()):
    barrier = pltpu.get_barrier_semaphore()
    count = len(always)
    for to in always:
        pl.semaphore_signal(barrier, inc=1, device_id=to, device_id_type=MESH)
    for there, to in maybe:

        @pl.when(there)
        def _(to=to):
            pl.semaphore_signal(barrier, inc=1, device_id=to, device_id_type=MESH)

        count = count + there.astype(jnp.int32)
    pl.semaphore_wait(barrier, count)


def patch_peers(d, p, size):
    return [(d, lax.rem(p + k, size)) for k in range(1, size)]


def params(number):
    return pltpu.CompilerParams(
        collective_id=number, has_side_effects=True, vmem_limit_bytes=VMEM_LIMIT
    )


def spread_kernel(chain, size, qs, wos, ups, dns, nms, nls, dys, cns,
                  wqkv, wo, up, dn, nm, nl, dy, cn,
                  loc, a_s, a_r, su, sd, sy, rz, ry, xs, xr, cs, cr):
    d, p, z, y, x, c = place()
    above, below = z + 1 < chain, z > 0
    up_dev, dn_dev = ((z + 1) * 2 + y, p), ((z - 1) * 2 + y, p)
    y_dev, x_dev, c_dev = (z * 2 + 1 - y, p), (d, (1 - x) * 2 + c), (d, x * 2 + 1 - c)
    px, pc = (1 - x) * 2 + c, x * 2 + 1 - c
    pd = (1 - x) * 2 + 1 - c
    meet(patch_peers(d, p, size) + [y_dev], [(above, up_dev), (below, dn_dev)])

    own = [
        (qs.at[p], wqkv.at[:, d, p]), (wos, wo.at[d, p]), (ups, up.at[:, d]), (dns, dn.at[:, d]),
        (nms, nm.at[:, p]), (nls, nl.at[:, p]), (dys, dy.at[p]), (cns, cn.at[p]),
    ]
    local = [pltpu.make_async_copy(a, b, loc.at[i]) for i, (a, b) in enumerate(own)]
    for copy in local:
        copy.start()
    swaps = []
    for k in range(1, size):
        q = lax.rem(p + k, size)
        swaps.append(remote(qs.at[q], wqkv.at[:, d, p], a_s.at[k], a_r.at[k], (d, q)))
    for copy in swaps:
        copy.start()

    rows = [(nms, nm), (nls, nl), (cns, cn), (dys, dy)]

    def slot(j, q):
        ref = rows[j][1] if j < 4 else wo
        return ref.at[q] if j in (2, 3) else ref.at[:, q]

    def row_copies(j):
        src = rows[j][0] if j < 4 else slot(j, p)
        return (
            remote(src, slot(j, p), xs.at[j], xr.at[j], x_dev),
            remote(src, slot(j, p), cs.at[j, 0], cr.at[j, 0], c_dev),
            remote(slot(j, px), slot(j, px), cs.at[j, 1], cr.at[j, 1], c_dev),
        )

    def start_rows(j):
        to_x, to_c, _ = row_copies(j)
        to_x.start()
        to_c.start()

    def pass_rows(j):
        to_x, _, on = row_copies(j)
        to_x.wait_recv()
        on.start()

    def end_rows(j):
        to_x, to_c, on = row_copies(j)
        to_c.wait_recv()
        on.wait_recv()
        to_x.wait_send()
        to_c.wait_send()
        on.wait_send()

    for j in range(4):
        start_rows(j)

    def piece(i, dd):
        return (wqkv.at[:, dd], wo.at[dd, p], up.at[:, dd], dn.at[:, dd])[i]

    first = (wqkv.at[:, d], wos, ups, dns)

    def hop(i, zz, sends, to, own_src=False):
        src = first[i] if own_src else piece(i, zz * 2 + y)
        return remote(src, piece(i, zz * 2 + y), sends.at[i, zz], rz.at[i, zz], to)

    def over(i, zz, own_src=False):
        src = first[i] if own_src else piece(i, zz * 2 + y)
        return remote(src, piece(i, zz * 2 + y), sy.at[i, zz], ry.at[i, zz], y_dev)

    def start_own(i):
        @pl.when(above)
        def _():
            hop(i, z, su, up_dev, True).start()

        @pl.when(below)
        def _():
            hop(i, z, sd, dn_dev, True).start()

        over(i, z, True).start()

    def forward(i):
        def step(s, carry):
            @pl.when(z - s >= 0)
            def _():
                hop(i, z - s, su, up_dev).wait_recv()

                @pl.when(above)
                def _():
                    hop(i, z - s, su, up_dev).start()

                over(i, z - s).start()

            @pl.when(z + s < chain)
            def _():
                hop(i, z + s, sd, dn_dev).wait_recv()

                @pl.when(below)
                def _():
                    hop(i, z + s, sd, dn_dev).start()

                over(i, z + s).start()

            return carry

        lax.fori_loop(1, chain, step, 0)

    def arrived(i):
        def step(zz, carry):
            src = piece(i, zz * 2 + 1 - y)
            remote(src, src, sy.at[i, zz], ry.at[i, zz], y_dev).wait_recv()
            return carry

        lax.fori_loop(0, chain, step, 0)

    def sent(i):
        def step(zz, carry):
            over(i, zz).wait_send()

            @pl.when(jnp.logical_and(above, zz <= z))
            def _():
                hop(i, zz, su, up_dev).wait_send()

            @pl.when(jnp.logical_and(below, zz >= z))
            def _():
                hop(i, zz, sd, dn_dev).wait_send()

            return carry

        lax.fori_loop(0, chain, step, 0)

    local[0].wait()
    for copy in swaps:
        copy.wait_recv()
    start_own(0)
    start_own(1)
    forward(0)
    start_own(2)
    forward(1)
    start_own(3)
    local[1].wait()
    arrived(1)
    start_rows(4)
    forward(2)
    for j in range(5):
        pass_rows(j)
    forward(3)
    arrived(0)
    arrived(2)
    arrived(3)
    for j in range(5):
        end_rows(j)
    for copy in swaps:
        copy.wait_send()
    for i in range(4):
        sent(i)
    for copy in local[2:]:
        copy.wait()


def spread(qs, wos, ups, dns, nms, nls, dys, cns, n, size):
    _, three, r, cols = qs.shape
    width = wos.shape[1]
    chain = n // 2
    g, patches, _ = nms.shape
    lat = nls.shape[1]
    return pl.pallas_call(
        functools.partial(spread_kernel, chain, size),
        name="spread",
        out_shape=(
            struct((three, n, size, r, cols), BF16),
            struct((n, size, r, width), BF16),
            struct((ups.shape[0], n, r, width), BF16),
            struct((dns.shape[0], n, r, width), BF16),
            struct((g, size, patches, width), BF16),
            struct((g, size, lat, width), BF16),
            struct((size,) + dys.shape, BF16),
            struct((size,) + cns.shape, F32),
        ),
        in_specs=[VMEM] * 8,
        out_specs=(ANY,) * 8,
        scratch_shapes=[
            DMA((8,)), DMA((size,)), DMA((size,)),
            DMA((4, chain)), DMA((4, chain)), DMA((4, chain)), DMA((4, chain)), DMA((4, chain)),
            DMA((5,)), DMA((5,)), DMA((5, 2)), DMA((5, 2)),
        ],
        compiler_params=params(0),
    )(qs, wos, ups, dns, nms, nls, dys, cns)


def to_rows_kernel(size, src, out, loc, ss, rs):
    d, p = lax.axis_index("dp"), lax.axis_index("patch")
    cols = src.shape[3]
    meet(patch_peers(d, p, size))
    here = out.at[:, :, pl.ds(pl.multiple_of(p * cols, cols), cols)]
    copies = []
    for k in range(1, size):
        q = lax.rem(p + k, size)
        copies.append(remote(src.at[:, q], here, ss.at[k], rs.at[k], (d, q)))
    for copy in copies:
        copy.start()
    mine = pltpu.make_async_copy(src.at[:, p], here, loc)
    mine.start()
    mine.wait()
    for copy in copies:
        copy.wait()


def to_rows(src, size, number):
    g, _, lat, cols = src.shape
    return pl.pallas_call(
        functools.partial(to_rows_kernel, size),
        name="to_rows",
        out_shape=struct((g, lat, size * cols), src.dtype),
        in_specs=[VMEM],
        out_specs=VMEM,
        scratch_shapes=[DMA, DMA((size,)), DMA((size,))],
        compiler_params=params(number),
    )(src)


def to_heads_kernel(size, src, out, loc, ss, rs):
    d, p = lax.axis_index("dp"), lax.axis_index("patch")
    cols = out.shape[3]
    meet(patch_peers(d, p, size))

    def part(q):
        return src.at[:, :, pl.ds(pl.multiple_of(q * cols, cols), cols)]

    copies = []
    for k in range(1, size):
        q = lax.rem(p + k, size)
        copies.append(remote(part(q), out.at[:, p], ss.at[k], rs.at[k], (d, q)))
    for copy in copies:
        copy.start()
    mine = pltpu.make_async_copy(part(p), out.at[:, p], loc)
    mine.start()
    mine.wait()
    for copy in copies:
        copy.wait()


def to_heads(src, size, number):
    g, lat, width = src.shape
    return pl.pallas_call(
        functools.partial(to_heads_kernel, size),
        name="to_heads",
        out_shape=struct((g, size, lat, width // size), src.dtype),
        in_specs=[VMEM],
        out_specs=VMEM,
        scratch_shapes=[DMA, DMA((size,)), DMA((size,))],
        compiler_params=params(number),
    )(src)


def join_rows_kernel(src, out, loc, ss, rs):
    d, p, z, y, x, c = place()
    x_dev, c_dev = (d, (1 - x) * 2 + c), (d, x * 2 + 1 - c)
    px = (1 - x) * 2 + c
    meet([x_dev, c_dev])
    to_x = remote(src, out.at[p], ss.at[0], rs.at[0], x_dev)
    to_c = remote(src, out.at[p], ss.at[1], rs.at[1], c_dev)
    on = remote(out.at[px], out.at[px], ss.at[2], rs.at[2], c_dev)
    to_x.start()
    to_c.start()
    mine = pltpu.make_async_copy(src, out.at[p], loc)
    mine.start()
    to_x.wait_recv()
    on.start()
    mine.wait()
    to_c.wait()
    on.wait()
    to_x.wait_send()


def join_rows(src, size, number):
    return pl.pallas_call(
        join_rows_kernel,
        name="join_rows",
        out_shape=struct((size,) + src.shape, src.dtype),
        in_specs=[VMEM],
        out_specs=VMEM,
        scratch_shapes=[DMA, DMA((3,)), DMA((3,))],
        compiler_params=params(number),
    )(src)


def split_rows_kernel(ins, src, out, half, mid, quarter, ss, rs):
    d, p, z, y, x, c = place()
    x_dev, c_dev = (d, (1 - x) * 2 + c), (d, x * 2 + 1 - c)
    meet([x_dev, c_dev])
    first = [remote(src.at[i, :, 1 - c], half.at[i], ss.at[i], rs.at[i], c_dev) for i in range(ins)]
    for copy in first:
        copy.start()
    second = []
    for i in range(ins):
        first[i].wait_recv()
        mid[i] = (half[i, 1 - x].astype(F32) + src[i, 1 - x, c].astype(F32)).astype(BF16)
        copy = remote(mid.at[i], quarter.at[i], ss.at[ins + i], rs.at[ins + i], x_dev)
        copy.start()
        second.append(copy)
    for i in range(ins):
        out[i] = half[i, x].astype(F32) + src[i, x, c].astype(F32)
    for i in range(ins):
        second[i].wait_recv()
        out[i] = out[i] + quarter[i].astype(F32)
    for copy in first + second:
        copy.wait_send()


def split_rows(src, number):
    ins, _, _, rows, width = src.shape
    return pl.pallas_call(
        functools.partial(split_rows_kernel, ins),
        name="split_rows",
        out_shape=struct((ins, rows, width), F32),
        in_specs=[VMEM],
        out_specs=VMEM,
        scratch_shapes=[
            pltpu.VMEM((ins, 2, rows, width), BF16),
            pltpu.VMEM((ins, rows, width), BF16),
            pltpu.VMEM((ins, rows, width), BF16),
            DMA((2 * ins,)), DMA((2 * ins,)),
        ],
        compiler_params=params(number),
    )(src)


def head_rows(q, hands):
    rows, cols = q.shape
    size = cols // hands
    lane = lax.broadcasted_iota(jnp.int32, (rows, cols), 1)
    zero = jnp.zeros_like(q)
    parts = [
        jnp.where(jnp.logical_and(lane >= h * size, lane < (h + 1) * size), q, zero)
        for h in range(hands)
    ]
    return jnp.concatenate(parts, axis=0)


def own_columns(full, hands):
    rows, cols = full.shape[0] // hands, full.shape[1]
    size = cols // hands
    lane = lax.broadcasted_iota(jnp.int32, (rows, cols), 1)
    out = jnp.zeros((rows, cols), F32)
    for h in range(hands):
        keep = jnp.logical_and(lane >= h * size, lane < (h + 1) * size)
        out = jnp.where(keep, full[h * rows : (h + 1) * rows], out)
    return out


def nt(a, b):
    return lax.dot_general(a, b, (((1,), (1,)), ((), ())), preferred_element_type=F32)


def nn(a, b):
    return lax.dot_general(a, b, (((1,), (0,)), ((), ())), preferred_element_type=F32)


def tn(a, b):
    return lax.dot_general(a, b, (((0,), (0,)), ((), ())), preferred_element_type=F32)


def soft(qb, kp, kl, real, scale):
    sp = nt(qb, kp) * scale
    sl = nt(qb, kl) * scale
    key = lax.broadcasted_iota(jnp.int32, sp.shape, 1).astype(F32)
    sp = jnp.where(key < real, sp, -1e30)
    peak = jnp.maximum(jnp.max(sp, axis=1, keepdims=True), jnp.max(sl, axis=1, keepdims=True))
    ep, el = jnp.exp(sp - peak), jnp.exp(sl - peak)
    total = jnp.sum(ep, axis=1, keepdims=True) + jnp.sum(el, axis=1, keepdims=True)
    return ep / total, el / total


def attend_kernel(hands, scale, real, q, kp, kl, vp, vl, out):
    g = pl.program_id(0)
    qb = head_rows(q[0], hands)
    pp, plat = soft(qb, kp[0], kl[0], real[g].astype(F32), scale)
    full = nn(pp.astype(BF16), vp[0]) + nn(plat.astype(BF16), vl[0])
    out[0] = own_columns(full, hands).astype(BF16)


def attend(real, q, kp, kl, vp, vl, hands, scale):
    g, lat, cols = q.shape
    patches = kp.shape[1]

    def spec(rows):
        return pl.BlockSpec((1, rows, cols), lambda i, real: (i, 0, 0))

    return pl.pallas_call(
        functools.partial(attend_kernel, hands, scale),
        name="attend",
        grid_spec=pltpu.PrefetchScalarGridSpec(
            num_scalar_prefetch=1,
            grid=(g,),
            in_specs=[spec(lat), spec(patches), spec(lat), spec(patches), spec(lat)],
            out_specs=spec(lat),
        ),
        out_shape=struct((g, lat, cols), BF16),
        compiler_params=pltpu.CompilerParams(dimension_semantics=("arbitrary",)),
    )(real, q, kp, kl, vp, vl)


def attend_back_kernel(hands, scale, real, q, kp, kl, vp, vl, da, dq, dkp, dkl, dvp, dvl):
    g = pl.program_id(0)
    qb = head_rows(q[0], hands)
    dab = head_rows(da[0], hands)
    pp, plat = soft(qb, kp[0], kl[0], real[g].astype(F32), scale)
    gp, gl = nt(dab, vp[0]), nt(dab, vl[0])
    delta = jnp.sum(pp * gp, axis=1, keepdims=True) + jnp.sum(plat * gl, axis=1, keepdims=True)
    sp, sl = (pp * (gp - delta)).astype(BF16), (plat * (gl - delta)).astype(BF16)
    dvp[0] = tn(pp.astype(BF16), dab).astype(BF16)
    dvl[0] = tn(plat.astype(BF16), dab).astype(BF16)
    dkp[0] = (tn(sp, qb) * scale).astype(BF16)
    dkl[0] = (tn(sl, qb) * scale).astype(BF16)
    full = nn(sp, kp[0]) + nn(sl, kl[0])
    dq[0] = (own_columns(full, hands) * scale).astype(BF16)


def attend_back(real, q, kp, kl, vp, vl, da, hands, scale):
    g, lat, cols = q.shape
    patches = kp.shape[1]

    def spec(rows):
        return pl.BlockSpec((1, rows, cols), lambda i, real: (i, 0, 0))

    return pl.pallas_call(
        functools.partial(attend_back_kernel, hands, scale),
        name="attend_back",
        grid_spec=pltpu.PrefetchScalarGridSpec(
            num_scalar_prefetch=1,
            grid=(g,),
            in_specs=[spec(lat), spec(patches), spec(lat), spec(patches), spec(lat), spec(lat)],
            out_specs=[spec(lat), spec(patches), spec(lat), spec(patches), spec(lat)],
        ),
        out_shape=(
            struct((g, lat, cols), BF16),
            struct((g, patches, cols), BF16),
            struct((g, lat, cols), BF16),
            struct((g, patches, cols), BF16),
            struct((g, lat, cols), BF16),
        ),
        compiler_params=pltpu.CompilerParams(dimension_semantics=("arbitrary",)),
    )(real, q, kp, kl, vp, vl, da)


def collect_kernel(chain, size, gq, gw, gu, gd, kp, kl,
                   oq, ow, ou, od, okp, okl,
                   yq, yw, yu, yd, uq, uw, uu, ud, dq, dw, du, dd,
                   wc, wsum, wx, total, kc, kx, lc, lx, fin,
                   ys, yr, us, ur, ds, dr, ks, kr, qs, qr):
    d, p, z, y, x, c = place()
    above, below = z + 1 < chain, z > 0
    up_dev, dn_dev = ((z + 1) * 2 + y, p), ((z - 1) * 2 + y, p)
    y_dev, x_dev, c_dev = (z * 2 + 1 - y, p), (d, (1 - x) * 2 + c), (d, x * 2 + 1 - c)
    meet(patch_peers(d, p, size) + [y_dev], [(above, up_dev), (below, dn_dev)])

    mine = (
        lambda k: gq.at[:, k], lambda k: total.at[k], lambda k: gu.at[:, k], lambda k: gd.at[:, k]
    )
    land_y, land_u, land_d = (yq, yw, yu, yd), (uq, uw, uu, ud), (dq, dw, du, dd)

    def over(i, zz):
        return remote(
            mine[i](zz * 2 + 1 - y), land_y[i].at[zz], ys.at[i, zz], yr.at[i, zz], y_dev
        )

    def send_over(i):
        def step(zz, carry):
            over(i, zz).start()
            return carry

        lax.fori_loop(0, chain, step, 0)

    def add_over(i):
        def step(zz, carry):
            over(i, zz).wait_recv()
            have = mine[i](zz * 2 + y)
            land_y[i][zz] = (land_y[i][zz].astype(F32) + have[...].astype(F32)).astype(BF16)
            return carry

        lax.fori_loop(0, chain, step, 0)

    def rise(i, zz):
        return remote(land_y[i].at[zz], land_u[i].at[zz], us.at[i, zz], ur.at[i, zz], up_dev)

    def fall(i, zz):
        return remote(land_y[i].at[zz], land_d[i].at[zz], ds.at[i, zz], dr.at[i, zz], dn_dev)

    def gather(i, zz, land):
        land_y[i][zz] = (land_y[i][zz].astype(F32) + land[i][zz].astype(F32)).astype(BF16)

    def along(i):
        def step(k, carry):
            s = chain - k

            @pl.when(z + s < chain)
            def _():
                @pl.when(below)
                def _():
                    rise(i, z + s).wait_recv()
                    gather(i, z + s, land_u)

                rise(i, z + s).start()

            @pl.when(z - s >= 0)
            def _():
                @pl.when(above)
                def _():
                    fall(i, z - s).wait_recv()
                    gather(i, z - s, land_d)

                fall(i, z - s).start()

            return carry

        lax.fori_loop(1, chain, step, 0)

    def finish(i, write):
        write(land_y[i][z].astype(F32))

        @pl.when(below)
        def _():
            rise(i, z).wait_recv()
            write(land_u[i][z].astype(F32), True)

        @pl.when(above)
        def _():
            fall(i, z).wait_recv()
            write(land_d[i][z].astype(F32), True)

    def into(ref):
        def write(value, more=False):
            ref[...] = ref[...] + value if more else value

        return write

    def sent(i):
        def step(zz, carry):
            over(i, zz).wait_send()

            @pl.when(zz > z)
            def _():
                rise(i, zz).wait_send()

            @pl.when(zz < z)
            def _():
                fall(i, zz).wait_send()

            return carry

        lax.fori_loop(0, chain, step, 0)

    send_over(2)
    w_core = remote(gw.at[:, :, 1 - c], wc, ks.at[0], kr.at[0], c_dev)
    p_core = remote(kp.at[:, :, 1 - c], kc, ks.at[1], kr.at[1], c_dev)
    l_core = remote(kl.at[:, :, 1 - c], lc, ks.at[2], kr.at[2], c_dev)
    w_core.start()
    p_core.start()
    l_core.start()
    send_over(3)
    send_over(0)

    w_core.wait_recv()

    def w_add(k, carry):
        wsum[k] = (wc[k, 1 - x].astype(F32) + gw[k, 1 - x, c].astype(F32)).astype(BF16)
        return carry

    lax.fori_loop(0, 2 * chain, w_add, 0)
    w_x = remote(wsum, wx, ks.at[3], kr.at[3], x_dev)
    w_x.start()

    p_core.wait_recv()
    images = kp.shape[0]

    def p_add(k, carry):
        kc[k] = (kc[k].astype(F32) + kp[k, :, c].astype(F32)).astype(BF16)
        return carry

    lax.fori_loop(0, images, p_add, 0)
    p_x = remote(kc.at[:, 1 - x], kx, ks.at[4], kr.at[4], x_dev)
    p_x.start()
    l_core.wait_recv()

    def l_add(k, carry):
        lc[k] = (lc[k].astype(F32) + kl[k, :, c].astype(F32)).astype(BF16)
        return carry

    lax.fori_loop(0, images, l_add, 0)
    l_x = remote(lc.at[:, 1 - x], lx, ks.at[5], kr.at[5], x_dev)
    l_x.start()

    w_x.wait_recv()

    def w_last(k, carry):
        total[k] = (
            wc[k, x].astype(F32) + gw[k, x, c].astype(F32) + wx[k].astype(F32)
        ).astype(BF16)
        return carry

    lax.fori_loop(0, 2 * chain, w_last, 0)
    send_over(1)

    add_over(2)
    along(2)
    add_over(3)
    along(3)
    add_over(0)
    along(0)
    add_over(1)
    along(1)
    finish(2, into(ou))
    finish(3, into(od))
    finish(0, into(fin))
    swaps = []
    for k in range(1, size):
        q = lax.rem(p + k, size)
        swaps.append(remote(fin.at[:, q], oq.at[p], qs.at[k], qr.at[k], (d, q)))
    for copy in swaps:
        copy.start()
    finish(1, into(ow))
    oq[p] = fin[:, p]

    p_x.wait_recv()

    def p_last(k, carry):
        okp[k] = kc[k, x].astype(F32) + kx[k].astype(F32)
        return carry

    lax.fori_loop(0, images, p_last, 0)
    l_x.wait_recv()

    def l_last(k, carry):
        okl[k] = lc[k, x].astype(F32) + lx[k].astype(F32)
        return carry

    lax.fori_loop(0, images, l_last, 0)
    for copy in swaps:
        copy.wait()
    for i in range(4):
        sent(i)
    for copy in (w_core, p_core, l_core, w_x, p_x, l_x):
        copy.wait_send()


def collect(gq, gw, gu, gd, kp, kl, n, size):
    chain = n // 2
    three, _, _, r, cols = gq.shape
    width = gw.shape[-1]
    fu, fd = gu.shape[0], gd.shape[0]
    g, two, _, patches, _ = kp.shape
    lat = kl.shape[3]
    lands = [
        ((three, size, r, cols)), ((r, width)), ((fu, r, width)), ((fd, r, width)),
    ]
    stage = [pltpu.VMEM((chain,) + s, BF16) for s in lands]
    return pl.pallas_call(
        functools.partial(collect_kernel, chain, size),
        name="collect",
        out_shape=(
            struct((size, three, r, cols), F32),
            struct((r, width), F32),
            struct((fu, r, width), F32),
            struct((fd, r, width), F32),
            struct((g, patches, width), F32),
            struct((g, lat, width), F32),
        ),
        in_specs=[VMEM] * 6,
        out_specs=(VMEM,) * 6,
        scratch_shapes=stage * 3
        + [
            pltpu.VMEM((n, two, r, width), BF16),
            pltpu.VMEM((n, r, width), BF16),
            pltpu.VMEM((n, r, width), BF16),
            pltpu.VMEM((n, r, width), BF16),
            pltpu.VMEM((g, two, patches, width), BF16),
            pltpu.VMEM((g, patches, width), BF16),
            pltpu.VMEM((g, two, lat, width), BF16),
            pltpu.VMEM((g, lat, width), BF16),
            pltpu.VMEM((three, size, r, cols), F32),
        ]
        + [DMA((4, chain))] * 6
        + [DMA((6,)), DMA((6,)), DMA((size,)), DMA((size,))],
        compiler_params=params(6),
    )(gq, gw, gu, gd, kp, kl)


def total_kernel(hops, src, out, hold, land, ss, rs):
    d, p = lax.axis_index("dp"), lax.axis_index("patch")

    def flip(v, bit):
        return v + bit - 2 * bit * lax.rem(lax.div(v, bit), 2)

    to = [(d, flip(p, b)) if kind else (flip(d, b), p) for kind, b in hops]
    meet(to)
    sends = []
    for i, who in enumerate(to):
        copy = remote(src if i == 0 else hold.at[i], land.at[i], ss.at[i], rs.at[i], who)
        copy.start()
        copy.wait_recv()
        sends.append(copy)
        value = (src[...] if i == 0 else hold[i]) + land[i]
        if i + 1 < len(to):
            hold[i + 1] = value
        else:
            out[...] = value
    for copy in sends:
        copy.wait_send()


def total(src, n, size):
    hops = [(True, 1 << b) for b in range(size.bit_length() - 1)]
    hops += [(False, 1 << b) for b in range(n.bit_length() - 1)]
    return pl.pallas_call(
        functools.partial(total_kernel, hops),
        name="total",
        out_shape=struct(src.shape, F32),
        in_specs=[VMEM],
        out_specs=VMEM,
        scratch_shapes=[
            pltpu.VMEM((len(hops),) + src.shape, F32),
            pltpu.VMEM((len(hops),) + src.shape, F32),
            DMA((len(hops),)), DMA((len(hops),)),
        ],
        compiler_params=params(7),
    )(src)


class Names:
    def __init__(self, pairs):
        self.__dict__.update(pairs)


def aligned(start, step, count=None):
    return pl.ds(pl.multiple_of(start * step, step), count or step)


def each(lo, hi, body):
    def step(k, carry):
        body(k)
        return carry

    lax.fori_loop(lo, hi, step, 0)


def unit_of(x):
    mean = jnp.mean(x, axis=-1, keepdims=True)
    centred = x - mean
    spread_ = jnp.mean(centred * centred, axis=-1, keepdims=True)
    scaled = lax.rsqrt(spread_ + 1e-05)
    return centred * scaled, scaled


def column_sum(a):
    return jnp.sum(a, axis=0, keepdims=True)


INPUTS = ("weights", "media", "latents", "cot", "mask", "norms")
OUTPUTS = ("media_grad", "latents_grad", "latents_out", "grads", "sums", "squares")


def crowd_of(images):
    return 3 if images % 3 == 0 else 1


def buffers(n, size, g, patches, lat, width, ups, r):
    chain, cols, own = n // 2, width // size, g * lat
    keys, rows, tiles = size * (patches + lat), patches + lat, width // 256
    crowd = crowd_of(g)
    crowds = g // crowd
    low = {
        "wqkv": (3, width, cols), "wo": (width // size, width), "ud": (3, ups, n * r, width),
        "nm": (g, size * patches, width), "nl": (g, size * lat, width), "dy": (size * own, width), "doa": (g, size * lat, width),
        "q": (g, size * lat, cols), "k": (g, keys, cols), "v": (g, keys, cols),
        "mixed": (g, size * lat, cols), "nf": (size * own, width),
        "hpart": (crowds, 2, 2, crowd * lat, width), "hhalf": (crowds, 2, crowd * lat, width),
        "hmid": (crowds, crowd * lat, width), "hquart": (crowds, crowd * lat, width),
        "gb": (ups, size * own, n * r), "du": (ups, size * own, n * r),
        "part": (2, tiles, 2, 2, own, 256), "half": (2, tiles, 2, own, 256),
        "mid": (2, tiles, own, 256), "quart": (2, tiles, own, 256),
        "dah": (g, size * lat, cols), "gwo": (2, size * r, width),
        "yq": (3, chain, size * r, cols), "zq": (3, chain + 1, size * r, cols),
        "yw": (size * r, width), "zw": (2, size * r, width),
        "yf": (2, chain, ups // 2, r, width), "zf": (2, chain + 1, ups // 2, r, width),
        "zb": (2, chain + 1, ups // 4, 2 * r, width), "yb": (2, ups // 4, r, width),
        "yn": (2, chain, ups // 4, r, width), "zn": (2, chain + 1, ups // 4, r, width),
        "kall": (2, 2, 2, rows, width), "kland": (g, 2, rows, width), "kx": (g, rows, width),
    }
    full = {
        "media": (g, patches, width), "latents": (g, lat, width), "cot": (g, lat, width),
        "norms": (6, width), "hidden": (own, width), "dhid": (own, width),
        "fin": (3, size * r, cols), "wfin": (size * r, width), "grads": (3 + 1 + 2 * ups, r, width), "gsum": (8, width),
        "flat": (3 + 1 + 2 * ups, r * width),
        "turn": (width // 128, (3 + 1 + 2 * ups) * r, 128),
        "cn": (size, (g + 15) // 16 * 16, size * patches),
        "nland": (size, 8, width), "nhold": (8, width), "dland": (n, 8, width),
        "sland": (size, 8, 128), "shold": (8, 128), "tland": (n, 8, 128), "sqr": (8, 128),
    }
    sems = {
        "loc": (7,), "ins": (5,), "outs": (3,), "mouts": (2,),
        "a_s": (size,), "a_r": (size,), "su": (7, chain), "sd": (7, chain), "sy": (7, chain),
        "rz": (7, chain), "ry": (7, chain), "was": (1,), "war": (size,), "ww": (5,),
        "hcs": (crowds,), "hcr": (crowds,), "hxs": (crowds,), "hxr": (crowds,),
        "nxs": (crowds,), "nxr": (crowds,), "ncs": (crowds, 2), "ncr": (crowds, 2),
        "dxs": (crowds,), "dxr": (crowds,), "dcs": (crowds, 2), "dcr": (crowds, 2),
        "ms": (crowds,), "mr": (crowds,), "mcs": (crowds, 2), "mcr": (crowds, 2),
        "xs": (3,), "xr": (3,), "cs": (3, 2), "cr": (3, 2),
        "ps": (2, tiles), "pr": (2, tiles), "qs": (2, tiles),
        "qr": (2, tiles), "gws": (3,), "gwr": (3,), "ks": (2,), "kr": (g,), "lxs": (g,), "lxr": (g,),
        "gyr": (7, chain), "gzr": (7, chain + 1),
        "es": (size,), "er": (size,),
        "bzr": (2, chain + 1), "bys": (2,), "byr": (2,),
        "fs": (3, size), "fr": (3, size),
        "n1s": (size,), "n1r": (size,), "n2s": (n,), "n2r": (n,), "s1r": (size,), "s2r": (n,), "s1s": (size,), "s2s": (n,),
    }
    scratch = [(k, pltpu.VMEM(s, BF16)) for k, s in low.items()]
    scratch += [(k, pltpu.VMEM(s, F32)) for k, s in full.items()]
    scratch += [("held", pltpu.VMEM((4 + 2 * ups, r, width), BF16))]
    scratch += [(k, DMA(s)) for k, s in sems.items()]
    return scratch


def step_kernel(n, size, hands, scale, names, *refs):
    chain = n // 2
    count = len(INPUTS) + len(OUTPUTS)
    into = Names(zip(INPUTS, refs[: len(INPUTS)]))
    out = Names(zip(OUTPUTS, refs[len(INPUTS) : count]))
    b = Names(zip(names, refs[count:]))
    d, p, z, y, x, c = place()
    held, media, latents, cot, norms = b.held, b.media, b.latents, b.cot, b.norms
    wqkv, wo, ud, nm, nl, dy, cn = b.wqkv, b.wo, b.ud, b.nm, b.nl, b.dy, b.cn
    q, k_, v_, mixed, hidden, nf, doa = b.q, b.k, b.v, b.mixed, b.hidden, b.nf, b.doa
    r, width = held.shape[1], held.shape[2]
    cols, ups = width // size, ud.shape[1]
    images, patches, _ = media.shape
    lat = latents.shape[1]
    own, keys, reals = images * lat, size * (patches + lat), size * patches
    tiles = width // 256
    above, below = z + 1 < chain, z > 0
    up_dev, dn_dev = ((z + 1) * 2 + y, p), ((z - 1) * 2 + y, p)
    y_dev, x_dev, c_dev = (z * 2 + 1 - y, p), (d, (1 - x) * 2 + c), (d, x * 2 + 1 - c)
    px = (1 - x) * 2 + c
    dp_peers = [(lax.rem(d + s, n), p) for s in range(1, n)]

    loads = [
        pltpu.make_async_copy(src, dst, b.ins.at[i])
        for i, (src, dst) in enumerate(
            ((into.weights, b.flat), (into.cot, cot), (into.norms, norms),
             (into.latents, latents), (into.media, media))
        )
    ]
    for copy in loads:
        copy.start()
    everyone_here = greet(patch_peers(d, p, size) + dp_peers)
    blocks = held.shape[0]
    loads[0].wait()
    for t in range(width // 128):
        for k in range(r):
            at = k * width + t * 128
            b.turn[t, pl.ds(k, blocks, stride=r), :] = b.flat[:, at : at + 128]
        held[:, :, t * 128 : (t + 1) * 128] = (
            b.turn[t].reshape(blocks, r, 128).astype(BF16)
        )
    loads[1].wait()
    dy[aligned(p, own)] = cot[...].reshape(own, width).astype(BF16)
    everyone_here()

    def lanes(k):
        return aligned(k, cols)

    half, quarter = ups // 2, ups // 4
    most = ups - quarter
    blocks_of = {
        3: (0, 0, half), 4: (0, half, half), 5: (1, 0, most), 6: (1, most, quarter),
    }
    def piece(i, dd):
        if i < 3:
            return wqkv.at[i, aligned(dd, size * r)]
        return ud.at[blocks_of[i][0], pl.ds(*blocks_of[i][1:]), aligned(dd, r)]

    first = [wqkv.at[i, aligned(d, size * r)] for i in range(3)]
    for i in range(3, 7):
        plane, start, many = blocks_of[i]
        first.append(held.at[pl.ds(4 + plane * ups + start, many)])
    here = wqkv.at[:, aligned(d * size + p, r)]
    def hop(i, zz, sends, to, own_src=False):
        src = first[i] if own_src else piece(i, zz * 2 + y)
        return remote(src, piece(i, zz * 2 + y), sends.at[i, zz], b.rz.at[i, zz], to)

    def over(i, zz, own_src=False):
        src = first[i] if own_src else piece(i, zz * 2 + y)
        return remote(src, piece(i, zz * 2 + y), b.sy.at[i, zz], b.ry.at[i, zz], y_dev)

    def start_own(i):
        @pl.when(above)
        def _():
            hop(i, z, b.su, up_dev, True).start()

        @pl.when(below)
        def _():
            hop(i, z, b.sd, dn_dev, True).start()

        over(i, z, True).start()

    swaps = []
    for k in range(1, size):
        to = lax.rem(p + k, size)
        swaps.append(
            remote(held.at[pl.ds(0, 3), :, lanes(to)], here, b.a_s.at[k], b.a_r.at[k], (d, to))
        )
    for copy in swaps:
        copy.start()
    wo_near = remote(
        held.at[3], wo.at[aligned(y * size + p, r)], b.was.at[0], b.war.at[p], (d, z)
    )
    wo_own = pltpu.make_async_copy(held.at[3], wo.at[aligned(y * size + p, r)], b.loc.at[1])

    @pl.when(z != p)
    def _():
        wo_near.start()

    @pl.when(z == p)
    def _():
        wo_own.start()

    start_own(3)
    over(6, z, True).start()
    local = [pltpu.make_async_copy(held.at[pl.ds(0, 3), :, lanes(p)], here, b.loc.at[0])]
    local += [pltpu.make_async_copy(first[i], piece(i, d), b.loc.at[i]) for i in range(3, 7)]
    for copy in local:
        copy.start()

    def forward(i, s):
        @pl.when(z - s >= 0)
        def _():
            hop(i, z - s, b.su, up_dev).wait_recv()

            @pl.when(above)
            def _():
                hop(i, z - s, b.su, up_dev).start()

            over(i, z - s).start()

        @pl.when(z + s < chain)
        def _():
            hop(i, z + s, b.sd, dn_dev).wait_recv()

            @pl.when(below)
            def _():
                hop(i, z + s, b.sd, dn_dev).start()

            over(i, z + s).start()

    def pair(k, zz):
        return ud.at[1, pl.ds(most + k * quarter, quarter), aligned(zz, 2 * r)]

    def pair_hop(k, zz, sends, to):
        return remote(pair(k, zz), pair(k, zz), sends.at[6 + k, zz], b.rz.at[6 + k, zz], to)

    def pair_start():
        for k in range(1):
            src = piece(6 + k, z * 2 + 1 - y)
            local[4 + k].wait()
            remote(src, src, b.sy.at[6 + k, z], b.ry.at[6 + k, z], y_dev).wait_recv()

            @pl.when(above)
            def _():
                pair_hop(k, z, b.su, up_dev).start()

            @pl.when(below)
            def _():
                pair_hop(k, z, b.sd, dn_dev).start()

    def pair_forward(s):
        for k in range(1):

            @pl.when(z - s >= 0)
            def _():
                pair_hop(k, z - s, b.su, up_dev).wait_recv()

                @pl.when(above)
                def _():
                    pair_hop(k, z - s, b.su, up_dev).start()

            @pl.when(z + s < chain)
            def _():
                pair_hop(k, z + s, b.sd, dn_dev).wait_recv()

                @pl.when(below)
                def _():
                    pair_hop(k, z + s, b.sd, dn_dev).start()

    def pair_sent():
        for k in range(1):
            over(6 + k, z).wait_send()

            def step(zz):
                @pl.when(jnp.logical_and(above, zz <= z))
                def _():
                    pair_hop(k, zz, b.su, up_dev).wait_send()

                @pl.when(jnp.logical_and(below, zz >= z))
                def _():
                    pair_hop(k, zz, b.sd, dn_dev).wait_send()

            each(0, chain, step)

    def arrived(i):
        def step(zz):
            src = piece(i, zz * 2 + 1 - y)
            remote(src, src, b.sy.at[i, zz], b.ry.at[i, zz], y_dev).wait_recv()

        each(0, chain, step)

    def sent(i):
        def step(zz):
            over(i, zz).wait_send()

            @pl.when(jnp.logical_and(above, zz <= z))
            def _():
                hop(i, zz, b.su, up_dev).wait_send()

            @pl.when(jnp.logical_and(below, zz >= z))
            def _():
                hop(i, zz, b.sd, dn_dev).wait_send()

        each(0, chain, step)

    class Rows:
        def __init__(self, slot, xs, xr, cs, cr, at, src=None):
            src = slot(p) if src is None else src
            self.to_x = remote(src, slot(p), xs.at[at], xr.at[at], x_dev)
            self.to_c = remote(src, slot(p), cs.at[at, 0], cr.at[at, 0], c_dev)
            self.on = remote(slot(px), slot(px), cs.at[at, 1], cr.at[at, 1], c_dev)

        def start(self):
            self.to_x.start()
            self.to_c.start()

        def forward(self):
            self.to_x.wait_recv()
            self.on.start()

        def have(self):
            self.to_c.wait_recv()
            self.on.wait_recv()

        def end(self):
            self.to_x.wait_send()
            self.to_c.wait_send()
            self.on.wait_send()

    def group(slot, j, src=None):
        return Rows(slot, b.xs, b.xr, b.cs, b.cr, j, src)

    lat_rows = group(lambda k: nl.at[:, aligned(k, lat)], 0)
    cn_rows = group(lambda k: cn.at[k], 1)
    dy_rows = group(lambda k: dy.at[aligned(k, own)], 2)

    def wo_block(k):
        return wo.at[aligned(k, size * r)]

    def wo_hop(e, to, k):
        return remote(wo_block(k), wo_block(k), b.ww.at[e], b.ww.at[3 + e // 2], to)

    def wo_pass(first_end, second_end):
        @pl.when(first_end)
        def _():
            wo_hop(0, up_dev, y).start()

        @pl.when(second_end)
        def _():
            wo_hop(1, dn_dev, y).start()

        wo_hop(2, y_dev, y).start()

    def wo_source():
        @pl.when(z == p)
        def _():
            for k in range(1, size):
                who = lax.rem(p + k, size)
                part = wo.at[aligned(y * size + who, r)]
                remote(part, part, b.was.at[0], b.war.at[who], (d, who)).wait_recv()
            wo_own.wait()
            wo_pass(above, below)

    def wo_stage(k):
        @pl.when(z == p + k)
        def _():
            wo_hop(0, up_dev, y).wait_recv()
            wo_pass(above, z < 0)

        @pl.when(z == p - k)
        def _():
            wo_hop(0, dn_dev, y).wait_recv()
            wo_pass(z < 0, below)

    def wo_have():
        wo_hop(2, y_dev, 1 - y).wait_recv()

    def wo_sent():
        @pl.when(jnp.logical_and(z >= p, above))
        def _():
            wo_hop(0, up_dev, y).wait_send()

        @pl.when(jnp.logical_and(z <= p, below))
        def _():
            wo_hop(1, dn_dev, y).wait_send()

        wo_hop(2, y_dev, y).wait_send()

        @pl.when(z != p)
        def _():
            wo_near.wait_send()

    crowd = crowd_of(images)
    crowds = images // crowd

    def media_rows(j):
        return Rows(
            lambda k: nm.at[aligned(j, crowd), aligned(k, patches)],
            b.ms, b.mr, b.mcs, b.mcr, j,
        )

    fold = crowd * lat

    def nf_rows(j):
        return Rows(
            lambda k: nf.at[pl.ds(pl.multiple_of(k * own + j * fold, fold), fold)],
            b.nxs, b.nxr, b.ncs, b.ncr, j,
        )

    def do_rows(j):
        return Rows(
            lambda k: doa.at[aligned(j, crowd), aligned(k, lat)],
            b.dxs, b.dxr, b.dcs, b.dcr, j,
        )

    loads[2].wait()
    loads[3].wait()
    media_gain, media_shift = 1.0 + norms[0:1, :], norms[1:2, :]
    latent_gain, latent_shift = 1.0 + norms[2:3, :], norms[3:4, :]
    ffn_gain, ffn_shift = 1.0 + norms[4:5, :], norms[5:6, :]

    def latent_norm(g):
        unit, _ = unit_of(latents[g])
        nl[g, aligned(p, lat)] = (unit * latent_gain + latent_shift).astype(BF16)

    def media_norm(g):
        unit, _ = unit_of(media[g])
        nm[g, aligned(p, patches)] = (unit * media_gain + media_shift).astype(BF16)

    dy_rows.start()
    cn[p] = jnp.zeros(cn.shape[1:], F32)
    counts = column_of((into.mask[...] > 0).astype(F32))
    cn[p, :images, :] = jnp.broadcast_to(counts, (images, cn.shape[2]))
    each(0, images, latent_norm)
    cn_rows.start()
    lat_rows.start()
    local[0].wait()
    for copy in swaps:
        copy.wait_recv()
    for i in range(3):
        start_own(i)
    loads[4].wait()
    each(0, images, media_norm)
    each(0, crowds, lambda j: media_rows(j).start())
    wo_source()
    for s in range(1, chain):
        for i in range(3):
            forward(i, s)
        if s == 1:
            start_own(4)
            dy_rows.forward()
            cn_rows.forward()
    lat_rows.forward()
    wo_stage(1)
    wo_stage(2)
    for s in range(1, chain - 1):
        forward(3, s)
        if s == 1:
            start_own(5)
    pair_start()
    media_rows(0).forward()
    for i in range(3):
        arrived(i)
    lat_rows.have()
    cn_rows.have()

    flat_nl = nl[...].reshape(images * size * lat, width)
    q[...] = nn(flat_nl, wqkv[0]).astype(BF16).reshape(images, size * lat, cols)
    k_[:, reals:] = nn(flat_nl, wqkv[1]).astype(BF16).reshape(images, size * lat, cols)
    v_[:, reals:] = nn(flat_nl, wqkv[2]).astype(BF16).reshape(images, size * lat, cols)

    def real_keys(g):
        real = cn[0, pl.ds(g, 1), :]
        for k in range(1, size):
            real = real + cn[k, pl.ds(g, 1), :]
        return real

    def image(g):
        k_[g, :reals] = nn(nm[g], wqkv[1]).astype(BF16)
        v_[g, :reals] = nn(nm[g], wqkv[2]).astype(BF16)
        pp, plat = soft(
            head_rows(q[g], hands), k_[g, :reals], k_[g, reals:], real_keys(g), scale
        )
        full = nn(pp.astype(BF16), v_[g, :reals]) + nn(plat.astype(BF16), v_[g, reals:])
        mixed[g] = own_columns(full, hands).astype(BF16)

    def hid_core(j):
        return remote(b.hpart.at[j, :, 1 - c], b.hhalf.at[j], b.hcs.at[j], b.hcr.at[j], c_dev)

    def hid_x(j):
        return remote(b.hmid.at[j], b.hquart.at[j], b.hxs.at[j], b.hxr.at[j], x_dev)

    def hid_part(j):
        rows = mixed[j * crowd : (j + 1) * crowd].reshape(crowd * size * lat, cols)
        for t in range(tiles):
            span = pl.ds(256 * t, 256)
            value = nn(rows, wo[:, span]).astype(BF16)
            for i in range(crowd):
                for e in range(size):
                    at = (i * size + e) * lat
                    b.hpart[j, e // 2, e % 2, i * lat : (i + 1) * lat, span] = value[at : at + lat]
        hid_core(j).start()

    def hid_pass(j):
        hid_core(j).wait_recv()
        b.hmid[j] = (b.hhalf[j, 1 - x].astype(F32) + b.hpart[j, 1 - x, c].astype(F32)).astype(BF16)
        hid_x(j).start()

    def hid_end(j):
        hid_x(j).wait_recv()
        value = (
            latents[j * crowd : (j + 1) * crowd].reshape(fold, width)
            + b.hhalf[j, x].astype(F32) + b.hpart[j, x, c].astype(F32) + b.hquart[j].astype(F32)
        )
        hidden[j * fold : (j + 1) * fold] = value
        unit, _ = unit_of(value)
        nf[pl.ds(pl.multiple_of(p * own + j * fold, fold), fold)] = (
            unit * ffn_gain + ffn_shift
        ).astype(BF16)
        nf_rows(j).start()

    pending = [(3, chain - 1)] + [(i, s) for i in (4, 5) for s in range(1, chain)]

    def forward_some(count):
        for _ in range(count):
            if pending:
                forward(*pending.pop(0))

    for j in range(crowds):
        if j:
            media_rows(j).forward()
            forward_some(1)
        media_rows(j).have()
        each(j * crowd, (j + 1) * crowd, image)
        if j == 0:
            for k in range(3, chain):
                wo_stage(k)
            wo_have()
        hid_part(j)
        if j > 0:
            hid_end(j - 1)
        forward_some(1)
        hid_pass(j)
        forward_some(1)
    forward_some(len(pending))
    for j in range(crowds - 1):
        nf_rows(j).forward()
    hid_end(crowds - 1)
    for s in range(1, chain - 1):
        pair_forward(s)
    dy_rows.have()
    for i in (3, 4, 5):
        arrived(i)
    for copy in local[1:4]:
        copy.wait()
    nf_rows(crowds - 1).forward()
    for j in range(crowds):
        nf_rows(j).have()

    def hidden_block(e):
        u = nt(nf[...], ud[0, e])
        into_active = nt(dy[...], ud[1, e])
        chance = 0.5 * (1.0 + lax.erf(u * math.sqrt(0.5)))
        slope = chance + u * jnp.exp(-0.5 * u * u) * (1.0 / math.sqrt(2.0 * math.pi))
        b.gb[e] = (u * chance).astype(BF16)
        b.du[e] = (into_active * slope).astype(BF16)

    def down_grad(e):
        for t in range(0, width, 512):
            ud[2, e, :, t : t + 512] = tn(b.gb[e], dy[:, t : t + 512]).astype(BF16)

    def up_grad(e):
        for t in range(0, width, 512):
            ud[0, e, :, t : t + 512] = tn(b.du[e], nf[:, t : t + 512]).astype(BF16)

    def part_core(i, t):
        return remote(
            b.part.at[i, t, :, 1 - c], b.half.at[i, t], b.ps.at[i, t], b.pr.at[i, t], c_dev
        )

    def part_x(i, t):
        return remote(b.mid.at[i, t], b.quart.at[i, t], b.qs.at[i, t], b.qr.at[i, t], x_dev)

    def part_of(i, acts, passing=False):
        def tile(t):
            span = aligned(t, 256)
            acc = nn(acts[0], ud[i, 0, :, span])
            for e in range(1, ups):
                acc = acc + nn(acts[e], ud[i, e, :, span])
            b.part[i, t] = acc.astype(BF16).reshape(2, 2, own, 256)
            part_core(i, t).start()
            if passing:
                @pl.when(t > 1)
                def _():
                    pass_tile(i, t - 2)

        each(0, tiles, tile)
        if passing:
            each(max(tiles - 2, 0), tiles, lambda t: pass_tile(i, t))

    def part_pass(i):
        each(0, tiles, lambda t: pass_tile(i, t))

    def pass_tile(i, t):
        part_core(i, t).wait_recv()
        b.mid[i, t] = (
            b.half[i, t, 1 - x].astype(F32) + b.part[i, t, 1 - x, c].astype(F32)
        ).astype(BF16)
        part_x(i, t).start()

    def part_end(i, write):
        def tile(t):
            part_x(i, t).wait_recv()
            write(
                aligned(t, 256),
                b.half[i, t, x].astype(F32) + b.part[i, t, x, c].astype(F32)
                + b.quart[i, t].astype(F32),
            )

        each(0, tiles, tile)

    def parts_sent(i):
        def tile(t):
            part_core(i, t).wait_send()
            part_x(i, t).wait_send()

        each(0, tiles, tile)

    def ffn_part(i, k):
        plane, start, many = {
            3: (2, 0, quarter), 4: (0, 0, half), 5: (0, half, half), 6: (2, most, quarter)
        }[i]
        return ud.at[plane, pl.ds(start, many), aligned(k, r)]

    class Staged:
        def stage(self, k):
            @pl.when(z == k)
            def _():
                each(0, chain - 1 - k, lambda t: self.move(
                    chain - 1 - t, k > 0, chain - t, up_dev
                ))

            @pl.when(chain - 1 - z == k)
            def _():
                each(0, chain - 1 - k, lambda t: self.move(t, k > 0, t, dn_dev))

    class Sum(Staged):
        def __init__(self, i, kind):
            self.i = i
            if kind == 0:
                self.mine = lambda k: wqkv.at[i, aligned(k, size * r)]
                self.ly, self.lz = b.yq.at[i], b.zq.at[i]
            else:
                self.mine = lambda k: ffn_part(i, k)
                self.ly = b.yf.at[i - 4] if i in (4, 5) else b.yn.at[i // 6]
                self.lz = b.zf.at[i - 4] if i in (4, 5) else b.zn.at[i // 6]

        def over(self, zt):
            return remote(
                self.mine(zt * 2 + 1 - y), self.ly.at[zt], b.sy.at[self.i, zt],
                b.gyr.at[self.i, zt], y_dev,
            )

        def along(self, zt, slot, to):
            return remote(
                self.ly.at[zt], self.lz.at[slot], b.su.at[self.i, zt], b.gzr.at[self.i, slot], to
            )

        def send(self):
            def step(k):
                s = chain - 1 - k

                @pl.when(z + s < chain)
                def _():
                    self.over(z + s).start()

                @pl.when(jnp.logical_and(z - s >= 0, s > 0))
                def _():
                    self.over(z - s).start()

            each(0, chain, step)

        def pair(self, zt):
            return self.ly[zt].astype(F32) + self.mine(zt * 2 + y)[...].astype(F32)

        def move(self, zt, more, slot, to):
            self.over(zt).wait_recv()
            if more:
                self.along(zt, slot, to).wait_recv()
                self.ly[zt] = (self.pair(zt) + self.lz[slot].astype(F32)).astype(BF16)
            else:
                self.ly[zt] = self.pair(zt).astype(BF16)
            self.along(zt, slot, to).start()

        def last(self, dst):
            self.over(z).wait_recv()
            dst[...] = self.pair(z)

            @pl.when(below)
            def _():
                self.along(z, z + 1, up_dev).wait_recv()
                dst[...] = dst[...] + self.lz[z + 1].astype(F32)

            @pl.when(above)
            def _():
                self.along(z, z, dn_dev).wait_recv()
                dst[...] = dst[...] + self.lz[z].astype(F32)

        def sent(self):
            def step(zt):
                self.over(zt).wait_send()

                @pl.when(zt != z)
                def _():
                    self.along(zt, 0, up_dev).wait_send()

            each(0, chain, step)

    class Cross(Staged):
        def __init__(self, k):
            self.k, self.blocks = k, pl.ds((1 + k) * quarter, quarter)
            self.lz, self.ly = b.zb.at[k], b.yb.at[k]

        def pair(self, zt):
            return ud.at[2, self.blocks, aligned(zt, 2 * r)]

        def along(self, zt, slot, to):
            return remote(
                self.pair(zt), self.lz.at[slot], b.sd.at[self.k, zt], b.bzr.at[self.k, slot], to
            )

        def move(self, zt, more, slot, to):
            if more:
                self.along(zt, slot, to).wait_recv()
                self.pair(zt)[...] = (
                    self.pair(zt)[...].astype(F32) + self.lz[slot].astype(F32)
                ).astype(BF16)
            self.along(zt, slot, to).start()

        def over(self):
            src = ud.at[2, self.blocks, aligned(z * 2 + 1 - y, r)]
            return remote(src, self.ly, b.bys.at[self.k], b.byr.at[self.k], y_dev)

        def meet(self, dst):
            theirs, ours = aligned(1 - y, r), aligned(y, r)
            far = ud.at[2, self.blocks, aligned(z * 2 + 1 - y, r)]
            near = ud.at[2, self.blocks, aligned(z * 2 + y, r)]
            dst[...] = near[...].astype(F32)

            def add(slot):
                dst[...] = dst[...] + self.lz[slot, :, ours].astype(F32)
                far[...] = (
                    far[...].astype(F32) + self.lz[slot, :, theirs].astype(F32)
                ).astype(BF16)

            @pl.when(below)
            def _():
                self.along(z, z + 1, up_dev).wait_recv()
                add(z + 1)

            @pl.when(above)
            def _():
                self.along(z, z, dn_dev).wait_recv()
                add(z)

            self.over().start()

        def last(self, dst):
            self.over().wait_recv()
            dst[...] = dst[...] + self.ly[...].astype(F32)

        def sent(self):
            self.over().wait_send()

            def step(zt):
                @pl.when(zt != z)
                def _():
                    self.along(zt, 0, up_dev).wait_send()

            each(0, chain, step)

    class Gather:
        def over(self):
            return remote(b.gwo.at[1 - y], b.yw, b.gws.at[0], b.gwr.at[0], y_dev)

        def rise(self):
            return remote(b.gwo.at[y], b.zw.at[0], b.gws.at[1], b.gwr.at[1], up_dev)

        def fall(self):
            return remote(b.gwo.at[y], b.zw.at[1], b.gws.at[2], b.gwr.at[2], dn_dev)

        def send(self):
            self.over().start()

        def add(self, k):
            b.gwo[y] = (b.gwo[y].astype(F32) + b.zw[k].astype(F32)).astype(BF16)

        def step(self, k):
            @pl.when(jnp.logical_or(
                jnp.logical_and(z < p, z == k), jnp.logical_and(z > p, chain - 1 - z == k)
            ))
            def _():
                self.over().wait_recv()
                b.gwo[y] = (b.gwo[y].astype(F32) + b.yw[...].astype(F32)).astype(BF16)

                @pl.when(z < p)
                def _():
                    if k:
                        self.rise().wait_recv()
                        self.add(0)
                    self.rise().start()

                @pl.when(z > p)
                def _():
                    if k:
                        self.fall().wait_recv()
                        self.add(1)
                    self.fall().start()

        def part(self, k, to):
            return remote(
                b.wfin.at[aligned(k, r)], b.grads.at[3], b.es.at[k], b.er.at[0], to
            )

        def last(self):
            @pl.when(z == p)
            def _():
                self.over().wait_recv()
                b.wfin[...] = b.gwo[y].astype(F32) + b.yw[...].astype(F32)

                @pl.when(below)
                def _():
                    self.rise().wait_recv()
                    b.wfin[...] = b.wfin[...] + b.zw[0].astype(F32)

                @pl.when(above)
                def _():
                    self.fall().wait_recv()
                    b.wfin[...] = b.wfin[...] + b.zw[1].astype(F32)

                for k in range(1, size):
                    to = lax.rem(p + k, size)
                    self.part(to, (d, to)).start()
                b.grads[3] = b.wfin[aligned(p, r)]

        def have(self):
            @pl.when(z != p)
            def _():
                self.part(0, (d, z)).wait_recv()

        def sent(self):
            self.over().wait_send()

            @pl.when(z < p)
            def _():
                self.rise().wait_send()

            @pl.when(z > p)
            def _():
                self.fall().wait_send()

            @pl.when(z == p)
            def _():
                for k in range(1, size):
                    to = lax.rem(p + k, size)
                    self.part(to, (d, to)).wait_send()

    crosses = [Cross(0), Cross(1)]

    qkv_sums, wo_sum = [Sum(i, 0) for i in range(3)], Gather()

    ffn_sums = {i: Sum(i, 2) for i in (3, 4, 5, 6)}

    each(0, quarter, hidden_block)
    each(0, quarter, down_grad)
    for i in range(6):
        sent(i)
    pair_sent()
    wo_sent()
    ffn_sums[3].send()
    for k in range(2):
        each((1 + k) * quarter, (2 + k) * quarter, hidden_block)
        each((1 + k) * quarter, (2 + k) * quarter, down_grad)
        crosses[k].stage(0)
    pair_forward(chain - 1)
    each(most, ups, hidden_block)
    each(most, ups, down_grad)
    ffn_sums[6].send()
    part_of(0, b.du, True)
    each(0, ups, up_grad)
    ffn_sums[4].send()
    ffn_sums[5].send()
    part_of(1, b.gb)

    def write_dhid(span, value):
        b.dhid[:, span] = value

    part_end(0, write_dhid)
    dn = b.dhid[...]
    unit, scaled = unit_of(hidden[...])
    b.gsum[...] = jnp.zeros_like(b.gsum)
    b.gsum[4:5, :] = column_sum(dn * unit)
    b.gsum[5:6, :] = column_sum(dn)
    b.dhid[...] = cot[...].reshape(own, width) + norm_back(dn, unit, scaled, ffn_gain)
    for j in range(crowds):
        doa[j * crowd : (j + 1) * crowd, aligned(p, lat)] = (
            b.dhid[j * fold : (j + 1) * fold].astype(BF16).reshape(crowd, lat, width)
        )
        do_rows(j).start()
    def stages(*pairs):
        for item, k in pairs:
            if k < chain - 1:
                item.stage(k)

    def head_grads(j):
        do_rows(j).have()
        rows = doa[j * crowd : (j + 1) * crowd].reshape(crowd * size * lat, width)
        b.dah[j * crowd : (j + 1) * crowd] = (
            nt(rows, wo[...]).astype(BF16).reshape(crowd, size * lat, cols)
        )

    def out_grad():
        for t in range(tiles):
            span = pl.ds(256 * t, 256)
            b.gwo[:, :, span] = tn(
                mixed[...].reshape(images * size * lat, cols),
                doa[:, :, span].reshape(images * size * lat, 256),
            ).astype(BF16).reshape(2, size * r, 256)

    def kin_core(g):
        return remote(
            b.kall.at[lax.rem(g, 2), 1 - c], b.kland.at[g], b.ks.at[lax.rem(g, 2)], b.kr.at[g], c_dev
        )

    def kin_x(g):
        return remote(b.kland.at[g, 1 - x], b.kx.at[g], b.lxs.at[g], b.lxr.at[g], x_dev)

    def image_back(g):
        slot = lax.rem(g, 2)
        qb, dab = head_rows(q[g], hands), head_rows(b.dah[g], hands)
        kp, kl, vp, vl = k_[g, :reals], k_[g, reals:], v_[g, :reals], v_[g, reals:]
        pp, plat = soft(qb, kp, kl, real_keys(g), scale)
        gp, gl = nt(dab, vp), nt(dab, vl)
        delta = column_of(pp * gp) + column_of(plat * gl)
        sp, sl = (pp * (gp - delta)).astype(BF16), (plat * (gl - delta)).astype(BF16)
        v_[g, :reals] = tn(pp.astype(BF16), dab).astype(BF16)
        v_[g, reals:] = tn(plat.astype(BF16), dab).astype(BF16)
        k_[g, :reals] = (tn(sp, qb) * scale).astype(BF16)
        k_[g, reals:] = (tn(sl, qb) * scale).astype(BF16)
        q[g] = (own_columns(nn(sp, kp) + nn(sl, kl), hands) * scale).astype(BF16)
        for t in range(tiles):
            span = pl.ds(256 * t, 256)
            rows = nt(k_[g], wqkv[1, span, :]) + nt(v_[g], wqkv[2, span, :])
            tail = rows[reals:] + nt(q[g], wqkv[0, span, :])
            for e in range(size):
                b.kall[slot, e % 2, e // 2, :patches, span] = (
                    rows[e * patches : (e + 1) * patches].astype(BF16)
                )
                b.kall[slot, e % 2, e // 2, patches:, span] = (
                    tail[e * lat : (e + 1) * lat].astype(BF16)
                )
        kin_core(g).start()

    def kin_mid(g):
        kin_core(g).wait_recv()
        b.kland[g] = (
            b.kland[g].astype(F32) + b.kall[lax.rem(g, 2), c].astype(F32)
        ).astype(BF16)
        kin_x(g).start()

    def media_out(g):
        return pltpu.make_async_copy(media.at[g], out.media_grad.at[g], b.mouts.at[lax.rem(g, 2)])

    def kin_last(g):
        kin_x(g).wait_recv()
        total_ = b.kland[g, x].astype(F32) + b.kx[g].astype(F32)
        grad = total_[:patches]
        unit, scaled = unit_of(media[g])
        b.gsum[0:1, :] = b.gsum[0:1, :] + column_sum(grad * unit)
        b.gsum[1:2, :] = b.gsum[1:2, :] + column_sum(grad)
        media[g] = norm_back(grad, unit, scaled, media_gain)

        @pl.when(g >= 2)
        def _():
            media_out(g - 2).wait()

        media_out(g).start()
        grad = total_[patches:]
        unit, scaled = unit_of(latents[g])
        b.gsum[2:3, :] = b.gsum[2:3, :] + column_sum(grad * unit)
        b.gsum[3:4, :] = b.gsum[3:4, :] + column_sum(grad)
        latents[g] = b.dhid[aligned(g, lat)] + norm_back(grad, unit, scaled, latent_gain)

    def back(g):
        @pl.when(g >= 2)
        def _():
            kin_core(g - 2).wait_send()

        image_back(g)

        @pl.when(g >= 1)
        def _():
            kin_mid(g - 1)

    down, first_up, last_up, more_down = (ffn_sums[i] for i in (3, 4, 5, 6))
    between = [
        [(crosses[1], 1), (first_up, 0), (crosses[0], 2)],
        [(crosses[1], 2), (down, 1)],
        [(more_down, 1), (last_up, 0)],
    ]
    stages((down, 0), (crosses[0], 1), (more_down, 0))
    do_rows(0).forward()
    for j in range(crowds):
        head_grads(j)
        if j + 1 < crowds:
            do_rows(j + 1).forward()
        else:
            out_grad()
            wo_sum.send()
        each(j * crowd, (j + 1) * crowd, back)
        if between:
            stages(*between.pop(0))
    kin_mid(images - 1)
    for pairs in between:
        stages(*pairs)
    for k in range(3, chain - 1):
        stages((crosses[0], k), (crosses[1], k))
    cross_rows = [
        b.grads.at[pl.ds(4 + ups + (1 + k) * quarter, quarter)] for k in range(2)
    ]

    def flat(a, n_rows):
        return a.reshape(images * n_rows, cols)

    def qkv_grad(j):
        def tile(t):
            span = aligned(t, 256)
            rows_l = nl[:, :, span].reshape(images * size * lat, 256)
            if j == 0:
                wqkv[0, span, :] = tn(rows_l, flat(q[...], size * lat)).astype(BF16)
                return
            rows_m = nm[:, :, span].reshape(images * reals, 256)
            ref = (k_, v_)[j - 1]
            wqkv[j, span, :] = (
                tn(rows_m, flat(ref[:, :reals], reals))
                + tn(rows_l, flat(ref[:, reals:], size * lat))
            ).astype(BF16)

        each(0, tiles, tile)
        qkv_sums[j].send()

    for item, rows in zip(crosses, cross_rows):
        item.meet(rows)
    qkv_grad(0)
    qkv_grad(2)
    qkv_grad(1)
    part_pass(1)
    waiting = [(0, (images + 2) // 3)]
    waiting += [(waiting[0][1], 2 * waiting[0][1]), (2 * waiting[0][1], images)]

    def last_keys():
        if waiting:
            each(*waiting.pop(0), kin_last)

    q_sum, k_sum, v_sum = qkv_sums
    wo_sum.step(0)
    stages((down, 2), (more_down, 2), (first_up, 1))
    last_keys()
    stages((q_sum, 0), (last_up, 1), (first_up, 2))
    last_keys()
    stages((v_sum, 0))
    wo_sum.step(1)
    stages((last_up, 2), (q_sum, 1), (k_sum, 0))
    last_keys()
    stages((v_sum, 1), (q_sum, 2))
    wo_sum.step(2)
    stages((k_sum, 1), (v_sum, 2), (k_sum, 2))
    for k in range(3, chain - 1):
        stages((q_sum, k), (v_sum, k), (k_sum, k))
        if k > 2:
            stages((down, k), (more_down, k), (first_up, k), (last_up, k))
            wo_sum.step(k)
    down.last(b.grads.at[pl.ds(4 + ups, quarter)])
    more_down.last(b.grads.at[pl.ds(4 + ups + most, quarter)])
    first_up.last(b.grads.at[pl.ds(4, half)])
    last_up.last(b.grads.at[pl.ds(4 + half, half)])
    for span in waiting:
        each(*span, kin_last)
    for item, rows in zip(crosses, cross_rows):
        item.last(rows)
    lat_copy = pltpu.make_async_copy(latents, out.latents_grad, b.outs.at[1])
    lat_copy.start()

    def write_out(span, value):
        hidden[:, span] = hidden[:, span] + value

    part_end(1, write_out)
    out_copy = pltpu.make_async_copy(hidden, out.latents_out, b.outs.at[0])
    out_copy.start()

    def share(src, land, hold, s1, r1, total_to, land2, s2, r2):
        land[p] = src[...]
        near = []
        for k in range(1, size):
            to = lax.rem(p + k, size)
            near.append(remote(src, land.at[p], s1.at[to], r1.at[p], (d, to)))
        for copy in near:
            copy.start()
        for k in range(1, size):
            who = lax.rem(p + k, size)
            remote(src, land.at[who], s1.at[who], r1.at[who], (d, who)).wait_recv()
        value = land[0]
        for k in range(1, size):
            value = value + land[k]
        hold[...] = value
        land2[d] = value
        far = []
        for k in range(1, n):
            to = lax.rem(d + k, n)
            far.append(remote(hold, land2.at[d], s2.at[to], r2.at[d], (to, p)))
        for copy in far:
            copy.start()

        def finish():
            for k in range(1, n):
                who = lax.rem(d + k, n)
                remote(hold, land2.at[who], s2.at[who], r2.at[who], (who, p)).wait_recv()
            value = land2[0]
            for k in range(1, n):
                value = value + land2[k]
            total_to[...] = value
            for copy in near + far:
                copy.wait_send()

        return finish

    norms_done = share(b.gsum, b.nland, b.nhold, b.n1s, b.n1r, out.sums, b.dland, b.n2s, b.n2r)
    ends = []
    for j in (0, 2, 1):
        if j == 1:
            wo_sum.last()
        qkv_sums[j].last(b.fin.at[j])
        for k in range(1, size):
            to = lax.rem(p + k, size)
            copy = remote(
                b.fin.at[j, aligned(to, r)], b.grads.at[j, :, lanes(p)],
                b.fs.at[j, k], b.fr.at[j, k], (d, to),
            )
            copy.start()
            ends.append(copy)
        b.grads[j, :, lanes(p)] = b.fin[j, aligned(p, r)]
    squares = jnp.zeros((8, 128), F32)

    def squares_of(i, squares):
        for t in range(0, width, 128):
            tile = b.grads[i, :, t : t + 128]
            squares = squares + jnp.sum((tile * tile).reshape(r // 8, 8, 128), axis=0)
        return squares

    for i in range(4, 4 + 2 * ups):
        squares = squares_of(i, squares)
    wo_sum.have()
    for copy in ends:
        copy.wait_recv()
    for i in range(4):
        squares = squares_of(i, squares)
    b.sqr[...] = squares
    squares_done = share(
        b.sqr, b.sland, b.shold, b.s1s, b.s1r, out.squares, b.tland, b.s2s, b.s2r
    )
    for t in range(width // 128):
        b.turn[t] = b.grads[:, :, t * 128 : (t + 1) * 128].reshape(blocks * r, 128)
        for k in range(r):
            at = k * width + t * 128
            b.flat[:, at : at + 128] = b.turn[t, pl.ds(k, blocks, stride=r), :]
    grads_copy = pltpu.make_async_copy(b.flat, out.grads, b.outs.at[2])
    grads_copy.start()
    norms_done()
    for copy in swaps + ends:
        copy.wait_send()
    for rows in (lat_rows, cn_rows, dy_rows):
        rows.end()
    for j in range(crowds):
        media_rows(j).end()
        nf_rows(j).end()
        do_rows(j).end()
        hid_core(j).wait_send()
        hid_x(j).wait_send()
    parts_sent(0)
    parts_sent(1)
    each(max(images - 2, 0), images, lambda g: kin_core(g).wait_send())
    each(0, images, lambda g: kin_x(g).wait_send())
    for item in qkv_sums:
        item.sent()
    wo_sum.sent()
    for item in ffn_sums.values():
        item.sent()
    for item in crosses:
        item.sent()
    each(max(images - 2, 0), images, lambda g: media_out(g).wait())
    out_copy.wait()
    lat_copy.wait()
    grads_copy.wait()
    squares_done()


def column_of(a):
    return jnp.sum(a, axis=1, keepdims=True)


def whole_step(weights, media, latents, cot, mask, norms, n, size, hands, scale):
    g, patches, width = media.shape
    blocks, r = weights.shape[0], weights.shape[1] // width
    lat = latents.shape[1]
    scratch = buffers(n, size, g, patches, lat, width, FF // width, r)
    return pl.pallas_call(
        functools.partial(step_kernel, n, size, hands, scale, [k for k, _ in scratch]),
        name="whole_step",
        out_shape=(
            struct((g, patches, width), F32),
            struct((g, lat, width), F32),
            struct((g * lat, width), F32),
            struct(weights.shape, F32),
            struct((8, width), F32),
            struct((8, 128), F32),
        ),
        in_specs=[ANY] * 4 + [VMEM] + [ANY],
        out_specs=(ANY,) * 4 + (VMEM,) * 2,
        scratch_shapes=[s for _, s in scratch],
        compiler_params=params(8),
    )(weights, media, latents, cot, mask, norms)


def finish_kernel(steps, sums, squares, *refs):
    arrays, norms, passed = refs[:5], refs[5:9], refs[9:12]
    grad_norm, new_weights, new_norms, ffn, passed_out = (
        refs[12], refs[13:18], refs[18:22], refs[22], refs[23:26]
    )
    hold, low, through, load, store, moved = refs[26], refs[27], refs[28:31], refs[31], refs[32], refs[33]
    part = arrays[0].shape[1] // steps

    def span(c):
        return pl.ds(c * part, part)

    loads = [
        [
            pltpu.make_async_copy(src.at[:, span(c)], hold.at[i, :, span(c)], load.at[i, c])
            for i, src in enumerate(arrays)
        ]
        for c in range(steps)
    ]
    into = [pltpu.make_async_copy(a, t, moved.at[0, i]) for i, (a, t) in enumerate(zip(passed, through))]
    away = [
        pltpu.make_async_copy(t, a, moved.at[1, i]) for i, (t, a) in enumerate(zip(through, passed_out))
    ]
    for c in range(steps):
        for copy in loads[c]:
            copy.start()
    for copy in into:
        copy.start()
    norm_grads = sums[:6, :]
    square = jnp.sum(squares[...], axis=0, keepdims=True)
    square = jnp.sum(square, axis=1, keepdims=True)
    rest = jnp.sum(norm_grads * norm_grads, axis=0, keepdims=True)
    length = jnp.sqrt(square + jnp.sum(rest, axis=1, keepdims=True))
    clip = jnp.minimum(1.0, 1.0 / (length + 1e-06))
    grad_norm[...] = jnp.broadcast_to(length, grad_norm.shape)
    for ref, value in zip(
        new_norms, adamw_update(*(ref[...] for ref in norms), norm_grads, clip, 0.0)
    ):
        ref[...] = value
    ffn[...] = norm_grads[4:6]
    stores = []
    for c in range(steps):
        for copy in loads[c]:
            copy.wait()
        new = adamw_update(*(hold[i, :, span(c)] for i in range(5)), clip, 0.1)
        for i in range(4):
            hold[i, :, span(c)] = new[i]
        low[:, span(c)] = new[0].astype(BF16)
        for i, out in enumerate(new_weights):
            src = hold.at[i, :, span(c)] if i < 4 else low.at[:, span(c)]
            copy = pltpu.make_async_copy(src, out.at[:, span(c)], store.at[i, c])
            copy.start()
            stores.append(copy)
        if c < 3:
            into[c].wait()
            away[c].start()
    for copy in stores + away:
        copy.wait()


def finish(sums, squares, weights, grads, norms, passed):
    steps = 4
    rows, flat = grads.shape
    six, width = norms[0].shape
    return pl.pallas_call(
        functools.partial(finish_kernel, steps),
        name="finish",
        in_specs=[VMEM] * 2 + [ANY] * 5 + [VMEM] * 4 + [ANY] * 3,
        out_specs=[VMEM] + [ANY] * 5 + [VMEM] * 5 + [ANY] * 3,
        out_shape=[struct((1, 128), F32)] + [struct(grads.shape, F32)] * 4
        + [struct(grads.shape, BF16)] + [struct((six, width), F32)] * 4
        + [struct((2, width), F32)] + [struct(a.shape, F32) for a in passed],
        scratch_shapes=[
            pltpu.VMEM((5, rows, flat), F32), pltpu.VMEM((rows, flat), BF16),
        ] + [pltpu.VMEM(a.shape, F32) for a in passed]
        + [DMA((5, steps)), DMA((5, steps)), DMA((2, 3))],
        compiler_params=pltpu.CompilerParams(vmem_limit_bytes=VMEM_LIMIT),
    )(sums, squares, *weights, grads, *norms, *passed)


def norm_parts(values, gain_row, shift_row):
    average = jnp.mean(values, axis=-1, keepdims=True)
    centred = values - average
    spread_ = jnp.mean(centred * centred, axis=-1, keepdims=True)
    scaled = lax.rsqrt(spread_ + 1e-05)
    unit_rows = centred * scaled
    return (unit_rows * gain_row + shift_row, unit_rows, scaled)


def norm_back(grad_out, unit_rows, scaled, gain_row):
    inner_grad = grad_out * gain_row
    plain_mean = jnp.mean(inner_grad, axis=-1, keepdims=True)
    cross_mean = jnp.mean(inner_grad * unit_rows, axis=-1, keepdims=True)
    return scaled * (inner_grad - plain_mean - unit_rows * cross_mean)


def gain_terms(grad_out, unit_rows):
    width = grad_out.shape[-1]
    flat_grad = grad_out.reshape(-1, width)
    flat_unit = unit_rows.reshape(-1, width)
    return [jnp.sum(flat_grad * flat_unit, axis=0), jnp.sum(flat_grad, axis=0)]


def exact_gelu(values):
    return jax.nn.gelu(values, approximate=False)


def adamw_update(parameter, first_m, second_m, average, gradient, factor, decay_rate):
    clipped = gradient * factor
    new_first = 0.9 * first_m + 0.1 * clipped
    new_second = 0.999 * second_m + 0.001 * clipped * clipped
    first_hat = new_first / (1.0 - 0.9**STEP)
    second_hat = new_second / (1.0 - 0.999**STEP)
    new_param = parameter - 0.02 * (
        first_hat / (jnp.sqrt(second_hat) + 1e-08) + decay_rate * parameter
    )
    new_avg = 0.8 * average + 0.2 * new_param
    return (new_param, new_first, new_second, new_avg)


def dot32(spec, a, b):
    return jnp.einsum(spec, a, b, preferred_element_type=F32)


def general_step(n, size, media_tokens, patch_mask, latents, cotangent, weights, weights_first,
              weights_second, weights_average, norm_params, norm_first, norm_second, norm_average):
    g, patches, width = media_tokens.shape
    lat = latents.shape[1]
    blocks = weights.shape[0]
    r = width // (n * size)
    cols = width // size
    hands = HEADS // size
    scale = 1.0 / math.sqrt(width // HEADS)
    ups = FF // width
    own = g * lat
    media_gain, latent_gain, ffn_gain = 1.0 + norm_params[0], 1.0 + norm_params[2], 1.0 + norm_params[4]

    held = weights.astype(BF16).reshape(blocks, r, width)
    qs = held[:3].reshape(3, r, size, cols).transpose(2, 0, 1, 3)
    media_norm, media_unit, media_scale = norm_parts(media_tokens, media_gain, norm_params[1])
    latent_norm, latent_unit, latent_scale = norm_parts(latents, latent_gain, norm_params[3])
    cot = cotangent.reshape(own, width)
    count_rows = (g + 15) // 16 * 16
    counts = jnp.sum((patch_mask > 0).astype(F32), axis=1)
    counts = jnp.broadcast_to(jnp.pad(counts, (0, count_rows - g))[:, None], (count_rows, 128))

    wqkv, wo, up, dn, nm, nl, dy, cn = spread(
        qs, held[3], held[4 : 4 + ups], held[4 + ups :],
        media_norm.astype(BF16), latent_norm.astype(BF16), cot.astype(BF16), counts, n, size,
    )
    wqkv = wqkv.reshape(3, width, cols)
    wo = wo.reshape(width, width)
    up = up.reshape(-1, width)
    dn = dn.reshape(-1, width)
    nm = nm.reshape(g * size * patches, width)
    nl = nl.reshape(g * size * lat, width)
    dy = dy.reshape(size * own, width)
    real = jnp.sum(cn[:, :g, 0], axis=0).astype(jnp.int32)

    def by_image(a):
        return a.astype(BF16).reshape(g, -1, cols)

    q = by_image(dot32("rd,de->re", nl, wqkv[0]))
    kp, kl = by_image(dot32("rd,de->re", nm, wqkv[1])), by_image(dot32("rd,de->re", nl, wqkv[1]))
    vp, vl = by_image(dot32("rd,de->re", nm, wqkv[2])), by_image(dot32("rd,de->re", nl, wqkv[2]))
    mixed = attend(real, q, kp, kl, vp, vl, hands, scale)
    ab = to_rows(mixed.reshape(g, size, lat, cols), size, 1).reshape(own, width)

    hidden = latents.reshape(own, width) + dot32("rd,de->re", ab, wo)
    ffn_norm, ffn_unit, ffn_scale = norm_parts(hidden, ffn_gain, norm_params[5])
    nf = join_rows(ffn_norm.astype(BF16), size, 2).reshape(size * own, width)
    u = dot32("rd,fd->rf", nf, up)
    active, pull = jax.vjp(exact_gelu, u)
    gb = active.astype(BF16)
    y_part = dot32("rf,fd->rd", gb, dn).astype(BF16)
    du = pull(dot32("rd,fd->rf", dy, dn))[0].astype(BF16)
    f_part = dot32("rf,fd->rd", du, up).astype(BF16)
    g_dn = dot32("rf,rd->fd", gb, dy).astype(BF16)
    g_up = dot32("rf,rd->fd", du, nf).astype(BF16)
    both = split_rows(jnp.stack([y_part, f_part]).reshape(2, 2, 2, own, width), 3)
    latents_out = (hidden + both[0]).reshape(g, lat, width)
    d_ffn = both[1]
    ffn_terms = gain_terms(d_ffn, ffn_unit)
    d_hidden = cot + norm_back(d_ffn, ffn_unit, ffn_scale, ffn_gain)

    do = d_hidden.astype(BF16)
    g_wo = dot32("rd,re->de", ab, do).astype(BF16)
    da = dot32("re,de->rd", do, wo).astype(BF16).reshape(g, lat, width)
    da = to_heads(da, size, 4).reshape(g, size * lat, cols)
    dq, dkp, dkl, dvp, dvl = attend_back(real, q, kp, kl, vp, vl, da, hands, scale)

    def flat(a):
        return a.reshape(-1, cols)

    dq, dkp, dkl, dvp, dvl = flat(dq), flat(dkp), flat(dkl), flat(dvp), flat(dvl)
    g_qkv = jnp.stack([
        dot32("rd,re->de", nl, dq),
        dot32("rd,re->de", nm, dkp) + dot32("rd,re->de", nl, dkl),
        dot32("rd,re->de", nm, dvp) + dot32("rd,re->de", nl, dvl),
    ]).astype(BF16)
    d_nm = (dot32("re,de->rd", dkp, wqkv[1]) + dot32("re,de->rd", dvp, wqkv[2])).astype(BF16)
    d_nl = (
        dot32("re,de->rd", dkl, wqkv[1]) + dot32("re,de->rd", dvl, wqkv[2])
        + dot32("re,de->rd", dq, wqkv[0])
    ).astype(BF16)

    oq, ow, ou, od, d_media, d_latent = collect(
        g_qkv.reshape(3, n, size, r, cols), g_wo.reshape(n, 2, 2, r, width),
        g_up.reshape(ups, n, r, width), g_dn.reshape(ups, n, r, width),
        d_nm.reshape(g, 2, 2, patches, width), d_nl.reshape(g, 2, 2, lat, width), n, size,
    )
    media_grad = norm_back(d_media, media_unit, media_scale, media_gain)
    latents_grad = d_hidden.reshape(g, lat, width) + norm_back(
        d_latent, latent_unit, latent_scale, latent_gain
    )
    grads = jnp.concatenate([
        oq.transpose(1, 2, 0, 3).reshape(3, r, width), ow[None], ou, od,
    ])
    square = jnp.broadcast_to(jnp.sum(grads * grads), (width,))
    rows = jnp.stack(
        gain_terms(d_media, media_unit) + gain_terms(d_latent, latent_unit) + ffn_terms
        + [square, jnp.zeros_like(square)]
    )
    sums = total(rows, n, size)
    return latents_out, media_grad, latents_grad, grads, sums[:6], sums[6, 0]


def on_device(n, size, media_tokens, patch_mask, latents, cotangent, weights, weights_first,
              weights_second, weights_average, norm_params, norm_first, norm_second, norm_average):
    g, patches, width = media_tokens.shape
    lat = latents.shape[1]
    r = width // (n * size)
    arrays = (
        media_tokens, patch_mask, latents, cotangent, weights, weights_first, weights_second,
        weights_average, norm_params, norm_first, norm_second, norm_average,
    )
    if r % 16 or lat % 16 or size != 4 or n != 2 * size or FF != 4 * width:
        latents_out, media_grad, latents_grad, grads, norm_grads, square = general_step(
            n, size, *arrays
        )
    else:
        media_grad, latents_grad, latents_out, grads, sums, squares = whole_step(
            weights, media_tokens, latents, cotangent, patch_mask, norm_params,
            n, size, HEADS // size, 1.0 / math.sqrt(width // HEADS),
        )
        done = finish(
            sums, squares, (weights, weights_first, weights_second, weights_average), grads,
            (norm_params, norm_first, norm_second, norm_average),
            (latents_out.reshape(g, lat, width), media_grad, latents_grad),
        )
        return (
            *done[11:14], done[0][0, 0], done[1], done[5], *done[2:5], *done[6:11],
        )
    grad_norm = jnp.sqrt(square + jnp.sum(norm_grads * norm_grads))
    clip = jnp.minimum(1.0, 1.0 / (grad_norm + 1e-06))
    new_w, new_first, new_second, new_avg = adamw_update(
        weights, weights_first, weights_second, weights_average,
        grads.reshape(weights.shape), clip, 0.1,
    )
    new_n, new_nf, new_ns, new_na = adamw_update(
        norm_params, norm_first, norm_second, norm_average, norm_grads, clip, 0.0
    )
    return (
        latents_out, media_grad, latents_grad, grad_norm, new_w, new_w.astype(BF16), new_first,
        new_second, new_avg, new_n, new_nf, new_ns, new_na, norm_grads[4:6],
    )


def solution(mesh):
    n, size = mesh.shape["dp"], mesh.shape["patch"]
    rows, weight = P("dp", "patch", None), P(None, ("dp", "patch"))
    return jax.shard_map(
        functools.partial(on_device, n, size),
        mesh=mesh,
        in_specs=(rows, P("dp", "patch"), rows, rows) + (weight,) * 4 + (P(),) * 4,
        out_specs=(rows, rows, rows, P()) + (weight,) * 5 + (P(),) * 5,
        check_vma=False,
    )
```

```python
import functools
import math

import jax
import jax.numpy as jnp
from jax import lax
from jax.experimental import pallas as pl
from jax.experimental.pallas import tpu as pltpu
from jax.sharding import PartitionSpec as P

HEADS = 16
FF = 4096
STEP = 7
MESH = pl.DeviceIdType.MESH
F32 = jnp.float32
BF16 = jnp.bfloat16
ANY = pl.BlockSpec(memory_space=pl.ANY)
VMEM = pl.BlockSpec(memory_space=pltpu.VMEM)
DMA = pltpu.SemaphoreType.DMA
VMEM_LIMIT = 64 * 1024 * 1024 - 65536


def struct(shape, kind):
    return jax.ShapeDtypeStruct(shape, kind)


def place():
    d, p = lax.axis_index("dp"), lax.axis_index("patch")
    return d, p, lax.div(d, 2), lax.rem(d, 2), lax.div(p, 2), lax.rem(p, 2)


def remote(src, dst, send, recv, to):
    return pltpu.make_async_remote_copy(
        src_ref=src, dst_ref=dst, send_sem=send, recv_sem=recv, device_id=to, device_id_type=MESH
    )


def greet(peers):
    barrier = pltpu.get_barrier_semaphore()
    for to in peers:
        pl.semaphore_signal(barrier, inc=1, device_id=to, device_id_type=MESH)
    return functools.partial(pl.semaphore_wait, barrier, len(peers))


def meet(always, maybe=()):
    barrier = pltpu.get_barrier_semaphore()
    count = len(always)
    for to in always:
        pl.semaphore_signal(barrier, inc=1, device_id=to, device_id_type=MESH)
    for there, to in maybe:

        @pl.when(there)
        def _(to=to):
            pl.semaphore_signal(barrier, inc=1, device_id=to, device_id_type=MESH)

        count = count + there.astype(jnp.int32)
    pl.semaphore_wait(barrier, count)


def patch_peers(d, p, size):
    return [(d, lax.rem(p + k, size)) for k in range(1, size)]


def params(number):
    return pltpu.CompilerParams(
        collective_id=number, has_side_effects=True, vmem_limit_bytes=VMEM_LIMIT
    )


def spread_kernel(chain, size, qs, wos, ups, dns, nms, nls, dys, cns,
                  wqkv, wo, up, dn, nm, nl, dy, cn,
                  loc, a_s, a_r, su, sd, sy, rz, ry, xs, xr, cs, cr):
    d, p, z, y, x, c = place()
    above, below = z + 1 < chain, z > 0
    up_dev, dn_dev = ((z + 1) * 2 + y, p), ((z - 1) * 2 + y, p)
    y_dev, x_dev, c_dev = (z * 2 + 1 - y, p), (d, (1 - x) * 2 + c), (d, x * 2 + 1 - c)
    px, pc = (1 - x) * 2 + c, x * 2 + 1 - c
    pd = (1 - x) * 2 + 1 - c
    meet(patch_peers(d, p, size) + [y_dev], [(above, up_dev), (below, dn_dev)])

    own = [
        (qs.at[p], wqkv.at[:, d, p]), (wos, wo.at[d, p]), (ups, up.at[:, d]), (dns, dn.at[:, d]),
        (nms, nm.at[:, p]), (nls, nl.at[:, p]), (dys, dy.at[p]), (cns, cn.at[p]),
    ]
    local = [pltpu.make_async_copy(a, b, loc.at[i]) for i, (a, b) in enumerate(own)]
    for copy in local:
        copy.start()
    swaps = []
    for k in range(1, size):
        q = lax.rem(p + k, size)
        swaps.append(remote(qs.at[q], wqkv.at[:, d, p], a_s.at[k], a_r.at[k], (d, q)))
    for copy in swaps:
        copy.start()

    rows = [(nms, nm), (nls, nl), (cns, cn), (dys, dy)]

    def slot(j, q):
        ref = rows[j][1] if j < 4 else wo
        return ref.at[q] if j in (2, 3) else ref.at[:, q]

    def row_copies(j):
        src = rows[j][0] if j < 4 else slot(j, p)
        return (
            remote(src, slot(j, p), xs.at[j], xr.at[j], x_dev),
            remote(src, slot(j, p), cs.at[j, 0], cr.at[j, 0], c_dev),
            remote(slot(j, px), slot(j, px), cs.at[j, 1], cr.at[j, 1], c_dev),
        )

    def start_rows(j):
        to_x, to_c, _ = row_copies(j)
        to_x.start()
        to_c.start()

    def pass_rows(j):
        to_x, _, on = row_copies(j)
        to_x.wait_recv()
        on.start()

    def end_rows(j):
        to_x, to_c, on = row_copies(j)
        to_c.wait_recv()
        on.wait_recv()
        to_x.wait_send()
        to_c.wait_send()
        on.wait_send()

    for j in range(4):
        start_rows(j)

    def piece(i, dd):
        return (wqkv.at[:, dd], wo.at[dd, p], up.at[:, dd], dn.at[:, dd])[i]

    first = (wqkv.at[:, d], wos, ups, dns)

    def hop(i, zz, sends, to, own_src=False):
        src = first[i] if own_src else piece(i, zz * 2 + y)
        return remote(src, piece(i, zz * 2 + y), sends.at[i, zz], rz.at[i, zz], to)

    def over(i, zz, own_src=False):
        src = first[i] if own_src else piece(i, zz * 2 + y)
        return remote(src, piece(i, zz * 2 + y), sy.at[i, zz], ry.at[i, zz], y_dev)

    def start_own(i):
        @pl.when(above)
        def _():
            hop(i, z, su, up_dev, True).start()

        @pl.when(below)
        def _():
            hop(i, z, sd, dn_dev, True).start()

        over(i, z, True).start()

    def forward(i):
        def step(s, carry):
            @pl.when(z - s >= 0)
            def _():
                hop(i, z - s, su, up_dev).wait_recv()

                @pl.when(above)
                def _():
                    hop(i, z - s, su, up_dev).start()

                over(i, z - s).start()

            @pl.when(z + s < chain)
            def _():
                hop(i, z + s, sd, dn_dev).wait_recv()

                @pl.when(below)
                def _():
                    hop(i, z + s, sd, dn_dev).start()

                over(i, z + s).start()

            return carry

        lax.fori_loop(1, chain, step, 0)

    def arrived(i):
        def step(zz, carry):
            src = piece(i, zz * 2 + 1 - y)
            remote(src, src, sy.at[i, zz], ry.at[i, zz], y_dev).wait_recv()
            return carry

        lax.fori_loop(0, chain, step, 0)

    def sent(i):
        def step(zz, carry):
            over(i, zz).wait_send()

            @pl.when(jnp.logical_and(above, zz <= z))
            def _():
                hop(i, zz, su, up_dev).wait_send()

            @pl.when(jnp.logical_and(below, zz >= z))
            def _():
                hop(i, zz, sd, dn_dev).wait_send()

            return carry

        lax.fori_loop(0, chain, step, 0)

    local[0].wait()
    for copy in swaps:
        copy.wait_recv()
    start_own(0)
    start_own(1)
    forward(0)
    start_own(2)
    forward(1)
    start_own(3)
    local[1].wait()
    arrived(1)
    start_rows(4)
    forward(2)
    for j in range(5):
        pass_rows(j)
    forward(3)
    arrived(0)
    arrived(2)
    arrived(3)
    for j in range(5):
        end_rows(j)
    for copy in swaps:
        copy.wait_send()
    for i in range(4):
        sent(i)
    for copy in local[2:]:
        copy.wait()


def spread(qs, wos, ups, dns, nms, nls, dys, cns, n, size):
    _, three, r, cols = qs.shape
    width = wos.shape[1]
    chain = n // 2
    g, patches, _ = nms.shape
    lat = nls.shape[1]
    return pl.pallas_call(
        functools.partial(spread_kernel, chain, size),
        name="spread",
        out_shape=(
            struct((three, n, size, r, cols), BF16),
            struct((n, size, r, width), BF16),
            struct((ups.shape[0], n, r, width), BF16),
            struct((dns.shape[0], n, r, width), BF16),
            struct((g, size, patches, width), BF16),
            struct((g, size, lat, width), BF16),
            struct((size,) + dys.shape, BF16),
            struct((size,) + cns.shape, F32),
        ),
        in_specs=[VMEM] * 8,
        out_specs=(ANY,) * 8,
        scratch_shapes=[
            DMA((8,)), DMA((size,)), DMA((size,)),
            DMA((4, chain)), DMA((4, chain)), DMA((4, chain)), DMA((4, chain)), DMA((4, chain)),
            DMA((5,)), DMA((5,)), DMA((5, 2)), DMA((5, 2)),
        ],
        compiler_params=params(0),
    )(qs, wos, ups, dns, nms, nls, dys, cns)


def to_rows_kernel(size, src, out, loc, ss, rs):
    d, p = lax.axis_index("dp"), lax.axis_index("patch")
    cols = src.shape[3]
    meet(patch_peers(d, p, size))
    here = out.at[:, :, pl.ds(pl.multiple_of(p * cols, cols), cols)]
    copies = []
    for k in range(1, size):
        q = lax.rem(p + k, size)
        copies.append(remote(src.at[:, q], here, ss.at[k], rs.at[k], (d, q)))
    for copy in copies:
        copy.start()
    mine = pltpu.make_async_copy(src.at[:, p], here, loc)
    mine.start()
    mine.wait()
    for copy in copies:
        copy.wait()


def to_rows(src, size, number):
    g, _, lat, cols = src.shape
    return pl.pallas_call(
        functools.partial(to_rows_kernel, size),
        name="to_rows",
        out_shape=struct((g, lat, size * cols), src.dtype),
        in_specs=[VMEM],
        out_specs=VMEM,
        scratch_shapes=[DMA, DMA((size,)), DMA((size,))],
        compiler_params=params(number),
    )(src)


def to_heads_kernel(size, src, out, loc, ss, rs):
    d, p = lax.axis_index("dp"), lax.axis_index("patch")
    cols = out.shape[3]
    meet(patch_peers(d, p, size))

    def part(q):
        return src.at[:, :, pl.ds(pl.multiple_of(q * cols, cols), cols)]

    copies = []
    for k in range(1, size):
        q = lax.rem(p + k, size)
        copies.append(remote(part(q), out.at[:, p], ss.at[k], rs.at[k], (d, q)))
    for copy in copies:
        copy.start()
    mine = pltpu.make_async_copy(part(p), out.at[:, p], loc)
    mine.start()
    mine.wait()
    for copy in copies:
        copy.wait()


def to_heads(src, size, number):
    g, lat, width = src.shape
    return pl.pallas_call(
        functools.partial(to_heads_kernel, size),
        name="to_heads",
        out_shape=struct((g, size, lat, width // size), src.dtype),
        in_specs=[VMEM],
        out_specs=VMEM,
        scratch_shapes=[DMA, DMA((size,)), DMA((size,))],
        compiler_params=params(number),
    )(src)


def join_rows_kernel(src, out, loc, ss, rs):
    d, p, z, y, x, c = place()
    x_dev, c_dev = (d, (1 - x) * 2 + c), (d, x * 2 + 1 - c)
    px = (1 - x) * 2 + c
    meet([x_dev, c_dev])
    to_x = remote(src, out.at[p], ss.at[0], rs.at[0], x_dev)
    to_c = remote(src, out.at[p], ss.at[1], rs.at[1], c_dev)
    on = remote(out.at[px], out.at[px], ss.at[2], rs.at[2], c_dev)
    to_x.start()
    to_c.start()
    mine = pltpu.make_async_copy(src, out.at[p], loc)
    mine.start()
    to_x.wait_recv()
    on.start()
    mine.wait()
    to_c.wait()
    on.wait()
    to_x.wait_send()


def join_rows(src, size, number):
    return pl.pallas_call(
        join_rows_kernel,
        name="join_rows",
        out_shape=struct((size,) + src.shape, src.dtype),
        in_specs=[VMEM],
        out_specs=VMEM,
        scratch_shapes=[DMA, DMA((3,)), DMA((3,))],
        compiler_params=params(number),
    )(src)


def split_rows_kernel(ins, src, out, half, mid, quarter, ss, rs):
    d, p, z, y, x, c = place()
    x_dev, c_dev = (d, (1 - x) * 2 + c), (d, x * 2 + 1 - c)
    meet([x_dev, c_dev])
    first = [remote(src.at[i, :, 1 - c], half.at[i], ss.at[i], rs.at[i], c_dev) for i in range(ins)]
    for copy in first:
        copy.start()
    second = []
    for i in range(ins):
        first[i].wait_recv()
        mid[i] = (half[i, 1 - x].astype(F32) + src[i, 1 - x, c].astype(F32)).astype(BF16)
        copy = remote(mid.at[i], quarter.at[i], ss.at[ins + i], rs.at[ins + i], x_dev)
        copy.start()
        second.append(copy)
    for i in range(ins):
        out[i] = half[i, x].astype(F32) + src[i, x, c].astype(F32)
    for i in range(ins):
        second[i].wait_recv()
        out[i] = out[i] + quarter[i].astype(F32)
    for copy in first + second:
        copy.wait_send()


def split_rows(src, number):
    ins, _, _, rows, width = src.shape
    return pl.pallas_call(
        functools.partial(split_rows_kernel, ins),
        name="split_rows",
        out_shape=struct((ins, rows, width), F32),
        in_specs=[VMEM],
        out_specs=VMEM,
        scratch_shapes=[
            pltpu.VMEM((ins, 2, rows, width), BF16),
            pltpu.VMEM((ins, rows, width), BF16),
            pltpu.VMEM((ins, rows, width), BF16),
            DMA((2 * ins,)), DMA((2 * ins,)),
        ],
        compiler_params=params(number),
    )(src)


def head_rows(q, hands):
    rows, cols = q.shape
    size = cols // hands
    lane = lax.broadcasted_iota(jnp.int32, (rows, cols), 1)
    zero = jnp.zeros_like(q)
    parts = [
        jnp.where(jnp.logical_and(lane >= h * size, lane < (h + 1) * size), q, zero)
        for h in range(hands)
    ]
    return jnp.concatenate(parts, axis=0)


def own_columns(full, hands):
    rows, cols = full.shape[0] // hands, full.shape[1]
    size = cols // hands
    lane = lax.broadcasted_iota(jnp.int32, (rows, cols), 1)
    out = jnp.zeros((rows, cols), F32)
    for h in range(hands):
        keep = jnp.logical_and(lane >= h * size, lane < (h + 1) * size)
        out = jnp.where(keep, full[h * rows : (h + 1) * rows], out)
    return out


def nt(a, b):
    return lax.dot_general(a, b, (((1,), (1,)), ((), ())), preferred_element_type=F32)


def nn(a, b):
    return lax.dot_general(a, b, (((1,), (0,)), ((), ())), preferred_element_type=F32)


def tn(a, b):
    return lax.dot_general(a, b, (((0,), (0,)), ((), ())), preferred_element_type=F32)


def soft(qb, kp, kl, real, scale):
    sp = nt(qb, kp) * scale
    sl = nt(qb, kl) * scale
    key = lax.broadcasted_iota(jnp.int32, sp.shape, 1).astype(F32)
    sp = jnp.where(key < real, sp, -1e30)
    peak = jnp.maximum(jnp.max(sp, axis=1, keepdims=True), jnp.max(sl, axis=1, keepdims=True))
    ep, el = jnp.exp(sp - peak), jnp.exp(sl - peak)
    total = jnp.sum(ep, axis=1, keepdims=True) + jnp.sum(el, axis=1, keepdims=True)
    return ep / total, el / total


def attend_kernel(hands, scale, real, q, kp, kl, vp, vl, out):
    g = pl.program_id(0)
    qb = head_rows(q[0], hands)
    pp, plat = soft(qb, kp[0], kl[0], real[g].astype(F32), scale)
    full = nn(pp.astype(BF16), vp[0]) + nn(plat.astype(BF16), vl[0])
    out[0] = own_columns(full, hands).astype(BF16)


def attend(real, q, kp, kl, vp, vl, hands, scale):
    g, lat, cols = q.shape
    patches = kp.shape[1]

    def spec(rows):
        return pl.BlockSpec((1, rows, cols), lambda i, real: (i, 0, 0))

    return pl.pallas_call(
        functools.partial(attend_kernel, hands, scale),
        name="attend",
        grid_spec=pltpu.PrefetchScalarGridSpec(
            num_scalar_prefetch=1,
            grid=(g,),
            in_specs=[spec(lat), spec(patches), spec(lat), spec(patches), spec(lat)],
            out_specs=spec(lat),
        ),
        out_shape=struct((g, lat, cols), BF16),
        compiler_params=pltpu.CompilerParams(dimension_semantics=("arbitrary",)),
    )(real, q, kp, kl, vp, vl)


def attend_back_kernel(hands, scale, real, q, kp, kl, vp, vl, da, dq, dkp, dkl, dvp, dvl):
    g = pl.program_id(0)
    qb = head_rows(q[0], hands)
    dab = head_rows(da[0], hands)
    pp, plat = soft(qb, kp[0], kl[0], real[g].astype(F32), scale)
    gp, gl = nt(dab, vp[0]), nt(dab, vl[0])
    delta = jnp.sum(pp * gp, axis=1, keepdims=True) + jnp.sum(plat * gl, axis=1, keepdims=True)
    sp, sl = (pp * (gp - delta)).astype(BF16), (plat * (gl - delta)).astype(BF16)
    dvp[0] = tn(pp.astype(BF16), dab).astype(BF16)
    dvl[0] = tn(plat.astype(BF16), dab).astype(BF16)
    dkp[0] = (tn(sp, qb) * scale).astype(BF16)
    dkl[0] = (tn(sl, qb) * scale).astype(BF16)
    full = nn(sp, kp[0]) + nn(sl, kl[0])
    dq[0] = (own_columns(full, hands) * scale).astype(BF16)


def attend_back(real, q, kp, kl, vp, vl, da, hands, scale):
    g, lat, cols = q.shape
    patches = kp.shape[1]

    def spec(rows):
        return pl.BlockSpec((1, rows, cols), lambda i, real: (i, 0, 0))

    return pl.pallas_call(
        functools.partial(attend_back_kernel, hands, scale),
        name="attend_back",
        grid_spec=pltpu.PrefetchScalarGridSpec(
            num_scalar_prefetch=1,
            grid=(g,),
            in_specs=[spec(lat), spec(patches), spec(lat), spec(patches), spec(lat), spec(lat)],
            out_specs=[spec(lat), spec(patches), spec(lat), spec(patches), spec(lat)],
        ),
        out_shape=(
            struct((g, lat, cols), BF16),
            struct((g, patches, cols), BF16),
            struct((g, lat, cols), BF16),
            struct((g, patches, cols), BF16),
            struct((g, lat, cols), BF16),
        ),
        compiler_params=pltpu.CompilerParams(dimension_semantics=("arbitrary",)),
    )(real, q, kp, kl, vp, vl, da)


def collect_kernel(chain, size, gq, gw, gu, gd, kp, kl,
                   oq, ow, ou, od, okp, okl,
                   yq, yw, yu, yd, uq, uw, uu, ud, dq, dw, du, dd,
                   wc, wsum, wx, total, kc, kx, lc, lx, fin,
                   ys, yr, us, ur, ds, dr, ks, kr, qs, qr):
    d, p, z, y, x, c = place()
    above, below = z + 1 < chain, z > 0
    up_dev, dn_dev = ((z + 1) * 2 + y, p), ((z - 1) * 2 + y, p)
    y_dev, x_dev, c_dev = (z * 2 + 1 - y, p), (d, (1 - x) * 2 + c), (d, x * 2 + 1 - c)
    meet(patch_peers(d, p, size) + [y_dev], [(above, up_dev), (below, dn_dev)])

    mine = (
        lambda k: gq.at[:, k], lambda k: total.at[k], lambda k: gu.at[:, k], lambda k: gd.at[:, k]
    )
    land_y, land_u, land_d = (yq, yw, yu, yd), (uq, uw, uu, ud), (dq, dw, du, dd)

    def over(i, zz):
        return remote(
            mine[i](zz * 2 + 1 - y), land_y[i].at[zz], ys.at[i, zz], yr.at[i, zz], y_dev
        )

    def send_over(i):
        def step(zz, carry):
            over(i, zz).start()
            return carry

        lax.fori_loop(0, chain, step, 0)

    def add_over(i):
        def step(zz, carry):
            over(i, zz).wait_recv()
            have = mine[i](zz * 2 + y)
            land_y[i][zz] = (land_y[i][zz].astype(F32) + have[...].astype(F32)).astype(BF16)
            return carry

        lax.fori_loop(0, chain, step, 0)

    def rise(i, zz):
        return remote(land_y[i].at[zz], land_u[i].at[zz], us.at[i, zz], ur.at[i, zz], up_dev)

    def fall(i, zz):
        return remote(land_y[i].at[zz], land_d[i].at[zz], ds.at[i, zz], dr.at[i, zz], dn_dev)

    def gather(i, zz, land):
        land_y[i][zz] = (land_y[i][zz].astype(F32) + land[i][zz].astype(F32)).astype(BF16)

    def along(i):
        def step(k, carry):
            s = chain - k

            @pl.when(z + s < chain)
            def _():
                @pl.when(below)
                def _():
                    rise(i, z + s).wait_recv()
                    gather(i, z + s, land_u)

                rise(i, z + s).start()

            @pl.when(z - s >= 0)
            def _():
                @pl.when(above)
                def _():
                    fall(i, z - s).wait_recv()
                    gather(i, z - s, land_d)

                fall(i, z - s).start()

            return carry

        lax.fori_loop(1, chain, step, 0)

    def finish(i, write):
        write(land_y[i][z].astype(F32))

        @pl.when(below)
        def _():
            rise(i, z).wait_recv()
            write(land_u[i][z].astype(F32), True)

        @pl.when(above)
        def _():
            fall(i, z).wait_recv()
            write(land_d[i][z].astype(F32), True)

    def into(ref):
        def write(value, more=False):
            ref[...] = ref[...] + value if more else value

        return write

    def sent(i):
        def step(zz, carry):
            over(i, zz).wait_send()

            @pl.when(zz > z)
            def _():
                rise(i, zz).wait_send()

            @pl.when(zz < z)
            def _():
                fall(i, zz).wait_send()

            return carry

        lax.fori_loop(0, chain, step, 0)

    send_over(2)
    w_core = remote(gw.at[:, :, 1 - c], wc, ks.at[0], kr.at[0], c_dev)
    p_core = remote(kp.at[:, :, 1 - c], kc, ks.at[1], kr.at[1], c_dev)
    l_core = remote(kl.at[:, :, 1 - c], lc, ks.at[2], kr.at[2], c_dev)
    w_core.start()
    p_core.start()
    l_core.start()
    send_over(3)
    send_over(0)

    w_core.wait_recv()

    def w_add(k, carry):
        wsum[k] = (wc[k, 1 - x].astype(F32) + gw[k, 1 - x, c].astype(F32)).astype(BF16)
        return carry

    lax.fori_loop(0, 2 * chain, w_add, 0)
    w_x = remote(wsum, wx, ks.at[3], kr.at[3], x_dev)
    w_x.start()

    p_core.wait_recv()
    images = kp.shape[0]

    def p_add(k, carry):
        kc[k] = (kc[k].astype(F32) + kp[k, :, c].astype(F32)).astype(BF16)
        return carry

    lax.fori_loop(0, images, p_add, 0)
    p_x = remote(kc.at[:, 1 - x], kx, ks.at[4], kr.at[4], x_dev)
    p_x.start()
    l_core.wait_recv()

    def l_add(k, carry):
        lc[k] = (lc[k].astype(F32) + kl[k, :, c].astype(F32)).astype(BF16)
        return carry

    lax.fori_loop(0, images, l_add, 0)
    l_x = remote(lc.at[:, 1 - x], lx, ks.at[5], kr.at[5], x_dev)
    l_x.start()

    w_x.wait_recv()

    def w_last(k, carry):
        total[k] = (
            wc[k, x].astype(F32) + gw[k, x, c].astype(F32) + wx[k].astype(F32)
        ).astype(BF16)
        return carry

    lax.fori_loop(0, 2 * chain, w_last, 0)
    send_over(1)

    add_over(2)
    along(2)
    add_over(3)
    along(3)
    add_over(0)
    along(0)
    add_over(1)
    along(1)
    finish(2, into(ou))
    finish(3, into(od))
    finish(0, into(fin))
    swaps = []
    for k in range(1, size):
        q = lax.rem(p + k, size)
        swaps.append(remote(fin.at[:, q], oq.at[p], qs.at[k], qr.at[k], (d, q)))
    for copy in swaps:
        copy.start()
    finish(1, into(ow))
    oq[p] = fin[:, p]

    p_x.wait_recv()

    def p_last(k, carry):
        okp[k] = kc[k, x].astype(F32) + kx[k].astype(F32)
        return carry

    lax.fori_loop(0, images, p_last, 0)
    l_x.wait_recv()

    def l_last(k, carry):
        okl[k] = lc[k, x].astype(F32) + lx[k].astype(F32)
        return carry

    lax.fori_loop(0, images, l_last, 0)
    for copy in swaps:
        copy.wait()
    for i in range(4):
        sent(i)
    for copy in (w_core, p_core, l_core, w_x, p_x, l_x):
        copy.wait_send()


def collect(gq, gw, gu, gd, kp, kl, n, size):
    chain = n // 2
    three, _, _, r, cols = gq.shape
    width = gw.shape[-1]
    fu, fd = gu.shape[0], gd.shape[0]
    g, two, _, patches, _ = kp.shape
    lat = kl.shape[3]
    lands = [
        ((three, size, r, cols)), ((r, width)), ((fu, r, width)), ((fd, r, width)),
    ]
    stage = [pltpu.VMEM((chain,) + s, BF16) for s in lands]
    return pl.pallas_call(
        functools.partial(collect_kernel, chain, size),
        name="collect",
        out_shape=(
            struct((size, three, r, cols), F32),
            struct((r, width), F32),
            struct((fu, r, width), F32),
            struct((fd, r, width), F32),
            struct((g, patches, width), F32),
            struct((g, lat, width), F32),
        ),
        in_specs=[VMEM] * 6,
        out_specs=(VMEM,) * 6,
        scratch_shapes=stage * 3
        + [
            pltpu.VMEM((n, two, r, width), BF16),
            pltpu.VMEM((n, r, width), BF16),
            pltpu.VMEM((n, r, width), BF16),
            pltpu.VMEM((n, r, width), BF16),
            pltpu.VMEM((g, two, patches, width), BF16),
            pltpu.VMEM((g, patches, width), BF16),
            pltpu.VMEM((g, two, lat, width), BF16),
            pltpu.VMEM((g, lat, width), BF16),
            pltpu.VMEM((three, size, r, cols), F32),
        ]
        + [DMA((4, chain))] * 6
        + [DMA((6,)), DMA((6,)), DMA((size,)), DMA((size,))],
        compiler_params=params(6),
    )(gq, gw, gu, gd, kp, kl)


def total_kernel(hops, src, out, hold, land, ss, rs):
    d, p = lax.axis_index("dp"), lax.axis_index("patch")

    def flip(v, bit):
        return v + bit - 2 * bit * lax.rem(lax.div(v, bit), 2)

    to = [(d, flip(p, b)) if kind else (flip(d, b), p) for kind, b in hops]
    meet(to)
    sends = []
    for i, who in enumerate(to):
        copy = remote(src if i == 0 else hold.at[i], land.at[i], ss.at[i], rs.at[i], who)
        copy.start()
        copy.wait_recv()
        sends.append(copy)
        value = (src[...] if i == 0 else hold[i]) + land[i]
        if i + 1 < len(to):
            hold[i + 1] = value
        else:
            out[...] = value
    for copy in sends:
        copy.wait_send()


def total(src, n, size):
    hops = [(True, 1 << b) for b in range(size.bit_length() - 1)]
    hops += [(False, 1 << b) for b in range(n.bit_length() - 1)]
    return pl.pallas_call(
        functools.partial(total_kernel, hops),
        name="total",
        out_shape=struct(src.shape, F32),
        in_specs=[VMEM],
        out_specs=VMEM,
        scratch_shapes=[
            pltpu.VMEM((len(hops),) + src.shape, F32),
            pltpu.VMEM((len(hops),) + src.shape, F32),
            DMA((len(hops),)), DMA((len(hops),)),
        ],
        compiler_params=params(7),
    )(src)


class Names:
    def __init__(self, pairs):
        self.__dict__.update(pairs)


def aligned(start, step, count=None):
    return pl.ds(pl.multiple_of(start * step, step), count or step)


def each(lo, hi, body):
    def step(k, carry):
        body(k)
        return carry

    lax.fori_loop(lo, hi, step, 0)


def unit_of(x):
    mean = jnp.mean(x, axis=-1, keepdims=True)
    centred = x - mean
    spread_ = jnp.mean(centred * centred, axis=-1, keepdims=True)
    scaled = lax.rsqrt(spread_ + 1e-05)
    return centred * scaled, scaled


def column_sum(a):
    return jnp.sum(a, axis=0, keepdims=True)


INPUTS = ("weights", "media", "latents", "cot", "mask", "norms")
OUTPUTS = ("media_grad", "latents_grad", "latents_out", "grads", "sums", "squares")


def crowd_of(images):
    return 3 if images % 3 == 0 else 1


def buffers(n, size, g, patches, lat, width, ups, r):
    chain, cols, own = n // 2, width // size, g * lat
    keys, rows, tiles = size * (patches + lat), patches + lat, width // 256
    crowd = crowd_of(g)
    crowds = g // crowd
    low = {
        "wqkv": (3, width, cols), "wo": (width // size, width), "ud": (3, ups, n * r, width),
        "nm": (g, size * patches, width), "nl": (g, size * lat, width), "dy": (size * own, width), "doa": (g, size * lat, width),
        "q": (g, size * lat, cols), "k": (g, keys, cols), "v": (g, keys, cols),
        "mixed": (g, size * lat, cols), "nf": (size * own, width),
        "hpart": (crowds, 2, 2, crowd * lat, width), "hhalf": (crowds, 2, crowd * lat, width),
        "hmid": (crowds, crowd * lat, width), "hquart": (crowds, crowd * lat, width),
        "gb": (ups, size * own, n * r), "du": (ups, size * own, n * r),
        "part": (2, tiles, 2, 2, own, 256), "half": (2, tiles, 2, own, 256),
        "mid": (2, tiles, own, 256), "quart": (2, tiles, own, 256),
        "dah": (g, size * lat, cols), "gwo": (2, size * r, width),
        "yq": (3, chain, size * r, cols), "zq": (3, chain + 1, size * r, cols),
        "yw": (size * r, width), "zw": (2, size * r, width),
        "yf": (2, chain, ups // 2, r, width), "zf": (2, chain + 1, ups // 2, r, width),
        "zb": (2, chain + 1, ups // 4, 2 * r, width), "yb": (2, ups // 4, r, width),
        "yn": (2, chain, ups // 4, r, width), "zn": (2, chain + 1, ups // 4, r, width),
        "kall": (2, 2, 2, rows, width), "kland": (g, 2, rows, width), "kx": (g, rows, width),
    }
    full = {
        "media": (g, patches, width), "latents": (g, lat, width), "cot": (g, lat, width),
        "norms": (6, width), "hidden": (own, width), "dhid": (own, width),
        "fin": (3, size * r, cols), "wfin": (size * r, width), "grads": (3 + 1 + 2 * ups, r, width), "gsum": (8, width),
        "flat": (3 + 1 + 2 * ups, r * width),
        "turn": (width // 128, (3 + 1 + 2 * ups) * r, 128),
        "cn": (size, (g + 15) // 16 * 16, size * patches),
        "nland": (size, 8, width), "nhold": (8, width), "dland": (n, 8, width),
        "sland": (size, 8, 128), "shold": (8, 128), "tland": (n, 8, 128), "sqr": (8, 128),
    }
    sems = {
        "loc": (7,), "ins": (5,), "outs": (3,), "mouts": (2,),
        "a_s": (size,), "a_r": (size,), "su": (7, chain), "sd": (7, chain), "sy": (7, chain),
        "rz": (7, chain), "ry": (7, chain), "was": (1,), "war": (size,), "ww": (5,),
        "hcs": (crowds,), "hcr": (crowds,), "hxs": (crowds,), "hxr": (crowds,),
        "nxs": (crowds,), "nxr": (crowds,), "ncs": (crowds, 2), "ncr": (crowds, 2),
        "dxs": (crowds,), "dxr": (crowds,), "dcs": (crowds, 2), "dcr": (crowds, 2),
        "ms": (crowds,), "mr": (crowds,), "mcs": (crowds, 2), "mcr": (crowds, 2),
        "xs": (3,), "xr": (3,), "cs": (3, 2), "cr": (3, 2),
        "ps": (2, tiles), "pr": (2, tiles), "qs": (2, tiles),
        "qr": (2, tiles), "gws": (3,), "gwr": (3,), "ks": (2,), "kr": (g,), "lxs": (g,), "lxr": (g,),
        "gyr": (7, chain), "gzr": (7, chain + 1),
        "es": (size,), "er": (size,),
        "bzr": (2, chain + 1), "bys": (2,), "byr": (2,),
        "fs": (3, size), "fr": (3, size),
        "n1s": (size,), "n1r": (size,), "n2s": (n,), "n2r": (n,), "s1r": (size,), "s2r": (n,), "s1s": (size,), "s2s": (n,),
    }
    scratch = [(k, pltpu.VMEM(s, BF16)) for k, s in low.items()]
    scratch += [(k, pltpu.VMEM(s, F32)) for k, s in full.items()]
    scratch += [("held", pltpu.VMEM((4 + 2 * ups, r, width), BF16))]
    scratch += [(k, DMA(s)) for k, s in sems.items()]
    return scratch


def step_kernel(n, size, hands, scale, names, *refs):
    chain = n // 2
    count = len(INPUTS) + len(OUTPUTS)
    into = Names(zip(INPUTS, refs[: len(INPUTS)]))
    out = Names(zip(OUTPUTS, refs[len(INPUTS) : count]))
    b = Names(zip(names, refs[count:]))
    d, p, z, y, x, c = place()
    held, media, latents, cot, norms = b.held, b.media, b.latents, b.cot, b.norms
    wqkv, wo, ud, nm, nl, dy, cn = b.wqkv, b.wo, b.ud, b.nm, b.nl, b.dy, b.cn
    q, k_, v_, mixed, hidden, nf, doa = b.q, b.k, b.v, b.mixed, b.hidden, b.nf, b.doa
    r, width = held.shape[1], held.shape[2]
    cols, ups = width // size, ud.shape[1]
    images, patches, _ = media.shape
    lat = latents.shape[1]
    own, keys, reals = images * lat, size * (patches + lat), size * patches
    tiles = width // 256
    above, below = z + 1 < chain, z > 0
    up_dev, dn_dev = ((z + 1) * 2 + y, p), ((z - 1) * 2 + y, p)
    y_dev, x_dev, c_dev = (z * 2 + 1 - y, p), (d, (1 - x) * 2 + c), (d, x * 2 + 1 - c)
    px = (1 - x) * 2 + c
    dp_peers = [(lax.rem(d + s, n), p) for s in range(1, n)]

    loads = [
        pltpu.make_async_copy(src, dst, b.ins.at[i])
        for i, (src, dst) in enumerate(
            ((into.weights, b.flat), (into.cot, cot), (into.norms, norms),
             (into.latents, latents), (into.media, media))
        )
    ]
    for copy in loads:
        copy.start()
    everyone_here = greet(patch_peers(d, p, size) + dp_peers)
    blocks = held.shape[0]
    loads[0].wait()
    for t in range(width // 128):
        for k in range(r):
            at = k * width + t * 128
            b.turn[t, pl.ds(k, blocks, stride=r), :] = b.flat[:, at : at + 128]
        held[:, :, t * 128 : (t + 1) * 128] = (
            b.turn[t].reshape(blocks, r, 128).astype(BF16)
        )
    loads[1].wait()
    dy[aligned(p, own)] = cot[...].reshape(own, width).astype(BF16)
    everyone_here()

    def lanes(k):
        return aligned(k, cols)

    half, quarter = ups // 2, ups // 4
    most = ups - quarter
    blocks_of = {
        3: (0, 0, half), 4: (0, half, half), 5: (1, 0, most), 6: (1, most, quarter),
    }
    def piece(i, dd):
        if i < 3:
            return wqkv.at[i, aligned(dd, size * r)]
        return ud.at[blocks_of[i][0], pl.ds(*blocks_of[i][1:]), aligned(dd, r)]

    first = [wqkv.at[i, aligned(d, size * r)] for i in range(3)]
    for i in range(3, 7):
        plane, start, many = blocks_of[i]
        first.append(held.at[pl.ds(4 + plane * ups + start, many)])
    here = wqkv.at[:, aligned(d * size + p, r)]
    def hop(i, zz, sends, to, own_src=False):
        src = first[i] if own_src else piece(i, zz * 2 + y)
        return remote(src, piece(i, zz * 2 + y), sends.at[i, zz], b.rz.at[i, zz], to)

    def over(i, zz, own_src=False):
        src = first[i] if own_src else piece(i, zz * 2 + y)
        return remote(src, piece(i, zz * 2 + y), b.sy.at[i, zz], b.ry.at[i, zz], y_dev)

    def start_own(i):
        @pl.when(above)
        def _():
            hop(i, z, b.su, up_dev, True).start()

        @pl.when(below)
        def _():
            hop(i, z, b.sd, dn_dev, True).start()

        over(i, z, True).start()

    swaps = []
    for k in range(1, size):
        to = lax.rem(p + k, size)
        swaps.append(
            remote(held.at[pl.ds(0, 3), :, lanes(to)], here, b.a_s.at[k], b.a_r.at[k], (d, to))
        )
    for copy in swaps:
        copy.start()
    wo_near = remote(
        held.at[3], wo.at[aligned(y * size + p, r)], b.was.at[0], b.war.at[p], (d, z)
    )
    wo_own = pltpu.make_async_copy(held.at[3], wo.at[aligned(y * size + p, r)], b.loc.at[1])

    @pl.when(z != p)
    def _():
        wo_near.start()

    @pl.when(z == p)
    def _():
        wo_own.start()

    start_own(3)
    over(6, z, True).start()
    local = [pltpu.make_async_copy(held.at[pl.ds(0, 3), :, lanes(p)], here, b.loc.at[0])]
    local += [pltpu.make_async_copy(first[i], piece(i, d), b.loc.at[i]) for i in range(3, 7)]
    for copy in local:
        copy.start()

    def forward(i, s):
        @pl.when(z - s >= 0)
        def _():
            hop(i, z - s, b.su, up_dev).wait_recv()

            @pl.when(above)
            def _():
                hop(i, z - s, b.su, up_dev).start()

            over(i, z - s).start()

        @pl.when(z + s < chain)
        def _():
            hop(i, z + s, b.sd, dn_dev).wait_recv()

            @pl.when(below)
            def _():
                hop(i, z + s, b.sd, dn_dev).start()

            over(i, z + s).start()

    def pair(k, zz):
        return ud.at[1, pl.ds(most + k * quarter, quarter), aligned(zz, 2 * r)]

    def pair_hop(k, zz, sends, to):
        return remote(pair(k, zz), pair(k, zz), sends.at[6 + k, zz], b.rz.at[6 + k, zz], to)

    def pair_start():
        for k in range(1):
            src = piece(6 + k, z * 2 + 1 - y)
            local[4 + k].wait()
            remote(src, src, b.sy.at[6 + k, z], b.ry.at[6 + k, z], y_dev).wait_recv()

            @pl.when(above)
            def _():
                pair_hop(k, z, b.su, up_dev).start()

            @pl.when(below)
            def _():
                pair_hop(k, z, b.sd, dn_dev).start()

    def pair_forward(s):
        for k in range(1):

            @pl.when(z - s >= 0)
            def _():
                pair_hop(k, z - s, b.su, up_dev).wait_recv()

                @pl.when(above)
                def _():
                    pair_hop(k, z - s, b.su, up_dev).start()

            @pl.when(z + s < chain)
            def _():
                pair_hop(k, z + s, b.sd, dn_dev).wait_recv()

                @pl.when(below)
                def _():
                    pair_hop(k, z + s, b.sd, dn_dev).start()

    def pair_sent():
        for k in range(1):
            over(6 + k, z).wait_send()

            def step(zz):
                @pl.when(jnp.logical_and(above, zz <= z))
                def _():
                    pair_hop(k, zz, b.su, up_dev).wait_send()

                @pl.when(jnp.logical_and(below, zz >= z))
                def _():
                    pair_hop(k, zz, b.sd, dn_dev).wait_send()

            each(0, chain, step)

    def arrived(i):
        def step(zz):
            src = piece(i, zz * 2 + 1 - y)
            remote(src, src, b.sy.at[i, zz], b.ry.at[i, zz], y_dev).wait_recv()

        each(0, chain, step)

    def sent(i):
        def step(zz):
            over(i, zz).wait_send()

            @pl.when(jnp.logical_and(above, zz <= z))
            def _():
                hop(i, zz, b.su, up_dev).wait_send()

            @pl.when(jnp.logical_and(below, zz >= z))
            def _():
                hop(i, zz, b.sd, dn_dev).wait_send()

        each(0, chain, step)

    class Rows:
        def __init__(self, slot, xs, xr, cs, cr, at, src=None):
            src = slot(p) if src is None else src
            self.to_x = remote(src, slot(p), xs.at[at], xr.at[at], x_dev)
            self.to_c = remote(src, slot(p), cs.at[at, 0], cr.at[at, 0], c_dev)
            self.on = remote(slot(px), slot(px), cs.at[at, 1], cr.at[at, 1], c_dev)

        def start(self):
            self.to_x.start()
            self.to_c.start()

        def forward(self):
            self.to_x.wait_recv()
            self.on.start()

        def have(self):
            self.to_c.wait_recv()
            self.on.wait_recv()

        def end(self):
            self.to_x.wait_send()
            self.to_c.wait_send()
            self.on.wait_send()

    def group(slot, j, src=None):
        return Rows(slot, b.xs, b.xr, b.cs, b.cr, j, src)

    lat_rows = group(lambda k: nl.at[:, aligned(k, lat)], 0)
    cn_rows = group(lambda k: cn.at[k], 1)
    dy_rows = group(lambda k: dy.at[aligned(k, own)], 2)

    def wo_block(k):
        return wo.at[aligned(k, size * r)]

    def wo_hop(e, to, k):
        return remote(wo_block(k), wo_block(k), b.ww.at[e], b.ww.at[3 + e // 2], to)

    def wo_pass(first_end, second_end):
        @pl.when(first_end)
        def _():
            wo_hop(0, up_dev, y).start()

        @pl.when(second_end)
        def _():
            wo_hop(1, dn_dev, y).start()

        wo_hop(2, y_dev, y).start()

    def wo_source():
        @pl.when(z == p)
        def _():
            for k in range(1, size):
                who = lax.rem(p + k, size)
                part = wo.at[aligned(y * size + who, r)]
                remote(part, part, b.was.at[0], b.war.at[who], (d, who)).wait_recv()
            wo_own.wait()
            wo_pass(above, below)

    def wo_stage(k):
        @pl.when(z == p + k)
        def _():
            wo_hop(0, up_dev, y).wait_recv()
            wo_pass(above, z < 0)

        @pl.when(z == p - k)
        def _():
            wo_hop(0, dn_dev, y).wait_recv()
            wo_pass(z < 0, below)

    def wo_have():
        wo_hop(2, y_dev, 1 - y).wait_recv()

    def wo_sent():
        @pl.when(jnp.logical_and(z >= p, above))
        def _():
            wo_hop(0, up_dev, y).wait_send()

        @pl.when(jnp.logical_and(z <= p, below))
        def _():
            wo_hop(1, dn_dev, y).wait_send()

        wo_hop(2, y_dev, y).wait_send()

        @pl.when(z != p)
        def _():
            wo_near.wait_send()

    crowd = crowd_of(images)
    crowds = images // crowd

    def media_rows(j):
        return Rows(
            lambda k: nm.at[aligned(j, crowd), aligned(k, patches)],
            b.ms, b.mr, b.mcs, b.mcr, j,
        )

    fold = crowd * lat

    def nf_rows(j):
        return Rows(
            lambda k: nf.at[pl.ds(pl.multiple_of(k * own + j * fold, fold), fold)],
            b.nxs, b.nxr, b.ncs, b.ncr, j,
        )

    def do_rows(j):
        return Rows(
            lambda k: doa.at[aligned(j, crowd), aligned(k, lat)],
            b.dxs, b.dxr, b.dcs, b.dcr, j,
        )

    loads[2].wait()
    loads[3].wait()
    media_gain, media_shift = 1.0 + norms[0:1, :], norms[1:2, :]
    latent_gain, latent_shift = 1.0 + norms[2:3, :], norms[3:4, :]
    ffn_gain, ffn_shift = 1.0 + norms[4:5, :], norms[5:6, :]

    def latent_norm(g):
        unit, _ = unit_of(latents[g])
        nl[g, aligned(p, lat)] = (unit * latent_gain + latent_shift).astype(BF16)

    def media_norm(g):
        unit, _ = unit_of(media[g])
        nm[g, aligned(p, patches)] = (unit * media_gain + media_shift).astype(BF16)

    dy_rows.start()
    cn[p] = jnp.zeros(cn.shape[1:], F32)
    counts = column_of((into.mask[...] > 0).astype(F32))
    cn[p, :images, :] = jnp.broadcast_to(counts, (images, cn.shape[2]))
    each(0, images, latent_norm)
    cn_rows.start()
    lat_rows.start()
    local[0].wait()
    for copy in swaps:
        copy.wait_recv()
    for i in range(3):
        start_own(i)
    loads[4].wait()
    each(0, images, media_norm)
    each(0, crowds, lambda j: media_rows(j).start())
    wo_source()
    for s in range(1, chain):
        for i in range(3):
            forward(i, s)
        if s == 1:
            dy_rows.forward()
            cn_rows.forward()
        if s == min(2, chain - 1):
            start_own(4)
    lat_rows.forward()
    wo_stage(1)
    wo_stage(2)
    for s in range(1, chain - 1):
        forward(3, s)
        if s == 1:
            start_own(5)
    pair_start()
    media_rows(0).forward()
    for i in range(3):
        arrived(i)
    lat_rows.have()
    cn_rows.have()

    flat_nl = nl[...].reshape(images * size * lat, width)
    q[...] = nn(flat_nl, wqkv[0]).astype(BF16).reshape(images, size * lat, cols)
    k_[:, reals:] = nn(flat_nl, wqkv[1]).astype(BF16).reshape(images, size * lat, cols)
    v_[:, reals:] = nn(flat_nl, wqkv[2]).astype(BF16).reshape(images, size * lat, cols)

    def real_keys(g):
        real = cn[0, pl.ds(g, 1), :]
        for k in range(1, size):
            real = real + cn[k, pl.ds(g, 1), :]
        return real

    def image(g):
        k_[g, :reals] = nn(nm[g], wqkv[1]).astype(BF16)
        v_[g, :reals] = nn(nm[g], wqkv[2]).astype(BF16)
        pp, plat = soft(
            head_rows(q[g], hands), k_[g, :reals], k_[g, reals:], real_keys(g), scale
        )
        full = nn(pp.astype(BF16), v_[g, :reals]) + nn(plat.astype(BF16), v_[g, reals:])
        mixed[g] = own_columns(full, hands).astype(BF16)

    def hid_core(j):
        return remote(b.hpart.at[j, :, 1 - c], b.hhalf.at[j], b.hcs.at[j], b.hcr.at[j], c_dev)

    def hid_x(j):
        return remote(b.hmid.at[j], b.hquart.at[j], b.hxs.at[j], b.hxr.at[j], x_dev)

    def hid_part(j):
        rows = mixed[j * crowd : (j + 1) * crowd].reshape(crowd * size * lat, cols)
        for t in range(tiles):
            span = pl.ds(256 * t, 256)
            value = nn(rows, wo[:, span]).astype(BF16)
            for i in range(crowd):
                for e in range(size):
                    at = (i * size + e) * lat
                    b.hpart[j, e // 2, e % 2, i * lat : (i + 1) * lat, span] = value[at : at + lat]
        hid_core(j).start()

    def hid_pass(j):
        hid_core(j).wait_recv()
        b.hmid[j] = (b.hhalf[j, 1 - x].astype(F32) + b.hpart[j, 1 - x, c].astype(F32)).astype(BF16)
        hid_x(j).start()

    def hid_end(j):
        hid_x(j).wait_recv()
        value = (
            latents[j * crowd : (j + 1) * crowd].reshape(fold, width)
            + b.hhalf[j, x].astype(F32) + b.hpart[j, x, c].astype(F32) + b.hquart[j].astype(F32)
        )
        hidden[j * fold : (j + 1) * fold] = value
        unit, _ = unit_of(value)
        nf[pl.ds(pl.multiple_of(p * own + j * fold, fold), fold)] = (
            unit * ffn_gain + ffn_shift
        ).astype(BF16)
        nf_rows(j).start()

    pending = [(3, chain - 1)] + [(i, s) for i in (4, 5) for s in range(1, chain)]

    def forward_some(count):
        for _ in range(count):
            if pending:
                forward(*pending.pop(0))

    for j in range(crowds):
        if j:
            media_rows(j).forward()
            forward_some(1)
        media_rows(j).have()
        each(j * crowd, (j + 1) * crowd, image)
        if j == 0:
            for k in range(3, chain):
                wo_stage(k)
            wo_have()
        hid_part(j)
        if j > 0:
            hid_end(j - 1)
        forward_some(1)
        hid_pass(j)
        forward_some(1)
    forward_some(len(pending))
    for j in range(crowds - 1):
        nf_rows(j).forward()
    hid_end(crowds - 1)
    for s in range(1, chain - 1):
        pair_forward(s)
    dy_rows.have()
    for i in (3, 4, 5):
        arrived(i)
    for copy in local[1:4]:
        copy.wait()
    nf_rows(crowds - 1).forward()
    for j in range(crowds):
        nf_rows(j).have()

    def hidden_block(e):
        u = nt(nf[...], ud[0, e])
        into_active = nt(dy[...], ud[1, e])
        chance = 0.5 * (1.0 + lax.erf(u * math.sqrt(0.5)))
        slope = chance + u * jnp.exp(-0.5 * u * u) * (1.0 / math.sqrt(2.0 * math.pi))
        b.gb[e] = (u * chance).astype(BF16)
        b.du[e] = (into_active * slope).astype(BF16)

    def down_grad(e):
        for t in range(0, width, 512):
            ud[2, e, :, t : t + 512] = tn(b.gb[e], dy[:, t : t + 512]).astype(BF16)

    def up_grad(e):
        for t in range(0, width, 512):
            ud[0, e, :, t : t + 512] = tn(b.du[e], nf[:, t : t + 512]).astype(BF16)

    def part_core(i, t):
        return remote(
            b.part.at[i, t, :, 1 - c], b.half.at[i, t], b.ps.at[i, t], b.pr.at[i, t], c_dev
        )

    def part_x(i, t):
        return remote(b.mid.at[i, t], b.quart.at[i, t], b.qs.at[i, t], b.qr.at[i, t], x_dev)

    def part_of(i, acts, passing=False):
        def tile(t):
            span = aligned(t, 256)
            acc = nn(acts[0], ud[i, 0, :, span])
            for e in range(1, ups):
                acc = acc + nn(acts[e], ud[i, e, :, span])
            b.part[i, t] = acc.astype(BF16).reshape(2, 2, own, 256)
            part_core(i, t).start()
            if passing:
                @pl.when(t > 1)
                def _():
                    pass_tile(i, t - 2)

        each(0, tiles, tile)
        if passing:
            each(max(tiles - 2, 0), tiles, lambda t: pass_tile(i, t))

    def part_pass(i):
        each(0, tiles, lambda t: pass_tile(i, t))

    def pass_tile(i, t):
        part_core(i, t).wait_recv()
        b.mid[i, t] = (
            b.half[i, t, 1 - x].astype(F32) + b.part[i, t, 1 - x, c].astype(F32)
        ).astype(BF16)
        part_x(i, t).start()

    def part_end(i, write):
        def tile(t):
            part_x(i, t).wait_recv()
            write(
                aligned(t, 256),
                b.half[i, t, x].astype(F32) + b.part[i, t, x, c].astype(F32)
                + b.quart[i, t].astype(F32),
            )

        each(0, tiles, tile)

    def parts_sent(i):
        def tile(t):
            part_core(i, t).wait_send()
            part_x(i, t).wait_send()

        each(0, tiles, tile)

    def ffn_part(i, k):
        plane, start, many = {
            3: (2, 0, quarter), 4: (0, 0, half), 5: (0, half, half), 6: (2, most, quarter)
        }[i]
        return ud.at[plane, pl.ds(start, many), aligned(k, r)]

    class Staged:
        def stage(self, k):
            @pl.when(z == k)
            def _():
                each(0, chain - 1 - k, lambda t: self.move(
                    chain - 1 - t, k > 0, chain - t, up_dev
                ))

            @pl.when(chain - 1 - z == k)
            def _():
                each(0, chain - 1 - k, lambda t: self.move(t, k > 0, t, dn_dev))

    class Sum(Staged):
        def __init__(self, i, kind):
            self.i = i
            if kind == 0:
                self.mine = lambda k: wqkv.at[i, aligned(k, size * r)]
                self.ly, self.lz = b.yq.at[i], b.zq.at[i]
            else:
                self.mine = lambda k: ffn_part(i, k)
                self.ly = b.yf.at[i - 4] if i in (4, 5) else b.yn.at[i // 6]
                self.lz = b.zf.at[i - 4] if i in (4, 5) else b.zn.at[i // 6]

        def over(self, zt):
            return remote(
                self.mine(zt * 2 + 1 - y), self.ly.at[zt], b.sy.at[self.i, zt],
                b.gyr.at[self.i, zt], y_dev,
            )

        def along(self, zt, slot, to):
            return remote(
                self.ly.at[zt], self.lz.at[slot], b.su.at[self.i, zt], b.gzr.at[self.i, slot], to
            )

        def send(self):
            def step(k):
                s = chain - 1 - k

                @pl.when(z + s < chain)
                def _():
                    self.over(z + s).start()

                @pl.when(jnp.logical_and(z - s >= 0, s > 0))
                def _():
                    self.over(z - s).start()

            each(0, chain, step)

        def pair(self, zt):
            return self.ly[zt].astype(F32) + self.mine(zt * 2 + y)[...].astype(F32)

        def move(self, zt, more, slot, to):
            self.over(zt).wait_recv()
            if more:
                self.along(zt, slot, to).wait_recv()
                self.ly[zt] = (self.pair(zt) + self.lz[slot].astype(F32)).astype(BF16)
            else:
                self.ly[zt] = self.pair(zt).astype(BF16)
            self.along(zt, slot, to).start()

        def last(self, dst):
            self.over(z).wait_recv()
            dst[...] = self.pair(z)

            @pl.when(below)
            def _():
                self.along(z, z + 1, up_dev).wait_recv()
                dst[...] = dst[...] + self.lz[z + 1].astype(F32)

            @pl.when(above)
            def _():
                self.along(z, z, dn_dev).wait_recv()
                dst[...] = dst[...] + self.lz[z].astype(F32)

        def sent(self):
            def step(zt):
                self.over(zt).wait_send()

                @pl.when(zt != z)
                def _():
                    self.along(zt, 0, up_dev).wait_send()

            each(0, chain, step)

    class Cross(Staged):
        def __init__(self, k):
            self.k, self.blocks = k, pl.ds((1 + k) * quarter, quarter)
            self.lz, self.ly = b.zb.at[k], b.yb.at[k]

        def pair(self, zt):
            return ud.at[2, self.blocks, aligned(zt, 2 * r)]

        def along(self, zt, slot, to):
            return remote(
                self.pair(zt), self.lz.at[slot], b.sd.at[self.k, zt], b.bzr.at[self.k, slot], to
            )

        def move(self, zt, more, slot, to):
            if more:
                self.along(zt, slot, to).wait_recv()
                self.pair(zt)[...] = (
                    self.pair(zt)[...].astype(F32) + self.lz[slot].astype(F32)
                ).astype(BF16)
            self.along(zt, slot, to).start()

        def over(self):
            src = ud.at[2, self.blocks, aligned(z * 2 + 1 - y, r)]
            return remote(src, self.ly, b.bys.at[self.k], b.byr.at[self.k], y_dev)

        def meet(self, dst):
            theirs, ours = aligned(1 - y, r), aligned(y, r)
            far = ud.at[2, self.blocks, aligned(z * 2 + 1 - y, r)]
            near = ud.at[2, self.blocks, aligned(z * 2 + y, r)]
            dst[...] = near[...].astype(F32)

            def add(slot):
                dst[...] = dst[...] + self.lz[slot, :, ours].astype(F32)
                far[...] = (
                    far[...].astype(F32) + self.lz[slot, :, theirs].astype(F32)
                ).astype(BF16)

            @pl.when(below)
            def _():
                self.along(z, z + 1, up_dev).wait_recv()
                add(z + 1)

            @pl.when(above)
            def _():
                self.along(z, z, dn_dev).wait_recv()
                add(z)

            self.over().start()

        def last(self, dst):
            self.over().wait_recv()
            dst[...] = dst[...] + self.ly[...].astype(F32)

        def sent(self):
            self.over().wait_send()

            def step(zt):
                @pl.when(zt != z)
                def _():
                    self.along(zt, 0, up_dev).wait_send()

            each(0, chain, step)

    class Gather:
        def over(self):
            return remote(b.gwo.at[1 - y], b.yw, b.gws.at[0], b.gwr.at[0], y_dev)

        def rise(self):
            return remote(b.gwo.at[y], b.zw.at[0], b.gws.at[1], b.gwr.at[1], up_dev)

        def fall(self):
            return remote(b.gwo.at[y], b.zw.at[1], b.gws.at[2], b.gwr.at[2], dn_dev)

        def send(self):
            self.over().start()

        def add(self, k):
            b.gwo[y] = (b.gwo[y].astype(F32) + b.zw[k].astype(F32)).astype(BF16)

        def step(self, k):
            @pl.when(jnp.logical_or(
                jnp.logical_and(z < p, z == k), jnp.logical_and(z > p, chain - 1 - z == k)
            ))
            def _():
                self.over().wait_recv()
                b.gwo[y] = (b.gwo[y].astype(F32) + b.yw[...].astype(F32)).astype(BF16)

                @pl.when(z < p)
                def _():
                    if k:
                        self.rise().wait_recv()
                        self.add(0)
                    self.rise().start()

                @pl.when(z > p)
                def _():
                    if k:
                        self.fall().wait_recv()
                        self.add(1)
                    self.fall().start()

        def part(self, k, to):
            return remote(
                b.wfin.at[aligned(k, r)], b.grads.at[3], b.es.at[k], b.er.at[0], to
            )

        def last(self):
            @pl.when(z == p)
            def _():
                self.over().wait_recv()
                b.wfin[...] = b.gwo[y].astype(F32) + b.yw[...].astype(F32)

                @pl.when(below)
                def _():
                    self.rise().wait_recv()
                    b.wfin[...] = b.wfin[...] + b.zw[0].astype(F32)

                @pl.when(above)
                def _():
                    self.fall().wait_recv()
                    b.wfin[...] = b.wfin[...] + b.zw[1].astype(F32)

                for k in range(1, size):
                    to = lax.rem(p + k, size)
                    self.part(to, (d, to)).start()
                b.grads[3] = b.wfin[aligned(p, r)]

        def have(self):
            @pl.when(z != p)
            def _():
                self.part(0, (d, z)).wait_recv()

        def sent(self):
            self.over().wait_send()

            @pl.when(z < p)
            def _():
                self.rise().wait_send()

            @pl.when(z > p)
            def _():
                self.fall().wait_send()

            @pl.when(z == p)
            def _():
                for k in range(1, size):
                    to = lax.rem(p + k, size)
                    self.part(to, (d, to)).wait_send()

    crosses = [Cross(0), Cross(1)]

    qkv_sums, wo_sum = [Sum(i, 0) for i in range(3)], Gather()

    ffn_sums = {i: Sum(i, 2) for i in (3, 4, 5, 6)}

    each(0, quarter, hidden_block)
    each(0, quarter, down_grad)
    for i in range(6):
        sent(i)
    pair_sent()
    wo_sent()
    ffn_sums[3].send()
    for k in range(2):
        each((1 + k) * quarter, (2 + k) * quarter, hidden_block)
        each((1 + k) * quarter, (2 + k) * quarter, down_grad)
        crosses[k].stage(0)
    pair_forward(chain - 1)
    each(most, ups, hidden_block)
    each(most, ups, down_grad)
    ffn_sums[6].send()
    part_of(0, b.du, True)
    each(0, ups, up_grad)
    ffn_sums[4].send()
    ffn_sums[5].send()
    part_of(1, b.gb)

    def write_dhid(span, value):
        b.dhid[:, span] = value

    part_end(0, write_dhid)
    dn = b.dhid[...]
    unit, scaled = unit_of(hidden[...])
    b.gsum[...] = jnp.zeros_like(b.gsum)
    b.gsum[4:5, :] = column_sum(dn * unit)
    b.gsum[5:6, :] = column_sum(dn)
    b.dhid[...] = cot[...].reshape(own, width) + norm_back(dn, unit, scaled, ffn_gain)
    for j in range(crowds):
        doa[j * crowd : (j + 1) * crowd, aligned(p, lat)] = (
            b.dhid[j * fold : (j + 1) * fold].astype(BF16).reshape(crowd, lat, width)
        )
        do_rows(j).start()
    def stages(*pairs):
        for item, k in pairs:
            if k < chain - 1:
                item.stage(k)

    def head_grads(j):
        do_rows(j).have()
        rows = doa[j * crowd : (j + 1) * crowd].reshape(crowd * size * lat, width)
        b.dah[j * crowd : (j + 1) * crowd] = (
            nt(rows, wo[...]).astype(BF16).reshape(crowd, size * lat, cols)
        )

    def out_grad():
        for t in range(tiles):
            span = pl.ds(256 * t, 256)
            b.gwo[:, :, span] = tn(
                mixed[...].reshape(images * size * lat, cols),
                doa[:, :, span].reshape(images * size * lat, 256),
            ).astype(BF16).reshape(2, size * r, 256)

    def kin_core(g):
        return remote(
            b.kall.at[lax.rem(g, 2), 1 - c], b.kland.at[g], b.ks.at[lax.rem(g, 2)], b.kr.at[g], c_dev
        )

    def kin_x(g):
        return remote(b.kland.at[g, 1 - x], b.kx.at[g], b.lxs.at[g], b.lxr.at[g], x_dev)

    def image_back(g):
        slot = lax.rem(g, 2)
        qb, dab = head_rows(q[g], hands), head_rows(b.dah[g], hands)
        kp, kl, vp, vl = k_[g, :reals], k_[g, reals:], v_[g, :reals], v_[g, reals:]
        pp, plat = soft(qb, kp, kl, real_keys(g), scale)
        gp, gl = nt(dab, vp), nt(dab, vl)
        delta = column_of(pp * gp) + column_of(plat * gl)
        sp, sl = (pp * (gp - delta)).astype(BF16), (plat * (gl - delta)).astype(BF16)
        v_[g, :reals] = tn(pp.astype(BF16), dab).astype(BF16)
        v_[g, reals:] = tn(plat.astype(BF16), dab).astype(BF16)
        k_[g, :reals] = (tn(sp, qb) * scale).astype(BF16)
        k_[g, reals:] = (tn(sl, qb) * scale).astype(BF16)
        q[g] = (own_columns(nn(sp, kp) + nn(sl, kl), hands) * scale).astype(BF16)
        for t in range(tiles):
            span = pl.ds(256 * t, 256)
            rows = nt(k_[g], wqkv[1, span, :]) + nt(v_[g], wqkv[2, span, :])
            tail = rows[reals:] + nt(q[g], wqkv[0, span, :])
            for e in range(size):
                b.kall[slot, e % 2, e // 2, :patches, span] = (
                    rows[e * patches : (e + 1) * patches].astype(BF16)
                )
                b.kall[slot, e % 2, e // 2, patches:, span] = (
                    tail[e * lat : (e + 1) * lat].astype(BF16)
                )
        kin_core(g).start()

    def kin_mid(g):
        kin_core(g).wait_recv()
        b.kland[g] = (
            b.kland[g].astype(F32) + b.kall[lax.rem(g, 2), c].astype(F32)
        ).astype(BF16)
        kin_x(g).start()

    def media_out(g):
        return pltpu.make_async_copy(media.at[g], out.media_grad.at[g], b.mouts.at[lax.rem(g, 2)])

    def kin_last(g):
        kin_x(g).wait_recv()
        total_ = b.kland[g, x].astype(F32) + b.kx[g].astype(F32)
        grad = total_[:patches]
        unit, scaled = unit_of(media[g])
        b.gsum[0:1, :] = b.gsum[0:1, :] + column_sum(grad * unit)
        b.gsum[1:2, :] = b.gsum[1:2, :] + column_sum(grad)
        media[g] = norm_back(grad, unit, scaled, media_gain)

        @pl.when(g >= 2)
        def _():
            media_out(g - 2).wait()

        media_out(g).start()
        grad = total_[patches:]
        unit, scaled = unit_of(latents[g])
        b.gsum[2:3, :] = b.gsum[2:3, :] + column_sum(grad * unit)
        b.gsum[3:4, :] = b.gsum[3:4, :] + column_sum(grad)
        latents[g] = b.dhid[aligned(g, lat)] + norm_back(grad, unit, scaled, latent_gain)

    def back(g):
        @pl.when(g >= 2)
        def _():
            kin_core(g - 2).wait_send()

        image_back(g)

        @pl.when(g >= 1)
        def _():
            kin_mid(g - 1)

    down, first_up, last_up, more_down = (ffn_sums[i] for i in (3, 4, 5, 6))
    between = [
        [(crosses[1], 1), (first_up, 0), (crosses[0], 2)],
        [(crosses[1], 2), (down, 1)],
        [(more_down, 1), (last_up, 0)],
    ]
    stages((down, 0), (crosses[0], 1), (more_down, 0))
    do_rows(0).forward()
    for j in range(crowds):
        head_grads(j)
        if j + 1 < crowds:
            do_rows(j + 1).forward()
        else:
            out_grad()
            wo_sum.send()
        each(j * crowd, (j + 1) * crowd, back)
        if between:
            stages(*between.pop(0))
    kin_mid(images - 1)
    for pairs in between:
        stages(*pairs)
    for k in range(3, chain - 1):
        stages((crosses[0], k), (crosses[1], k))
    cross_rows = [
        b.grads.at[pl.ds(4 + ups + (1 + k) * quarter, quarter)] for k in range(2)
    ]

    def flat(a, n_rows):
        return a.reshape(images * n_rows, cols)

    def qkv_grad(j):
        def tile(t):
            span = aligned(t, 256)
            rows_l = nl[:, :, span].reshape(images * size * lat, 256)
            if j == 0:
                wqkv[0, span, :] = tn(rows_l, flat(q[...], size * lat)).astype(BF16)
                return
            rows_m = nm[:, :, span].reshape(images * reals, 256)
            ref = (k_, v_)[j - 1]
            wqkv[j, span, :] = (
                tn(rows_m, flat(ref[:, :reals], reals))
                + tn(rows_l, flat(ref[:, reals:], size * lat))
            ).astype(BF16)

        each(0, tiles, tile)
        qkv_sums[j].send()

    for item, rows in zip(crosses, cross_rows):
        item.meet(rows)
    qkv_grad(0)
    qkv_grad(2)
    qkv_grad(1)
    part_pass(1)
    waiting = [(0, (images + 2) // 3)]
    waiting += [(waiting[0][1], 2 * waiting[0][1]), (2 * waiting[0][1], images)]

    def last_keys():
        if waiting:
            each(*waiting.pop(0), kin_last)

    q_sum, k_sum, v_sum = qkv_sums
    wo_sum.step(0)
    stages((down, 2), (more_down, 2), (first_up, 1))
    last_keys()
    stages((q_sum, 0), (last_up, 1), (first_up, 2))
    last_keys()
    stages((v_sum, 0))
    wo_sum.step(1)
    stages((last_up, 2), (q_sum, 1), (k_sum, 0))
    last_keys()
    stages((v_sum, 1), (q_sum, 2))
    wo_sum.step(2)
    stages((k_sum, 1), (v_sum, 2), (k_sum, 2))
    for k in range(3, chain - 1):
        stages((q_sum, k), (v_sum, k), (k_sum, k))
        if k > 2:
            stages((down, k), (more_down, k), (first_up, k), (last_up, k))
            wo_sum.step(k)
    down.last(b.grads.at[pl.ds(4 + ups, quarter)])
    more_down.last(b.grads.at[pl.ds(4 + ups + most, quarter)])
    first_up.last(b.grads.at[pl.ds(4, half)])
    last_up.last(b.grads.at[pl.ds(4 + half, half)])
    for span in waiting:
        each(*span, kin_last)
    for item, rows in zip(crosses, cross_rows):
        item.last(rows)
    lat_copy = pltpu.make_async_copy(latents, out.latents_grad, b.outs.at[1])
    lat_copy.start()

    def write_out(span, value):
        hidden[:, span] = hidden[:, span] + value

    part_end(1, write_out)
    out_copy = pltpu.make_async_copy(hidden, out.latents_out, b.outs.at[0])
    out_copy.start()

    def share(src, land, hold, s1, r1, total_to, land2, s2, r2):
        land[p] = src[...]
        near = []
        for k in range(1, size):
            to = lax.rem(p + k, size)
            near.append(remote(src, land.at[p], s1.at[to], r1.at[p], (d, to)))
        for copy in near:
            copy.start()
        for k in range(1, size):
            who = lax.rem(p + k, size)
            remote(src, land.at[who], s1.at[who], r1.at[who], (d, who)).wait_recv()
        value = land[0]
        for k in range(1, size):
            value = value + land[k]
        hold[...] = value
        land2[d] = value
        far = []
        for k in range(1, n):
            to = lax.rem(d + k, n)
            far.append(remote(hold, land2.at[d], s2.at[to], r2.at[d], (to, p)))
        for copy in far:
            copy.start()

        def finish():
            for k in range(1, n):
                who = lax.rem(d + k, n)
                remote(hold, land2.at[who], s2.at[who], r2.at[who], (who, p)).wait_recv()
            value = land2[0]
            for k in range(1, n):
                value = value + land2[k]
            total_to[...] = value
            for copy in near + far:
                copy.wait_send()

        return finish

    norms_done = share(b.gsum, b.nland, b.nhold, b.n1s, b.n1r, out.sums, b.dland, b.n2s, b.n2r)
    ends = []
    for j in (0, 2, 1):
        if j == 1:
            wo_sum.last()
        qkv_sums[j].last(b.fin.at[j])
        for k in range(1, size):
            to = lax.rem(p + k, size)
            copy = remote(
                b.fin.at[j, aligned(to, r)], b.grads.at[j, :, lanes(p)],
                b.fs.at[j, k], b.fr.at[j, k], (d, to),
            )
            copy.start()
            ends.append(copy)
        b.grads[j, :, lanes(p)] = b.fin[j, aligned(p, r)]
    squares = jnp.zeros((8, 128), F32)

    def squares_of(i, squares):
        for t in range(0, width, 128):
            tile = b.grads[i, :, t : t + 128]
            squares = squares + jnp.sum((tile * tile).reshape(r // 8, 8, 128), axis=0)
        return squares

    for i in range(4, 4 + 2 * ups):
        squares = squares_of(i, squares)
    wo_sum.have()
    for copy in ends:
        copy.wait_recv()
    for i in range(4):
        squares = squares_of(i, squares)
    b.sqr[...] = squares
    squares_done = share(
        b.sqr, b.sland, b.shold, b.s1s, b.s1r, out.squares, b.tland, b.s2s, b.s2r
    )
    for t in range(width // 128):
        b.turn[t] = b.grads[:, :, t * 128 : (t + 1) * 128].reshape(blocks * r, 128)
        for k in range(r):
            at = k * width + t * 128
            b.flat[:, at : at + 128] = b.turn[t, pl.ds(k, blocks, stride=r), :]
    grads_copy = pltpu.make_async_copy(b.flat, out.grads, b.outs.at[2])
    grads_copy.start()
    norms_done()
    for copy in swaps + ends:
        copy.wait_send()
    for rows in (lat_rows, cn_rows, dy_rows):
        rows.end()
    for j in range(crowds):
        media_rows(j).end()
        nf_rows(j).end()
        do_rows(j).end()
        hid_core(j).wait_send()
        hid_x(j).wait_send()
    parts_sent(0)
    parts_sent(1)
    each(max(images - 2, 0), images, lambda g: kin_core(g).wait_send())
    each(0, images, lambda g: kin_x(g).wait_send())
    for item in qkv_sums:
        item.sent()
    wo_sum.sent()
    for item in ffn_sums.values():
        item.sent()
    for item in crosses:
        item.sent()
    each(max(images - 2, 0), images, lambda g: media_out(g).wait())
    out_copy.wait()
    lat_copy.wait()
    grads_copy.wait()
    squares_done()


def column_of(a):
    return jnp.sum(a, axis=1, keepdims=True)


def whole_step(weights, media, latents, cot, mask, norms, n, size, hands, scale):
    g, patches, width = media.shape
    blocks, r = weights.shape[0], weights.shape[1] // width
    lat = latents.shape[1]
    scratch = buffers(n, size, g, patches, lat, width, FF // width, r)
    return pl.pallas_call(
        functools.partial(step_kernel, n, size, hands, scale, [k for k, _ in scratch]),
        name="whole_step",
        out_shape=(
            struct((g, patches, width), F32),
            struct((g, lat, width), F32),
            struct((g * lat, width), F32),
            struct(weights.shape, F32),
            struct((8, width), F32),
            struct((8, 128), F32),
        ),
        in_specs=[ANY] * 4 + [VMEM] + [ANY],
        out_specs=(ANY,) * 4 + (VMEM,) * 2,
        scratch_shapes=[s for _, s in scratch],
        compiler_params=params(8),
    )(weights, media, latents, cot, mask, norms)


def finish_kernel(steps, sums, squares, *refs):
    arrays, norms, passed = refs[:5], refs[5:9], refs[9:12]
    grad_norm, new_weights, new_norms, ffn, passed_out = (
        refs[12], refs[13:18], refs[18:22], refs[22], refs[23:26]
    )
    hold, low, through, load, store, moved = refs[26], refs[27], refs[28:31], refs[31], refs[32], refs[33]
    part = arrays[0].shape[1] // steps

    def span(c):
        return pl.ds(c * part, part)

    loads = [
        [
            pltpu.make_async_copy(src.at[:, span(c)], hold.at[i, :, span(c)], load.at[i, c])
            for i, src in enumerate(arrays)
        ]
        for c in range(steps)
    ]
    into = [pltpu.make_async_copy(a, t, moved.at[0, i]) for i, (a, t) in enumerate(zip(passed, through))]
    away = [
        pltpu.make_async_copy(t, a, moved.at[1, i]) for i, (t, a) in enumerate(zip(through, passed_out))
    ]
    for c in range(steps):
        for copy in loads[c]:
            copy.start()
    for copy in into:
        copy.start()
    norm_grads = sums[:6, :]
    square = jnp.sum(squares[...], axis=0, keepdims=True)
    square = jnp.sum(square, axis=1, keepdims=True)
    rest = jnp.sum(norm_grads * norm_grads, axis=0, keepdims=True)
    length = jnp.sqrt(square + jnp.sum(rest, axis=1, keepdims=True))
    clip = jnp.minimum(1.0, 1.0 / (length + 1e-06))
    grad_norm[...] = jnp.broadcast_to(length, grad_norm.shape)
    for ref, value in zip(
        new_norms, adamw_update(*(ref[...] for ref in norms), norm_grads, clip, 0.0)
    ):
        ref[...] = value
    ffn[...] = norm_grads[4:6]
    stores = []
    for c in range(steps):
        for copy in loads[c]:
            copy.wait()
        new = adamw_update(*(hold[i, :, span(c)] for i in range(5)), clip, 0.1)
        for i in range(4):
            hold[i, :, span(c)] = new[i]
        low[:, span(c)] = new[0].astype(BF16)
        for i, out in enumerate(new_weights):
            src = hold.at[i, :, span(c)] if i < 4 else low.at[:, span(c)]
            copy = pltpu.make_async_copy(src, out.at[:, span(c)], store.at[i, c])
            copy.start()
            stores.append(copy)
        if c < 3:
            into[c].wait()
            away[c].start()
    for copy in stores + away:
        copy.wait()


def finish(sums, squares, weights, grads, norms, passed):
    steps = 4
    rows, flat = grads.shape
    six, width = norms[0].shape
    return pl.pallas_call(
        functools.partial(finish_kernel, steps),
        name="finish",
        in_specs=[VMEM] * 2 + [ANY] * 5 + [VMEM] * 4 + [ANY] * 3,
        out_specs=[VMEM] + [ANY] * 5 + [VMEM] * 5 + [ANY] * 3,
        out_shape=[struct((1, 128), F32)] + [struct(grads.shape, F32)] * 4
        + [struct(grads.shape, BF16)] + [struct((six, width), F32)] * 4
        + [struct((2, width), F32)] + [struct(a.shape, F32) for a in passed],
        scratch_shapes=[
            pltpu.VMEM((5, rows, flat), F32), pltpu.VMEM((rows, flat), BF16),
        ] + [pltpu.VMEM(a.shape, F32) for a in passed]
        + [DMA((5, steps)), DMA((5, steps)), DMA((2, 3))],
        compiler_params=pltpu.CompilerParams(vmem_limit_bytes=VMEM_LIMIT),
    )(sums, squares, *weights, grads, *norms, *passed)


def norm_parts(values, gain_row, shift_row):
    average = jnp.mean(values, axis=-1, keepdims=True)
    centred = values - average
    spread_ = jnp.mean(centred * centred, axis=-1, keepdims=True)
    scaled = lax.rsqrt(spread_ + 1e-05)
    unit_rows = centred * scaled
    return (unit_rows * gain_row + shift_row, unit_rows, scaled)


def norm_back(grad_out, unit_rows, scaled, gain_row):
    inner_grad = grad_out * gain_row
    plain_mean = jnp.mean(inner_grad, axis=-1, keepdims=True)
    cross_mean = jnp.mean(inner_grad * unit_rows, axis=-1, keepdims=True)
    return scaled * (inner_grad - plain_mean - unit_rows * cross_mean)


def gain_terms(grad_out, unit_rows):
    width = grad_out.shape[-1]
    flat_grad = grad_out.reshape(-1, width)
    flat_unit = unit_rows.reshape(-1, width)
    return [jnp.sum(flat_grad * flat_unit, axis=0), jnp.sum(flat_grad, axis=0)]


def exact_gelu(values):
    return jax.nn.gelu(values, approximate=False)


def adamw_update(parameter, first_m, second_m, average, gradient, factor, decay_rate):
    clipped = gradient * factor
    new_first = 0.9 * first_m + 0.1 * clipped
    new_second = 0.999 * second_m + 0.001 * clipped * clipped
    first_hat = new_first / (1.0 - 0.9**STEP)
    second_hat = new_second / (1.0 - 0.999**STEP)
    new_param = parameter - 0.02 * (
        first_hat / (jnp.sqrt(second_hat) + 1e-08) + decay_rate * parameter
    )
    new_avg = 0.8 * average + 0.2 * new_param
    return (new_param, new_first, new_second, new_avg)


def dot32(spec, a, b):
    return jnp.einsum(spec, a, b, preferred_element_type=F32)


def general_step(n, size, media_tokens, patch_mask, latents, cotangent, weights, weights_first,
              weights_second, weights_average, norm_params, norm_first, norm_second, norm_average):
    g, patches, width = media_tokens.shape
    lat = latents.shape[1]
    blocks = weights.shape[0]
    r = width // (n * size)
    cols = width // size
    hands = HEADS // size
    scale = 1.0 / math.sqrt(width // HEADS)
    ups = FF // width
    own = g * lat
    media_gain, latent_gain, ffn_gain = 1.0 + norm_params[0], 1.0 + norm_params[2], 1.0 + norm_params[4]

    held = weights.astype(BF16).reshape(blocks, r, width)
    qs = held[:3].reshape(3, r, size, cols).transpose(2, 0, 1, 3)
    media_norm, media_unit, media_scale = norm_parts(media_tokens, media_gain, norm_params[1])
    latent_norm, latent_unit, latent_scale = norm_parts(latents, latent_gain, norm_params[3])
    cot = cotangent.reshape(own, width)
    count_rows = (g + 15) // 16 * 16
    counts = jnp.sum((patch_mask > 0).astype(F32), axis=1)
    counts = jnp.broadcast_to(jnp.pad(counts, (0, count_rows - g))[:, None], (count_rows, 128))

    wqkv, wo, up, dn, nm, nl, dy, cn = spread(
        qs, held[3], held[4 : 4 + ups], held[4 + ups :],
        media_norm.astype(BF16), latent_norm.astype(BF16), cot.astype(BF16), counts, n, size,
    )
    wqkv = wqkv.reshape(3, width, cols)
    wo = wo.reshape(width, width)
    up = up.reshape(-1, width)
    dn = dn.reshape(-1, width)
    nm = nm.reshape(g * size * patches, width)
    nl = nl.reshape(g * size * lat, width)
    dy = dy.reshape(size * own, width)
    real = jnp.sum(cn[:, :g, 0], axis=0).astype(jnp.int32)

    def by_image(a):
        return a.astype(BF16).reshape(g, -1, cols)

    q = by_image(dot32("rd,de->re", nl, wqkv[0]))
    kp, kl = by_image(dot32("rd,de->re", nm, wqkv[1])), by_image(dot32("rd,de->re", nl, wqkv[1]))
    vp, vl = by_image(dot32("rd,de->re", nm, wqkv[2])), by_image(dot32("rd,de->re", nl, wqkv[2]))
    mixed = attend(real, q, kp, kl, vp, vl, hands, scale)
    ab = to_rows(mixed.reshape(g, size, lat, cols), size, 1).reshape(own, width)

    hidden = latents.reshape(own, width) + dot32("rd,de->re", ab, wo)
    ffn_norm, ffn_unit, ffn_scale = norm_parts(hidden, ffn_gain, norm_params[5])
    nf = join_rows(ffn_norm.astype(BF16), size, 2).reshape(size * own, width)
    u = dot32("rd,fd->rf", nf, up)
    active, pull = jax.vjp(exact_gelu, u)
    gb = active.astype(BF16)
    y_part = dot32("rf,fd->rd", gb, dn).astype(BF16)
    du = pull(dot32("rd,fd->rf", dy, dn))[0].astype(BF16)
    f_part = dot32("rf,fd->rd", du, up).astype(BF16)
    g_dn = dot32("rf,rd->fd", gb, dy).astype(BF16)
    g_up = dot32("rf,rd->fd", du, nf).astype(BF16)
    both = split_rows(jnp.stack([y_part, f_part]).reshape(2, 2, 2, own, width), 3)
    latents_out = (hidden + both[0]).reshape(g, lat, width)
    d_ffn = both[1]
    ffn_terms = gain_terms(d_ffn, ffn_unit)
    d_hidden = cot + norm_back(d_ffn, ffn_unit, ffn_scale, ffn_gain)

    do = d_hidden.astype(BF16)
    g_wo = dot32("rd,re->de", ab, do).astype(BF16)
    da = dot32("re,de->rd", do, wo).astype(BF16).reshape(g, lat, width)
    da = to_heads(da, size, 4).reshape(g, size * lat, cols)
    dq, dkp, dkl, dvp, dvl = attend_back(real, q, kp, kl, vp, vl, da, hands, scale)

    def flat(a):
        return a.reshape(-1, cols)

    dq, dkp, dkl, dvp, dvl = flat(dq), flat(dkp), flat(dkl), flat(dvp), flat(dvl)
    g_qkv = jnp.stack([
        dot32("rd,re->de", nl, dq),
        dot32("rd,re->de", nm, dkp) + dot32("rd,re->de", nl, dkl),
        dot32("rd,re->de", nm, dvp) + dot32("rd,re->de", nl, dvl),
    ]).astype(BF16)
    d_nm = (dot32("re,de->rd", dkp, wqkv[1]) + dot32("re,de->rd", dvp, wqkv[2])).astype(BF16)
    d_nl = (
        dot32("re,de->rd", dkl, wqkv[1]) + dot32("re,de->rd", dvl, wqkv[2])
        + dot32("re,de->rd", dq, wqkv[0])
    ).astype(BF16)

    oq, ow, ou, od, d_media, d_latent = collect(
        g_qkv.reshape(3, n, size, r, cols), g_wo.reshape(n, 2, 2, r, width),
        g_up.reshape(ups, n, r, width), g_dn.reshape(ups, n, r, width),
        d_nm.reshape(g, 2, 2, patches, width), d_nl.reshape(g, 2, 2, lat, width), n, size,
    )
    media_grad = norm_back(d_media, media_unit, media_scale, media_gain)
    latents_grad = d_hidden.reshape(g, lat, width) + norm_back(
        d_latent, latent_unit, latent_scale, latent_gain
    )
    grads = jnp.concatenate([
        oq.transpose(1, 2, 0, 3).reshape(3, r, width), ow[None], ou, od,
    ])
    square = jnp.broadcast_to(jnp.sum(grads * grads), (width,))
    rows = jnp.stack(
        gain_terms(d_media, media_unit) + gain_terms(d_latent, latent_unit) + ffn_terms
        + [square, jnp.zeros_like(square)]
    )
    sums = total(rows, n, size)
    return latents_out, media_grad, latents_grad, grads, sums[:6], sums[6, 0]


def on_device(n, size, media_tokens, patch_mask, latents, cotangent, weights, weights_first,
              weights_second, weights_average, norm_params, norm_first, norm_second, norm_average):
    g, patches, width = media_tokens.shape
    lat = latents.shape[1]
    r = width // (n * size)
    arrays = (
        media_tokens, patch_mask, latents, cotangent, weights, weights_first, weights_second,
        weights_average, norm_params, norm_first, norm_second, norm_average,
    )
    if r % 16 or lat % 16 or size != 4 or n != 2 * size or FF != 4 * width:
        latents_out, media_grad, latents_grad, grads, norm_grads, square = general_step(
            n, size, *arrays
        )
    else:
        media_grad, latents_grad, latents_out, grads, sums, squares = whole_step(
            weights, media_tokens, latents, cotangent, patch_mask, norm_params,
            n, size, HEADS // size, 1.0 / math.sqrt(width // HEADS),
        )
        done = finish(
            sums, squares, (weights, weights_first, weights_second, weights_average), grads,
            (norm_params, norm_first, norm_second, norm_average),
            (latents_out.reshape(g, lat, width), media_grad, latents_grad),
        )
        return (
            *done[11:14], done[0][0, 0], done[1], done[5], *done[2:5], *done[6:11],
        )
    grad_norm = jnp.sqrt(square + jnp.sum(norm_grads * norm_grads))
    clip = jnp.minimum(1.0, 1.0 / (grad_norm + 1e-06))
    new_w, new_first, new_second, new_avg = adamw_update(
        weights, weights_first, weights_second, weights_average,
        grads.reshape(weights.shape), clip, 0.1,
    )
    new_n, new_nf, new_ns, new_na = adamw_update(
        norm_params, norm_first, norm_second, norm_average, norm_grads, clip, 0.0
    )
    return (
        latents_out, media_grad, latents_grad, grad_norm, new_w, new_w.astype(BF16), new_first,
        new_second, new_avg, new_n, new_nf, new_ns, new_na, norm_grads[4:6],
    )


def solution(mesh):
    n, size = mesh.shape["dp"], mesh.shape["patch"]
    rows, weight = P("dp", "patch", None), P(None, ("dp", "patch"))
    return jax.shard_map(
        functools.partial(on_device, n, size),
        mesh=mesh,
        in_specs=(rows, P("dp", "patch"), rows, rows) + (weight,) * 4 + (P(),) * 4,
        out_specs=(rows, rows, rows, P()) + (weight,) * 5 + (P(),) * 5,
        check_vma=False,
    )
```
